32 devices in a mesh: group: 2 (over core), dp: 16 (over z, y, x).
Axes of the slice: x: 2, y: 2, z: 4, core: 2. Of those that a mesh axis runs over, the one named last changes fastest.
Arguments:
- patches: bfloat16 [2, 16, 512, 768], P(None, 'dp'), may hold values from -6 to 6
- segments: int32 [2, 16, 512], P(None, 'dp'), may hold values from 0 to 4, never falling along the last dimension, each value on 1 to 196 neighbouring positions
- positions: int32 [2, 16, 320], P(None, 'dp'), may hold values from 0 to 511, as said below
- owners: int32 [10752], replicated, may hold values from 0 to 10751, each once
- master: float32 [10752, 768], P(('group', 'dp')), may hold values from -0.21875 to 0.21875
- moment_one: float32 [10752, 768], P(('group', 'dp')), may hold values from -2.3841858e-06 to 2.3841858e-06
- moment_two: float32 [10752, 768], P(('group', 'dp')), may hold values from 3.8e-15 to 1.5e-14
- teacher: float32 [10752, 768], P(('group', 'dp')), may hold values from -0.21875 to 0.21875
- gains: float32 [4, 768], replicated, may hold values from 0.5 to 1.5
- gain_one: float32 [4, 768], replicated, may hold values from -2.2888184e-05 to 2.2888184e-05
- gain_two: float32 [4, 768], replicated, may hold values from 7.7e-13 to 3.1e-12
- teacher_gains: float32 [4, 768], replicated, may hold values from 0.5 to 1.5
- step_count: int32 [1], replicated, may hold values from 2 to 20
Outputs:
- loss_out: float32 [1], replicated
- clip_norm: float32 [1], replicated
- moment_one_new: float32 [10752, 768], P(('group', 'dp'))
- moment_two_new: float32 [10752, 768], P(('group', 'dp'))
- master_new: float32 [10752, 768], P(('group', 'dp'))
- teacher_new: float32 [10752, 768], P(('group', 'dp'))
- gain_one_new: float32 [4, 768], replicated
- gain_two_new: float32 [4, 768], replicated
The draws below stay inside these ranges and needn't reach their ends.
Inputs may be any that keep to these rules, and one draw needn't show every extreme that they name: Within one row the 320 positions are distinct slots. `segments`: along a row segment ids never fall; id 4 is the padding at the row's end; each id covers 1 to 196 slots and some id covers exactly 196. owners is a permutation.
All inputs are finite; a program needn't handle non-finite values.
Results may differ from the reference program's by a relative error of at most 0.008.
The reference program's roundings to bfloat16 on the way count: a program that leaves them out, or rounds other values in their place, can miss the bound.
Values may be sent and summed in bfloat16 or wider, within the bound.
A program may use at most 320 MiB of HBM per device.

```python
import math
import jax
import jax.numpy as jnp
import numpy as np
from jax import lax

D = 768
HEADS = 12
HEAD_DIM = 64
FF = 3072
SLOTS = 512
IMGS = 4
SEG_MOST = 196
MASKED = 320
MICRO_BATCHES = 2
ROWS = 16
NBLK = 10752


def draw_positions(key, part):
    key_list = jax.random.split(key, MICRO_BATCHES * ROWS)

    def choose_slots(one_key):
        return jax.random.permutation(one_key, SLOTS)[:MASKED].astype(jnp.int32)
    return jax.vmap(choose_slots)(key_list).reshape(MICRO_BATCHES, ROWS, MASKED)


def shard_levels(own_key, extent, pieces, low, top_value):
    factor_of, own = 1.0, jax.random.fold_in(own_key, 6)
    for axis_at, shards_of in pieces:
        draws = jnp.exp(jax.random.uniform(jax.random.fold_in(own, axis_at), (shards_of,), jnp.float32, low / len(pieces), top_value / len(pieces)))
        factor_of = factor_of * jnp.repeat(draws, extent[axis_at] // shards_of).reshape([-1 if axis == axis_at else 1 for axis in range(len(extent))])
    return factor_of


def split_up(number_of, total, reach, lean):
    portions = [(1 << 20) // math.isqrt(rank ** lean) + 1 for rank in range(2, number_of + 1)]
    surplus, holding = total - reach - (number_of - 1), [1] * (number_of - 1)
    while surplus > 0:
        free = [i for i in range(number_of - 1) if holding[i] < reach]
        whole, budget = sum([portions[i] for i in free]), surplus
        for i in free:
            extra = min(reach - holding[i], max(1, budget * portions[i] // whole), surplus)
            holding[i] = holding[i] + extra
            surplus = surplus - extra
    return np.array([reach] + holding)


def ragged(stream_key, number_of, total, bound, slope):
    if number_of == 2:
        one = jax.random.randint(stream_key, (), max(1, total - bound), min(bound, total - 1) + 1)
        return jnp.stack([one, total - one])
    tallies = jnp.asarray(split_up(number_of, total, bound, slope), jnp.int32)
    pairs = (number_of - 1) // 2
    donor, sink = tallies[1:1 + 2 * pairs:2], tallies[2:2 + 2 * pairs:2]
    slack = jnp.minimum(donor - 1, bound - sink)
    passed = jax.random.randint(jax.random.fold_in(stream_key, 1), (pairs,), 0, 1 << 20) % (slack + 1)
    tallies = tallies.at[1:1 + 2 * pairs:2].set(donor - passed).at[2:2 + 2 * pairs:2].set(sink + passed)
    return tallies[jax.random.permutation(jax.random.fold_in(stream_key, 2), number_of)]


def scatter_about(rng, dims, width, limit, cuts=(), kind=jnp.bfloat16):
    loudness = shard_levels(rng, dims, cuts, -0.22, 0.18) if cuts else 1.0
    result = jax.random.normal(rng, dims, jnp.float32) * width * loudness
    return jnp.minimum(jnp.maximum(result, -limit), limit).astype(kind)


def setup_inputs(seed: int = 0) -> dict:
    splits = jax.random.split(jax.random.key(seed), 14)
    patches = scatter_about(splits[0], (MICRO_BATCHES, ROWS, SLOTS, D), 1.0, 6.0, ((1, 16),))
    segments = jax.vmap(lambda own: jnp.searchsorted(jnp.cumsum(ragged(own, IMGS + 1, SLOTS, SEG_MOST, 2)), jnp.arange(SLOTS), side="right"))(jax.random.split(splits[1], MICRO_BATCHES * ROWS)).reshape((MICRO_BATCHES, ROWS, SLOTS)).astype(jnp.int32)
    positions = draw_positions(jax.random.fold_in(splits[13], 71), 0)
    owners = jax.random.permutation(splits[3], NBLK).astype(jnp.int32)
    master = scatter_about(splits[4], (NBLK, D), D ** -0.5, 0.21875, ((0, 32),), jnp.float32)
    moment_one = scatter_about(splits[5], (NBLK, D), (1.5e-7), 2.384185791015625e-06, ((0, 32),), jnp.float32)
    moment_two = jnp.clip(jnp.exp(math.log(1.499999973677505e-14) - 1.37304915 * jax.random.uniform(splits[6], (NBLK, D), jnp.float32) ** shard_levels(splits[6], (NBLK, D), ((0, 32),), -0.2, 0.2)), 3.79999986555371e-15, 1.499999973677505e-14)
    teacher = scatter_about(splits[7], (NBLK, D), D ** -0.5, 0.21875, ((0, 32),), jnp.float32)
    gains = jnp.clip(1.0 + 0.1 * jax.random.normal(splits[8], (4, D), jnp.float32), 0.5, 1.5)
    gain_one = scatter_about(splits[9], (4, D), (1.5e-6), 2.288818359375e-05, (), jnp.float32)
    gain_two = jnp.clip(jnp.exp(jax.random.uniform(splits[10], (4, D), jnp.float32, math.log(7.700000034284449e-13), math.log(3.100000074349185e-12))), 7.700000034284449e-13, 3.100000074349185e-12)
    teacher_gains = jnp.clip(1.0 + 0.1 * jax.random.normal(splits[11], (4, D), jnp.float32), 0.5, 1.5)
    step_count = jax.random.randint(splits[12], (1,), 2, 21).astype(jnp.int32)
    return dict(patches=patches, segments=segments, positions=positions, owners=owners, master=master, moment_one=moment_one, moment_two=moment_two, teacher=teacher, gains=gains, gain_one=gain_one, gain_two=gain_two, teacher_gains=teacher_gains, step_count=step_count)


@jax.custom_vjp
def low(v):
    return lax.optimization_barrier(v.astype(jnp.bfloat16)).astype(jnp.float32)

@jax.custom_vjp
def low_back(v):
    return v

def low_keep(v):
    return (low(v), None)

def low_pass(kept, grad):
    return (grad,)

def back_keep(v):
    return (v, None)

def back_low(kept, grad):
    return (low(grad),)
low.defvjp(low_keep, low_pass)
low_back.defvjp(back_keep, back_low)
HIGH = lax.Precision.HIGHEST
SOFTMAX_TEMPER = 0.05
CLIP = 0.004
RATE = 0.05
BETA_ONE = 0.9
BETA_TWO = 0.999
ADAM_EPS = 1e-08
DECAY = 0.05
EMA_KEEP = 0.9
MASK_FILL = -1000000000.0

def matrix_product(first_op, second_op):
    return jnp.dot(first_op, second_op, precision=HIGH)

def layer_norm(tensor, gain_vec):
    centre = tensor - lax.optimization_barrier(jnp.mean(tensor, axis=-1, keepdims=True))
    return centre * lax.rsqrt(lax.optimization_barrier(jnp.mean(centre * centre, axis=-1, keepdims=True)) + 1e-06) * gain_vec

def normalize_unit(rows_in):
    return rows_in * lax.rsqrt(lax.optimization_barrier(jnp.sum(rows_in * rows_in, axis=-1, keepdims=True)) + 1e-06)

def pooled_features(tensor, segment_index):
    member = (segment_index[None, :] == jnp.arange(IMGS, dtype=jnp.int32)[:, None]).astype(jnp.float32)
    return matrix_product(member, tensor) / lax.optimization_barrier(jnp.sum(member, axis=1, keepdims=True))

def unpack(flat_rows):
    return (flat_rows[0:D], flat_rows[D:2 * D], flat_rows[2 * D:3 * D], flat_rows[3 * D:6 * D].reshape(D, 3 * D), flat_rows[6 * D:6 * D + FF].reshape(D, FF), flat_rows[6 * D + FF:6 * D + 2 * FF])

def encode(flat_rows, gain_set, patch_row, segment_index, slot_mask, student):
    proj_embed, proj_out, proj_head, proj_qkv, proj_up, proj_down = unpack(flat_rows)
    embedded = low_back(matrix_product(patch_row, proj_embed))
    if student:
        embedded = jnp.where(slot_mask[:, None] > 0, gain_set[3][None, :], embedded)
    attn_in = low(layer_norm(embedded, gain_set[0]))
    triple = low(low_back(matrix_product(attn_in, proj_qkv))).reshape(SLOTS, 3, HEADS, HEAD_DIM)
    scores = low_back(jnp.einsum('qhd,khd->hqk', triple[:, 0], triple[:, 1], precision=HIGH) * HEAD_DIM ** (-0.5))
    scores = jnp.where((segment_index[:, None] == segment_index[None, :])[None], scores, MASK_FILL)
    probs = low(jax.nn.softmax(scores, axis=-1))
    mixed_heads = jnp.einsum('hqk,khd->qhd', probs, triple[:, 2], precision=HIGH).reshape(SLOTS, D)
    middle = embedded + low_back(matrix_product(low(low_back(mixed_heads)), proj_out))
    hidden = low_back(matrix_product(low(layer_norm(middle, gain_set[1])), proj_up))
    block_out = middle + low_back(matrix_product(low(jax.nn.gelu(hidden, approximate=True)), proj_down))
    if student:
        return low_back(matrix_product(low(layer_norm(block_out, gain_set[2])), proj_head))
    return low(layer_norm(block_out, 1.0))

def row_loss(flat_rows, gain_set, patch_row, segment_index, places, target, memory_bank_rows, row_idx):
    slot_mask = jnp.zeros((SLOTS,), jnp.float32).at[places].set(1.0)
    prediction_head = encode(flat_rows, gain_set, patch_row, segment_index, slot_mask, True)
    valid_mask = (segment_index[places] < IMGS).astype(jnp.float32)
    differ = prediction_head[places] - target[places]
    magnitude = jnp.abs(differ)
    huber_term = jnp.where(magnitude < 1.0, 0.5 * differ * differ, magnitude - 0.5)
    regress = jnp.sum(valid_mask[:, None] * huber_term)
    class_logits = low_back(matrix_product(low(normalize_unit(pooled_features(prediction_head, segment_index))), memory_bank_rows.T)) / SOFTMAX_TEMPER
    label_ids = row_idx * IMGS + jnp.arange(IMGS, dtype=jnp.int32)
    picked = jnp.take_along_axis(class_logits, label_ids[:, None], axis=1)[:, 0]
    contrast = jnp.sum(jax.nn.logsumexp(class_logits, axis=-1) - picked)
    return (regress, contrast)

def adam_update(weight, first_state, second_state, gradient, step_value, decay_rate):
    first_state = BETA_ONE * first_state + (1.0 - BETA_ONE) * gradient
    second_state = BETA_TWO * second_state + (1.0 - BETA_TWO) * gradient * gradient
    fix_one = 1.0 - jnp.power(BETA_ONE, step_value)
    fix_two = 1.0 - jnp.power(BETA_TWO, step_value)
    update = first_state / fix_one / (jnp.sqrt(second_state / fix_two) + ADAM_EPS)
    return (weight - RATE * (update + decay_rate * weight), first_state, second_state)

def reference(patches, segments, positions, owners, master, moment_one, moment_two, teacher, gains, gain_one, gain_two, teacher_gains, step_count):
    inverse = jnp.zeros((NBLK,), jnp.int32).at[owners].set(jnp.arange(NBLK, dtype=jnp.int32))
    student_flat = low(master)[inverse]
    teacher_flat = low(teacher)[inverse]
    listed_count = jnp.float32(MASKED * ROWS * MICRO_BATCHES)
    patch_data = patches.astype(jnp.float32)
    target_list = []
    bank_list = []
    for batch_idx in range(MICRO_BATCHES):

        def teacher_row(inputs):
            patch_row, segment_index = inputs
            target = encode(teacher_flat, teacher_gains, patch_row, segment_index, None, False)
            return (target, low(normalize_unit(pooled_features(target, segment_index))))
        target, memory_bank_rows = lax.map(teacher_row, (patch_data[batch_idx], segments[batch_idx]))
        target_list.append(target)
        bank_list.append(memory_bank_rows.reshape(ROWS * IMGS, D))

    def objective(flat_rows, gain_set):
        loss_value = jnp.zeros((), jnp.float32)
        for batch_idx in range(MICRO_BATCHES):
            memory_bank_rows = bank_list[batch_idx]

            def row_term(inputs):
                patch_row, segment_index, places, target, row_idx = inputs
                return row_loss(flat_rows, gain_set, patch_row, segment_index, places, target, memory_bank_rows, row_idx)
            regress, contrast = lax.map(jax.checkpoint(row_term), (patch_data[batch_idx], segments[batch_idx], positions[batch_idx], target_list[batch_idx], jnp.arange(ROWS, dtype=jnp.int32)))
            loss_value = loss_value + jnp.sum(regress) / (listed_count * D) + jnp.sum(contrast) / (IMGS * ROWS * MICRO_BATCHES)
        return loss_value
    loss_value, pullback = jax.vjp(objective, student_flat, gains)
    grad_flat, grad_gains = pullback(jnp.ones_like(loss_value))
    grad_own = grad_flat[owners]
    grad_norm = jnp.sqrt(jnp.sum(grad_own * grad_own) + jnp.sum(grad_gains * grad_gains))
    factor = jnp.minimum(1.0, CLIP / grad_norm)
    step_value = step_count[0].astype(jnp.float32)
    master_new, one_new, two_new = adam_update(master, moment_one, moment_two, grad_own * factor, step_value, DECAY)
    gone_new, gtwo_new = adam_update(gains, gain_one, gain_two, grad_gains * factor, step_value, 0.0)[1:]
    teacher_new = EMA_KEEP * teacher + (1.0 - EMA_KEEP) * master_new
    return (loss_value.reshape(1), grad_norm.reshape(1), one_new, two_new, master_new, teacher_new, gone_new, gtwo_new)
```

```python
import functools

import jax
import jax.numpy as jnp
from jax import lax
from jax.experimental import pallas as pl
from jax.experimental.pallas import tpu as pltpu
from jax.sharding import PartitionSpec as P

HEADS = 12
HEAD_DIM = 64
IMGS = 4
MASKED = 320
MICRO_BATCHES = 2
LANES = 128
SUBLANES = 8

SOFTMAX_TEMPER = 0.05
CLIP = 0.004
RATE = 0.05
BETA_ONE = 0.9
BETA_TWO = 0.999
ADAM_EPS = 1e-08
DECAY = 0.05
EMA_KEEP = 0.9
MASK_FILL = -1000000000.0

BF = jnp.bfloat16
F32 = jnp.float32
VMEM_LIMIT = 67_000_000
GELU_A = 0.7978845608028654
GELU_B = 0.044715


def nn(a, b):
    return jnp.dot(a, b, preferred_element_type=F32)


def nt(a, b):
    return lax.dot_general(a, b, (((1,), (1,)), ((), ())), preferred_element_type=F32)


def unit_list(width, inner):
    cuts = inner // width
    return (
        [(0, 1), (width, 1), (2 * width, 1)]
        + [(3 * width + j, 3) for j in range(3)]
        + [(6 * width + j, cuts) for j in range(cuts)]
        + [(6 * width + inner + width * j, 1) for j in range(cuts)]
    )


def any_spec():
    return pl.BlockSpec(memory_space=pl.ANY)


def smem_spec():
    return pl.BlockSpec(memory_space=pltpu.SMEM)


def place_kernel(units, role, owners, teach, learn, out, rows_scr, inbuf, stage, outbuf, in_sem, out_sem):
    blocks, rows, width = teach.shape
    cols = width // LANES

    def fetch(b, slot):
        @pl.when(role[0] == 0)
        def _():
            pltpu.make_async_copy(teach.at[b], inbuf.at[slot], in_sem.at[slot]).start()

        @pl.when(role[0] != 0)
        def _():
            pltpu.make_async_copy(learn.at[b], inbuf.at[slot], in_sem.at[slot]).start()

    fetch(0, 0)

    def block(b, carry):
        slot = lax.rem(b, 2)
        pltpu.make_async_copy(teach.at[b], inbuf.at[slot], in_sem.at[slot]).wait()

        @pl.when(b + 1 < blocks)
        def _():
            fetch(b + 1, 1 - slot)

        for c in range(cols):
            stage[pl.ds(c, rows, stride=SUBLANES), :] = inbuf[slot, :, c * LANES : (c + 1) * LANES].astype(F32)

        def move(r, carry):
            dst = pl.multiple_of(owners[b * rows + r] * SUBLANES, SUBLANES)
            src = pl.multiple_of(r * SUBLANES, SUBLANES)
            rows_scr[pl.ds(dst, SUBLANES), :] = stage[pl.ds(src, SUBLANES), :]
            return carry

        return lax.fori_loop(0, rows, move, carry, unroll=14)

    lax.fori_loop(0, blocks, block, 0)
    for u, (first, step) in enumerate(units):
        slot = u % 2
        if u >= 2:
            pltpu.make_async_copy(outbuf.at[slot], out.at[u - 2], out_sem.at[slot]).wait()
        for c in range(cols):
            outbuf[slot, :, c * LANES : (c + 1) * LANES] = rows_scr[
                pl.ds(first * SUBLANES + c, width, stride=step * SUBLANES), :
            ].astype(BF)
        pltpu.make_async_copy(outbuf.at[slot], out.at[u], out_sem.at[slot]).start()
    for u in (len(units) - 2, len(units) - 1):
        pltpu.make_async_copy(outbuf.at[u % 2], out.at[u], out_sem.at[u % 2]).wait()


def place_weights(role, owners, teach, learn, units):
    blocks, rows, width = teach.shape
    total = owners.shape[0]
    return pl.pallas_call(
        functools.partial(place_kernel, units),
        name="place_weights",
        out_shape=jax.ShapeDtypeStruct((len(units), width, width), BF),
        in_specs=[smem_spec(), smem_spec(), any_spec(), any_spec()],
        out_specs=any_spec(),
        scratch_shapes=[
            pltpu.VMEM((total * SUBLANES, LANES), F32),
            pltpu.VMEM((2, rows, width), BF),
            pltpu.VMEM((rows * SUBLANES, LANES), F32),
            pltpu.VMEM((2, width, width), BF),
            pltpu.SemaphoreType.DMA((2,)),
            pltpu.SemaphoreType.DMA((2,)),
        ],
        compiler_params=pltpu.CompilerParams(vmem_limit_bytes=VMEM_LIMIT),
    )(role, owners, teach, learn)


def layer_stats(tensor):
    centre = tensor - jnp.mean(tensor, axis=-1, keepdims=True)
    scaled = lax.rsqrt(jnp.mean(centre * centre, axis=-1, keepdims=True) + 1e-06)
    return centre * scaled, scaled


def column_of(row):
    n = row.shape[1]
    eye = lax.broadcasted_iota(jnp.int32, (n, n), 0) == lax.broadcasted_iota(jnp.int32, (n, n), 1)
    return jnp.sum(jnp.where(eye, row, 0), axis=1, keepdims=True)


def flag_column(pos, slots):
    hit = lax.broadcasted_iota(jnp.int32, (slots, pos.shape[1]), 0) == pos
    return jnp.max(jnp.where(hit, 1, 0), axis=1, keepdims=True)


def fill_bias(bias, seg_col, seg_row):
    bias[...] = jnp.where(seg_col == seg_row, 0.0, MASK_FILL)


def half(x, h):
    low = lax.broadcasted_iota(jnp.int32, (1, LANES), 1) < HEAD_DIM
    keep = low if h == 0 else jnp.logical_not(low)
    return jnp.where(keep, x, jnp.zeros_like(x))


def fwd_kernel(role, patch, seg, pos, gain, w_hbm, e_out, qkv, lse, o_out, x1_out, x2_out, tgt, bank, w, bias, sem):
    i = pl.program_id(0)
    slots, width = patch.shape[1:]
    pieces = w_hbm.shape[0]
    cuts = (pieces - 6) // 2
    order = [0, 3, 4, 5, 1]
    for j in range(cuts):
        order += [6 + j, 6 + cuts + j]

    @pl.when(i == 0)
    def _():
        for u in order:
            pltpu.make_async_copy(w_hbm.at[u], w.at[u], sem.at[u]).start()

    def need(u):
        @pl.when(i == 0)
        def _():
            pltpu.make_async_copy(w_hbm.at[u], w.at[u], sem.at[u]).wait()

    seg_row = seg[0]
    seg_col = column_of(seg_row)
    fill_bias(bias, seg_col, seg_row)
    flags = flag_column(pos[0], slots) * role[0]
    need(0)
    e = nn(patch[0], w[0])
    e = jnp.where(flags > 0, gain[3:4, :], e)
    e_out[0] = e
    a = (layer_stats(e)[0] * gain[0:1, :]).astype(BF)
    for j in range(3):
        need(3 + j)
        qkv[j] = nn(a, w[3 + j]).astype(BF)

    def pair(p, carry):
        cs = pl.ds(pl.multiple_of(p * LANES, LANES), LANES)
        q2, k2, v2 = qkv[0, :, cs], qkv[1, :, cs], qkv[2, :, cs]
        k2 = k2 * jnp.asarray(HEAD_DIM**-0.5, BF)
        v_t = v2.T
        outs = []
        for h in range(2):
            s = nt(half(k2, h), q2) + bias[...]
            top = jnp.max(s, axis=0, keepdims=True)
            ex = jnp.exp(s - top)
            total = jnp.sum(ex, axis=0, keepdims=True)
            lse[0, pl.ds(2 * p + h, 1), :] = top + jnp.log(total)
            probs = (ex * (1.0 / total)).astype(BF)
            outs.append(nn(v_t[h * HEAD_DIM : (h + 1) * HEAD_DIM, :], probs))
        o_out[0, :, cs] = jnp.concatenate(outs, axis=0).T.astype(BF)
        return carry

    lax.fori_loop(0, HEADS // 2, pair, 0)
    need(1)
    x1 = e_out[0] + nn(o_out[0], w[1])
    x1_out[0] = x1
    a2 = (layer_stats(x1)[0] * gain[1:2, :]).astype(BF)
    acc = x1
    for j in range(cuts):
        need(6 + j)
        hid = nn(a2, w[6 + j])
        act = (hid * (0.5 * (1.0 + jnp.tanh(GELU_A * (hid + GELU_B * hid * hid * hid))))).astype(BF)
        need(6 + cuts + j)
        acc = acc + nn(act, w[6 + cuts + j])
    x2_out[0] = acc

    @pl.when(role[0] == 0)
    def _():
        t = layer_stats(x2_out[0])[0].astype(BF)
        tgt[0] = t
        t = t.astype(F32)
        for m in range(IMGS):
            inside = seg_col == m
            size = jnp.sum(jnp.where(inside, 1.0, 0.0), axis=0, keepdims=True)
            pooled = jnp.sum(jnp.where(inside, t, 0.0), axis=0, keepdims=True) / size
            unit = pooled * lax.rsqrt(jnp.sum(pooled * pooled, axis=-1, keepdims=True) + 1e-06)
            bank[0, m : m + 1, :] = unit.astype(BF)


def forward(role, patch, seg, pos, gain, w):
    batches, slots, width = patch.shape
    pieces = w.shape[0]
    tok = lambda dt: jax.ShapeDtypeStruct((batches, slots, width), dt)
    row = pl.BlockSpec((1, slots, width), lambda i: (i, 0, 0))
    return pl.pallas_call(
        fwd_kernel,
        name="forward",
        grid=(batches,),
        out_shape=(
            tok(F32),
            jax.ShapeDtypeStruct((3, batches * slots, width), BF),
            jax.ShapeDtypeStruct((batches, HEADS, slots), F32),
            tok(BF),
            tok(F32),
            tok(F32),
            tok(BF),
            jax.ShapeDtypeStruct((batches, IMGS, width), BF),
        ),
        in_specs=[
            smem_spec(),
            row,
            pl.BlockSpec((1, 1, slots), lambda i: (i, 0, 0)),
            pl.BlockSpec((1, 1, pos.shape[2]), lambda i: (i, 0, 0)),
            pl.BlockSpec((4, width), lambda i: (0, 0)),
            any_spec(),
        ],
        out_specs=(
            row,
            pl.BlockSpec((3, slots, width), lambda i: (0, i, 0)),
            pl.BlockSpec((1, HEADS, slots), lambda i: (i, 0, 0)),
            row,
            row,
            row,
            row,
            pl.BlockSpec((1, IMGS, width), lambda i: (i, 0, 0)),
        ),
        scratch_shapes=[
            pltpu.VMEM((pieces, width, width), BF),
            pltpu.VMEM((slots, slots), F32),
            pltpu.SemaphoreType.DMA((pieces,)),
        ],
        compiler_params=pltpu.CompilerParams(vmem_limit_bytes=VMEM_LIMIT),
    )(role, patch, seg, pos, gain, w)


def norm_back(grad_out, normed, scaled, gain_vec):
    grad_hat = grad_out * gain_vec
    inner = jnp.mean(grad_hat * normed, axis=-1, keepdims=True)
    grad_in = scaled * (grad_hat - jnp.mean(grad_hat, axis=-1, keepdims=True) - normed * inner)
    return grad_in, jnp.sum(grad_out * normed, axis=0, keepdims=True)


def bwd_kernel(
    listed, place, seg, pos, gain, e_in, qkv, lse, x1_in, x2_in, tgt, banks, w_hbm,
    head_out, attn_out, ffn_out, act_out, de_out, mid_out, pred_out, dqkv, du_out, down_out, small,
    w, bias, top_scr, pool_scr, sem,
):
    i = pl.program_id(0)
    role = place[0]
    slots, width = e_in.shape[1:]
    pieces = w_hbm.shape[0]
    cuts = (pieces - 6) // 2

    @pl.when(role == 0)
    def _():
        small[...] = jnp.zeros_like(small)

    @pl.when(role != 0)
    def _():
        order = [2]
        for j in range(cuts):
            order += [6 + cuts + j, 6 + j]
        order += [1, 3, 4, 5]

        @pl.when(i == 0)
        def _():
            for u in order:
                pltpu.make_async_copy(w_hbm.at[u], w.at[u - 1], sem.at[u]).start()
            small[...] = jnp.zeros_like(small)

        def need(u):
            @pl.when(i == 0)
            def _():
                pltpu.make_async_copy(w_hbm.at[u], w.at[u - 1], sem.at[u]).wait()

        seg_row = seg[0]
        seg_col = column_of(seg_row)
        fill_bias(bias, seg_col, seg_row)
        flags = flag_column(pos[0], slots)
        n3, r3 = layer_stats(x2_in[0])
        head_in = (n3 * gain[2:3, :]).astype(BF)
        head_out[0] = head_in
        need(2)
        pred = nn(head_in, w[1])
        valid = jnp.where(seg_col < IMGS, flags, 0).astype(F32)
        diff = pred - tgt[0].astype(F32)
        size = jnp.abs(diff)
        huber = jnp.where(size < 1.0, 0.5 * diff * diff, size - 0.5)
        regress = jnp.sum(jnp.sum(valid * huber, axis=1, keepdims=True), axis=0, keepdims=True)
        count = listed[0] * width
        grad_pred = valid * (jnp.clip(diff, -1.0, 1.0) / count)
        pool_scr[...] = jnp.zeros_like(pool_scr)
        for m in range(IMGS):
            inside = seg_col == m
            tally = jnp.sum(jnp.where(inside, 1.0, 0.0), axis=0, keepdims=True)
            pool_scr[m : m + 1, :] = jnp.sum(jnp.where(inside, pred, 0.0), axis=0, keepdims=True) / tally
        pooled = pool_scr[...]
        length = lax.rsqrt(jnp.sum(pooled * pooled, axis=-1, keepdims=True) + 1e-06)
        unit = pooled * length
        memory = banks[0]
        choices = memory.shape[0]
        logits = nt(unit.astype(BF), memory) / SOFTMAX_TEMPER
        row_id = lax.broadcasted_iota(jnp.int32, logits.shape, 0)
        real = row_id < IMGS
        picked = jnp.where(
            real & (lax.broadcasted_iota(jnp.int32, logits.shape, 1) == place[1] * IMGS + row_id), 1.0, 0.0
        )
        peak = jnp.max(logits, axis=-1, keepdims=True)
        ex = jnp.exp(logits - peak)
        total = jnp.sum(ex, axis=-1, keepdims=True)
        each = peak + jnp.log(total) - jnp.sum(logits * picked, axis=-1, keepdims=True)
        contrast = jnp.sum(jnp.where(real[:, 0:1], each, 0.0), axis=0, keepdims=True)
        scale = choices * MICRO_BATCHES
        grad_logits = (jnp.where(real, ex / total - picked, 0.0) / scale / SOFTMAX_TEMPER).astype(BF)
        grad_unit = nn(grad_logits, memory)
        grad_pool = length * (grad_unit - unit * jnp.sum(grad_unit * unit, axis=1, keepdims=True))
        pool_scr[...] = grad_pool
        for m in range(IMGS):
            inside = seg_col == m
            tally = jnp.sum(jnp.where(inside, 1.0, 0.0), axis=0, keepdims=True)
            grad_pred = grad_pred + jnp.where(inside, pool_scr[m : m + 1, :] / tally, 0.0)
        low = grad_pred.astype(BF)
        pred_out[0] = low
        loss = regress / count + contrast / scale
        small[4:5, :] += jnp.broadcast_to(loss, (1, width))
        grad_top, gain_three = norm_back(nt(low, w[1]), n3, r3, gain[2:3, :])
        small[2:3, :] += gain_three
        top_scr[...] = grad_top
        down = grad_top.astype(BF)
        down_out[0] = down
        n2, r2 = layer_stats(x1_in[0])
        ffn_in = (n2 * gain[1:2, :]).astype(BF)
        ffn_out[0] = ffn_in
        acc = None
        for j in range(cuts):
            need(6 + cuts + j)
            grad_act = nt(down, w[5 + cuts + j])
            need(6 + j)
            hid = nn(ffn_in, w[5 + j])
            th = jnp.tanh(GELU_A * (hid + GELU_B * hid * hid * hid))
            cdf = 0.5 * (1.0 + th)
            act_out[j] = (hid * cdf).astype(BF)
            slope = cdf + hid * (0.5 * (1.0 - th * th)) * (GELU_A * (1.0 + 3.0 * GELU_B * hid * hid))
            du = (grad_act * slope).astype(BF)
            du_out[j] = du
            part = nt(du, w[5 + j])
            acc = part if acc is None else acc + part
        grad_ffn, gain_two = norm_back(acc, n2, r2, gain[1:2, :])
        small[1:2, :] += gain_two
        mid = top_scr[...] + grad_ffn
        top_scr[...] = mid
        mid_low = mid.astype(BF)
        mid_out[0] = mid_low
        need(1)
        de_out[0] = nt(mid_low, w[0]).astype(BF)

        def pair(p, carry):
            cs = pl.ds(pl.multiple_of(p * LANES, LANES), LANES)
            q2, k2, v2, g2 = qkv[0, :, cs], qkv[1, :, cs], qkv[2, :, cs], de_out[0, :, cs]
            k_scaled = k2 * jnp.asarray(HEAD_DIM**-0.5, BF)
            k_t = k2.T
            dq, dk, dv = [], 0.0, 0.0
            for h in range(2):
                s = nt(half(k_scaled, h), q2) + bias[...]
                probs = jnp.exp(s - lse[0, pl.ds(2 * p + h, 1), :])
                dp = nt(half(v2, h), g2)
                centre = jnp.sum(probs * dp, axis=0, keepdims=True)
                ds = (probs * (dp - centre)).astype(BF)
                dv = dv + nn(probs.astype(BF), half(g2, h))
                dk = dk + nn(ds, half(q2, h))
                dq.append(nn(k_t[h * HEAD_DIM : (h + 1) * HEAD_DIM, :], ds))
            dqkv[0, :, cs] = (jnp.concatenate(dq, axis=0) * HEAD_DIM**-0.5).T.astype(BF)
            dqkv[1, :, cs] = (dk * HEAD_DIM**-0.5).astype(BF)
            dqkv[2, :, cs] = dv.astype(BF)
            return carry

        lax.fori_loop(0, HEADS // 2, pair, 0)
        acc = None
        for j in range(3):
            need(3 + j)
            part = nt(dqkv[j], w[2 + j])
            acc = part if acc is None else acc + part
        n1, r1 = layer_stats(e_in[0])
        attn_out[0] = (n1 * gain[0:1, :]).astype(BF)
        grad_attn, gain_one = norm_back(acc, n1, r1, gain[0:1, :])
        small[0:1, :] += gain_one
        start = top_scr[...] + grad_attn
        hidden_slot = flags > 0
        small[3:4, :] += jnp.sum(jnp.where(hidden_slot, start, 0.0), axis=0, keepdims=True)
        de_out[0] = jnp.where(hidden_slot, 0.0, start).astype(BF)


def backward(listed, place, seg, pos, gain, saved, tgt, banks, w):
    e, qkv, lse, x1, x2 = saved
    batches, slots, width = e.shape
    pieces = w.shape[0]
    cuts = (pieces - 6) // 2
    once = pl.Buffered(1)
    tok = lambda n: jax.ShapeDtypeStruct((n, batches * slots, width), BF)
    row_in = pl.BlockSpec((1, slots, width), lambda i: (i, 0, 0), pipeline_mode=once)
    piece = lambda n: pl.BlockSpec((n, slots, width), lambda i: (0, i, 0))
    return pl.pallas_call(
        bwd_kernel,
        name="backward",
        grid=(batches,),
        out_shape=(
            tok(1), tok(1), tok(1), tok(cuts), tok(1), tok(1), tok(1), tok(3), tok(cuts), tok(1),
            jax.ShapeDtypeStruct((SUBLANES, width), F32),
        ),
        in_specs=[
            smem_spec(),
            smem_spec(),
            pl.BlockSpec((1, 1, slots), lambda i: (i, 0, 0)),
            pl.BlockSpec((1, 1, pos.shape[2]), lambda i: (i, 0, 0)),
            pl.BlockSpec((4, width), lambda i: (0, 0)),
            row_in,
            pl.BlockSpec((3, slots, width), lambda i: (0, i, 0), pipeline_mode=once),
            pl.BlockSpec((1, HEADS, slots), lambda i: (i, 0, 0)),
            row_in,
            row_in,
            row_in,
            pl.BlockSpec((1,) + banks.shape[1:], lambda i: (i, 0, 0), pipeline_mode=once),
            any_spec(),
        ],
        out_specs=(
            piece(1), piece(1), piece(1), piece(cuts), piece(1), piece(1), piece(1), piece(3), piece(cuts), piece(1),
            pl.BlockSpec((SUBLANES, width), lambda i: (0, 0)),
        ),
        scratch_shapes=[
            pltpu.VMEM((pieces - 1, width, width), BF),
            pltpu.VMEM((slots, slots), F32),
            pltpu.VMEM((slots, width), F32),
            pltpu.VMEM((SUBLANES, width), F32),
            pltpu.SemaphoreType.DMA((pieces,)),
        ],
        compiler_params=pltpu.CompilerParams(vmem_limit_bytes=VMEM_LIMIT),
    )(listed, place, seg, pos, gain, e, qkv, lse, x1, x2, tgt, banks, w)


def grads_kernel(
    units, plan, cuts, role, owners, patch, mixed, head, attn, ffn, act, de, mid, pred, dqkv, du, down, out,
    rows_scr, x_buf, x_t, g_buf, stage, outbuf, x_sem, g_sem, out_sem,
):
    blocks, rows, width = out.shape
    cols = width // LANES
    lefts = {"patch": patch, "mixed": mixed, "head": head, "attn": attn, "ffn": ffn, "act": act}
    rights = {"de": de, "mid": mid, "pred": pred, "dqkv": dqkv, "du": du, "down": down}

    @pl.when(role[0] == 0)
    def _():
        outbuf[...] = jnp.zeros_like(outbuf)

        def put(b, carry):
            pltpu.make_async_copy(outbuf.at[0], out.at[b], out_sem.at[0]).start()
            return carry

        def done(b, carry):
            pltpu.make_async_copy(outbuf.at[0], out.at[b], out_sem.at[0]).wait()
            return carry

        lax.fori_loop(0, blocks, put, 0)
        lax.fori_loop(0, blocks, done, 0)

    @pl.when(role[0] != 0)
    def _():
        lcopies, rcopies = [], []
        lkeys, rkeys = [], []
        steps = []
        for u, (left, right) in enumerate(plan):
            if not lkeys or lkeys[-1] != left:
                slot = len(lkeys) % 2
                lcopies.append(pltpu.make_async_copy(lefts[left[0]].at[left[1]], x_buf.at[slot], x_sem.at[slot]))
                lkeys.append(left)
                fresh_l = True
            else:
                fresh_l = False
            if not rkeys or rkeys[-1] != right:
                slot = len(rkeys) % 2
                rcopies.append(pltpu.make_async_copy(rights[right[0]].at[right[1]], g_buf.at[slot], g_sem.at[slot]))
                rkeys.append(right)
                fresh_r = True
            else:
                fresh_r = False
            steps.append((u, len(lkeys) - 1, fresh_l, len(rkeys) - 1, fresh_r))
        lcopies[0].start()
        rcopies[0].start()
        for u, li, fresh_l, ri, fresh_r in steps:
            if fresh_l:
                lcopies[li].wait()
                if li + 1 < len(lcopies):
                    lcopies[li + 1].start()
                x_t[...] = x_buf[li % 2].T
            if fresh_r:
                rcopies[ri].wait()
                if ri + 1 < len(rcopies):
                    rcopies[ri + 1].start()
            first, step = units[u]
            wide = 2 * LANES

            def tile(n, carry):
                part = nn(x_t[...], g_buf[ri % 2, :, pl.ds(pl.multiple_of(n * wide, wide), wide)])
                for c in range(2):
                    rows_scr[pl.ds(first * SUBLANES + 2 * n + c, width, stride=step * SUBLANES), :] = part[
                        :, c * LANES : (c + 1) * LANES
                    ]
                return carry

            lax.fori_loop(0, width // wide, tile, 0)

        def block(b, carry):
            slot = lax.rem(b, 2)

            def move(r, carry):
                src = pl.multiple_of(owners[b * rows + r] * SUBLANES, SUBLANES)
                dst = pl.multiple_of(r * SUBLANES, SUBLANES)
                stage[pl.ds(dst, SUBLANES), :] = rows_scr[pl.ds(src, SUBLANES), :]
                return carry

            lax.fori_loop(0, rows, move, 0, unroll=14)

            @pl.when(b >= 2)
            def _():
                pltpu.make_async_copy(outbuf.at[slot], out.at[b - 2], out_sem.at[slot]).wait()

            for c in range(cols):
                outbuf[slot, :, c * LANES : (c + 1) * LANES] = stage[pl.ds(c, rows, stride=SUBLANES), :].astype(BF)
            pltpu.make_async_copy(outbuf.at[slot], out.at[b], out_sem.at[slot]).start()
            return carry

        lax.fori_loop(0, blocks, block, 0)
        for b in (blocks - 2, blocks - 1):
            pltpu.make_async_copy(outbuf.at[b % 2], out.at[b], out_sem.at[b % 2]).wait()


def weight_grads(role, owners, lefts, rights, units, blocks):
    tokens, width = lefts[0].shape[1:]
    cuts = lefts[-1].shape[0]
    total = owners.shape[0]
    rows = total // blocks
    plan = (
        [(("patch", 0), ("de", 0)), (("mixed", 0), ("mid", 0)), (("head", 0), ("pred", 0))]
        + [(("attn", 0), ("dqkv", j)) for j in range(3)]
        + [(("ffn", 0), ("du", j)) for j in range(cuts)]
        + [(("act", j), ("down", 0)) for j in range(cuts)]
    )
    return pl.pallas_call(
        functools.partial(grads_kernel, units, plan, cuts),
        name="weight_grads",
        out_shape=jax.ShapeDtypeStruct((blocks, rows, width), BF),
        in_specs=[smem_spec(), smem_spec()] + [any_spec()] * 12,
        out_specs=any_spec(),
        scratch_shapes=[
            pltpu.VMEM((total * SUBLANES, LANES), F32),
            pltpu.VMEM((2, tokens, width), BF),
            pltpu.VMEM((width, tokens), BF),
            pltpu.VMEM((2, tokens, width), BF),
            pltpu.VMEM((rows * SUBLANES, LANES), F32),
            pltpu.VMEM((2, rows, width), BF),
            pltpu.SemaphoreType.DMA((2,)),
            pltpu.SemaphoreType.DMA((2,)),
            pltpu.SemaphoreType.DMA((2,)),
        ],
        compiler_params=pltpu.CompilerParams(vmem_limit_bytes=VMEM_LIMIT),
    )(role, owners, *lefts, *rights)


def shifted(block, axis, distance):
    devices = range(lax.axis_size(axis))
    route = [(i - distance, i) for i in devices if i - distance in devices]
    return lax.ppermute(block, axis, route)


def adam_update(weight, first_state, second_state, gradient, step_value, decay_rate):
    first_state = BETA_ONE * first_state + (1.0 - BETA_ONE) * gradient
    second_state = BETA_TWO * second_state + (1.0 - BETA_TWO) * gradient * gradient
    fix_one = 1.0 - jnp.power(BETA_ONE, step_value)
    fix_two = 1.0 - jnp.power(BETA_TWO, step_value)
    update = first_state / fix_one / (jnp.sqrt(second_state / fix_two) + ADAM_EPS)
    return (weight - RATE * (update + decay_rate * weight), first_state, second_state)


def body(
    patches,
    segments,
    positions,
    owners,
    master,
    moment_one,
    moment_two,
    teacher,
    gains,
    gain_one,
    gain_two,
    teacher_gains,
    step_count,
):
    core = lax.axis_index("group")
    width = patches.shape[3]
    slots = patches.shape[2]
    row_total = owners.shape[0]
    inner = (row_total - 6 * width) // 2
    units = unit_list(width, inner)
    devices = lax.axis_size("group") * lax.axis_size("dp")
    own_rows = row_total // devices
    role = core.astype(jnp.int32).reshape(1)
    place = jnp.stack([core, lax.axis_index("dp")]).astype(jnp.int32)
    listed = jnp.full((1,), MASKED * lax.axis_size("dp") * MICRO_BATCHES, F32)

    learn = lax.all_gather(master.astype(BF), ("group", "dp"), axis=0)
    teach = lax.all_gather(teacher.astype(BF), ("group", "dp"), axis=0)
    w = place_weights(role, owners, teach, learn, units)
    gain_set = jnp.where(core == 1, gains, teacher_gains)
    patch = patches[:, 0]
    seg = segments
    pos = positions
    e, qkv, lse, mixed, x1, x2, tgt, bank = forward(role, patch, seg, pos, gain_set, w)
    tgt, bank = shifted((tgt, bank), "group", 1)
    banks = lax.all_gather(bank, "dp", axis=1, tiled=True)
    head, attn, ffn, act, de, mid, pred, dqkv, du, down, small = backward(
        listed, place, seg, pos, gain_set, (e, qkv, lse, x1, x2), tgt, banks, w
    )
    flat = lambda a: a.reshape(1, MICRO_BATCHES * slots, width)
    blocked = weight_grads(
        role,
        owners,
        (flat(patch), flat(mixed), head, attn, ffn, act),
        (de, mid, pred, dqkv, du, down),
        units,
        devices,
    )
    owned_grad = lax.psum_scatter(blocked, ("group", "dp"), scatter_dimension=0, tiled=True)
    owned_grad = owned_grad.reshape(own_rows, width).astype(F32)
    square_own = jnp.sum(owned_grad * owned_grad)
    small, square_sum = lax.psum((small, square_own), ("group", "dp"))
    gain_sum, loss_sum = small[0:4], small[4, 0]
    grad_norm = jnp.sqrt(square_sum + jnp.sum(gain_sum * gain_sum))
    factor = jnp.minimum(1.0, CLIP / grad_norm)
    step_value = step_count[0].astype(F32)
    master_new, one_new, two_new = adam_update(
        master, moment_one, moment_two, owned_grad * factor, step_value, DECAY
    )
    gone_new, gtwo_new = adam_update(gains, gain_one, gain_two, gain_sum * factor, step_value, 0.0)[1:]
    teacher_new = EMA_KEEP * teacher + (1.0 - EMA_KEEP) * master_new
    return (
        loss_sum.reshape(1),
        grad_norm.reshape(1),
        one_new,
        two_new,
        master_new,
        teacher_new,
        gone_new,
        gtwo_new,
    )


def solution(mesh):
    rows = P(("group", "dp"), None)
    in_specs = (
        P(None, "dp", None, None),
        P(None, "dp", None),
        P(None, "dp", None),
        P(),
        rows,
        rows,
        rows,
        rows,
        P(),
        P(),
        P(),
        P(),
        P(),
    )
    out_specs = (P(), P(), rows, rows, rows, rows, P(), P())
    return jax.shard_map(body, mesh=mesh, in_specs=in_specs, out_specs=out_specs, check_vma=False)
```

```python
import functools

import jax
import jax.numpy as jnp
from jax import lax
from jax.experimental import pallas as pl
from jax.experimental.pallas import tpu as pltpu
from jax.sharding import PartitionSpec as P

HEADS = 12
HEAD_DIM = 64
IMGS = 4
MASKED = 320
MICRO_BATCHES = 2
LANES = 128
SUBLANES = 8

SOFTMAX_TEMPER = 0.05
CLIP = 0.004
RATE = 0.05
BETA_ONE = 0.9
BETA_TWO = 0.999
ADAM_EPS = 1e-08
DECAY = 0.05
EMA_KEEP = 0.9
MASK_FILL = -1000000000.0

BF = jnp.bfloat16
F32 = jnp.float32
VMEM_LIMIT = 67_000_000
GELU_A = 0.7978845608028654
GELU_B = 0.044715


def nn(a, b):
    return jnp.dot(a, b, preferred_element_type=F32)


def nt(a, b):
    return lax.dot_general(a, b, (((1,), (1,)), ((), ())), preferred_element_type=F32)


def unit_list(width, inner):
    cuts = inner // width
    return (
        [(0, 1), (width, 1), (2 * width, 1)]
        + [(3 * width + j, 3) for j in range(3)]
        + [(6 * width + j, cuts) for j in range(cuts)]
        + [(6 * width + inner + width * j, 1) for j in range(cuts)]
    )


def any_spec():
    return pl.BlockSpec(memory_space=pl.ANY)


def smem_spec():
    return pl.BlockSpec(memory_space=pltpu.SMEM)


MESH = pl.DeviceIdType.MESH
KERNEL_CHIPS = 16


def chip_grid(chips):
    sizes, turn, left, prime = [1, 1, 1], 0, chips, 2
    while left > 1:
        while left % prime:
            prime += 1
        sizes[turn % 3] *= prime
        turn += 1
        left //= prime
    return tuple(sizes)


def strides_of(grid):
    return (grid[1] * grid[2], grid[2], 1)


def coords_of(index, grid):
    return (index // (grid[1] * grid[2]), lax.rem(index // grid[2], grid[1]), lax.rem(index, grid[2]))


def guarded(conditions, action):
    conditions = [c for c in conditions if c is not None]
    if not conditions:
        return action()
    both = conditions[0]
    for c in conditions[1:]:
        both = jnp.logical_and(both, c)
    pl.when(both)(action)


def lanes_of(width):
    unit = width // 6
    orders = [((1, 0, 2), 2), ((2, 0, 1), 2), ((0, 2, 1), 1), ((0, 1, 2), 1)]
    routes, first = [], 0
    for order, share in orders:
        routes.append((order, first, share * unit))
        first += share * unit
    return routes


def offsets(length):
    if length <= 2:
        return list(range(length))
    return [0] + [sign * far for far in range(1, length) for sign in (1, -1)]


def route_events(grid, routes):
    events = []
    for c, (order, _, _) in enumerate(routes):
        stack = [()]
        for d in order:
            stack = [r + (o,) for r in stack for o in offsets(grid[d])]
        events += [(sum(abs(o) * 2**i for i, o in enumerate(r)), c, r) for r in stack]
    return [(c, r) for _, c, r in sorted(events, key=lambda e: e[0])]


def onward(grid, order, r):
    last = max([i for i in range(3) if r[i]], default=-1)
    outs = []
    if last >= 0 and grid[order[last]] > 2:
        outs.append((order[last], 1 if r[last] > 0 else -1))
    for d in order[last + 1 :]:
        if grid[d] == 2:
            outs.append((d, 1))
        elif grid[d] > 2:
            outs += [(d, 1), (d, -1)]
    return outs


def neighbour(me, coords, grid, d, sign):
    step = strides_of(grid)[d]
    if grid[d] == 2:
        return me + (1 - 2 * coords[d]) * step, None
    place = coords[d] + sign
    return me + sign * step, jnp.logical_and(place >= 0, place < grid[d])


def origin(me, coords, grid, order, r):
    index, conditions = me, []
    for d, o in zip(order, r):
        if o == 0:
            continue
        step = strides_of(grid)[d]
        if grid[d] == 2:
            index = index + (1 - 2 * coords[d]) * step
        else:
            place = coords[d] - o
            index = index - o * step
            conditions.append(jnp.logical_and(place >= 0, place < grid[d]))
    return index, conditions


def slot_of(grid, d, sign):
    first = sum([1 if n <= 2 else 2 for n in grid[:d]])
    return first if grid[d] <= 2 or sign > 0 else first + 1


def slots_of(grid):
    return sum([1 if n <= 2 else 2 for n in grid])


def greet(me, coords, grid, group):
    barrier = pltpu.get_barrier_semaphore()
    near = [neighbour(me, coords, grid, d, s) for d in range(3) for s in ((1,) if grid[d] == 2 else (1, -1)) if grid[d] > 1]
    for index, there in near:
        guarded([there], lambda: pl.semaphore_signal(barrier, 1, device_id={"dp": index}, device_id_type=MESH))
    pl.semaphore_signal(barrier, 1, device_id={"group": 1 - group}, device_id_type=MESH)
    pl.semaphore_wait(barrier, 1 + sum([1 if there is None else there.astype(jnp.int32) for _, there in near]))


def gather_kernel(grid, both, out, swap_sem, send_sem, recv_sem):
    group, me = lax.axis_index("group"), lax.axis_index("dp")
    coords = coords_of(me, grid)
    routes = lanes_of(both.shape[2])
    events = route_events(grid, routes)
    keep = pltpu.make_async_copy(both.at[group], out.at[me, group], swap_sem.at[2])
    keep.start()
    greet(me, coords, grid, group)
    swap = pltpu.make_async_remote_copy(
        both.at[1 - group], out.at[me, group], swap_sem.at[0], swap_sem.at[1], {"group": 1 - group}, MESH
    )
    swap.start()
    keep.wait()
    swap.wait()

    def visit(c, r, act):
        order, first, wide = routes[c]
        block, real = origin(me, coords, grid, order, r)
        part = out.at[block, :, :, first : first + wide]

        def run():
            copies = []
            for d, sign in onward(grid, order, r):
                index, there = neighbour(me, coords, grid, d, sign)
                copies.append(
                    (
                        there,
                        pltpu.make_async_remote_copy(
                            part,
                            part,
                            send_sem.at[c, slot_of(grid, d, sign), block],
                            recv_sem.at[c, block],
                            {"dp": index},
                            MESH,
                        ),
                    )
                )
            act(part, recv_sem.at[c, block], any(r), copies)

        guarded(real, run)

    def forward_on(part, arrival_sem, remote, copies):
        if remote:
            pltpu.make_async_remote_copy(part, part, swap_sem.at[0], arrival_sem, {"dp": me}, MESH).wait_recv()
        for there, copy in copies:
            guarded([there], copy.start)

    def finish(part, arrival_sem, remote, copies):
        for there, copy in copies:
            guarded([there], copy.wait_send)

    for c, r in events:
        visit(c, r, forward_on)
    for c, r in events:
        visit(c, r, finish)


def gather_weights(both, chips):
    grid = chip_grid(chips)
    _, rows, width = both.shape
    return pl.pallas_call(
        functools.partial(gather_kernel, grid),
        name="gather_weights",
        out_shape=jax.ShapeDtypeStruct((chips, 2, rows, width), BF),
        in_specs=[pl.BlockSpec(memory_space=pltpu.VMEM)],
        out_specs=any_spec(),
        scratch_shapes=[
            pltpu.SemaphoreType.DMA((3,)),
            pltpu.SemaphoreType.DMA((4, slots_of(grid), chips)),
            pltpu.SemaphoreType.DMA((4, chips)),
        ],
        compiler_params=pltpu.CompilerParams(
            collective_id=1, has_side_effects=True, vmem_limit_bytes=VMEM_LIMIT
        ),
    )(both)


def reduce_kernel(grid, blocked, out, acc, heard, load_sem, half_sem, send_sem, recv_sem):
    group, me = lax.axis_index("group"), lax.axis_index("dp")
    coords = coords_of(me, grid)
    rows, width = out.shape
    routes = lanes_of(width)
    events = route_events(grid, routes)[::-1]
    tall = max([t for t in range(16, 49, 16) if rows % t == 0], default=rows)

    def spot(c, r):
        return tuple(r[routes[c][0].index(d)] for d in range(3))

    firsts = list(dict.fromkeys([spot(c, r) for c, r in events]))
    greet(me, coords, grid, group)

    def load(where, act):
        block, real = origin(me, coords, grid, (0, 1, 2), where)
        local = pltpu.make_async_copy(blocked.at[1, block], acc.at[block], load_sem.at[block])
        half = pltpu.make_async_remote_copy(
            blocked.at[0, block], acc.at[block], half_sem.at[0, block], half_sem.at[1, block], {"group": 1 - group}, MESH
        )
        guarded(real, lambda: act(local, half))

    def load_start(local, half):
        @pl.when(group == 1)
        def _():
            half.start()
            local.start()

    def load_wait(local, half):
        @pl.when(group == 1)
        def _():
            local.wait()

        @pl.when(group == 0)
        def _():
            half.wait_recv()

    def load_end(local, half):
        @pl.when(group == 1)
        def _():
            half.wait_send()

    for where in firsts:
        load(where, load_start)

    def parent(c, r, block):
        order, first, wide = routes[c]
        i = max([i for i in range(3) if r[i]])
        sign = 1 if r[i] > 0 else -1
        index, _ = neighbour(me, coords, grid, order[i], -sign)
        slot = slot_of(grid, order[i], sign)
        return pltpu.make_async_remote_copy(
            acc.at[block, :, first : first + wide],
            heard.at[slot, block, :, first : first + wide],
            send_sem.at[c, block],
            recv_sem.at[c, slot, block],
            {"dp": index},
            MESH,
        )

    def visit(c, r):
        order, first, wide = routes[c]
        block, real = origin(me, coords, grid, order, r)

        def run():
            children = [(slot_of(grid, d, s), neighbour(me, coords, grid, d, s)[1]) for d, s in onward(grid, order, r)]
            for slot, there in children:
                part = heard.at[slot, block, :, first : first + wide]
                arrival = pltpu.make_async_remote_copy(
                    part, part, send_sem.at[c, block], recv_sem.at[c, slot, block], {"dp": me}, MESH
                )
                guarded([there], arrival.wait_recv)

            if any(r):
                for slot, there in children:

                    def total(slot=slot):
                        def piece(k, carry):
                            at = (pl.ds(pl.multiple_of(k * tall, tall), tall), slice(first, first + wide))
                            acc[(block,) + at] = (
                                acc[(block,) + at].astype(F32) + heard[(slot, block) + at].astype(F32)
                            ).astype(BF)
                            return carry

                        lax.fori_loop(0, rows // tall, piece, 0)

                    guarded([there], total)
                parent(c, r, block).start()
            else:

                def first_piece(k, carry):
                    at = (pl.ds(pl.multiple_of(k * tall, tall), tall), slice(first, first + wide))
                    out[at] = acc[(block,) + at].astype(F32)
                    return carry

                lax.fori_loop(0, rows // tall, first_piece, 0)
                for slot, there in children:

                    def total(slot=slot):
                        def piece(k, carry):
                            at = (pl.ds(pl.multiple_of(k * tall, tall), tall), slice(first, first + wide))
                            out[at] = out[at] + heard[(slot, block) + at].astype(F32)
                            return carry

                        lax.fori_loop(0, rows // tall, piece, 0)

                    guarded([there], total)

        guarded(real, run)

    ready = set()
    for c, r in events:
        if spot(c, r) not in ready:
            ready.add(spot(c, r))
            load(spot(c, r), load_wait)
        visit(c, r)
    for c, r in events:
        if any(r):
            block, real = origin(me, coords, grid, routes[c][0], r)
            guarded(real, parent(c, r, block).wait_send)
    for where in firsts:
        load(where, load_end)


def reduce_grads(blocked, chips):
    grid = chip_grid(chips)
    _, _, rows, width = blocked.shape
    return pl.pallas_call(
        functools.partial(reduce_kernel, grid),
        name="reduce_grads",
        out_shape=jax.ShapeDtypeStruct((rows, width), F32),
        in_specs=[any_spec()],
        out_specs=pl.BlockSpec(memory_space=pltpu.VMEM),
        scratch_shapes=[
            pltpu.VMEM((chips, rows, width), BF),
            pltpu.VMEM((slots_of(grid), chips, rows, width), BF),
            pltpu.SemaphoreType.DMA((chips,)),
            pltpu.SemaphoreType.DMA((2, chips)),
            pltpu.SemaphoreType.DMA((4, chips)),
            pltpu.SemaphoreType.DMA((4, slots_of(grid), chips)),
        ],
        compiler_params=pltpu.CompilerParams(
            collective_id=2, has_side_effects=True, vmem_limit_bytes=VMEM_LIMIT
        ),
    )(blocked)


def exchange_kernel(tgt, bank, tgt_out, banks, tgt_sem, send_sem, recv_sem):
    group, me = lax.axis_index("group"), lax.axis_index("dp")
    chips = banks.shape[0]
    barrier = pltpu.get_barrier_semaphore()

    def hail(k, carry):
        pl.semaphore_signal(barrier, 1, device_id=(1 - group, lax.rem(me + k, chips)), device_id_type=MESH)
        return carry

    lax.fori_loop(0, chips, hail, 0)
    pl.semaphore_wait(barrier, chips)
    across = pltpu.make_async_remote_copy(
        tgt, tgt_out, tgt_sem.at[0], tgt_sem.at[1], {"group": 1 - group}, MESH
    )

    def note(k):
        other = lax.rem(me + k, chips)
        return pltpu.make_async_remote_copy(
            bank, banks.at[me], send_sem.at[k], recv_sem.at[me], (1 - group, other), MESH
        )

    @pl.when(group == 0)
    def _():
        def give(k, carry):
            note(k).start()
            return carry

        def given(k, carry):
            note(k).wait_send()
            return carry

        across.start()
        lax.fori_loop(0, chips, give, 0)
        lax.fori_loop(0, chips, given, 0)
        across.wait_send()

    @pl.when(group == 1)
    def _():
        def take(k, carry):
            pltpu.make_async_remote_copy(
                bank, banks.at[k], send_sem.at[k], recv_sem.at[k], (1 - group, me), MESH
            ).wait_recv()
            return carry

        lax.fori_loop(0, chips, take, 0)
        across.wait_recv()


def exchange_targets(tgt, bank, chips):
    return pl.pallas_call(
        exchange_kernel,
        name="exchange_targets",
        out_shape=(jax.ShapeDtypeStruct(tgt.shape, BF), jax.ShapeDtypeStruct((chips,) + bank.shape, BF)),
        in_specs=[any_spec(), any_spec()],
        out_specs=(any_spec(), any_spec()),
        scratch_shapes=[
            pltpu.SemaphoreType.DMA((2,)),
            pltpu.SemaphoreType.DMA((chips,)),
            pltpu.SemaphoreType.DMA((chips,)),
        ],
        compiler_params=pltpu.CompilerParams(collective_id=3, has_side_effects=True),
    )(tgt, bank)


def sum_kernel(grid, tile, out, heard, send_sem, recv_sem):
    group, me = lax.axis_index("group"), lax.axis_index("dp")
    coords = coords_of(me, grid)
    lengths = (2,) + grid
    mine = (group,) + coords
    peers = []
    for s, length in enumerate(lengths):
        for k in range(1, length):
            other = lax.rem(mine[s] + k, length)
            if s == 0:
                peers.append((s, k, (other, me)))
            else:
                peers.append((s, k, (group, me + (other - mine[s]) * strides_of(grid)[s - 1])))
    barrier = pltpu.get_barrier_semaphore()
    for _, _, device in peers:
        pl.semaphore_signal(barrier, 1, device_id=device, device_id_type=MESH)
    pl.semaphore_wait(barrier, len(peers))
    out[...] = tile[...]
    for s, length in enumerate(lengths):
        if length == 1:
            continue
        heard[s, mine[s]] = out[...]
        copies = [
            pltpu.make_async_remote_copy(
                heard.at[s, mine[s]], heard.at[s, mine[s]], send_sem.at[s, k], recv_sem.at[s, mine[s]], device, MESH
            )
            for t, k, device in peers
            if t == s
        ]
        for copy in copies:
            copy.start()
        for k in range(1, length):
            other = lax.rem(mine[s] + k, length)
            pltpu.make_async_remote_copy(
                heard.at[s, other], heard.at[s, other], send_sem.at[s, k], recv_sem.at[s, other], (group, me), MESH
            ).wait_recv()
        total = heard[s, 0]
        for k in range(1, length):
            total = total + heard[s, k]
        out[...] = total
        for copy in copies:
            copy.wait_send()


def sum_tiles(tile, chips):
    grid = chip_grid(chips)
    most = max((2,) + grid)
    return pl.pallas_call(
        functools.partial(sum_kernel, grid),
        name="sum_tiles",
        out_shape=jax.ShapeDtypeStruct(tile.shape, F32),
        in_specs=[pl.BlockSpec(memory_space=pltpu.VMEM)],
        out_specs=pl.BlockSpec(memory_space=pltpu.VMEM),
        scratch_shapes=[
            pltpu.VMEM((4, most) + tile.shape, F32),
            pltpu.SemaphoreType.DMA((4, most)),
            pltpu.SemaphoreType.DMA((4, most)),
        ],
        compiler_params=pltpu.CompilerParams(collective_id=4, has_side_effects=True),
    )(tile)


def place_kernel(units, owners, model, out, rows_scr, inbuf, stage, outbuf, in_sem, out_sem):
    chips, cores, rows, width = model.shape
    blocks = cores * chips
    cols = width // LANES

    def fetch(b, slot):
        return pltpu.make_async_copy(model.at[lax.rem(b, chips), b // chips], inbuf.at[slot], in_sem.at[slot])

    fetch(0, 0).start()

    def block(b, carry):
        slot = lax.rem(b, 2)
        fetch(b, slot).wait()

        @pl.when(b + 1 < blocks)
        def _():
            fetch(b + 1, 1 - slot).start()

        for c in range(cols):
            stage[pl.ds(c, rows, stride=SUBLANES), :] = inbuf[slot, :, c * LANES : (c + 1) * LANES].astype(F32)

        def move(r, carry):
            dst = pl.multiple_of(owners[b * rows + r] * SUBLANES, SUBLANES)
            src = pl.multiple_of(r * SUBLANES, SUBLANES)
            rows_scr[pl.ds(dst, SUBLANES), :] = stage[pl.ds(src, SUBLANES), :]
            return carry

        return lax.fori_loop(0, rows, move, carry, unroll=14)

    lax.fori_loop(0, blocks, block, 0)
    for u, (first, step) in enumerate(units):
        slot = u % 2
        if u >= 2:
            pltpu.make_async_copy(outbuf.at[slot], out.at[u - 2], out_sem.at[slot]).wait()
        for c in range(cols):
            outbuf[slot, :, c * LANES : (c + 1) * LANES] = rows_scr[
                pl.ds(first * SUBLANES + c, width, stride=step * SUBLANES), :
            ].astype(BF)
        pltpu.make_async_copy(outbuf.at[slot], out.at[u], out_sem.at[slot]).start()
    for u in (len(units) - 2, len(units) - 1):
        pltpu.make_async_copy(outbuf.at[u % 2], out.at[u], out_sem.at[u % 2]).wait()


def place_weights(owners, model, units):
    _, _, rows, width = model.shape
    total = owners.shape[0]
    return pl.pallas_call(
        functools.partial(place_kernel, units),
        name="place_weights",
        out_shape=jax.ShapeDtypeStruct((len(units), width, width), BF),
        in_specs=[smem_spec(), any_spec()],
        out_specs=any_spec(),
        scratch_shapes=[
            pltpu.VMEM((total * SUBLANES, LANES), F32),
            pltpu.VMEM((2, rows, width), BF),
            pltpu.VMEM((rows * SUBLANES, LANES), F32),
            pltpu.VMEM((2, width, width), BF),
            pltpu.SemaphoreType.DMA((2,)),
            pltpu.SemaphoreType.DMA((2,)),
        ],
        compiler_params=pltpu.CompilerParams(vmem_limit_bytes=VMEM_LIMIT),
    )(owners, model)


def layer_stats(tensor):
    centre = tensor - jnp.mean(tensor, axis=-1, keepdims=True)
    scaled = lax.rsqrt(jnp.mean(centre * centre, axis=-1, keepdims=True) + 1e-06)
    return centre * scaled, scaled


def column_of(row):
    n = row.shape[1]
    eye = lax.broadcasted_iota(jnp.int32, (n, n), 0) == lax.broadcasted_iota(jnp.int32, (n, n), 1)
    return jnp.sum(jnp.where(eye, row, 0), axis=1, keepdims=True)


def flag_column(pos, slots):
    hit = lax.broadcasted_iota(jnp.int32, (slots, pos.shape[1]), 0) == pos
    return jnp.max(jnp.where(hit, 1, 0), axis=1, keepdims=True)


def fill_bias(bias, seg_col, seg_row):
    bias[...] = jnp.where(seg_col == seg_row, 0.0, MASK_FILL)


def half(x, h):
    low = lax.broadcasted_iota(jnp.int32, (1, LANES), 1) < HEAD_DIM
    keep = low if h == 0 else jnp.logical_not(low)
    return jnp.where(keep, x, jnp.zeros_like(x))


def fwd_kernel(role, patch, seg, pos, gain, w_hbm, e_out, qkv, lse, o_out, x1_out, x2_out, tgt, bank, w, bias, sem):
    i = pl.program_id(0)
    slots, width = patch.shape[1:]
    pieces = w_hbm.shape[0]
    cuts = (pieces - 6) // 2
    order = [0, 3, 4, 5, 1]
    for j in range(cuts):
        order += [6 + j, 6 + cuts + j]

    @pl.when(i == 0)
    def _():
        for u in order:
            pltpu.make_async_copy(w_hbm.at[u], w.at[u], sem.at[u]).start()

    def need(u):
        @pl.when(i == 0)
        def _():
            pltpu.make_async_copy(w_hbm.at[u], w.at[u], sem.at[u]).wait()

    seg_row = seg[0]
    seg_col = column_of(seg_row)
    fill_bias(bias, seg_col, seg_row)
    flags = flag_column(pos[0], slots) * role[0]
    need(0)
    e = nn(patch[0], w[0])
    e = jnp.where(flags > 0, gain[3:4, :], e)
    e_out[0] = e
    a = (layer_stats(e)[0] * gain[0:1, :]).astype(BF)
    for j in range(3):
        need(3 + j)
        qkv[j] = nn(a, w[3 + j]).astype(BF)

    def pair(p, carry):
        cs = pl.ds(pl.multiple_of(p * LANES, LANES), LANES)
        q2, k2, v2 = qkv[0, :, cs], qkv[1, :, cs], qkv[2, :, cs]
        k2 = k2 * jnp.asarray(HEAD_DIM**-0.5, BF)
        v_t = v2.T
        outs = []
        for h in range(2):
            s = nt(half(k2, h), q2) + bias[...]
            top = jnp.max(s, axis=0, keepdims=True)
            ex = jnp.exp(s - top)
            total = jnp.sum(ex, axis=0, keepdims=True)
            lse[0, pl.ds(2 * p + h, 1), :] = top + jnp.log(total)
            probs = (ex * (1.0 / total)).astype(BF)
            outs.append(nn(v_t[h * HEAD_DIM : (h + 1) * HEAD_DIM, :], probs))
        o_out[0, :, cs] = jnp.concatenate(outs, axis=0).T.astype(BF)
        return carry

    lax.fori_loop(0, HEADS // 2, pair, 0)
    need(1)
    x1 = e_out[0] + nn(o_out[0], w[1])
    x1_out[0] = x1
    a2 = (layer_stats(x1)[0] * gain[1:2, :]).astype(BF)
    acc = x1
    for j in range(cuts):
        need(6 + j)
        hid = nn(a2, w[6 + j])
        act = (hid * (0.5 * (1.0 + jnp.tanh(GELU_A * (hid + GELU_B * hid * hid * hid))))).astype(BF)
        need(6 + cuts + j)
        acc = acc + nn(act, w[6 + cuts + j])
    x2_out[0] = acc

    @pl.when(role[0] == 0)
    def _():
        t = layer_stats(x2_out[0])[0].astype(BF)
        tgt[0] = t
        t = t.astype(F32)
        for m in range(IMGS):
            inside = seg_col == m
            size = jnp.sum(jnp.where(inside, 1.0, 0.0), axis=0, keepdims=True)
            pooled = jnp.sum(jnp.where(inside, t, 0.0), axis=0, keepdims=True) / size
            unit = pooled * lax.rsqrt(jnp.sum(pooled * pooled, axis=-1, keepdims=True) + 1e-06)
            bank[0, m : m + 1, :] = unit.astype(BF)


def forward(role, patch, seg, pos, gain, w):
    batches, slots, width = patch.shape
    pieces = w.shape[0]
    tok = lambda dt: jax.ShapeDtypeStruct((batches, slots, width), dt)
    row = pl.BlockSpec((1, slots, width), lambda i: (i, 0, 0))
    return pl.pallas_call(
        fwd_kernel,
        name="forward",
        grid=(batches,),
        out_shape=(
            tok(F32),
            jax.ShapeDtypeStruct((3, batches * slots, width), BF),
            jax.ShapeDtypeStruct((batches, HEADS, slots), F32),
            tok(BF),
            tok(F32),
            tok(F32),
            tok(BF),
            jax.ShapeDtypeStruct((batches, IMGS, width), BF),
        ),
        in_specs=[
            smem_spec(),
            row,
            pl.BlockSpec((1, 1, slots), lambda i: (i, 0, 0)),
            pl.BlockSpec((1, 1, pos.shape[2]), lambda i: (i, 0, 0)),
            pl.BlockSpec((4, width), lambda i: (0, 0)),
            any_spec(),
        ],
        out_specs=(
            row,
            pl.BlockSpec((3, slots, width), lambda i: (0, i, 0)),
            pl.BlockSpec((1, HEADS, slots), lambda i: (i, 0, 0)),
            row,
            row,
            row,
            row,
            pl.BlockSpec((1, IMGS, width), lambda i: (i, 0, 0)),
        ),
        scratch_shapes=[
            pltpu.VMEM((pieces, width, width), BF),
            pltpu.VMEM((slots, slots), F32),
            pltpu.SemaphoreType.DMA((pieces,)),
        ],
        compiler_params=pltpu.CompilerParams(vmem_limit_bytes=VMEM_LIMIT),
    )(role, patch, seg, pos, gain, w)


def norm_back(grad_out, normed, scaled, gain_vec):
    grad_hat = grad_out * gain_vec
    inner = jnp.mean(grad_hat * normed, axis=-1, keepdims=True)
    grad_in = scaled * (grad_hat - jnp.mean(grad_hat, axis=-1, keepdims=True) - normed * inner)
    return grad_in, jnp.sum(grad_out * normed, axis=0, keepdims=True)


def bwd_kernel(
    listed, place, seg, pos, gain, e_in, qkv, lse, x1_in, x2_in, tgt, banks, w_hbm,
    head_out, attn_out, ffn_out, act_out, de_out, mid_out, pred_out, dqkv, du_out, down_out, small,
    w, bias, top_scr, pool_scr, sem,
):
    i = pl.program_id(0)
    role = place[0]
    slots, width = e_in.shape[1:]
    pieces = w_hbm.shape[0]
    cuts = (pieces - 6) // 2

    @pl.when(role == 0)
    def _():
        small[...] = jnp.zeros_like(small)

    @pl.when(role != 0)
    def _():
        order = [2]
        for j in range(cuts):
            order += [6 + cuts + j, 6 + j]
        order += [1, 3, 4, 5]

        @pl.when(i == 0)
        def _():
            for u in order:
                pltpu.make_async_copy(w_hbm.at[u], w.at[u - 1], sem.at[u]).start()
            small[...] = jnp.zeros_like(small)

        def need(u):
            @pl.when(i == 0)
            def _():
                pltpu.make_async_copy(w_hbm.at[u], w.at[u - 1], sem.at[u]).wait()

        seg_row = seg[0]
        seg_col = column_of(seg_row)
        fill_bias(bias, seg_col, seg_row)
        flags = flag_column(pos[0], slots)
        n3, r3 = layer_stats(x2_in[0])
        head_in = (n3 * gain[2:3, :]).astype(BF)
        head_out[0] = head_in
        need(2)
        pred = nn(head_in, w[1])
        valid = jnp.where(seg_col < IMGS, flags, 0).astype(F32)
        diff = pred - tgt[0].astype(F32)
        size = jnp.abs(diff)
        huber = jnp.where(size < 1.0, 0.5 * diff * diff, size - 0.5)
        regress = jnp.sum(jnp.sum(valid * huber, axis=1, keepdims=True), axis=0, keepdims=True)
        count = listed[0] * width
        grad_pred = valid * (jnp.clip(diff, -1.0, 1.0) / count)
        pool_scr[...] = jnp.zeros_like(pool_scr)
        for m in range(IMGS):
            inside = seg_col == m
            tally = jnp.sum(jnp.where(inside, 1.0, 0.0), axis=0, keepdims=True)
            pool_scr[m : m + 1, :] = jnp.sum(jnp.where(inside, pred, 0.0), axis=0, keepdims=True) / tally
        pooled = pool_scr[...]
        length = lax.rsqrt(jnp.sum(pooled * pooled, axis=-1, keepdims=True) + 1e-06)
        unit = pooled * length
        memory = banks[0]
        choices = memory.shape[0]
        logits = nt(unit.astype(BF), memory) / SOFTMAX_TEMPER
        row_id = lax.broadcasted_iota(jnp.int32, logits.shape, 0)
        real = row_id < IMGS
        picked = jnp.where(
            real & (lax.broadcasted_iota(jnp.int32, logits.shape, 1) == place[1] * IMGS + row_id), 1.0, 0.0
        )
        peak = jnp.max(logits, axis=-1, keepdims=True)
        ex = jnp.exp(logits - peak)
        total = jnp.sum(ex, axis=-1, keepdims=True)
        each = peak + jnp.log(total) - jnp.sum(logits * picked, axis=-1, keepdims=True)
        contrast = jnp.sum(jnp.where(real[:, 0:1], each, 0.0), axis=0, keepdims=True)
        scale = choices * MICRO_BATCHES
        grad_logits = (jnp.where(real, ex / total - picked, 0.0) / scale / SOFTMAX_TEMPER).astype(BF)
        grad_unit = nn(grad_logits, memory)
        grad_pool = length * (grad_unit - unit * jnp.sum(grad_unit * unit, axis=1, keepdims=True))
        pool_scr[...] = grad_pool
        for m in range(IMGS):
            inside = seg_col == m
            tally = jnp.sum(jnp.where(inside, 1.0, 0.0), axis=0, keepdims=True)
            grad_pred = grad_pred + jnp.where(inside, pool_scr[m : m + 1, :] / tally, 0.0)
        low = grad_pred.astype(BF)
        pred_out[0] = low
        loss = regress / count + contrast / scale
        small[4:5, :] += jnp.broadcast_to(loss, (1, width))
        grad_top, gain_three = norm_back(nt(low, w[1]), n3, r3, gain[2:3, :])
        small[2:3, :] += gain_three
        top_scr[...] = grad_top
        down = grad_top.astype(BF)
        down_out[0] = down
        n2, r2 = layer_stats(x1_in[0])
        ffn_in = (n2 * gain[1:2, :]).astype(BF)
        ffn_out[0] = ffn_in
        acc = None
        for j in range(cuts):
            need(6 + cuts + j)
            grad_act = nt(down, w[5 + cuts + j])
            need(6 + j)
            hid = nn(ffn_in, w[5 + j])
            th = jnp.tanh(GELU_A * (hid + GELU_B * hid * hid * hid))
            cdf = 0.5 * (1.0 + th)
            act_out[j] = (hid * cdf).astype(BF)
            slope = cdf + hid * (0.5 * (1.0 - th * th)) * (GELU_A * (1.0 + 3.0 * GELU_B * hid * hid))
            du = (grad_act * slope).astype(BF)
            du_out[j] = du
            part = nt(du, w[5 + j])
            acc = part if acc is None else acc + part
        grad_ffn, gain_two = norm_back(acc, n2, r2, gain[1:2, :])
        small[1:2, :] += gain_two
        mid = top_scr[...] + grad_ffn
        top_scr[...] = mid
        mid_low = mid.astype(BF)
        mid_out[0] = mid_low
        need(1)
        de_out[0] = nt(mid_low, w[0]).astype(BF)

        def pair(p, carry):
            cs = pl.ds(pl.multiple_of(p * LANES, LANES), LANES)
            q2, k2, v2, g2 = qkv[0, :, cs], qkv[1, :, cs], qkv[2, :, cs], de_out[0, :, cs]
            k_scaled = k2 * jnp.asarray(HEAD_DIM**-0.5, BF)
            k_t = k2.T
            dq, dk, dv = [], 0.0, 0.0
            for h in range(2):
                s = nt(half(k_scaled, h), q2) + bias[...]
                probs = jnp.exp(s - lse[0, pl.ds(2 * p + h, 1), :])
                dp = nt(half(v2, h), g2)
                centre = jnp.sum(probs * dp, axis=0, keepdims=True)
                ds = (probs * (dp - centre)).astype(BF)
                dv = dv + nn(probs.astype(BF), half(g2, h))
                dk = dk + nn(ds, half(q2, h))
                dq.append(nn(k_t[h * HEAD_DIM : (h + 1) * HEAD_DIM, :], ds))
            dqkv[0, :, cs] = (jnp.concatenate(dq, axis=0) * HEAD_DIM**-0.5).T.astype(BF)
            dqkv[1, :, cs] = (dk * HEAD_DIM**-0.5).astype(BF)
            dqkv[2, :, cs] = dv.astype(BF)
            return carry

        lax.fori_loop(0, HEADS // 2, pair, 0)
        acc = None
        for j in range(3):
            need(3 + j)
            part = nt(dqkv[j], w[2 + j])
            acc = part if acc is None else acc + part
        n1, r1 = layer_stats(e_in[0])
        attn_out[0] = (n1 * gain[0:1, :]).astype(BF)
        grad_attn, gain_one = norm_back(acc, n1, r1, gain[0:1, :])
        small[0:1, :] += gain_one
        start = top_scr[...] + grad_attn
        hidden_slot = flags > 0
        small[3:4, :] += jnp.sum(jnp.where(hidden_slot, start, 0.0), axis=0, keepdims=True)
        de_out[0] = jnp.where(hidden_slot, 0.0, start).astype(BF)


def backward(listed, place, seg, pos, gain, saved, tgt, banks, w):
    e, qkv, lse, x1, x2 = saved
    batches, slots, width = e.shape
    pieces = w.shape[0]
    cuts = (pieces - 6) // 2
    once = pl.Buffered(1)
    tok = lambda n: jax.ShapeDtypeStruct((n, batches * slots, width), BF)
    row_in = pl.BlockSpec((1, slots, width), lambda i: (i, 0, 0), pipeline_mode=once)
    piece = lambda n: pl.BlockSpec((n, slots, width), lambda i: (0, i, 0))
    return pl.pallas_call(
        bwd_kernel,
        name="backward",
        grid=(batches,),
        out_shape=(
            tok(1), tok(1), tok(1), tok(cuts), tok(1), tok(1), tok(1), tok(3), tok(cuts), tok(1),
            jax.ShapeDtypeStruct((SUBLANES, width), F32),
        ),
        in_specs=[
            smem_spec(),
            smem_spec(),
            pl.BlockSpec((1, 1, slots), lambda i: (i, 0, 0)),
            pl.BlockSpec((1, 1, pos.shape[2]), lambda i: (i, 0, 0)),
            pl.BlockSpec((4, width), lambda i: (0, 0)),
            row_in,
            pl.BlockSpec((3, slots, width), lambda i: (0, i, 0), pipeline_mode=once),
            pl.BlockSpec((1, HEADS, slots), lambda i: (i, 0, 0)),
            row_in,
            row_in,
            row_in,
            pl.BlockSpec((1,) + banks.shape[1:], lambda i: (i, 0, 0), pipeline_mode=once),
            any_spec(),
        ],
        out_specs=(
            piece(1), piece(1), piece(1), piece(cuts), piece(1), piece(1), piece(1), piece(3), piece(cuts), piece(1),
            pl.BlockSpec((SUBLANES, width), lambda i: (0, 0)),
        ),
        scratch_shapes=[
            pltpu.VMEM((pieces - 1, width, width), BF),
            pltpu.VMEM((slots, slots), F32),
            pltpu.VMEM((slots, width), F32),
            pltpu.VMEM((SUBLANES, width), F32),
            pltpu.SemaphoreType.DMA((pieces,)),
        ],
        compiler_params=pltpu.CompilerParams(vmem_limit_bytes=VMEM_LIMIT),
    )(listed, place, seg, pos, gain, e, qkv, lse, x1, x2, tgt, banks, w)


def grads_kernel(
    units, plan, cuts, role, owners, patch, mixed, head, attn, ffn, act, de, mid, pred, dqkv, du, down, out,
    rows_scr, x_buf, x_t, g_buf, stage, outbuf, x_sem, g_sem, out_sem,
):
    blocks, rows, width = out.shape
    cols = width // LANES
    lefts = {"patch": patch, "mixed": mixed, "head": head, "attn": attn, "ffn": ffn, "act": act}
    rights = {"de": de, "mid": mid, "pred": pred, "dqkv": dqkv, "du": du, "down": down}

    @pl.when(role[0] == 0)
    def _():
        outbuf[...] = jnp.zeros_like(outbuf)

        def put(b, carry):
            pltpu.make_async_copy(outbuf.at[0], out.at[b], out_sem.at[0]).start()
            return carry

        def done(b, carry):
            pltpu.make_async_copy(outbuf.at[0], out.at[b], out_sem.at[0]).wait()
            return carry

        lax.fori_loop(0, blocks, put, 0)
        lax.fori_loop(0, blocks, done, 0)

    @pl.when(role[0] != 0)
    def _():
        lcopies, rcopies = [], []
        lkeys, rkeys = [], []
        steps = []
        for u, (left, right) in enumerate(plan):
            if not lkeys or lkeys[-1] != left:
                slot = len(lkeys) % 2
                lcopies.append(pltpu.make_async_copy(lefts[left[0]].at[left[1]], x_buf.at[slot], x_sem.at[slot]))
                lkeys.append(left)
                fresh_l = True
            else:
                fresh_l = False
            if not rkeys or rkeys[-1] != right:
                slot = len(rkeys) % 2
                rcopies.append(pltpu.make_async_copy(rights[right[0]].at[right[1]], g_buf.at[slot], g_sem.at[slot]))
                rkeys.append(right)
                fresh_r = True
            else:
                fresh_r = False
            steps.append((u, len(lkeys) - 1, fresh_l, len(rkeys) - 1, fresh_r))
        lcopies[0].start()
        rcopies[0].start()
        for u, li, fresh_l, ri, fresh_r in steps:
            if fresh_l:
                lcopies[li].wait()
                if li + 1 < len(lcopies):
                    lcopies[li + 1].start()
                x_t[...] = x_buf[li % 2].T
            if fresh_r:
                rcopies[ri].wait()
                if ri + 1 < len(rcopies):
                    rcopies[ri + 1].start()
            first, step = units[u]
            wide = 2 * LANES

            def tile(n, carry):
                part = nn(x_t[...], g_buf[ri % 2, :, pl.ds(pl.multiple_of(n * wide, wide), wide)])
                for c in range(2):
                    rows_scr[pl.ds(first * SUBLANES + 2 * n + c, width, stride=step * SUBLANES), :] = part[
                        :, c * LANES : (c + 1) * LANES
                    ]
                return carry

            lax.fori_loop(0, width // wide, tile, 0)

        def block(b, carry):
            slot = lax.rem(b, 2)

            def move(r, carry):
                src = pl.multiple_of(owners[b * rows + r] * SUBLANES, SUBLANES)
                dst = pl.multiple_of(r * SUBLANES, SUBLANES)
                stage[pl.ds(dst, SUBLANES), :] = rows_scr[pl.ds(src, SUBLANES), :]
                return carry

            lax.fori_loop(0, rows, move, 0, unroll=14)

            @pl.when(b >= 2)
            def _():
                pltpu.make_async_copy(outbuf.at[slot], out.at[b - 2], out_sem.at[slot]).wait()

            for c in range(cols):
                outbuf[slot, :, c * LANES : (c + 1) * LANES] = stage[pl.ds(c, rows, stride=SUBLANES), :].astype(BF)
            pltpu.make_async_copy(outbuf.at[slot], out.at[b], out_sem.at[slot]).start()
            return carry

        lax.fori_loop(0, blocks, block, 0)
        for b in (blocks - 2, blocks - 1):
            pltpu.make_async_copy(outbuf.at[b % 2], out.at[b], out_sem.at[b % 2]).wait()


def weight_grads(role, owners, lefts, rights, units, blocks):
    tokens, width = lefts[0].shape[1:]
    cuts = lefts[-1].shape[0]
    total = owners.shape[0]
    rows = total // blocks
    plan = (
        [(("patch", 0), ("de", 0)), (("mixed", 0), ("mid", 0)), (("head", 0), ("pred", 0))]
        + [(("attn", 0), ("dqkv", j)) for j in range(3)]
        + [(("ffn", 0), ("du", j)) for j in range(cuts)]
        + [(("act", j), ("down", 0)) for j in range(cuts)]
    )
    return pl.pallas_call(
        functools.partial(grads_kernel, units, plan, cuts),
        name="weight_grads",
        out_shape=jax.ShapeDtypeStruct((blocks, rows, width), BF),
        in_specs=[smem_spec(), smem_spec()] + [any_spec()] * 12,
        out_specs=any_spec(),
        scratch_shapes=[
            pltpu.VMEM((total * SUBLANES, LANES), F32),
            pltpu.VMEM((2, tokens, width), BF),
            pltpu.VMEM((width, tokens), BF),
            pltpu.VMEM((2, tokens, width), BF),
            pltpu.VMEM((rows * SUBLANES, LANES), F32),
            pltpu.VMEM((2, rows, width), BF),
            pltpu.SemaphoreType.DMA((2,)),
            pltpu.SemaphoreType.DMA((2,)),
            pltpu.SemaphoreType.DMA((2,)),
        ],
        compiler_params=pltpu.CompilerParams(vmem_limit_bytes=VMEM_LIMIT),
    )(role, owners, *lefts, *rights)


def adam_update(weight, first_state, second_state, gradient, step_value, decay_rate):
    first_state = BETA_ONE * first_state + (1.0 - BETA_ONE) * gradient
    second_state = BETA_TWO * second_state + (1.0 - BETA_TWO) * gradient * gradient
    fix_one = 1.0 - jnp.power(BETA_ONE, step_value)
    fix_two = 1.0 - jnp.power(BETA_TWO, step_value)
    update = first_state / fix_one / (jnp.sqrt(second_state / fix_two) + ADAM_EPS)
    return (weight - RATE * (update + decay_rate * weight), first_state, second_state)


def body(
    patches,
    segments,
    positions,
    owners,
    master,
    moment_one,
    moment_two,
    teacher,
    gains,
    gain_one,
    gain_two,
    teacher_gains,
    step_count,
):
    core = lax.axis_index("group")
    width = patches.shape[3]
    slots = patches.shape[2]
    row_total = owners.shape[0]
    inner = (row_total - 6 * width) // 2
    units = unit_list(width, inner)
    chips = lax.axis_size("dp")
    devices = lax.axis_size("group") * chips
    own_rows = row_total // devices
    role = core.astype(jnp.int32).reshape(1)
    place = jnp.stack([core, lax.axis_index("dp")]).astype(jnp.int32)
    listed = jnp.full((1,), MASKED * lax.axis_size("dp") * MICRO_BATCHES, F32)

    both = jnp.stack([teacher, master]).astype(BF)
    if chips <= KERNEL_CHIPS:
        model = gather_weights(both, chips)
    else:
        parts = lax.all_gather(both, ("dp", "group"), axis=1)
        model = jnp.where(core == 1, parts[1], parts[0]).reshape(chips, 2, own_rows, width)
    w = place_weights(owners, model, units)
    gain_set = jnp.where(core == 1, gains, teacher_gains)
    patch = patches[:, 0]
    seg = segments
    pos = positions
    e, qkv, lse, mixed, x1, x2, tgt, bank = forward(role, patch, seg, pos, gain_set, w)
    tgt, banks = exchange_targets(tgt, bank, chips)
    banks = jnp.swapaxes(banks, 0, 1).reshape(MICRO_BATCHES, chips * IMGS, width)
    head, attn, ffn, act, de, mid, pred, dqkv, du, down, small = backward(
        listed, place, seg, pos, gain_set, (e, qkv, lse, x1, x2), tgt, banks, w
    )
    flat = lambda a: a.reshape(1, MICRO_BATCHES * slots, width)
    blocked = weight_grads(
        role,
        owners,
        (flat(patch), flat(mixed), head, attn, ffn, act),
        (de, mid, pred, dqkv, du, down),
        units,
        devices,
    )
    if chips <= KERNEL_CHIPS:
        owned_grad = reduce_grads(blocked.reshape(2, chips, own_rows, width), chips)
    else:
        owned_grad = lax.psum_scatter(blocked, ("group", "dp"), scatter_dimension=0, tiled=True)
        owned_grad = owned_grad.reshape(own_rows, width).astype(F32)
    square_own = jnp.sum(owned_grad * owned_grad)
    row_id = lax.broadcasted_iota(jnp.int32, small.shape, 0)
    small = sum_tiles(jnp.where(row_id == 5, square_own, small), chips)
    gain_sum, loss_sum, square_sum = small[0:4], small[4, 0], small[5, 0]
    grad_norm = jnp.sqrt(square_sum + jnp.sum(gain_sum * gain_sum))
    factor = jnp.minimum(1.0, CLIP / grad_norm)
    step_value = step_count[0].astype(F32)
    master_new, one_new, two_new = adam_update(
        master, moment_one, moment_two, owned_grad * factor, step_value, DECAY
    )
    gone_new, gtwo_new = adam_update(gains, gain_one, gain_two, gain_sum * factor, step_value, 0.0)[1:]
    teacher_new = EMA_KEEP * teacher + (1.0 - EMA_KEEP) * master_new
    return (
        loss_sum.reshape(1),
        grad_norm.reshape(1),
        one_new,
        two_new,
        master_new,
        teacher_new,
        gone_new,
        gtwo_new,
    )


def solution(mesh):
    rows = P(("group", "dp"), None)
    in_specs = (
        P(None, "dp", None, None),
        P(None, "dp", None),
        P(None, "dp", None),
        P(),
        rows,
        rows,
        rows,
        rows,
        P(),
        P(),
        P(),
        P(),
        P(),
    )
    out_specs = (P(), P(), rows, rows, rows, rows, P(), P())
    return jax.shard_map(body, mesh=mesh, in_specs=in_specs, out_specs=out_specs, check_vma=False)
```

```python
import functools

import jax
import jax.numpy as jnp
from jax import lax
from jax.experimental import pallas as pl
from jax.experimental.pallas import tpu as pltpu
from jax.sharding import PartitionSpec as P

HEADS = 12
HEAD_DIM = 64
IMGS = 4
MASKED = 320
MICRO_BATCHES = 2
LANES = 128
SUBLANES = 8
TILE = SUBLANES * SUBLANES

SOFTMAX_TEMPER = 0.05
CLIP = 0.004
RATE = 0.05
BETA_ONE = 0.9
BETA_TWO = 0.999
ADAM_EPS = 1e-08
DECAY = 0.05
EMA_KEEP = 0.9
MASK_FILL = -1000000000.0

BF = jnp.bfloat16
F32 = jnp.float32
VMEM_LIMIT = 67_000_000
GELU_A = 0.7978845608028654
GELU_B = 0.044715


def nn(a, b):
    return jnp.dot(a, b, preferred_element_type=F32)


def nt(a, b):
    return lax.dot_general(a, b, (((1,), (1,)), ((), ())), preferred_element_type=F32)


def piece_rows(flat, width, inner):
    cuts = inner // width
    qkv, up = flat - 3 * width, flat - 6 * width
    inside = jnp.where(flat < 6 * width, (3 + qkv % 3) * width + qkv // 3, (6 + up % cuts) * width + up // cuts)
    return jnp.where((flat >= 3 * width) & (flat < 6 * width + inner), inside, flat)


def any_spec():
    return pl.BlockSpec(memory_space=pl.ANY)


def smem_spec():
    return pl.BlockSpec(memory_space=pltpu.SMEM)


MESH = pl.DeviceIdType.MESH
KERNEL_CHIPS = 16


def chip_grid(chips):
    sizes, turn, left, prime = [1, 1, 1], 0, chips, 2
    while left > 1:
        while left % prime:
            prime += 1
        sizes[turn % 3] *= prime
        turn += 1
        left //= prime
    return tuple(sizes)


def strides_of(grid):
    return (grid[1] * grid[2], grid[2], 1)


def coords_of(index, grid):
    return (index // (grid[1] * grid[2]), lax.rem(index // grid[2], grid[1]), lax.rem(index, grid[2]))


def guarded(conditions, action):
    conditions = [c for c in conditions if c is not None]
    if not conditions:
        return action()
    both = conditions[0]
    for c in conditions[1:]:
        both = jnp.logical_and(both, c)
    pl.when(both)(action)


def lanes_of(width):
    unit = width // 6
    orders = [((1, 0, 2), 2), ((2, 0, 1), 2), ((0, 2, 1), 1), ((0, 1, 2), 1)]
    routes, first = [], 0
    for order, share in orders:
        routes.append((order, first, share * unit))
        first += share * unit
    return routes


def offsets(length):
    if length <= 2:
        return list(range(length))
    return [0] + [sign * far for far in range(1, length) for sign in (1, -1)]


def route_events(grid, routes):
    events = []
    for c, (order, _, _) in enumerate(routes):
        stack = [()]
        for d in order:
            stack = [r + (o,) for r in stack for o in offsets(grid[d])]
        events += [(sum(abs(o) * 2**i for i, o in enumerate(r)), c, r) for r in stack]
    return [(c, r) for _, c, r in sorted(events, key=lambda e: e[0])]


def onward(grid, order, r):
    last = max([i for i in range(3) if r[i]], default=-1)
    outs = []
    if last >= 0 and grid[order[last]] > 2:
        outs.append((order[last], 1 if r[last] > 0 else -1))
    for d in order[last + 1 :]:
        if grid[d] == 2:
            outs.append((d, 1))
        elif grid[d] > 2:
            outs += [(d, 1), (d, -1)]
    return outs


def neighbour(me, coords, grid, d, sign):
    step = strides_of(grid)[d]
    if grid[d] == 2:
        return me + (1 - 2 * coords[d]) * step, None
    place = coords[d] + sign
    return me + sign * step, jnp.logical_and(place >= 0, place < grid[d])


def origin(me, coords, grid, order, r):
    index, conditions = me, []
    for d, o in zip(order, r):
        if o == 0:
            continue
        step = strides_of(grid)[d]
        if grid[d] == 2:
            index = index + (1 - 2 * coords[d]) * step
        else:
            place = coords[d] - o
            index = index - o * step
            conditions.append(jnp.logical_and(place >= 0, place < grid[d]))
    return index, conditions


def slot_of(grid, d, sign):
    first = sum([1 if n <= 2 else 2 for n in grid[:d]])
    return first if grid[d] <= 2 or sign > 0 else first + 1


def slots_of(grid):
    return sum([1 if n <= 2 else 2 for n in grid])


def greet(me, coords, grid, group):
    barrier = pltpu.get_barrier_semaphore()
    near = [neighbour(me, coords, grid, d, s) for d in range(3) for s in ((1,) if grid[d] == 2 else (1, -1)) if grid[d] > 1]
    for index, there in near:
        guarded([there], lambda: pl.semaphore_signal(barrier, 1, device_id={"dp": index}, device_id_type=MESH))
    pl.semaphore_signal(barrier, 1, device_id={"group": 1 - group}, device_id_type=MESH)
    pl.semaphore_wait(barrier, 1 + sum([1 if there is None else there.astype(jnp.int32) for _, there in near]))


def gather_kernel(grid, both, out, swap_sem, send_sem, recv_sem):
    group, me = lax.axis_index("group"), lax.axis_index("dp")
    coords = coords_of(me, grid)
    routes = lanes_of(both.shape[2])
    events = route_events(grid, routes)
    keep = pltpu.make_async_copy(both.at[group], out.at[me, group], swap_sem.at[2])
    keep.start()
    greet(me, coords, grid, group)
    swap = pltpu.make_async_remote_copy(
        both.at[1 - group], out.at[me, group], swap_sem.at[0], swap_sem.at[1], {"group": 1 - group}, MESH
    )
    swap.start()
    keep.wait()
    swap.wait()

    def visit(c, r, act):
        order, first, wide = routes[c]
        block, real = origin(me, coords, grid, order, r)
        part = out.at[block, :, :, first : first + wide]

        def run():
            copies = []
            for d, sign in onward(grid, order, r):
                index, there = neighbour(me, coords, grid, d, sign)
                copies.append(
                    (
                        there,
                        pltpu.make_async_remote_copy(
                            part,
                            part,
                            send_sem.at[c, slot_of(grid, d, sign), block],
                            recv_sem.at[c, block],
                            {"dp": index},
                            MESH,
                        ),
                    )
                )
            act(part, recv_sem.at[c, block], any(r), copies)

        guarded(real, run)

    def forward_on(part, arrival_sem, remote, copies):
        if remote:
            pltpu.make_async_remote_copy(part, part, swap_sem.at[0], arrival_sem, {"dp": me}, MESH).wait_recv()
        for there, copy in copies:
            guarded([there], copy.start)

    def finish(part, arrival_sem, remote, copies):
        for there, copy in copies:
            guarded([there], copy.wait_send)

    for c, r in events:
        visit(c, r, forward_on)
    for c, r in events:
        visit(c, r, finish)


def gather_weights(both, chips):
    grid = chip_grid(chips)
    _, rows, width = both.shape
    return pl.pallas_call(
        functools.partial(gather_kernel, grid),
        name="gather_weights",
        out_shape=jax.ShapeDtypeStruct((chips, 2, rows, width), BF),
        in_specs=[pl.BlockSpec(memory_space=pltpu.VMEM)],
        out_specs=any_spec(),
        scratch_shapes=[
            pltpu.SemaphoreType.DMA((3,)),
            pltpu.SemaphoreType.DMA((4, slots_of(grid), chips)),
            pltpu.SemaphoreType.DMA((4, chips)),
        ],
        compiler_params=pltpu.CompilerParams(
            collective_id=1, has_side_effects=True, vmem_limit_bytes=VMEM_LIMIT
        ),
    )(both)


def reduce_kernel(grid, blocked, out, acc, heard, load_sem, half_sem, send_sem, recv_sem):
    group, me = lax.axis_index("group"), lax.axis_index("dp")
    coords = coords_of(me, grid)
    rows, width = out.shape
    routes = lanes_of(width)
    events = route_events(grid, routes)[::-1]
    tall = max([t for t in range(16, 49, 16) if rows % t == 0], default=rows)

    def spot(c, r):
        return tuple(r[routes[c][0].index(d)] for d in range(3))

    firsts = list(dict.fromkeys([spot(c, r) for c, r in events]))
    greet(me, coords, grid, group)

    def load(where, act):
        block, real = origin(me, coords, grid, (0, 1, 2), where)
        local = pltpu.make_async_copy(blocked.at[1, block], acc.at[block], load_sem.at[block])
        half = pltpu.make_async_remote_copy(
            blocked.at[0, block], acc.at[block], half_sem.at[0, block], half_sem.at[1, block], {"group": 1 - group}, MESH
        )
        guarded(real, lambda: act(local, half))

    def load_start(local, half):
        @pl.when(group == 1)
        def _():
            half.start()
            local.start()

    def load_wait(local, half):
        @pl.when(group == 1)
        def _():
            local.wait()

        @pl.when(group == 0)
        def _():
            half.wait_recv()

    def load_end(local, half):
        @pl.when(group == 1)
        def _():
            half.wait_send()

    for where in firsts:
        load(where, load_start)

    def parent(c, r, block):
        order, first, wide = routes[c]
        i = max([i for i in range(3) if r[i]])
        sign = 1 if r[i] > 0 else -1
        index, _ = neighbour(me, coords, grid, order[i], -sign)
        slot = slot_of(grid, order[i], sign)
        return pltpu.make_async_remote_copy(
            acc.at[block, :, first : first + wide],
            heard.at[slot, block, :, first : first + wide],
            send_sem.at[c, block],
            recv_sem.at[c, slot, block],
            {"dp": index},
            MESH,
        )

    def visit(c, r):
        order, first, wide = routes[c]
        block, real = origin(me, coords, grid, order, r)

        def run():
            children = [(slot_of(grid, d, s), neighbour(me, coords, grid, d, s)[1]) for d, s in onward(grid, order, r)]
            for slot, there in children:
                part = heard.at[slot, block, :, first : first + wide]
                arrival = pltpu.make_async_remote_copy(
                    part, part, send_sem.at[c, block], recv_sem.at[c, slot, block], {"dp": me}, MESH
                )
                guarded([there], arrival.wait_recv)

            if any(r):
                for slot, there in children:

                    def total(slot=slot):
                        def piece(k, carry):
                            at = (pl.ds(pl.multiple_of(k * tall, tall), tall), slice(first, first + wide))
                            acc[(block,) + at] = (
                                acc[(block,) + at].astype(F32) + heard[(slot, block) + at].astype(F32)
                            ).astype(BF)
                            return carry

                        lax.fori_loop(0, rows // tall, piece, 0)

                    guarded([there], total)
                parent(c, r, block).start()
            else:

                def first_piece(k, carry):
                    at = (pl.ds(pl.multiple_of(k * tall, tall), tall), slice(first, first + wide))
                    out[at] = acc[(block,) + at].astype(F32)
                    return carry

                lax.fori_loop(0, rows // tall, first_piece, 0)
                for slot, there in children:

                    def total(slot=slot):
                        def piece(k, carry):
                            at = (pl.ds(pl.multiple_of(k * tall, tall), tall), slice(first, first + wide))
                            out[at] = out[at] + heard[(slot, block) + at].astype(F32)
                            return carry

                        lax.fori_loop(0, rows // tall, piece, 0)

                    guarded([there], total)

        guarded(real, run)

    ready = set()
    for c, r in events:
        if spot(c, r) not in ready:
            ready.add(spot(c, r))
            load(spot(c, r), load_wait)
        visit(c, r)
    for c, r in events:
        if any(r):
            block, real = origin(me, coords, grid, routes[c][0], r)
            guarded(real, parent(c, r, block).wait_send)
    for where in firsts:
        load(where, load_end)


def reduce_grads(blocked, chips):
    grid = chip_grid(chips)
    _, _, rows, width = blocked.shape
    return pl.pallas_call(
        functools.partial(reduce_kernel, grid),
        name="reduce_grads",
        out_shape=jax.ShapeDtypeStruct((rows, width), F32),
        in_specs=[any_spec()],
        out_specs=pl.BlockSpec(memory_space=pltpu.VMEM),
        scratch_shapes=[
            pltpu.VMEM((chips, rows, width), BF),
            pltpu.VMEM((slots_of(grid), chips, rows, width), BF),
            pltpu.SemaphoreType.DMA((chips,)),
            pltpu.SemaphoreType.DMA((2, chips)),
            pltpu.SemaphoreType.DMA((4, chips)),
            pltpu.SemaphoreType.DMA((4, slots_of(grid), chips)),
        ],
        compiler_params=pltpu.CompilerParams(
            collective_id=2, has_side_effects=True, vmem_limit_bytes=VMEM_LIMIT
        ),
    )(blocked)


def exchange_kernel(tgt, bank, tgt_out, banks, tgt_sem, send_sem, recv_sem):
    group, me = lax.axis_index("group"), lax.axis_index("dp")
    chips = banks.shape[0]
    barrier = pltpu.get_barrier_semaphore()

    def hail(k, carry):
        pl.semaphore_signal(barrier, 1, device_id=(1 - group, lax.rem(me + k, chips)), device_id_type=MESH)
        return carry

    lax.fori_loop(0, chips, hail, 0)
    pl.semaphore_wait(barrier, chips)
    across = pltpu.make_async_remote_copy(
        tgt, tgt_out, tgt_sem.at[0], tgt_sem.at[1], {"group": 1 - group}, MESH
    )

    def note(k):
        other = lax.rem(me + k, chips)
        return pltpu.make_async_remote_copy(
            bank, banks.at[me], send_sem.at[k], recv_sem.at[me], (1 - group, other), MESH
        )

    @pl.when(group == 0)
    def _():
        def give(k, carry):
            note(k).start()
            return carry

        def given(k, carry):
            note(k).wait_send()
            return carry

        across.start()
        lax.fori_loop(0, chips, give, 0)
        lax.fori_loop(0, chips, given, 0)
        across.wait_send()

    @pl.when(group == 1)
    def _():
        def take(k, carry):
            pltpu.make_async_remote_copy(
                bank, banks.at[k], send_sem.at[k], recv_sem.at[k], (1 - group, me), MESH
            ).wait_recv()
            return carry

        lax.fori_loop(0, chips, take, 0)
        across.wait_recv()


def exchange_targets(tgt, bank, chips):
    return pl.pallas_call(
        exchange_kernel,
        name="exchange_targets",
        out_shape=(jax.ShapeDtypeStruct(tgt.shape, BF), jax.ShapeDtypeStruct((chips,) + bank.shape, BF)),
        in_specs=[any_spec(), any_spec()],
        out_specs=(any_spec(), any_spec()),
        scratch_shapes=[
            pltpu.SemaphoreType.DMA((2,)),
            pltpu.SemaphoreType.DMA((chips,)),
            pltpu.SemaphoreType.DMA((chips,)),
        ],
        compiler_params=pltpu.CompilerParams(collective_id=3, has_side_effects=True),
    )(tgt, bank)


def sum_kernel(grid, tile, out, heard, send_sem, recv_sem):
    group, me = lax.axis_index("group"), lax.axis_index("dp")
    coords = coords_of(me, grid)
    lengths = (2,) + grid
    mine = (group,) + coords
    peers = []
    for s, length in enumerate(lengths):
        for k in range(1, length):
            other = lax.rem(mine[s] + k, length)
            if s == 0:
                peers.append((s, k, (other, me)))
            else:
                peers.append((s, k, (group, me + (other - mine[s]) * strides_of(grid)[s - 1])))
    barrier = pltpu.get_barrier_semaphore()
    for _, _, device in peers:
        pl.semaphore_signal(barrier, 1, device_id=device, device_id_type=MESH)
    pl.semaphore_wait(barrier, len(peers))
    out[...] = tile[...]
    for s, length in enumerate(lengths):
        if length == 1:
            continue
        heard[s, mine[s]] = out[...]
        copies = [
            pltpu.make_async_remote_copy(
                heard.at[s, mine[s]], heard.at[s, mine[s]], send_sem.at[s, k], recv_sem.at[s, mine[s]], device, MESH
            )
            for t, k, device in peers
            if t == s
        ]
        for copy in copies:
            copy.start()
        for k in range(1, length):
            other = lax.rem(mine[s] + k, length)
            pltpu.make_async_remote_copy(
                heard.at[s, other], heard.at[s, other], send_sem.at[s, k], recv_sem.at[s, other], (group, me), MESH
            ).wait_recv()
        total = heard[s, 0]
        for k in range(1, length):
            total = total + heard[s, k]
        out[...] = total
        for copy in copies:
            copy.wait_send()


def sum_tiles(tile, chips):
    grid = chip_grid(chips)
    most = max((2,) + grid)
    return pl.pallas_call(
        functools.partial(sum_kernel, grid),
        name="sum_tiles",
        out_shape=jax.ShapeDtypeStruct(tile.shape, F32),
        in_specs=[pl.BlockSpec(memory_space=pltpu.VMEM)],
        out_specs=pl.BlockSpec(memory_space=pltpu.VMEM),
        scratch_shapes=[
            pltpu.VMEM((4, most) + tile.shape, F32),
            pltpu.SemaphoreType.DMA((4, most)),
            pltpu.SemaphoreType.DMA((4, most)),
        ],
        compiler_params=pltpu.CompilerParams(collective_id=4, has_side_effects=True),
    )(tile)


def place_kernel(spots, model, out, rows_scr, inbuf, stage, outbuf, in_sem, out_sem):
    chips, cores, rows, width = model.shape
    blocks = cores * chips
    cols = width // LANES
    deep, wide = inbuf.shape[0], outbuf.shape[0]
    group = max([g for g in range(1, 17) if rows % g == 0])

    def fetch(b, slot):
        return pltpu.make_async_copy(model.at[lax.rem(b, chips), b // chips], inbuf.at[slot], in_sem.at[slot])

    for b in range(deep - 1):
        fetch(b, b).start()

    def block(b, carry):
        slot = lax.rem(b, deep)
        fetch(b, slot).wait()

        @pl.when(b + deep - 1 < blocks)
        def _():
            fetch(b + deep - 1, lax.rem(b + deep - 1, deep)).start()

        for c in range(cols):
            stage[pl.ds(c, rows, stride=SUBLANES), :] = inbuf[slot, :, c * LANES : (c + 1) * LANES].astype(F32)

        def move(q, carry):
            first = q * group
            to = [spots[b * rows + first + j] for j in range(group)]
            held = [stage[pl.ds(pl.multiple_of((first + j) * SUBLANES, SUBLANES), SUBLANES), :] for j in range(group)]
            for j in range(group):
                rows_scr[pl.ds(to[j], SUBLANES, stride=SUBLANES), :] = held[j]
            return carry

        return lax.fori_loop(0, rows // group, move, carry)

    lax.fori_loop(0, blocks, block, 0)
    pieces = out.shape[0]
    for u in range(pieces):
        slot = u % wide
        if u >= wide:
            pltpu.make_async_copy(outbuf.at[slot], out.at[u - wide], out_sem.at[slot]).wait()

        def pack(k, carry):
            to = pl.ds(pl.multiple_of(k * 16, 16), 16)
            for c in range(cols):
                first = (u * width // SUBLANES + 2 * k) * TILE + c * SUBLANES
                halves = [rows_scr[pl.ds(pl.multiple_of(first + TILE * h, SUBLANES), SUBLANES), :] for h in range(2)]
                outbuf[slot, to, c * LANES : (c + 1) * LANES] = jnp.concatenate(halves, axis=0).astype(BF)
            return carry

        lax.fori_loop(0, width // 16, pack, 0)
        pltpu.make_async_copy(outbuf.at[slot], out.at[u], out_sem.at[slot]).start()
    for u in range(pieces - wide, pieces):
        pltpu.make_async_copy(outbuf.at[u % wide], out.at[u], out_sem.at[u % wide]).wait()


def place_weights(spots, model):
    _, _, rows, width = model.shape
    total = spots.shape[0]
    return pl.pallas_call(
        place_kernel,
        name="place_weights",
        out_shape=jax.ShapeDtypeStruct((total // width, width, width), BF),
        in_specs=[smem_spec(), any_spec()],
        out_specs=any_spec(),
        scratch_shapes=[
            pltpu.VMEM((total * SUBLANES, LANES), F32),
            pltpu.VMEM((8, rows, width), BF),
            pltpu.VMEM((rows * SUBLANES, LANES), F32),
            pltpu.VMEM((4, width, width), BF),
            pltpu.SemaphoreType.DMA((8,)),
            pltpu.SemaphoreType.DMA((4,)),
        ],
        compiler_params=pltpu.CompilerParams(vmem_limit_bytes=VMEM_LIMIT),
    )(spots, model)


def layer_stats(tensor):
    centre = tensor - jnp.mean(tensor, axis=-1, keepdims=True)
    scaled = lax.rsqrt(jnp.mean(centre * centre, axis=-1, keepdims=True) + 1e-06)
    return centre * scaled, scaled


def column_of(row):
    n = row.shape[1]
    eye = lax.broadcasted_iota(jnp.int32, (n, n), 0) == lax.broadcasted_iota(jnp.int32, (n, n), 1)
    return jnp.sum(jnp.where(eye, row, 0), axis=1, keepdims=True)


def flag_column(pos, slots):
    hit = lax.broadcasted_iota(jnp.int32, (slots, pos.shape[1]), 0) == pos
    return jnp.max(jnp.where(hit, 1, 0), axis=1, keepdims=True)


def fill_bias(bias, seg_col, seg_row):
    bias[...] = jnp.where(seg_col == seg_row, 0.0, MASK_FILL)


def half(x, h):
    low = lax.broadcasted_iota(jnp.int32, (1, LANES), 1) < HEAD_DIM
    keep = low if h == 0 else jnp.logical_not(low)
    return jnp.where(keep, x, jnp.zeros_like(x))


def fwd_kernel(role, patch, seg, pos, gain, w_hbm, e_out, qkv, lse, o_out, x1_out, x2_out, tgt, bank, w, bias, sem):
    i = pl.program_id(0)
    slots, width = patch.shape[1:]
    pieces = w_hbm.shape[0]
    cuts = (pieces - 6) // 2
    order = [0, 3, 4, 5, 1]
    for j in range(cuts):
        order += [6 + j, 6 + cuts + j]

    @pl.when(i == 0)
    def _():
        for u in order:
            pltpu.make_async_copy(w_hbm.at[u], w.at[u], sem.at[u]).start()

    def need(u):
        @pl.when(i == 0)
        def _():
            pltpu.make_async_copy(w_hbm.at[u], w.at[u], sem.at[u]).wait()

    seg_row = seg[0]
    seg_col = column_of(seg_row)
    fill_bias(bias, seg_col, seg_row)
    flags = flag_column(pos[0], slots) * role[0]
    need(0)
    e = nn(patch[0], w[0])
    e = jnp.where(flags > 0, gain[3:4, :], e)
    e_out[0] = e
    a = (layer_stats(e)[0] * gain[0:1, :]).astype(BF)
    for j in range(3):
        need(3 + j)
        qkv[j] = nn(a, w[3 + j]).astype(BF)

    def pair(p, carry):
        cs = pl.ds(pl.multiple_of(p * LANES, LANES), LANES)
        q2, k2, v2 = qkv[0, :, cs], qkv[1, :, cs], qkv[2, :, cs]
        k2 = k2 * jnp.asarray(HEAD_DIM**-0.5, BF)
        v_t = v2.T
        outs = []
        for h in range(2):
            s = nt(half(k2, h), q2) + bias[...]
            top = jnp.max(s, axis=0, keepdims=True)
            ex = jnp.exp(s - top)
            total = jnp.sum(ex, axis=0, keepdims=True)
            lse[0, pl.ds(2 * p + h, 1), :] = top + jnp.log(total)
            probs = (ex * (1.0 / total)).astype(BF)
            outs.append(nn(v_t[h * HEAD_DIM : (h + 1) * HEAD_DIM, :], probs))
        o_out[0, :, cs] = jnp.concatenate(outs, axis=0).T.astype(BF)
        return carry

    lax.fori_loop(0, HEADS // 2, pair, 0)
    need(1)
    x1 = e_out[0] + nn(o_out[0], w[1])
    x1_out[0] = x1
    a2 = (layer_stats(x1)[0] * gain[1:2, :]).astype(BF)
    acc = x1
    for j in range(cuts):
        need(6 + j)
        hid = nn(a2, w[6 + j])
        act = (hid * (0.5 * (1.0 + jnp.tanh(GELU_A * (hid + GELU_B * hid * hid * hid))))).astype(BF)
        need(6 + cuts + j)
        acc = acc + nn(act, w[6 + cuts + j])
    x2_out[0] = acc

    @pl.when(role[0] == 0)
    def _():
        t = layer_stats(x2_out[0])[0].astype(BF)
        tgt[0] = t
        t = t.astype(F32)
        for m in range(IMGS):
            inside = seg_col == m
            size = jnp.sum(jnp.where(inside, 1.0, 0.0), axis=0, keepdims=True)
            pooled = jnp.sum(jnp.where(inside, t, 0.0), axis=0, keepdims=True) / size
            unit = pooled * lax.rsqrt(jnp.sum(pooled * pooled, axis=-1, keepdims=True) + 1e-06)
            bank[0, m : m + 1, :] = unit.astype(BF)


def forward(role, patch, seg, pos, gain, w):
    batches, slots, width = patch.shape
    pieces = w.shape[0]
    tok = lambda dt: jax.ShapeDtypeStruct((batches, slots, width), dt)
    row = pl.BlockSpec((1, slots, width), lambda i: (i, 0, 0))
    return pl.pallas_call(
        fwd_kernel,
        name="forward",
        grid=(batches,),
        out_shape=(
            tok(F32),
            jax.ShapeDtypeStruct((3, batches * slots, width), BF),
            jax.ShapeDtypeStruct((batches, HEADS, slots), F32),
            tok(BF),
            tok(F32),
            tok(F32),
            tok(BF),
            jax.ShapeDtypeStruct((batches, IMGS, width), BF),
        ),
        in_specs=[
            smem_spec(),
            row,
            pl.BlockSpec((1, 1, slots), lambda i: (i, 0, 0)),
            pl.BlockSpec((1, 1, pos.shape[2]), lambda i: (i, 0, 0)),
            pl.BlockSpec((4, width), lambda i: (0, 0)),
            any_spec(),
        ],
        out_specs=(
            row,
            pl.BlockSpec((3, slots, width), lambda i: (0, i, 0)),
            pl.BlockSpec((1, HEADS, slots), lambda i: (i, 0, 0)),
            row,
            row,
            row,
            row,
            pl.BlockSpec((1, IMGS, width), lambda i: (i, 0, 0)),
        ),
        scratch_shapes=[
            pltpu.VMEM((pieces, width, width), BF),
            pltpu.VMEM((slots, slots), F32),
            pltpu.SemaphoreType.DMA((pieces,)),
        ],
        compiler_params=pltpu.CompilerParams(vmem_limit_bytes=VMEM_LIMIT),
    )(role, patch, seg, pos, gain, w)


def norm_back(grad_out, normed, scaled, gain_vec):
    grad_hat = grad_out * gain_vec
    inner = jnp.mean(grad_hat * normed, axis=-1, keepdims=True)
    grad_in = scaled * (grad_hat - jnp.mean(grad_hat, axis=-1, keepdims=True) - normed * inner)
    return grad_in, jnp.sum(grad_out * normed, axis=0, keepdims=True)


def bwd_kernel(
    listed, place, seg, pos, gain, e_in, qkv, lse, x1_in, x2_in, tgt, banks, w_hbm,
    head_out, attn_out, ffn_out, act_out, de_out, mid_out, pred_out, dqkv, du_out, down_out, small,
    w, bias, top_scr, pool_scr, sem,
):
    i = pl.program_id(0)
    role = place[0]
    slots, width = e_in.shape[1:]
    pieces = w_hbm.shape[0]
    cuts = (pieces - 6) // 2

    @pl.when(role == 0)
    def _():
        small[...] = jnp.zeros_like(small)

    @pl.when(role != 0)
    def _():
        order = [2]
        for j in range(cuts):
            order += [6 + cuts + j, 6 + j]
        order += [1, 3, 4, 5]

        @pl.when(i == 0)
        def _():
            for u in order:
                pltpu.make_async_copy(w_hbm.at[u], w.at[u - 1], sem.at[u]).start()
            small[...] = jnp.zeros_like(small)

        def need(u):
            @pl.when(i == 0)
            def _():
                pltpu.make_async_copy(w_hbm.at[u], w.at[u - 1], sem.at[u]).wait()

        seg_row = seg[0]
        seg_col = column_of(seg_row)
        fill_bias(bias, seg_col, seg_row)
        flags = flag_column(pos[0], slots)
        n3, r3 = layer_stats(x2_in[0])
        head_in = (n3 * gain[2:3, :]).astype(BF)
        head_out[0] = head_in
        need(2)
        pred = nn(head_in, w[1])
        valid = jnp.where(seg_col < IMGS, flags, 0).astype(F32)
        diff = pred - tgt[0].astype(F32)
        size = jnp.abs(diff)
        huber = jnp.where(size < 1.0, 0.5 * diff * diff, size - 0.5)
        regress = jnp.sum(jnp.sum(valid * huber, axis=1, keepdims=True), axis=0, keepdims=True)
        count = listed[0] * width
        grad_pred = valid * (jnp.clip(diff, -1.0, 1.0) / count)
        pool_scr[...] = jnp.zeros_like(pool_scr)
        for m in range(IMGS):
            inside = seg_col == m
            tally = jnp.sum(jnp.where(inside, 1.0, 0.0), axis=0, keepdims=True)
            pool_scr[m : m + 1, :] = jnp.sum(jnp.where(inside, pred, 0.0), axis=0, keepdims=True) / tally
        pooled = pool_scr[...]
        length = lax.rsqrt(jnp.sum(pooled * pooled, axis=-1, keepdims=True) + 1e-06)
        unit = pooled * length
        memory = banks[0]
        choices = memory.shape[0]
        logits = nt(unit.astype(BF), memory) / SOFTMAX_TEMPER
        row_id = lax.broadcasted_iota(jnp.int32, logits.shape, 0)
        real = row_id < IMGS
        picked = jnp.where(
            real & (lax.broadcasted_iota(jnp.int32, logits.shape, 1) == place[1] * IMGS + row_id), 1.0, 0.0
        )
        peak = jnp.max(logits, axis=-1, keepdims=True)
        ex = jnp.exp(logits - peak)
        total = jnp.sum(ex, axis=-1, keepdims=True)
        each = peak + jnp.log(total) - jnp.sum(logits * picked, axis=-1, keepdims=True)
        contrast = jnp.sum(jnp.where(real[:, 0:1], each, 0.0), axis=0, keepdims=True)
        scale = choices * MICRO_BATCHES
        grad_logits = (jnp.where(real, ex / total - picked, 0.0) / scale / SOFTMAX_TEMPER).astype(BF)
        grad_unit = nn(grad_logits, memory)
        grad_pool = length * (grad_unit - unit * jnp.sum(grad_unit * unit, axis=1, keepdims=True))
        pool_scr[...] = grad_pool
        for m in range(IMGS):
            inside = seg_col == m
            tally = jnp.sum(jnp.where(inside, 1.0, 0.0), axis=0, keepdims=True)
            grad_pred = grad_pred + jnp.where(inside, pool_scr[m : m + 1, :] / tally, 0.0)
        low = grad_pred.astype(BF)
        pred_out[0] = low
        loss = regress / count + contrast / scale
        small[4:5, :] += jnp.broadcast_to(loss, (1, width))
        grad_top, gain_three = norm_back(nt(low, w[1]), n3, r3, gain[2:3, :])
        small[2:3, :] += gain_three
        top_scr[...] = grad_top
        down = grad_top.astype(BF)
        down_out[0] = down
        n2, r2 = layer_stats(x1_in[0])
        ffn_in = (n2 * gain[1:2, :]).astype(BF)
        ffn_out[0] = ffn_in
        acc = None
        for j in range(cuts):
            need(6 + cuts + j)
            grad_act = nt(down, w[5 + cuts + j])
            need(6 + j)
            hid = nn(ffn_in, w[5 + j])
            th = jnp.tanh(GELU_A * (hid + GELU_B * hid * hid * hid))
            cdf = 0.5 * (1.0 + th)
            act_out[j] = (hid * cdf).astype(BF)
            slope = cdf + hid * (0.5 * (1.0 - th * th)) * (GELU_A * (1.0 + 3.0 * GELU_B * hid * hid))
            du = (grad_act * slope).astype(BF)
            du_out[j] = du
            part = nt(du, w[5 + j])
            acc = part if acc is None else acc + part
        grad_ffn, gain_two = norm_back(acc, n2, r2, gain[1:2, :])
        small[1:2, :] += gain_two
        mid = top_scr[...] + grad_ffn
        top_scr[...] = mid
        mid_low = mid.astype(BF)
        mid_out[0] = mid_low
        need(1)
        de_out[0] = nt(mid_low, w[0]).astype(BF)

        def pair(p, carry):
            cs = pl.ds(pl.multiple_of(p * LANES, LANES), LANES)
            q2, k2, v2, g2 = qkv[0, :, cs], qkv[1, :, cs], qkv[2, :, cs], de_out[0, :, cs]
            k_scaled = k2 * jnp.asarray(HEAD_DIM**-0.5, BF)
            k_t = k2.T
            dq, dk, dv = [], 0.0, 0.0
            for h in range(2):
                s = nt(half(k_scaled, h), q2) + bias[...]
                probs = jnp.exp(s - lse[0, pl.ds(2 * p + h, 1), :])
                dp = nt(half(v2, h), g2)
                centre = jnp.sum(probs * dp, axis=0, keepdims=True)
                ds = (probs * (dp - centre)).astype(BF)
                dv = dv + nn(probs.astype(BF), half(g2, h))
                dk = dk + nn(ds, half(q2, h))
                dq.append(nn(k_t[h * HEAD_DIM : (h + 1) * HEAD_DIM, :], ds))
            dqkv[0, :, cs] = (jnp.concatenate(dq, axis=0) * HEAD_DIM**-0.5).T.astype(BF)
            dqkv[1, :, cs] = (dk * HEAD_DIM**-0.5).astype(BF)
            dqkv[2, :, cs] = dv.astype(BF)
            return carry

        lax.fori_loop(0, HEADS // 2, pair, 0)
        acc = None
        for j in range(3):
            need(3 + j)
            part = nt(dqkv[j], w[2 + j])
            acc = part if acc is None else acc + part
        n1, r1 = layer_stats(e_in[0])
        attn_out[0] = (n1 * gain[0:1, :]).astype(BF)
        grad_attn, gain_one = norm_back(acc, n1, r1, gain[0:1, :])
        small[0:1, :] += gain_one
        start = top_scr[...] + grad_attn
        hidden_slot = flags > 0
        small[3:4, :] += jnp.sum(jnp.where(hidden_slot, start, 0.0), axis=0, keepdims=True)
        de_out[0] = jnp.where(hidden_slot, 0.0, start).astype(BF)


def backward(listed, place, seg, pos, gain, saved, tgt, banks, w):
    e, qkv, lse, x1, x2 = saved
    batches, slots, width = e.shape
    pieces = w.shape[0]
    cuts = (pieces - 6) // 2
    once = pl.Buffered(1)
    tok = lambda n: jax.ShapeDtypeStruct((n, batches * slots, width), BF)
    row_in = pl.BlockSpec((1, slots, width), lambda i: (i, 0, 0), pipeline_mode=once)
    piece = lambda n: pl.BlockSpec((n, slots, width), lambda i: (0, i, 0))
    return pl.pallas_call(
        bwd_kernel,
        name="backward",
        grid=(batches,),
        out_shape=(
            tok(1), tok(1), tok(1), tok(cuts), tok(1), tok(1), tok(1), tok(3), tok(cuts), tok(1),
            jax.ShapeDtypeStruct((SUBLANES, width), F32),
        ),
        in_specs=[
            smem_spec(),
            smem_spec(),
            pl.BlockSpec((1, 1, slots), lambda i: (i, 0, 0)),
            pl.BlockSpec((1, 1, pos.shape[2]), lambda i: (i, 0, 0)),
            pl.BlockSpec((4, width), lambda i: (0, 0)),
            row_in,
            pl.BlockSpec((3, slots, width), lambda i: (0, i, 0), pipeline_mode=once),
            pl.BlockSpec((1, HEADS, slots), lambda i: (i, 0, 0)),
            row_in,
            row_in,
            row_in,
            pl.BlockSpec((1,) + banks.shape[1:], lambda i: (i, 0, 0), pipeline_mode=once),
            any_spec(),
        ],
        out_specs=(
            piece(1), piece(1), piece(1), piece(cuts), piece(1), piece(1), piece(1), piece(3), piece(cuts), piece(1),
            pl.BlockSpec((SUBLANES, width), lambda i: (0, 0)),
        ),
        scratch_shapes=[
            pltpu.VMEM((pieces - 1, width, width), BF),
            pltpu.VMEM((slots, slots), F32),
            pltpu.VMEM((slots, width), F32),
            pltpu.VMEM((SUBLANES, width), F32),
            pltpu.SemaphoreType.DMA((pieces,)),
        ],
        compiler_params=pltpu.CompilerParams(vmem_limit_bytes=VMEM_LIMIT),
    )(listed, place, seg, pos, gain, e, qkv, lse, x1, x2, tgt, banks, w)


def grads_kernel(
    plan, role, places, patch, mixed, head, attn, ffn, act, de, mid, pred, dqkv, du, down, out,
    rows_scr, x_buf, x_t, g_buf, stage, outbuf, x_sem, g_sem, out_sem,
):
    blocks, rows, width = out.shape
    cols = width // LANES
    deep, wide_out = x_buf.shape[0], outbuf.shape[0]
    group = max([g for g in range(SUBLANES, 49, SUBLANES) if rows % g == 0], default=rows)
    lefts = {"patch": patch, "mixed": mixed, "head": head, "attn": attn, "ffn": ffn, "act": act}
    rights = {"de": de, "mid": mid, "pred": pred, "dqkv": dqkv, "du": du, "down": down}

    @pl.when(role[0] == 0)
    def _():
        outbuf[...] = jnp.zeros_like(outbuf)

        def put(b, carry):
            pltpu.make_async_copy(outbuf.at[0], out.at[b], out_sem.at[0]).start()
            return carry

        def done(b, carry):
            pltpu.make_async_copy(outbuf.at[0], out.at[b], out_sem.at[0]).wait()
            return carry

        lax.fori_loop(0, blocks, put, 0)
        lax.fori_loop(0, blocks, done, 0)

    @pl.when(role[0] != 0)
    def _():
        lcopies, rcopies = [], []
        lkeys, rkeys = [], []
        steps = []
        for u, (left, right) in enumerate(plan):
            if not lkeys or lkeys[-1] != left:
                slot = len(lkeys) % deep
                lcopies.append(pltpu.make_async_copy(lefts[left[0]].at[left[1]], x_buf.at[slot], x_sem.at[slot]))
                lkeys.append(left)
                fresh_l = True
            else:
                fresh_l = False
            if not rkeys or rkeys[-1] != right:
                slot = len(rkeys) % deep
                rcopies.append(pltpu.make_async_copy(rights[right[0]].at[right[1]], g_buf.at[slot], g_sem.at[slot]))
                rkeys.append(right)
                fresh_r = True
            else:
                fresh_r = False
            steps.append((u, len(lkeys) - 1, fresh_l, len(rkeys) - 1, fresh_r))
        for copy in lcopies[: deep - 1] + rcopies[: deep - 1]:
            copy.start()
        for u, li, fresh_l, ri, fresh_r in steps:
            if fresh_l:
                lcopies[li].wait()
                if li + deep - 1 < len(lcopies):
                    lcopies[li + deep - 1].start()
                x_t[...] = x_buf[li % deep].T
            if fresh_r:
                rcopies[ri].wait()
                if ri + deep - 1 < len(rcopies):
                    rcopies[ri + deep - 1].start()
            wide = 2 * LANES

            def tile(n, carry):
                part = nn(x_t[...], g_buf[ri % deep, :, pl.ds(pl.multiple_of(n * wide, wide), wide)])
                for c in range(2):
                    rows_scr[pl.ds(u * width * SUBLANES + 2 * n + c, width, stride=SUBLANES), :] = part[
                        :, c * LANES : (c + 1) * LANES
                    ]
                return carry

            lax.fori_loop(0, width // wide, tile, 0)

        def block(b, carry):
            slot = lax.rem(b, wide_out)

            def move(q, carry):
                came = [pl.multiple_of(places[b * rows + q * group + j] * SUBLANES, SUBLANES) for j in range(group)]
                held = [rows_scr[pl.ds(first, SUBLANES), :] for first in came]
                for j in range(group):
                    to = q * (group // SUBLANES) * TILE + j // SUBLANES * TILE + j % SUBLANES
                    stage[pl.ds(to, SUBLANES, stride=SUBLANES), :] = held[j]
                return carry

            lax.fori_loop(0, rows // group, move, 0)

            @pl.when(b >= wide_out)
            def _():
                pltpu.make_async_copy(outbuf.at[slot], out.at[b - wide_out], out_sem.at[slot]).wait()

            for first in range(0, rows, 16):
                tall = min(16, rows - first)
                for c in range(cols):
                    at = first * SUBLANES + c * SUBLANES
                    both = jnp.concatenate([stage[at : at + SUBLANES, :], stage[at + TILE : at + TILE + SUBLANES, :]], 0)
                    outbuf[slot, first : first + tall, c * LANES : (c + 1) * LANES] = both[:tall].astype(BF)
            pltpu.make_async_copy(outbuf.at[slot], out.at[b], out_sem.at[slot]).start()
            return carry

        lax.fori_loop(0, blocks, block, 0)
        for b in range(blocks - wide_out, blocks):
            pltpu.make_async_copy(outbuf.at[b % wide_out], out.at[b], out_sem.at[b % wide_out]).wait()


def weight_grads(role, places, lefts, rights, blocks):
    tokens, width = lefts[0].shape[1:]
    cuts = lefts[-1].shape[0]
    total = places.shape[0]
    rows = total // blocks
    plan = (
        [(("patch", 0), ("de", 0)), (("mixed", 0), ("mid", 0)), (("head", 0), ("pred", 0))]
        + [(("attn", 0), ("dqkv", j)) for j in range(3)]
        + [(("ffn", 0), ("du", j)) for j in range(cuts)]
        + [(("act", j), ("down", 0)) for j in range(cuts)]
    )
    return pl.pallas_call(
        functools.partial(grads_kernel, plan),
        name="weight_grads",
        out_shape=jax.ShapeDtypeStruct((blocks, rows, width), BF),
        in_specs=[smem_spec(), smem_spec()] + [any_spec()] * 12,
        out_specs=any_spec(),
        scratch_shapes=[
            pltpu.VMEM((total * SUBLANES, LANES), F32),
            pltpu.VMEM((3, tokens, width), BF),
            pltpu.VMEM((width, tokens), BF),
            pltpu.VMEM((3, tokens, width), BF),
            pltpu.VMEM((pl.cdiv(rows, 16) * 2 * TILE, LANES), F32),
            pltpu.VMEM((4, rows, width), BF),
            pltpu.SemaphoreType.DMA((3,)),
            pltpu.SemaphoreType.DMA((3,)),
            pltpu.SemaphoreType.DMA((4,)),
        ],
        compiler_params=pltpu.CompilerParams(vmem_limit_bytes=VMEM_LIMIT),
    )(role, places, *lefts, *rights)


def adam_update(weight, first_state, second_state, gradient, step_value, decay_rate):
    first_state = BETA_ONE * first_state + (1.0 - BETA_ONE) * gradient
    second_state = BETA_TWO * second_state + (1.0 - BETA_TWO) * gradient * gradient
    fix_one = 1.0 - jnp.power(BETA_ONE, step_value)
    fix_two = 1.0 - jnp.power(BETA_TWO, step_value)
    update = first_state / fix_one / (jnp.sqrt(second_state / fix_two) + ADAM_EPS)
    return (weight - RATE * (update + decay_rate * weight), first_state, second_state)


def body(
    patches,
    segments,
    positions,
    owners,
    master,
    moment_one,
    moment_two,
    teacher,
    gains,
    gain_one,
    gain_two,
    teacher_gains,
    step_count,
):
    core = lax.axis_index("group")
    width = patches.shape[3]
    slots = patches.shape[2]
    row_total = owners.shape[0]
    inner = (row_total - 6 * width) // 2
    places = piece_rows(owners, width, inner)
    spots = places // SUBLANES * TILE + places % SUBLANES
    chips = lax.axis_size("dp")
    devices = lax.axis_size("group") * chips
    own_rows = row_total // devices
    role = core.astype(jnp.int32).reshape(1)
    place = jnp.stack([core, lax.axis_index("dp")]).astype(jnp.int32)
    listed = jnp.full((1,), MASKED * lax.axis_size("dp") * MICRO_BATCHES, F32)

    both = jnp.stack([teacher, master]).astype(BF)
    if chips <= KERNEL_CHIPS:
        model = gather_weights(both, chips)
    else:
        parts = lax.all_gather(both, ("dp", "group"), axis=1)
        model = jnp.where(core == 1, parts[1], parts[0]).reshape(chips, 2, own_rows, width)
    w = place_weights(spots, model)
    gain_set = jnp.where(core == 1, gains, teacher_gains)
    patch = patches[:, 0]
    seg = segments
    pos = positions
    e, qkv, lse, mixed, x1, x2, tgt, bank = forward(role, patch, seg, pos, gain_set, w)
    tgt, banks = exchange_targets(tgt, bank, chips)
    banks = jnp.swapaxes(banks, 0, 1).reshape(MICRO_BATCHES, chips * IMGS, width)
    head, attn, ffn, act, de, mid, pred, dqkv, du, down, small = backward(
        listed, place, seg, pos, gain_set, (e, qkv, lse, x1, x2), tgt, banks, w
    )
    flat = lambda a: a.reshape(1, MICRO_BATCHES * slots, width)
    blocked = weight_grads(
        role,
        places,
        (flat(patch), flat(mixed), head, attn, ffn, act),
        (de, mid, pred, dqkv, du, down),
        devices,
    )
    if chips <= KERNEL_CHIPS:
        owned_grad = reduce_grads(blocked.reshape(2, chips, own_rows, width), chips)
    else:
        owned_grad = lax.psum_scatter(blocked, ("group", "dp"), scatter_dimension=0, tiled=True)
        owned_grad = owned_grad.reshape(own_rows, width).astype(F32)
    square_own = jnp.sum(owned_grad * owned_grad)
    row_id = lax.broadcasted_iota(jnp.int32, small.shape, 0)
    small = sum_tiles(jnp.where(row_id == 5, square_own, small), chips)
    gain_sum, loss_sum, square_sum = small[0:4], small[4, 0], small[5, 0]
    grad_norm = jnp.sqrt(square_sum + jnp.sum(gain_sum * gain_sum))
    factor = jnp.minimum(1.0, CLIP / grad_norm)
    step_value = step_count[0].astype(F32)
    master_new, one_new, two_new = adam_update(
        master, moment_one, moment_two, owned_grad * factor, step_value, DECAY
    )
    gone_new, gtwo_new = adam_update(gains, gain_one, gain_two, gain_sum * factor, step_value, 0.0)[1:]
    teacher_new = EMA_KEEP * teacher + (1.0 - EMA_KEEP) * master_new
    return (
        loss_sum.reshape(1),
        grad_norm.reshape(1),
        one_new,
        two_new,
        master_new,
        teacher_new,
        gone_new,
        gtwo_new,
    )


def solution(mesh):
    rows = P(("group", "dp"), None)
    in_specs = (
        P(None, "dp", None, None),
        P(None, "dp", None),
        P(None, "dp", None),
        P(),
        rows,
        rows,
        rows,
        rows,
        P(),
        P(),
        P(),
        P(),
        P(),
    )
    out_specs = (P(), P(), rows, rows, rows, rows, P(), P())
    return jax.shard_map(body, mesh=mesh, in_specs=in_specs, out_specs=out_specs, check_vma=False)
```

```python
import functools

import jax
import jax.numpy as jnp
from jax import lax
from jax.experimental import pallas as pl
from jax.experimental.pallas import tpu as pltpu
from jax.sharding import PartitionSpec as P

HEADS = 12
HEAD_DIM = 64
IMGS = 4
MASKED = 320
MICRO_BATCHES = 2
LANES = 128
SUBLANES = 8
TILE = SUBLANES * SUBLANES

SOFTMAX_TEMPER = 0.05
CLIP = 0.004
RATE = 0.05
BETA_ONE = 0.9
BETA_TWO = 0.999
ADAM_EPS = 1e-08
DECAY = 0.05
EMA_KEEP = 0.9
MASK_FILL = -1000000000.0

BF = jnp.bfloat16
F32 = jnp.float32
VMEM_LIMIT = 67_000_000
GELU_A = 0.7978845608028654
GELU_B = 0.044715


def nn(a, b):
    return jnp.dot(a, b, preferred_element_type=F32)


def nt(a, b):
    return lax.dot_general(a, b, (((1,), (1,)), ((), ())), preferred_element_type=F32)


def piece_rows(flat, width, inner):
    cuts = inner // width
    qkv, up = flat - 3 * width, flat - 6 * width
    inside = jnp.where(flat < 6 * width, (3 + qkv % 3) * width + qkv // 3, (6 + up % cuts) * width + up // cuts)
    return jnp.where((flat >= 3 * width) & (flat < 6 * width + inner), inside, flat)


def any_spec():
    return pl.BlockSpec(memory_space=pl.ANY)


def smem_spec():
    return pl.BlockSpec(memory_space=pltpu.SMEM)


MESH = pl.DeviceIdType.MESH
KERNEL_CHIPS = 16


def chip_grid(chips):
    sizes, turn, left, prime = [1, 1, 1], 0, chips, 2
    while left > 1:
        while left % prime:
            prime += 1
        sizes[turn % 3] *= prime
        turn += 1
        left //= prime
    return tuple(sizes)


def strides_of(grid):
    return (grid[1] * grid[2], grid[2], 1)


def coords_of(index, grid):
    return (index // (grid[1] * grid[2]), lax.rem(index // grid[2], grid[1]), lax.rem(index, grid[2]))


def guarded(conditions, action):
    conditions = [c for c in conditions if c is not None]
    if not conditions:
        return action()
    both = conditions[0]
    for c in conditions[1:]:
        both = jnp.logical_and(both, c)
    pl.when(both)(action)


def lanes_of(width):
    unit = width // 6
    orders = [((1, 0, 2), 2), ((2, 0, 1), 2), ((0, 2, 1), 1), ((0, 1, 2), 1)]
    routes, first = [], 0
    for order, share in orders:
        routes.append((order, first, share * unit))
        first += share * unit
    return routes


def offsets(length):
    if length <= 2:
        return list(range(length))
    return [0] + [sign * far for far in range(1, length) for sign in (1, -1)]


def route_events(grid, routes):
    events = []
    for c, (order, _, _) in enumerate(routes):
        stack = [()]
        for d in order:
            stack = [r + (o,) for r in stack for o in offsets(grid[d])]
        events += [(sum(abs(o) * 2**i for i, o in enumerate(r)), c, r) for r in stack]
    return [(c, r) for _, c, r in sorted(events, key=lambda e: e[0])]


def onward(grid, order, r):
    last = max([i for i in range(3) if r[i]], default=-1)
    outs = []
    if last >= 0 and grid[order[last]] > 2:
        outs.append((order[last], 1 if r[last] > 0 else -1))
    for d in order[last + 1 :]:
        if grid[d] == 2:
            outs.append((d, 1))
        elif grid[d] > 2:
            outs += [(d, 1), (d, -1)]
    return outs


def neighbour(me, coords, grid, d, sign):
    step = strides_of(grid)[d]
    if grid[d] == 2:
        return me + (1 - 2 * coords[d]) * step, None
    place = coords[d] + sign
    return me + sign * step, jnp.logical_and(place >= 0, place < grid[d])


def origin(me, coords, grid, order, r):
    index, conditions = me, []
    for d, o in zip(order, r):
        if o == 0:
            continue
        step = strides_of(grid)[d]
        if grid[d] == 2:
            index = index + (1 - 2 * coords[d]) * step
        else:
            place = coords[d] - o
            index = index - o * step
            conditions.append(jnp.logical_and(place >= 0, place < grid[d]))
    return index, conditions


def slot_of(grid, d, sign):
    first = sum([1 if n <= 2 else 2 for n in grid[:d]])
    return first if grid[d] <= 2 or sign > 0 else first + 1


def slots_of(grid):
    return sum([1 if n <= 2 else 2 for n in grid])


def greet(me, coords, grid, group):
    barrier = pltpu.get_barrier_semaphore()
    near = [neighbour(me, coords, grid, d, s) for d in range(3) for s in ((1,) if grid[d] == 2 else (1, -1)) if grid[d] > 1]
    for index, there in near:
        guarded([there], lambda: pl.semaphore_signal(barrier, 1, device_id={"dp": index}, device_id_type=MESH))
    pl.semaphore_signal(barrier, 1, device_id={"group": 1 - group}, device_id_type=MESH)
    pl.semaphore_wait(barrier, 1 + sum([1 if there is None else there.astype(jnp.int32) for _, there in near]))


def gather_kernel(grid, both, out, swap_sem, send_sem, recv_sem):
    group, me = lax.axis_index("group"), lax.axis_index("dp")
    coords = coords_of(me, grid)
    routes = lanes_of(both.shape[2])
    events = route_events(grid, routes)
    keep = pltpu.make_async_copy(both.at[group], out.at[me, group], swap_sem.at[2])
    keep.start()
    greet(me, coords, grid, group)
    swap = pltpu.make_async_remote_copy(
        both.at[1 - group], out.at[me, group], swap_sem.at[0], swap_sem.at[1], {"group": 1 - group}, MESH
    )
    swap.start()
    keep.wait()
    swap.wait()

    def visit(c, r, act):
        order, first, wide = routes[c]
        block, real = origin(me, coords, grid, order, r)
        part = out.at[block, :, :, first : first + wide]

        def run():
            copies = []
            for d, sign in onward(grid, order, r):
                index, there = neighbour(me, coords, grid, d, sign)
                copies.append(
                    (
                        there,
                        pltpu.make_async_remote_copy(
                            part,
                            part,
                            send_sem.at[c, slot_of(grid, d, sign), block],
                            recv_sem.at[c, block],
                            {"dp": index},
                            MESH,
                        ),
                    )
                )
            act(part, recv_sem.at[c, block], any(r), copies)

        guarded(real, run)

    def forward_on(part, arrival_sem, remote, copies):
        if remote:
            pltpu.make_async_remote_copy(part, part, swap_sem.at[0], arrival_sem, {"dp": me}, MESH).wait_recv()
        for there, copy in copies:
            guarded([there], copy.start)

    def finish(part, arrival_sem, remote, copies):
        for there, copy in copies:
            guarded([there], copy.wait_send)

    for c, r in events:
        visit(c, r, forward_on)
    for c, r in events:
        visit(c, r, finish)


def gather_weights(both, chips):
    grid = chip_grid(chips)
    _, rows, width = both.shape
    return pl.pallas_call(
        functools.partial(gather_kernel, grid),
        name="gather_weights",
        out_shape=jax.ShapeDtypeStruct((chips, 2, rows, width), BF),
        in_specs=[pl.BlockSpec(memory_space=pltpu.VMEM)],
        out_specs=any_spec(),
        scratch_shapes=[
            pltpu.SemaphoreType.DMA((3,)),
            pltpu.SemaphoreType.DMA((4, slots_of(grid), chips)),
            pltpu.SemaphoreType.DMA((4, chips)),
        ],
        compiler_params=pltpu.CompilerParams(
            collective_id=1, has_side_effects=True, vmem_limit_bytes=VMEM_LIMIT
        ),
    )(both)


def reduce_kernel(grid, blocked, out, acc, heard, load_sem, half_sem, send_sem, recv_sem):
    group, me = lax.axis_index("group"), lax.axis_index("dp")
    coords = coords_of(me, grid)
    rows, width = out.shape
    routes = lanes_of(width)
    events = route_events(grid, routes)[::-1]
    across = slots_of(grid)
    tall = max([t for t in range(16, 49, 16) if rows % t == 0], default=rows)

    def spot(c, r):
        return tuple(r[routes[c][0].index(d)] for d in range(3))

    firsts = list(dict.fromkeys([spot(c, r) for c, r in events]))
    greet(me, coords, grid, group)

    def load(where, act):
        block, real = origin(me, coords, grid, (0, 1, 2), where)
        local = pltpu.make_async_copy(blocked.at[group, block], acc.at[block], load_sem.at[block])
        half = pltpu.make_async_remote_copy(
            blocked.at[1 - group, block],
            heard.at[across, block],
            half_sem.at[0, block],
            half_sem.at[1, block],
            {"group": 1 - group},
            MESH,
        )
        guarded(real, lambda: act(local, half))

    def load_start(local, half):
        half.start()
        local.start()

    def load_wait(local, half):
        local.wait()
        half.wait_recv()

    def load_end(local, half):
        half.wait_send()

    for where in firsts:
        load(where, load_start)

    def parent(c, r, block):
        order, first, wide = routes[c]
        i = max([i for i in range(3) if r[i]])
        sign = 1 if r[i] > 0 else -1
        index, _ = neighbour(me, coords, grid, order[i], -sign)
        slot = slot_of(grid, order[i], sign)
        return pltpu.make_async_remote_copy(
            acc.at[block, :, first : first + wide],
            heard.at[slot, block, :, first : first + wide],
            send_sem.at[c, block],
            recv_sem.at[c, slot, block],
            {"dp": index},
            MESH,
        )

    def visit(c, r):
        order, first, wide = routes[c]
        block, real = origin(me, coords, grid, order, r)

        def run():
            children = [(slot_of(grid, d, s), neighbour(me, coords, grid, d, s)[1]) for d, s in onward(grid, order, r)]
            for slot, there in children:
                part = heard.at[slot, block, :, first : first + wide]
                arrival = pltpu.make_async_remote_copy(
                    part, part, send_sem.at[c, block], recv_sem.at[c, slot, block], {"dp": me}, MESH
                )
                guarded([there], arrival.wait_recv)
            children = [(across, None)] + children

            if any(r):
                for slot, there in children:

                    def total(slot=slot):
                        def piece(k, carry):
                            at = (pl.ds(pl.multiple_of(k * tall, tall), tall), slice(first, first + wide))
                            acc[(block,) + at] = (
                                acc[(block,) + at].astype(F32) + heard[(slot, block) + at].astype(F32)
                            ).astype(BF)
                            return carry

                        lax.fori_loop(0, rows // tall, piece, 0)

                    guarded([there], total)
                parent(c, r, block).start()
            else:

                def first_piece(k, carry):
                    at = (pl.ds(pl.multiple_of(k * tall, tall), tall), slice(first, first + wide))
                    out[at] = acc[(block,) + at].astype(F32)
                    return carry

                lax.fori_loop(0, rows // tall, first_piece, 0)
                for slot, there in children:

                    def total(slot=slot):
                        def piece(k, carry):
                            at = (pl.ds(pl.multiple_of(k * tall, tall), tall), slice(first, first + wide))
                            out[at] = out[at] + heard[(slot, block) + at].astype(F32)
                            return carry

                        lax.fori_loop(0, rows // tall, piece, 0)

                    guarded([there], total)

        guarded(real, run)

    ready = set()
    for c, r in events:
        if spot(c, r) not in ready:
            ready.add(spot(c, r))
            load(spot(c, r), load_wait)
        visit(c, r)
    for c, r in events:
        if any(r):
            block, real = origin(me, coords, grid, routes[c][0], r)
            guarded(real, parent(c, r, block).wait_send)
    for where in firsts:
        load(where, load_end)


def reduce_grads(blocked, chips):
    grid = chip_grid(chips)
    _, _, rows, width = blocked.shape
    return pl.pallas_call(
        functools.partial(reduce_kernel, grid),
        name="reduce_grads",
        out_shape=jax.ShapeDtypeStruct((rows, width), F32),
        in_specs=[any_spec()],
        out_specs=pl.BlockSpec(memory_space=pltpu.VMEM),
        scratch_shapes=[
            pltpu.VMEM((chips, rows, width), BF),
            pltpu.VMEM((slots_of(grid) + 1, chips, rows, width), BF),
            pltpu.SemaphoreType.DMA((chips,)),
            pltpu.SemaphoreType.DMA((2, chips)),
            pltpu.SemaphoreType.DMA((4, chips)),
            pltpu.SemaphoreType.DMA((4, slots_of(grid), chips)),
        ],
        compiler_params=pltpu.CompilerParams(
            collective_id=2, has_side_effects=True, vmem_limit_bytes=VMEM_LIMIT
        ),
    )(blocked)


def exchange_kernel(*refs):
    count = (len(refs) - 7) // 2
    bank, states, banks = refs[count], refs[count + 1 : 2 * count + 1], refs[2 * count + 1]
    state_send, state_recv, send_sem, recv_sem, own_sem = refs[2 * count + 2 :]
    group, me = lax.axis_index("group"), lax.axis_index("dp")
    chips = banks.shape[0]
    barrier = pltpu.get_barrier_semaphore()

    def hail(target):
        def one(k, carry):
            pl.semaphore_signal(barrier, 1, device_id=(target, lax.rem(me + k, chips)), device_id_type=MESH)
            return carry

        return one

    @pl.when(group == 0)
    def _():
        lax.fori_loop(1, chips, hail(0), 0)
        lax.fori_loop(0, chips, hail(1), 0)

    @pl.when(group == 1)
    def _():
        lax.fori_loop(0, chips, hail(0), 0)

    pl.semaphore_wait(barrier, chips + (1 - group) * (chips - 1))

    def crossing(k):
        ref = states[k]
        if k == count - 1:
            part = ref.at[1]
        elif len(ref.shape) == 3 and ref.shape[0] == 3:
            part = ref.at[:, : ref.shape[1] // MICRO_BATCHES, :]
        else:
            part = ref.at[0]
        return pltpu.make_async_remote_copy(
            part, part, state_send.at[k], state_recv.at[k], {"group": 1 - group}, MESH
        )

    def note(core, k):
        return pltpu.make_async_remote_copy(
            bank.at[core],
            banks.at[me],
            send_sem.at[core, k],
            recv_sem.at[me],
            (core, lax.rem(me + k, chips)),
            MESH,
        )

    def each(core, act):
        def one(k, carry):
            act(note(core, k))
            return carry

        return one

    def take(k, carry):
        pltpu.make_async_remote_copy(
            bank.at[0], banks.at[k], send_sem.at[0, 0], recv_sem.at[k], (1 - group, me), MESH
        ).wait_recv()
        return carry

    @pl.when(group == 0)
    def _():
        own = pltpu.make_async_copy(bank.at[0], banks.at[me], own_sem)
        own.start()
        lax.fori_loop(1, chips, each(0, lambda copy: copy.start()), 0)
        lax.fori_loop(0, chips, each(1, lambda copy: copy.start()), 0)
        targets = crossing(count - 1)
        targets.start()
        own.wait()
        lax.fori_loop(1, chips, lambda k, carry: take(lax.rem(me + k, chips), carry), 0)
        for k in range(count - 1):
            crossing(k).wait_recv()
        lax.fori_loop(1, chips, each(0, lambda copy: copy.wait_send()), 0)
        lax.fori_loop(0, chips, each(1, lambda copy: copy.wait_send()), 0)
        targets.wait_send()

    @pl.when(group == 1)
    def _():
        copies = [crossing(k) for k in range(count - 1)]
        for copy in copies:
            copy.start()
        lax.fori_loop(0, chips, take, 0)
        crossing(count - 1).wait_recv()
        for copy in copies:
            copy.wait_send()


def exchange_states(states, bank, chips):
    count = len(states)
    outs = pl.pallas_call(
        exchange_kernel,
        name="exchange_states",
        out_shape=tuple(jax.ShapeDtypeStruct(a.shape, a.dtype) for a in states)
        + (jax.ShapeDtypeStruct((chips,) + bank.shape[1:], BF),),
        in_specs=[any_spec()] * (count + 1),
        out_specs=(any_spec(),) * (count + 1),
        scratch_shapes=[
            pltpu.SemaphoreType.DMA((count,)),
            pltpu.SemaphoreType.DMA((count,)),
            pltpu.SemaphoreType.DMA((2, chips)),
            pltpu.SemaphoreType.DMA((chips,)),
            pltpu.SemaphoreType.DMA,
        ],
        input_output_aliases={k: k for k in range(count)},
        compiler_params=pltpu.CompilerParams(collective_id=3, has_side_effects=True),
    )(*states, bank)
    return outs[:-1], outs[-1]


def sum_kernel(grid, tile, out, heard, send_sem, recv_sem):
    group, me = lax.axis_index("group"), lax.axis_index("dp")
    coords = coords_of(me, grid)
    lengths = (2,) + grid
    mine = (group,) + coords
    peers = []
    for s, length in enumerate(lengths):
        for k in range(1, length):
            other = lax.rem(mine[s] + k, length)
            if s == 0:
                peers.append((s, k, (other, me)))
            else:
                peers.append((s, k, (group, me + (other - mine[s]) * strides_of(grid)[s - 1])))
    barrier = pltpu.get_barrier_semaphore()
    for _, _, device in peers:
        pl.semaphore_signal(barrier, 1, device_id=device, device_id_type=MESH)
    pl.semaphore_wait(barrier, len(peers))
    out[...] = tile[...]
    for s, length in enumerate(lengths):
        if length == 1:
            continue
        heard[s, mine[s]] = out[...]
        copies = [
            pltpu.make_async_remote_copy(
                heard.at[s, mine[s]], heard.at[s, mine[s]], send_sem.at[s, k], recv_sem.at[s, mine[s]], device, MESH
            )
            for t, k, device in peers
            if t == s
        ]
        for copy in copies:
            copy.start()
        for k in range(1, length):
            other = lax.rem(mine[s] + k, length)
            pltpu.make_async_remote_copy(
                heard.at[s, other], heard.at[s, other], send_sem.at[s, k], recv_sem.at[s, other], (group, me), MESH
            ).wait_recv()
        total = heard[s, 0]
        for k in range(1, length):
            total = total + heard[s, k]
        out[...] = total
        for copy in copies:
            copy.wait_send()


def sum_tiles(tile, chips):
    grid = chip_grid(chips)
    most = max((2,) + grid)
    return pl.pallas_call(
        functools.partial(sum_kernel, grid),
        name="sum_tiles",
        out_shape=jax.ShapeDtypeStruct(tile.shape, F32),
        in_specs=[pl.BlockSpec(memory_space=pltpu.VMEM)],
        out_specs=pl.BlockSpec(memory_space=pltpu.VMEM),
        scratch_shapes=[
            pltpu.VMEM((4, most) + tile.shape, F32),
            pltpu.SemaphoreType.DMA((4, most)),
            pltpu.SemaphoreType.DMA((4, most)),
        ],
        compiler_params=pltpu.CompilerParams(collective_id=4, has_side_effects=True),
    )(tile)


def place_kernel(spots, model, out, rows_scr, inbuf, stage, outbuf, in_sem, out_sem):
    chips, cores, rows, width = model.shape
    blocks = cores * chips
    cols = width // LANES
    deep, wide = inbuf.shape[0], outbuf.shape[0]
    group = max([g for g in range(1, 17) if rows % g == 0])

    def fetch(b, slot):
        return pltpu.make_async_copy(model.at[lax.rem(b, chips), b // chips], inbuf.at[slot], in_sem.at[slot])

    for b in range(deep - 1):
        fetch(b, b).start()

    def block(b, carry):
        slot = lax.rem(b, deep)
        fetch(b, slot).wait()

        @pl.when(b + deep - 1 < blocks)
        def _():
            fetch(b + deep - 1, lax.rem(b + deep - 1, deep)).start()

        for c in range(cols):
            stage[pl.ds(c, rows, stride=SUBLANES), :] = inbuf[slot, :, c * LANES : (c + 1) * LANES].astype(F32)

        def move(q, carry):
            first = q * group
            to = [spots[b * rows + first + j] for j in range(group)]
            held = [stage[pl.ds(pl.multiple_of((first + j) * SUBLANES, SUBLANES), SUBLANES), :] for j in range(group)]
            for j in range(group):
                rows_scr[pl.ds(to[j], SUBLANES, stride=SUBLANES), :] = held[j]
            return carry

        return lax.fori_loop(0, rows // group, move, carry)

    lax.fori_loop(0, blocks, block, 0)
    pieces = out.shape[0]
    for u in range(pieces):
        slot = u % wide
        if u >= wide:
            pltpu.make_async_copy(outbuf.at[slot], out.at[u - wide], out_sem.at[slot]).wait()

        def pack(k, carry):
            to = pl.ds(pl.multiple_of(k * 16, 16), 16)
            for c in range(cols):
                first = (u * width // SUBLANES + 2 * k) * TILE + c * SUBLANES
                halves = [rows_scr[pl.ds(pl.multiple_of(first + TILE * h, SUBLANES), SUBLANES), :] for h in range(2)]
                outbuf[slot, to, c * LANES : (c + 1) * LANES] = jnp.concatenate(halves, axis=0).astype(BF)
            return carry

        lax.fori_loop(0, width // 16, pack, 0)
        pltpu.make_async_copy(outbuf.at[slot], out.at[u], out_sem.at[slot]).start()
    for u in range(pieces - wide, pieces):
        pltpu.make_async_copy(outbuf.at[u % wide], out.at[u], out_sem.at[u % wide]).wait()


def place_weights(spots, model):
    _, _, rows, width = model.shape
    total = spots.shape[0]
    return pl.pallas_call(
        place_kernel,
        name="place_weights",
        out_shape=jax.ShapeDtypeStruct((total // width, width, width), BF),
        in_specs=[smem_spec(), any_spec()],
        out_specs=any_spec(),
        scratch_shapes=[
            pltpu.VMEM((total * SUBLANES, LANES), F32),
            pltpu.VMEM((8, rows, width), BF),
            pltpu.VMEM((rows * SUBLANES, LANES), F32),
            pltpu.VMEM((4, width, width), BF),
            pltpu.SemaphoreType.DMA((8,)),
            pltpu.SemaphoreType.DMA((4,)),
        ],
        compiler_params=pltpu.CompilerParams(vmem_limit_bytes=VMEM_LIMIT),
    )(spots, model)


def layer_stats(tensor):
    centre = tensor - jnp.mean(tensor, axis=-1, keepdims=True)
    scaled = lax.rsqrt(jnp.mean(centre * centre, axis=-1, keepdims=True) + 1e-06)
    return centre * scaled, scaled


def column_of(row):
    n = row.shape[1]
    eye = lax.broadcasted_iota(jnp.int32, (n, n), 0) == lax.broadcasted_iota(jnp.int32, (n, n), 1)
    return jnp.sum(jnp.where(eye, row, 0), axis=1, keepdims=True)


def flag_column(pos, slots):
    hit = lax.broadcasted_iota(jnp.int32, (slots, pos.shape[1]), 0) == pos
    return jnp.max(jnp.where(hit, 1, 0), axis=1, keepdims=True)


def fill_bias(bias, seg_col, seg_row):
    bias[...] = jnp.where(seg_col == seg_row, 0.0, MASK_FILL)


def half(x, h):
    low = lax.broadcasted_iota(jnp.int32, (1, LANES), 1) < HEAD_DIM
    keep = low if h == 0 else jnp.logical_not(low)
    return jnp.where(keep, x, jnp.zeros_like(x))


def fwd_kernel(role, patch, seg, pos, gain, w_hbm, e_out, qkv, lse, o_out, x1_out, x2_out, tgt, bank, w, bias, sem):
    i = pl.program_id(0)
    slots, width = patch.shape[1:]
    pieces = w_hbm.shape[0]
    cuts = (pieces - 6) // 2
    order = [0, 3, 4, 5, 1]
    for j in range(cuts):
        order += [6 + j, 6 + cuts + j]

    @pl.when(i == 0)
    def _():
        for u in order:
            pltpu.make_async_copy(w_hbm.at[u], w.at[u], sem.at[u]).start()

    def need(u):
        @pl.when(i == 0)
        def _():
            pltpu.make_async_copy(w_hbm.at[u], w.at[u], sem.at[u]).wait()

    seg_row = seg[0]
    seg_col = column_of(seg_row)
    fill_bias(bias, seg_col, seg_row)
    flags = flag_column(pos[0], slots) * role[0]
    need(0)
    e = nn(patch[0], w[0])
    e = jnp.where(flags > 0, gain[3:4, :], e)
    e_out[0] = e
    a = (layer_stats(e)[0] * gain[0:1, :]).astype(BF)
    for j in range(3):
        need(3 + j)
        qkv[j] = nn(a, w[3 + j]).astype(BF)

    def pair(p, carry):
        cs = pl.ds(pl.multiple_of(p * LANES, LANES), LANES)
        q2, k2, v2 = qkv[0, :, cs], qkv[1, :, cs], qkv[2, :, cs]
        k2 = k2 * jnp.asarray(HEAD_DIM**-0.5, BF)
        v_t = v2.T
        outs = []
        for h in range(2):
            s = nt(half(k2, h), q2) + bias[...]
            top = jnp.max(s, axis=0, keepdims=True)
            ex = jnp.exp(s - top)
            total = jnp.sum(ex, axis=0, keepdims=True)
            lse[0, pl.ds(2 * p + h, 1), :] = top + jnp.log(total)
            probs = (ex * (1.0 / total)).astype(BF)
            outs.append(nn(v_t[h * HEAD_DIM : (h + 1) * HEAD_DIM, :], probs))
        o_out[0, :, cs] = jnp.concatenate(outs, axis=0).T.astype(BF)
        return carry

    lax.fori_loop(0, HEADS // 2, pair, 0)
    need(1)
    x1 = e_out[0] + nn(o_out[0], w[1])
    x1_out[0] = x1
    a2 = (layer_stats(x1)[0] * gain[1:2, :]).astype(BF)
    acc = x1
    for j in range(cuts):
        need(6 + j)
        hid = nn(a2, w[6 + j])
        act = (hid * (0.5 * (1.0 + jnp.tanh(GELU_A * (hid + GELU_B * hid * hid * hid))))).astype(BF)
        need(6 + cuts + j)
        acc = acc + nn(act, w[6 + cuts + j])
    x2_out[0] = acc

    @pl.when(role[0] == 0)
    def _():
        t = layer_stats(x2_out[0])[0].astype(BF)
        tgt[0] = t
        t = t.astype(F32)
        for m in range(IMGS):
            inside = seg_col == m
            size = jnp.sum(jnp.where(inside, 1.0, 0.0), axis=0, keepdims=True)
            pooled = jnp.sum(jnp.where(inside, t, 0.0), axis=0, keepdims=True) / size
            unit = pooled * lax.rsqrt(jnp.sum(pooled * pooled, axis=-1, keepdims=True) + 1e-06)
            bank[0, m : m + 1, :] = unit.astype(BF)


def forward(role, patch, seg, pos, gain, w):
    batches, slots, width = patch.shape
    pieces = w.shape[0]
    tok = lambda dt: jax.ShapeDtypeStruct((batches, slots, width), dt)
    row = pl.BlockSpec((1, slots, width), lambda i: (i, 0, 0))
    return pl.pallas_call(
        fwd_kernel,
        name="forward",
        grid=(batches,),
        out_shape=(
            tok(F32),
            jax.ShapeDtypeStruct((3, batches * slots, width), BF),
            jax.ShapeDtypeStruct((batches, HEADS, slots), F32),
            tok(BF),
            tok(F32),
            tok(F32),
            tok(BF),
            jax.ShapeDtypeStruct((batches, IMGS, width), BF),
        ),
        in_specs=[
            smem_spec(),
            row,
            pl.BlockSpec((1, 1, slots), lambda i: (i, 0, 0)),
            pl.BlockSpec((1, 1, pos.shape[2]), lambda i: (i, 0, 0)),
            pl.BlockSpec((4, width), lambda i: (0, 0)),
            any_spec(),
        ],
        out_specs=(
            row,
            pl.BlockSpec((3, slots, width), lambda i: (0, i, 0)),
            pl.BlockSpec((1, HEADS, slots), lambda i: (i, 0, 0)),
            row,
            row,
            row,
            row,
            pl.BlockSpec((1, IMGS, width), lambda i: (i, 0, 0)),
        ),
        scratch_shapes=[
            pltpu.VMEM((pieces, width, width), BF),
            pltpu.VMEM((slots, slots), F32),
            pltpu.SemaphoreType.DMA((pieces,)),
        ],
        compiler_params=pltpu.CompilerParams(vmem_limit_bytes=VMEM_LIMIT),
        cost_estimate=pl.CostEstimate(
            flops=2 * batches * slots * width * width * pieces, bytes_accessed=2 * w.size, transcendentals=0
        ),
    )(role, patch, seg, pos, gain, w)


def norm_back(grad_out, normed, scaled, gain_vec):
    grad_hat = grad_out * gain_vec
    inner = jnp.mean(grad_hat * normed, axis=-1, keepdims=True)
    grad_in = scaled * (grad_hat - jnp.mean(grad_hat, axis=-1, keepdims=True) - normed * inner)
    return grad_in, jnp.sum(grad_out * normed, axis=0, keepdims=True)


def bwd_kernel(
    listed, place, seg, pos, gain, lse, banks, e_hbm, qkv_hbm, x1_hbm, x2_hbm, tgt_hbm, w_own, w_far,
    head_out, attn_out, ffn_out, act_out, de_out, mid_out, pred_out, dqkv_out, du_out, down_out, small,
    w, bias, top_scr, pool_scr, e_in, qkv, x1_in, x2_in, tgt,
    head_v, attn_v, ffn_v, act_v, de_v, mid_v, pred_v, dqkv, du_v, down_v, sem, in_sem, out_sem,
):
    role = place[0]
    slots, width = e_in.shape
    pieces = w_own.shape[0]
    cuts = (pieces - 6) // 2
    tokens = pl.ds(pl.multiple_of(role * slots, slots), slots)

    def bring(k, source, target):
        copy = pltpu.make_async_copy(source, target, in_sem.at[k])
        copy.start()
        return copy

    def bring_piece(u):
        @pl.when(role == 0)
        def _():
            pltpu.make_async_copy(w_far.at[u], w.at[u - 1], sem.at[u]).start()

        @pl.when(role != 0)
        def _():
            pltpu.make_async_copy(w_own.at[u], w.at[u - 1], sem.at[u]).start()

    def need(u):
        pltpu.make_async_copy(w_own.at[u], w.at[u - 1], sem.at[u]).wait()

    taken = []

    def keep(source, target):
        copy = pltpu.make_async_copy(source, target, out_sem.at[len(taken)])
        copy.start()
        taken.append(copy)

    x2_copy = bring(0, x2_hbm.at[role], x2_in)
    bring_piece(2)
    tgt_copy = bring(1, tgt_hbm.at[role], tgt)
    x1_copy = bring(2, x1_hbm.at[role], x1_in)
    for j in range(cuts):
        bring_piece(6 + cuts + j)
        bring_piece(6 + j)
    bring_piece(1)
    qkv_copy = bring(3, qkv_hbm.at[:, tokens, :], qkv)
    for j in range(3):
        bring_piece(3 + j)
    e_copy = bring(4, e_hbm.at[role], e_in)
    small[...] = jnp.zeros_like(small)

    seg_row = seg[role]
    seg_col = column_of(seg_row)
    fill_bias(bias, seg_col, seg_row)
    flags = flag_column(pos[role], slots)
    x2_copy.wait()
    n3, r3 = layer_stats(x2_in[...])
    head_in = (n3 * gain[2:3, :]).astype(BF)
    head_v[...] = head_in
    keep(head_v, head_out.at[0])
    need(2)
    pred = nn(head_in, w[1])
    valid = jnp.where(seg_col < IMGS, flags, 0).astype(F32)
    tgt_copy.wait()
    diff = pred - tgt[...].astype(F32)
    size = jnp.abs(diff)
    huber = jnp.where(size < 1.0, 0.5 * diff * diff, size - 0.5)
    regress = jnp.sum(jnp.sum(valid * huber, axis=1, keepdims=True), axis=0, keepdims=True)
    count = listed[0] * width
    grad_pred = valid * (jnp.clip(diff, -1.0, 1.0) / count)
    pool_scr[...] = jnp.zeros_like(pool_scr)
    for m in range(IMGS):
        inside = seg_col == m
        tally = jnp.sum(jnp.where(inside, 1.0, 0.0), axis=0, keepdims=True)
        pool_scr[m : m + 1, :] = jnp.sum(jnp.where(inside, pred, 0.0), axis=0, keepdims=True) / tally
    pooled = pool_scr[...]
    length = lax.rsqrt(jnp.sum(pooled * pooled, axis=-1, keepdims=True) + 1e-06)
    unit = pooled * length
    memory = banks[...]
    choices = memory.shape[0]
    logits = nt(unit.astype(BF), memory) / SOFTMAX_TEMPER
    row_id = lax.broadcasted_iota(jnp.int32, logits.shape, 0)
    real = row_id < IMGS
    picked = jnp.where(
        real & (lax.broadcasted_iota(jnp.int32, logits.shape, 1) == place[1] * IMGS + row_id), 1.0, 0.0
    )
    peak = jnp.max(logits, axis=-1, keepdims=True)
    ex = jnp.exp(logits - peak)
    total = jnp.sum(ex, axis=-1, keepdims=True)
    each = peak + jnp.log(total) - jnp.sum(logits * picked, axis=-1, keepdims=True)
    contrast = jnp.sum(jnp.where(real[:, 0:1], each, 0.0), axis=0, keepdims=True)
    scale = choices * MICRO_BATCHES
    grad_logits = (jnp.where(real, ex / total - picked, 0.0) / scale / SOFTMAX_TEMPER).astype(BF)
    grad_unit = nn(grad_logits, memory)
    grad_pool = length * (grad_unit - unit * jnp.sum(grad_unit * unit, axis=1, keepdims=True))
    pool_scr[...] = grad_pool
    for m in range(IMGS):
        inside = seg_col == m
        tally = jnp.sum(jnp.where(inside, 1.0, 0.0), axis=0, keepdims=True)
        grad_pred = grad_pred + jnp.where(inside, pool_scr[m : m + 1, :] / tally, 0.0)
    low = grad_pred.astype(BF)
    pred_v[...] = low
    keep(pred_v, pred_out.at[0])
    loss = regress / count + contrast / scale
    small[4:5, :] += jnp.broadcast_to(loss, (1, width))
    grad_top, gain_three = norm_back(nt(low, w[1]), n3, r3, gain[2:3, :])
    small[2:3, :] += gain_three
    top_scr[...] = grad_top
    down = grad_top.astype(BF)
    down_v[...] = down
    keep(down_v, down_out.at[0])
    x1_copy.wait()
    n2, r2 = layer_stats(x1_in[...])
    ffn_in = (n2 * gain[1:2, :]).astype(BF)
    ffn_v[...] = ffn_in
    keep(ffn_v, ffn_out.at[0])
    acc = None
    for j in range(cuts):
        need(6 + cuts + j)
        grad_act = nt(down, w[5 + cuts + j])
        need(6 + j)
        hid = nn(ffn_in, w[5 + j])
        th = jnp.tanh(GELU_A * (hid + GELU_B * hid * hid * hid))
        cdf = 0.5 * (1.0 + th)
        act_v[j] = (hid * cdf).astype(BF)
        keep(act_v.at[j], act_out.at[j])
        slope = cdf + hid * (0.5 * (1.0 - th * th)) * (GELU_A * (1.0 + 3.0 * GELU_B * hid * hid))
        du = (grad_act * slope).astype(BF)
        du_v[j] = du
        keep(du_v.at[j], du_out.at[j])
        part = nt(du, w[5 + j])
        acc = part if acc is None else acc + part
    grad_ffn, gain_two = norm_back(acc, n2, r2, gain[1:2, :])
    small[1:2, :] += gain_two
    mid = top_scr[...] + grad_ffn
    top_scr[...] = mid
    mid_low = mid.astype(BF)
    mid_v[...] = mid_low
    keep(mid_v, mid_out.at[0])
    need(1)
    de_v[...] = nt(mid_low, w[0]).astype(BF)
    qkv_copy.wait()

    def pair(p, carry):
        cs = pl.ds(pl.multiple_of(p * LANES, LANES), LANES)
        q2, k2, v2, g2 = qkv[0, :, cs], qkv[1, :, cs], qkv[2, :, cs], de_v[:, cs]
        k_scaled = k2 * jnp.asarray(HEAD_DIM**-0.5, BF)
        k_t = k2.T
        dq, dk, dv = [], 0.0, 0.0
        for h in range(2):
            s = nt(half(k_scaled, h), q2) + bias[...]
            probs = jnp.exp(s - lse[role, pl.ds(2 * p + h, 1), :])
            dp = nt(half(v2, h), g2)
            centre = jnp.sum(probs * dp, axis=0, keepdims=True)
            ds = (probs * (dp - centre)).astype(BF)
            dv = dv + nn(probs.astype(BF), half(g2, h))
            dk = dk + nn(ds, half(q2, h))
            dq.append(nn(k_t[h * HEAD_DIM : (h + 1) * HEAD_DIM, :], ds))
        dqkv[0, :, cs] = (jnp.concatenate(dq, axis=0) * HEAD_DIM**-0.5).T.astype(BF)
        dqkv[1, :, cs] = (dk * HEAD_DIM**-0.5).astype(BF)
        dqkv[2, :, cs] = dv.astype(BF)
        return carry

    lax.fori_loop(0, HEADS // 2, pair, 0)
    keep(dqkv, dqkv_out)
    acc = None
    for j in range(3):
        need(3 + j)
        part = nt(dqkv[j], w[2 + j])
        acc = part if acc is None else acc + part
    e_copy.wait()
    n1, r1 = layer_stats(e_in[...])
    attn_v[...] = (n1 * gain[0:1, :]).astype(BF)
    keep(attn_v, attn_out.at[0])
    grad_attn, gain_one = norm_back(acc, n1, r1, gain[0:1, :])
    small[0:1, :] += gain_one
    start = top_scr[...] + grad_attn
    hidden_slot = flags > 0
    small[3:4, :] += jnp.sum(jnp.where(hidden_slot, start, 0.0), axis=0, keepdims=True)
    de_v[...] = jnp.where(hidden_slot, 0.0, start).astype(BF)
    keep(de_v, de_out.at[0])
    for copy in taken:
        copy.wait()


def backward(listed, place, seg, pos, gain, lse, banks, e, qkv, x1, x2, tgt, w_own, w_far):
    _, slots, width = e.shape
    pieces = w_own.shape[0]
    cuts = (pieces - 6) // 2
    counts = (1, 1, 1, cuts, 1, 1, 1, 3, cuts, 1)
    vmem = pl.BlockSpec(memory_space=pltpu.VMEM)
    tok = lambda n, dt: pltpu.VMEM((n, slots, width) if n > 1 else (slots, width), dt)
    return pl.pallas_call(
        bwd_kernel,
        name="backward",
        out_shape=tuple(jax.ShapeDtypeStruct((n, slots, width), BF) for n in counts)
        + (jax.ShapeDtypeStruct((SUBLANES, width), F32),),
        in_specs=[smem_spec(), smem_spec()] + [vmem] * 5 + [any_spec()] * 7,
        out_specs=(any_spec(),) * len(counts) + (vmem,),
        scratch_shapes=[
            pltpu.VMEM((pieces - 1, width, width), BF),
            pltpu.VMEM((slots, slots), F32),
            pltpu.VMEM((slots, width), F32),
            pltpu.VMEM((SUBLANES, width), F32),
            tok(1, F32),
            tok(3, BF),
            tok(1, F32),
            tok(1, F32),
            tok(1, BF),
        ]
        + [tok(n, BF) for n in counts]
        + [
            pltpu.SemaphoreType.DMA((pieces,)),
            pltpu.SemaphoreType.DMA((5,)),
            pltpu.SemaphoreType.DMA((sum(counts),)),
        ],
        compiler_params=pltpu.CompilerParams(vmem_limit_bytes=VMEM_LIMIT),
    )(listed, place, seg, pos, gain, lse, banks, e, qkv, x1, x2, tgt, w_own, w_far)


def grads_kernel(
    plan, role, places, patch, mixed, head, attn, ffn, act, de, mid, pred, dqkv, du, down, out,
    rows_scr, x_buf, x_t, g_buf, stage, outbuf, x_sem, g_sem, out_sem,
):
    blocks, rows, width = out.shape
    cols = width // LANES
    deep, wide_out = x_buf.shape[0], outbuf.shape[0]
    group = max([g for g in range(SUBLANES, 49, SUBLANES) if rows % g == 0], default=rows)
    lefts = {"patch": patch, "mixed": mixed, "head": head, "attn": attn, "ffn": ffn, "act": act}
    rights = {"de": de, "mid": mid, "pred": pred, "dqkv": dqkv, "du": du, "down": down}

    def left_of(key):
        name, index = key
        return lefts[name].at[role[0] if name in ("patch", "mixed") else index]

    lcopies, rcopies = [], []
    lkeys, rkeys = [], []
    steps = []
    for u, (left, right) in enumerate(plan):
        if not lkeys or lkeys[-1] != left:
            slot = len(lkeys) % deep
            lcopies.append(pltpu.make_async_copy(left_of(left), x_buf.at[slot], x_sem.at[slot]))
            lkeys.append(left)
            fresh_l = True
        else:
            fresh_l = False
        if not rkeys or rkeys[-1] != right:
            slot = len(rkeys) % deep
            rcopies.append(pltpu.make_async_copy(rights[right[0]].at[right[1]], g_buf.at[slot], g_sem.at[slot]))
            rkeys.append(right)
            fresh_r = True
        else:
            fresh_r = False
        steps.append((u, len(lkeys) - 1, fresh_l, len(rkeys) - 1, fresh_r))
    for copy in lcopies[: deep - 1] + rcopies[: deep - 1]:
        copy.start()
    for u, li, fresh_l, ri, fresh_r in steps:
        if fresh_l:
            lcopies[li].wait()
            if li + deep - 1 < len(lcopies):
                lcopies[li + deep - 1].start()
            x_t[...] = x_buf[li % deep].T
        if fresh_r:
            rcopies[ri].wait()
            if ri + deep - 1 < len(rcopies):
                rcopies[ri + deep - 1].start()
        wide = 2 * LANES

        def tile(n, carry):
            part = nn(x_t[...], g_buf[ri % deep, :, pl.ds(pl.multiple_of(n * wide, wide), wide)])
            for c in range(2):
                rows_scr[pl.ds(u * width * SUBLANES + 2 * n + c, width, stride=SUBLANES), :] = part[
                    :, c * LANES : (c + 1) * LANES
                ]
            return carry

        lax.fori_loop(0, width // wide, tile, 0)

    def block(b, carry):
        slot = lax.rem(b, wide_out)

        def move(q, carry):
            came = [pl.multiple_of(places[b * rows + q * group + j] * SUBLANES, SUBLANES) for j in range(group)]
            held = [rows_scr[pl.ds(first, SUBLANES), :] for first in came]
            for j in range(group):
                to = q * (group // SUBLANES) * TILE + j // SUBLANES * TILE + j % SUBLANES
                stage[pl.ds(to, SUBLANES, stride=SUBLANES), :] = held[j]
            return carry

        lax.fori_loop(0, rows // group, move, 0)

        @pl.when(b >= wide_out)
        def _():
            pltpu.make_async_copy(outbuf.at[slot], out.at[b - wide_out], out_sem.at[slot]).wait()

        for first in range(0, rows, 16):
            tall = min(16, rows - first)
            for c in range(cols):
                at = first * SUBLANES + c * SUBLANES
                both = jnp.concatenate([stage[at : at + SUBLANES, :], stage[at + TILE : at + TILE + SUBLANES, :]], 0)
                outbuf[slot, first : first + tall, c * LANES : (c + 1) * LANES] = both[:tall].astype(BF)
        pltpu.make_async_copy(outbuf.at[slot], out.at[b], out_sem.at[slot]).start()
        return carry

    lax.fori_loop(0, blocks, block, 0)
    for b in range(blocks - wide_out, blocks):
        pltpu.make_async_copy(outbuf.at[b % wide_out], out.at[b], out_sem.at[b % wide_out]).wait()


def weight_grads(role, places, lefts, rights, blocks):
    tokens, width = lefts[0].shape[1:]
    cuts = lefts[-1].shape[0]
    total = places.shape[0]
    rows = total // blocks
    plan = (
        [(("patch", 0), ("de", 0)), (("mixed", 0), ("mid", 0)), (("head", 0), ("pred", 0))]
        + [(("attn", 0), ("dqkv", j)) for j in range(3)]
        + [(("ffn", 0), ("du", j)) for j in range(cuts)]
        + [(("act", j), ("down", 0)) for j in range(cuts)]
    )
    return pl.pallas_call(
        functools.partial(grads_kernel, plan),
        name="weight_grads",
        out_shape=jax.ShapeDtypeStruct((blocks, rows, width), BF),
        in_specs=[smem_spec(), smem_spec()] + [any_spec()] * 12,
        out_specs=any_spec(),
        scratch_shapes=[
            pltpu.VMEM((total * SUBLANES, LANES), F32),
            pltpu.VMEM((4, tokens, width), BF),
            pltpu.VMEM((width, tokens), BF),
            pltpu.VMEM((4, tokens, width), BF),
            pltpu.VMEM((pl.cdiv(rows, 16) * 2 * TILE, LANES), F32),
            pltpu.VMEM((4, rows, width), BF),
            pltpu.SemaphoreType.DMA((4,)),
            pltpu.SemaphoreType.DMA((4,)),
            pltpu.SemaphoreType.DMA((4,)),
        ],
        compiler_params=pltpu.CompilerParams(vmem_limit_bytes=VMEM_LIMIT),
    )(role, places, *lefts, *rights)


def adam_update(weight, first_state, second_state, gradient, step_value, decay_rate):
    first_state = BETA_ONE * first_state + (1.0 - BETA_ONE) * gradient
    second_state = BETA_TWO * second_state + (1.0 - BETA_TWO) * gradient * gradient
    fix_one = 1.0 - jnp.power(BETA_ONE, step_value)
    fix_two = 1.0 - jnp.power(BETA_TWO, step_value)
    update = first_state / fix_one / (jnp.sqrt(second_state / fix_two) + ADAM_EPS)
    return (weight - RATE * (update + decay_rate * weight), first_state, second_state)


def body(
    patches,
    segments,
    positions,
    owners,
    master,
    moment_one,
    moment_two,
    teacher,
    gains,
    gain_one,
    gain_two,
    teacher_gains,
    step_count,
):
    core = lax.axis_index("group")
    width = patches.shape[3]
    slots = patches.shape[2]
    row_total = owners.shape[0]
    inner = (row_total - 6 * width) // 2
    places = piece_rows(owners, width, inner)
    spots = places // SUBLANES * TILE + places % SUBLANES
    chips = lax.axis_size("dp")
    devices = lax.axis_size("group") * chips
    own_rows = row_total // devices
    role = core.astype(jnp.int32).reshape(1)
    place = jnp.stack([core, lax.axis_index("dp")]).astype(jnp.int32)
    listed = jnp.full((1,), MASKED * lax.axis_size("dp") * MICRO_BATCHES, F32)

    both = jnp.stack([teacher, master]).astype(BF)
    if chips <= KERNEL_CHIPS:
        model = gather_weights(both, chips)
    else:
        parts = lax.all_gather(both, ("dp", "group"), axis=1)
        model = jnp.where(core == 1, parts[1], parts[0]).reshape(chips, 2, own_rows, width)
    w = place_weights(spots, model)
    w_far = lax.ppermute(w, "group", [(1, 0)])
    gain_set = jnp.where(core == 1, gains, teacher_gains)
    patch = patches[:, 0]
    seg = segments
    pos = positions
    e, qkv, lse, mixed, x1, x2, tgt, bank = forward(role, patch, seg, pos, gain_set, w)
    (e, qkv, lse, mixed, x1, x2, tgt), banks = exchange_states((e, qkv, lse, mixed, x1, x2, tgt), bank, chips)
    banks = banks.reshape(chips * IMGS, width)
    head, attn, ffn, act, de, mid, pred, dqkv, du, down, small = backward(
        listed, place, seg, pos, gains, lse, banks, e, qkv, x1, x2, tgt, w, w_far
    )
    blocked = weight_grads(
        role, places, (patch, mixed, head, attn, ffn, act), (de, mid, pred, dqkv, du, down), devices
    )
    if chips <= KERNEL_CHIPS:
        owned_grad = reduce_grads(blocked.reshape(2, chips, own_rows, width), chips)
    else:
        owned_grad = lax.psum_scatter(blocked, ("group", "dp"), scatter_dimension=0, tiled=True)
        owned_grad = owned_grad.reshape(own_rows, width).astype(F32)
    square_own = jnp.sum(owned_grad * owned_grad)
    row_id = lax.broadcasted_iota(jnp.int32, small.shape, 0)
    small = sum_tiles(jnp.where(row_id == 5, square_own, small), chips)
    gain_sum, loss_sum, square_sum = small[0:4], small[4, 0], small[5, 0]
    grad_norm = jnp.sqrt(square_sum + jnp.sum(gain_sum * gain_sum))
    factor = jnp.minimum(1.0, CLIP / grad_norm)
    step_value = step_count[0].astype(F32)
    master_new, one_new, two_new = adam_update(
        master, moment_one, moment_two, owned_grad * factor, step_value, DECAY
    )
    gone_new, gtwo_new = adam_update(gains, gain_one, gain_two, gain_sum * factor, step_value, 0.0)[1:]
    teacher_new = EMA_KEEP * teacher + (1.0 - EMA_KEEP) * master_new
    return (
        loss_sum.reshape(1),
        grad_norm.reshape(1),
        one_new,
        two_new,
        master_new,
        teacher_new,
        gone_new,
        gtwo_new,
    )


def solution(mesh):
    rows = P(("group", "dp"), None)
    in_specs = (
        P(None, "dp", None, None),
        P(None, "dp", None),
        P(None, "dp", None),
        P(),
        rows,
        rows,
        rows,
        rows,
        P(),
        P(),
        P(),
        P(),
        P(),
    )
    out_specs = (P(), P(), rows, rows, rows, rows, P(), P())
    return jax.shard_map(body, mesh=mesh, in_specs=in_specs, out_specs=out_specs, check_vma=False)
```

```python
import functools

import jax
import jax.numpy as jnp
from jax import lax
from jax.experimental import pallas as pl
from jax.experimental.pallas import tpu as pltpu
from jax.sharding import PartitionSpec as P

HEADS = 12
HEAD_DIM = 64
IMGS = 4
MASKED = 320
MICRO_BATCHES = 2
LANES = 128
SUBLANES = 8
TILE = SUBLANES * SUBLANES

SOFTMAX_TEMPER = 0.05
CLIP = 0.004
RATE = 0.05
BETA_ONE = 0.9
BETA_TWO = 0.999
ADAM_EPS = 1e-08
DECAY = 0.05
EMA_KEEP = 0.9
MASK_FILL = -1000000000.0

BF = jnp.bfloat16
F32 = jnp.float32
VMEM_LIMIT = 67_000_000
GELU_A = 0.7978845608028654
GELU_B = 0.044715


def nn(a, b):
    return jnp.dot(a, b, preferred_element_type=F32)


def nt(a, b):
    return lax.dot_general(a, b, (((1,), (1,)), ((), ())), preferred_element_type=F32)


def piece_rows(flat, width, inner):
    cuts = inner // width
    qkv, up = flat - 3 * width, flat - 6 * width
    inside = jnp.where(flat < 6 * width, (3 + qkv % 3) * width + qkv // 3, (6 + up % cuts) * width + up // cuts)
    return jnp.where((flat >= 3 * width) & (flat < 6 * width + inner), inside, flat)


def any_spec():
    return pl.BlockSpec(memory_space=pl.ANY)


def smem_spec():
    return pl.BlockSpec(memory_space=pltpu.SMEM)


MESH = pl.DeviceIdType.MESH
KERNEL_CHIPS = 16


def chip_grid(chips):
    sizes, turn, left, prime = [1, 1, 1], 0, chips, 2
    while left > 1:
        while left % prime:
            prime += 1
        sizes[turn % 3] *= prime
        turn += 1
        left //= prime
    return tuple(sizes)


def strides_of(grid):
    return (grid[1] * grid[2], grid[2], 1)


def coords_of(index, grid):
    return (index // (grid[1] * grid[2]), lax.rem(index // grid[2], grid[1]), lax.rem(index, grid[2]))


def guarded(conditions, action):
    conditions = [c for c in conditions if c is not None]
    if not conditions:
        return action()
    both = conditions[0]
    for c in conditions[1:]:
        both = jnp.logical_and(both, c)
    pl.when(both)(action)


def lanes_of(width):
    unit = width // 6
    orders = [((1, 0, 2), 2), ((2, 0, 1), 2), ((0, 2, 1), 1), ((0, 1, 2), 1)]
    routes, first = [], 0
    for order, share in orders:
        routes.append((order, first, share * unit))
        first += share * unit
    return routes


def offsets(length):
    if length <= 2:
        return list(range(length))
    return [0] + [sign * far for far in range(1, length) for sign in (1, -1)]


def route_events(grid, routes):
    events = []
    for c, (order, _, _) in enumerate(routes):
        stack = [()]
        for d in order:
            stack = [r + (o,) for r in stack for o in offsets(grid[d])]
        events += [(sum(abs(o) * 2**i for i, o in enumerate(r)), c, r) for r in stack]
    return [(c, r) for _, c, r in sorted(events, key=lambda e: e[0])]


def onward(grid, order, r):
    last = max([i for i in range(3) if r[i]], default=-1)
    outs = []
    if last >= 0 and grid[order[last]] > 2:
        outs.append((order[last], 1 if r[last] > 0 else -1))
    for d in order[last + 1 :]:
        if grid[d] == 2:
            outs.append((d, 1))
        elif grid[d] > 2:
            outs += [(d, 1), (d, -1)]
    return outs


def neighbour(me, coords, grid, d, sign):
    step = strides_of(grid)[d]
    if grid[d] == 2:
        return me + (1 - 2 * coords[d]) * step, None
    place = coords[d] + sign
    return me + sign * step, jnp.logical_and(place >= 0, place < grid[d])


def origin(me, coords, grid, order, r):
    index, conditions = me, []
    for d, o in zip(order, r):
        if o == 0:
            continue
        step = strides_of(grid)[d]
        if grid[d] == 2:
            index = index + (1 - 2 * coords[d]) * step
        else:
            place = coords[d] - o
            index = index - o * step
            conditions.append(jnp.logical_and(place >= 0, place < grid[d]))
    return index, conditions


def slot_of(grid, d, sign):
    first = sum([1 if n <= 2 else 2 for n in grid[:d]])
    return first if grid[d] <= 2 or sign > 0 else first + 1


def slots_of(grid):
    return sum([1 if n <= 2 else 2 for n in grid])


def greet(me, coords, grid, group):
    barrier = pltpu.get_barrier_semaphore()
    near = [neighbour(me, coords, grid, d, s) for d in range(3) for s in ((1,) if grid[d] == 2 else (1, -1)) if grid[d] > 1]
    for index, there in near:
        guarded([there], lambda: pl.semaphore_signal(barrier, 1, device_id={"dp": index}, device_id_type=MESH))
    pl.semaphore_signal(barrier, 1, device_id={"group": 1 - group}, device_id_type=MESH)
    pl.semaphore_wait(barrier, 1 + sum([1 if there is None else there.astype(jnp.int32) for _, there in near]))


def gather_kernel(grid, learn, teach, out, both, swap_sem, send_sem, recv_sem):
    group, me = lax.axis_index("group"), lax.axis_index("dp")
    coords = coords_of(me, grid)
    routes = lanes_of(both.shape[2])
    events = route_events(grid, routes)
    both[0] = teach[...].astype(BF)
    both[1] = learn[...].astype(BF)
    greet(me, coords, grid, group)
    keep = pltpu.make_async_copy(both.at[group], out.at[me, group], swap_sem.at[2])
    keep.start()
    swap = pltpu.make_async_remote_copy(
        both.at[1 - group], out.at[me, group], swap_sem.at[0], swap_sem.at[1], {"group": 1 - group}, MESH
    )
    swap.start()
    keep.wait()
    swap.wait()

    def visit(c, r, act):
        order, first, wide = routes[c]
        block, real = origin(me, coords, grid, order, r)
        part = out.at[block, :, :, first : first + wide]

        def run():
            copies = []
            for d, sign in onward(grid, order, r):
                index, there = neighbour(me, coords, grid, d, sign)
                copies.append(
                    (
                        there,
                        pltpu.make_async_remote_copy(
                            part,
                            part,
                            send_sem.at[c, slot_of(grid, d, sign), block],
                            recv_sem.at[c, block],
                            {"dp": index},
                            MESH,
                        ),
                    )
                )
            act(part, recv_sem.at[c, block], any(r), copies)

        guarded(real, run)

    def forward_on(part, arrival_sem, remote, copies):
        if remote:
            pltpu.make_async_remote_copy(part, part, swap_sem.at[0], arrival_sem, {"dp": me}, MESH).wait_recv()
        for there, copy in copies:
            guarded([there], copy.start)

    def finish(part, arrival_sem, remote, copies):
        for there, copy in copies:
            guarded([there], copy.wait_send)

    for c, r in events:
        visit(c, r, forward_on)
    for c, r in events:
        visit(c, r, finish)


def gather_weights(learn, teach, chips):
    grid = chip_grid(chips)
    rows, width = learn.shape
    return pl.pallas_call(
        functools.partial(gather_kernel, grid),
        name="gather_weights",
        out_shape=jax.ShapeDtypeStruct((chips, 2, rows, width), BF),
        in_specs=[pl.BlockSpec(memory_space=pltpu.VMEM)] * 2,
        out_specs=any_spec(),
        scratch_shapes=[
            pltpu.VMEM((2, rows, width), BF),
            pltpu.SemaphoreType.DMA((3,)),
            pltpu.SemaphoreType.DMA((4, slots_of(grid), chips)),
            pltpu.SemaphoreType.DMA((4, chips)),
        ],
        compiler_params=pltpu.CompilerParams(
            collective_id=1, has_side_effects=True, vmem_limit_bytes=VMEM_LIMIT
        ),
    )(learn, teach)


def sum_peers(group, me, grid):
    plane = grid[1] * grid[2]
    at, level = lax.rem(me, plane), me // plane
    place = (group * plane + at, level)
    sizes = (2 * plane, grid[0])
    peers = []
    for k in range(1, sizes[0]):
        other = lax.rem(place[0] + k, sizes[0])
        peers.append((0, k, (other // plane, level * plane + lax.rem(other, plane))))
    for k in range(1, sizes[1]):
        peers.append((1, k, (group, lax.rem(level + k, sizes[1]) * plane + at)))
    return place, sizes, peers


def sum_stages(place, sizes, peers, total, notes, note_send, note_recv):
    for s, size in enumerate(sizes):
        notes[s, place[s]] = total[...]
        copies = [
            pltpu.make_async_remote_copy(
                notes.at[s, place[s]], notes.at[s, place[s]], note_send.at[s, k], note_recv.at[s, place[s]], device, MESH
            )
            for t, k, device in peers
            if t == s
        ]
        for copy in copies:
            copy.start()
        for k in range(1, size):
            other = lax.rem(place[s] + k, size)
            part = notes.at[s, other]
            pltpu.make_async_remote_copy(
                part, part, note_send.at[s, k], note_recv.at[s, other], peers[0][2], MESH
            ).wait_recv()
        result = notes[s, 0]
        for k in range(1, size):
            result = result + notes[s, k]
        total[...] = result
        for copy in copies:
            copy.wait_send()


def reduce_kernel(
    grid, blocked, small, out, total, acc, heard, notes, load_sem, half_sem, send_sem, recv_sem, note_send, note_recv
):
    group, me = lax.axis_index("group"), lax.axis_index("dp")
    coords = coords_of(me, grid)
    rows, width = out.shape
    routes = lanes_of(width)
    events = route_events(grid, routes)[::-1]
    across = slots_of(grid)
    tall = max([t for t in range(16, 49, 16) if rows % t == 0], default=rows)

    def spot(c, r):
        return tuple(r[routes[c][0].index(d)] for d in range(3))

    firsts = list(dict.fromkeys([spot(c, r) for c, r in events]))
    place, sizes, peers = sum_peers(group, me, grid)
    barrier = pltpu.get_barrier_semaphore()
    for _, _, device in peers:
        pl.semaphore_signal(barrier, 1, device_id=device, device_id_type=MESH)
    pl.semaphore_wait(barrier, len(peers))

    def load(where, act):
        block, real = origin(me, coords, grid, (0, 1, 2), where)
        local = pltpu.make_async_copy(blocked.at[group, block], acc.at[block], load_sem.at[block])
        half = pltpu.make_async_remote_copy(
            blocked.at[1 - group, block],
            heard.at[across, block],
            half_sem.at[0, block],
            half_sem.at[1, block],
            {"group": 1 - group},
            MESH,
        )
        guarded(real, lambda: act(local, half))

    def load_start(local, half):
        half.start()
        local.start()

    def load_wait(local, half):
        local.wait()
        half.wait_recv()

    def load_end(local, half):
        half.wait_send()

    for where in firsts:
        load(where, load_start)

    def parent(c, r, block):
        order, first, wide = routes[c]
        i = max([i for i in range(3) if r[i]])
        sign = 1 if r[i] > 0 else -1
        index, _ = neighbour(me, coords, grid, order[i], -sign)
        slot = slot_of(grid, order[i], sign)
        return pltpu.make_async_remote_copy(
            acc.at[block, :, first : first + wide],
            heard.at[slot, block, :, first : first + wide],
            send_sem.at[c, block],
            recv_sem.at[c, slot, block],
            {"dp": index},
            MESH,
        )

    def visit(c, r):
        order, first, wide = routes[c]
        block, real = origin(me, coords, grid, order, r)

        def run():
            children = [(slot_of(grid, d, s), neighbour(me, coords, grid, d, s)[1]) for d, s in onward(grid, order, r)]
            for slot, there in children:
                part = heard.at[slot, block, :, first : first + wide]
                arrival = pltpu.make_async_remote_copy(
                    part, part, send_sem.at[c, block], recv_sem.at[c, slot, block], {"dp": me}, MESH
                )
                guarded([there], arrival.wait_recv)
            children = [(across, None)] + children

            if any(r):
                for slot, there in children:

                    def total(slot=slot):
                        def piece(k, carry):
                            at = (pl.ds(pl.multiple_of(k * tall, tall), tall), slice(first, first + wide))
                            acc[(block,) + at] = (
                                acc[(block,) + at].astype(F32) + heard[(slot, block) + at].astype(F32)
                            ).astype(BF)
                            return carry

                        lax.fori_loop(0, rows // tall, piece, 0)

                    guarded([there], total)
                parent(c, r, block).start()
            else:

                def first_piece(k, carry):
                    at = (pl.ds(pl.multiple_of(k * tall, tall), tall), slice(first, first + wide))
                    out[at] = acc[(block,) + at].astype(F32)
                    return carry

                lax.fori_loop(0, rows // tall, first_piece, 0)
                for slot, there in children:

                    def total(slot=slot):
                        def piece(k, carry):
                            at = (pl.ds(pl.multiple_of(k * tall, tall), tall), slice(first, first + wide))
                            out[at] = out[at] + heard[(slot, block) + at].astype(F32)
                            return carry

                        lax.fori_loop(0, rows // tall, piece, 0)

                    guarded([there], total)

        guarded(real, run)

    ready = set()
    for c, r in events:
        if spot(c, r) not in ready:
            ready.add(spot(c, r))
            load(spot(c, r), load_wait)
        visit(c, r)
    def squares(k, carry):
        part = out[pl.ds(pl.multiple_of(k * tall, tall), tall), :]
        return carry + jnp.sum(part * part, axis=0, keepdims=True)

    square = lax.fori_loop(0, rows // tall, squares, jnp.zeros((1, width), F32))
    row_id = lax.broadcasted_iota(jnp.int32, total.shape, 0)
    total[...] = jnp.where(row_id == 5, square, small[...])
    sum_stages(place, sizes, peers, total, notes, note_send, note_recv)
    for c, r in events:
        if any(r):
            block, real = origin(me, coords, grid, routes[c][0], r)
            guarded(real, parent(c, r, block).wait_send)
    for where in firsts:
        load(where, load_end)


def reduce_grads(blocked, small, chips):
    grid = chip_grid(chips)
    _, _, rows, width = blocked.shape
    most = max(grid[0], 2 * grid[1] * grid[2])
    return pl.pallas_call(
        functools.partial(reduce_kernel, grid),
        name="reduce_grads",
        out_shape=(jax.ShapeDtypeStruct((rows, width), F32), jax.ShapeDtypeStruct(small.shape, F32)),
        in_specs=[any_spec(), pl.BlockSpec(memory_space=pltpu.VMEM)],
        out_specs=(pl.BlockSpec(memory_space=pltpu.VMEM),) * 2,
        scratch_shapes=[
            pltpu.VMEM((chips, rows, width), BF),
            pltpu.VMEM((slots_of(grid) + 1, chips, rows, width), BF),
            pltpu.VMEM((2, most) + small.shape, F32),
            pltpu.SemaphoreType.DMA((chips,)),
            pltpu.SemaphoreType.DMA((2, chips)),
            pltpu.SemaphoreType.DMA((4, chips)),
            pltpu.SemaphoreType.DMA((4, slots_of(grid), chips)),
            pltpu.SemaphoreType.DMA((2, most)),
            pltpu.SemaphoreType.DMA((2, most)),
        ],
        compiler_params=pltpu.CompilerParams(
            collective_id=2, has_side_effects=True, vmem_limit_bytes=VMEM_LIMIT
        ),
    )(blocked, small)


def exchange_kernel(*refs):
    count = (len(refs) - 7) // 2
    bank, states, banks = refs[count], refs[count + 1 : 2 * count + 1], refs[2 * count + 1]
    state_send, state_recv, send_sem, recv_sem, own_sem = refs[2 * count + 2 :]
    group, me = lax.axis_index("group"), lax.axis_index("dp")
    chips = banks.shape[0]
    barrier = pltpu.get_barrier_semaphore()

    def hail(target):
        def one(k, carry):
            pl.semaphore_signal(barrier, 1, device_id=(target, lax.rem(me + k, chips)), device_id_type=MESH)
            return carry

        return one

    @pl.when(group == 0)
    def _():
        lax.fori_loop(1, chips, hail(0), 0)
        lax.fori_loop(0, chips, hail(1), 0)

    @pl.when(group == 1)
    def _():
        lax.fori_loop(0, chips, hail(0), 0)

    pl.semaphore_wait(barrier, chips + (1 - group) * (chips - 1))

    def crossing(k):
        ref = states[k]
        if k == count - 1:
            part = ref.at[1]
        elif len(ref.shape) == 3 and ref.shape[0] == 3:
            part = ref.at[:, : ref.shape[1] // MICRO_BATCHES, :]
        else:
            part = ref.at[0]
        return pltpu.make_async_remote_copy(
            part, part, state_send.at[k], state_recv.at[k], {"group": 1 - group}, MESH
        )

    def note(core, k):
        return pltpu.make_async_remote_copy(
            bank.at[core],
            banks.at[me],
            send_sem.at[core, k],
            recv_sem.at[me],
            (core, lax.rem(me + k, chips)),
            MESH,
        )

    def each(core, act):
        def one(k, carry):
            act(note(core, k))
            return carry

        return one

    def take(k, carry):
        pltpu.make_async_remote_copy(
            bank.at[0], banks.at[k], send_sem.at[0, 0], recv_sem.at[k], (1 - group, me), MESH
        ).wait_recv()
        return carry

    @pl.when(group == 0)
    def _():
        own = pltpu.make_async_copy(bank.at[0], banks.at[me], own_sem)
        own.start()
        lax.fori_loop(1, chips, each(0, lambda copy: copy.start()), 0)
        lax.fori_loop(0, chips, each(1, lambda copy: copy.start()), 0)
        targets = crossing(count - 1)
        targets.start()
        own.wait()
        lax.fori_loop(1, chips, lambda k, carry: take(lax.rem(me + k, chips), carry), 0)
        for k in range(count - 1):
            crossing(k).wait_recv()
        lax.fori_loop(1, chips, each(0, lambda copy: copy.wait_send()), 0)
        lax.fori_loop(0, chips, each(1, lambda copy: copy.wait_send()), 0)
        targets.wait_send()

    @pl.when(group == 1)
    def _():
        copies = [crossing(k) for k in range(count - 1)]
        for copy in copies:
            copy.start()
        lax.fori_loop(0, chips, take, 0)
        crossing(count - 1).wait_recv()
        for copy in copies:
            copy.wait_send()


def exchange_states(states, bank, chips):
    count = len(states)
    outs = pl.pallas_call(
        exchange_kernel,
        name="exchange_states",
        out_shape=tuple(jax.ShapeDtypeStruct(a.shape, a.dtype) for a in states)
        + (jax.ShapeDtypeStruct((chips,) + bank.shape[1:], BF),),
        in_specs=[any_spec()] * (count + 1),
        out_specs=(any_spec(),) * (count + 1),
        scratch_shapes=[
            pltpu.SemaphoreType.DMA((count,)),
            pltpu.SemaphoreType.DMA((count,)),
            pltpu.SemaphoreType.DMA((2, chips)),
            pltpu.SemaphoreType.DMA((chips,)),
            pltpu.SemaphoreType.DMA,
        ],
        input_output_aliases={k: k for k in range(count)},
        compiler_params=pltpu.CompilerParams(collective_id=3, has_side_effects=True),
    )(*states, bank)
    return outs[:-1], outs[-1]


def place_kernel(spots, model, out, rows_scr, inbuf, stage, outbuf, in_sem, out_sem):
    chips, cores, rows, width = model.shape
    blocks = cores * chips
    cols = width // LANES
    deep, wide = inbuf.shape[0], outbuf.shape[0]
    group = max([g for g in range(1, 17) if rows % g == 0])

    def fetch(b, slot):
        return pltpu.make_async_copy(model.at[lax.rem(b, chips), b // chips], inbuf.at[slot], in_sem.at[slot])

    for b in range(deep - 1):
        fetch(b, b).start()

    def block(b, carry):
        slot = lax.rem(b, deep)
        fetch(b, slot).wait()

        @pl.when(b + deep - 1 < blocks)
        def _():
            fetch(b + deep - 1, lax.rem(b + deep - 1, deep)).start()

        for c in range(cols):
            stage[pl.ds(c, rows, stride=SUBLANES), :] = inbuf[slot, :, c * LANES : (c + 1) * LANES].astype(F32)

        def move(q, carry):
            first = q * group
            to = [spots[b * rows + first + j] for j in range(group)]
            held = [stage[pl.ds(pl.multiple_of((first + j) * SUBLANES, SUBLANES), SUBLANES), :] for j in range(group)]
            for j in range(group):
                rows_scr[pl.ds(to[j], SUBLANES, stride=SUBLANES), :] = held[j]
            return carry

        return lax.fori_loop(0, rows // group, move, carry)

    lax.fori_loop(0, blocks, block, 0)
    pieces = out.shape[0]
    for u in range(pieces):
        slot = u % wide
        if u >= wide:
            pltpu.make_async_copy(outbuf.at[slot], out.at[u - wide], out_sem.at[slot]).wait()

        def pack(k, carry):
            to = pl.ds(pl.multiple_of(k * 16, 16), 16)
            for c in range(cols):
                first = (u * width // SUBLANES + 2 * k) * TILE + c * SUBLANES
                halves = [rows_scr[pl.ds(pl.multiple_of(first + TILE * h, SUBLANES), SUBLANES), :] for h in range(2)]
                outbuf[slot, to, c * LANES : (c + 1) * LANES] = jnp.concatenate(halves, axis=0).astype(BF)
            return carry

        lax.fori_loop(0, width // 16, pack, 0)
        pltpu.make_async_copy(outbuf.at[slot], out.at[u], out_sem.at[slot]).start()
    for u in range(pieces - wide, pieces):
        pltpu.make_async_copy(outbuf.at[u % wide], out.at[u], out_sem.at[u % wide]).wait()


def place_weights(spots, model):
    _, _, rows, width = model.shape
    total = spots.shape[0]
    return pl.pallas_call(
        place_kernel,
        name="place_weights",
        out_shape=jax.ShapeDtypeStruct((total // width, width, width), BF),
        in_specs=[smem_spec(), any_spec()],
        out_specs=any_spec(),
        scratch_shapes=[
            pltpu.VMEM((total * SUBLANES, LANES), F32),
            pltpu.VMEM((8, rows, width), BF),
            pltpu.VMEM((rows * SUBLANES, LANES), F32),
            pltpu.VMEM((4, width, width), BF),
            pltpu.SemaphoreType.DMA((8,)),
            pltpu.SemaphoreType.DMA((4,)),
        ],
        compiler_params=pltpu.CompilerParams(vmem_limit_bytes=VMEM_LIMIT),
    )(spots, model)


def layer_stats(tensor):
    centre = tensor - jnp.mean(tensor, axis=-1, keepdims=True)
    scaled = lax.rsqrt(jnp.mean(centre * centre, axis=-1, keepdims=True) + 1e-06)
    return centre * scaled, scaled


def column_of(row):
    n = row.shape[1]
    eye = lax.broadcasted_iota(jnp.int32, (n, n), 0) == lax.broadcasted_iota(jnp.int32, (n, n), 1)
    return jnp.sum(jnp.where(eye, row, 0), axis=1, keepdims=True)


def flag_column(pos, slots):
    hit = lax.broadcasted_iota(jnp.int32, (slots, pos.shape[1]), 0) == pos
    return jnp.max(jnp.where(hit, 1, 0), axis=1, keepdims=True)


def fill_bias(bias, seg_col, seg_row):
    bias[...] = jnp.where(seg_col == seg_row, 0.0, MASK_FILL)


def half(x, h):
    low = lax.broadcasted_iota(jnp.int32, (1, LANES), 1) < HEAD_DIM
    keep = low if h == 0 else jnp.logical_not(low)
    return jnp.where(keep, x, jnp.zeros_like(x))


def fwd_kernel(patch, seg, pos, gains, teacher_gains, w_hbm, e_out, qkv, lse, o_out, x1_out, x2_out, tgt, bank, w, bias, gain, sem):
    i = pl.program_id(0)
    role = lax.axis_index("group")
    gain[...] = jnp.where(role == 0, teacher_gains[...], gains[...])
    slots, width = patch.shape[1:]
    pieces = w_hbm.shape[0]
    cuts = (pieces - 6) // 2
    order = [0, 3, 4, 5, 1]
    for j in range(cuts):
        order += [6 + j, 6 + cuts + j]

    @pl.when(i == 0)
    def _():
        for u in order:
            pltpu.make_async_copy(w_hbm.at[u], w.at[u], sem.at[u]).start()

    def need(u):
        @pl.when(i == 0)
        def _():
            pltpu.make_async_copy(w_hbm.at[u], w.at[u], sem.at[u]).wait()

    seg_row = seg[0]
    seg_col = column_of(seg_row)
    fill_bias(bias, seg_col, seg_row)
    flags = flag_column(pos[0], slots) * role
    need(0)
    e = nn(patch[0], w[0])
    e = jnp.where(flags > 0, gain[3:4, :], e)
    e_out[0] = e
    a = (layer_stats(e)[0] * gain[0:1, :]).astype(BF)
    for j in range(3):
        need(3 + j)
        qkv[j] = nn(a, w[3 + j]).astype(BF)

    def pair(p, carry):
        cs = pl.ds(pl.multiple_of(p * LANES, LANES), LANES)
        q2, k2, v2 = qkv[0, :, cs], qkv[1, :, cs], qkv[2, :, cs]
        k2 = k2 * jnp.asarray(HEAD_DIM**-0.5, BF)
        v_t = v2.T
        outs = []
        for h in range(2):
            s = nt(half(k2, h), q2) + bias[...]
            top = jnp.max(s, axis=0, keepdims=True)
            ex = jnp.exp(s - top)
            total = jnp.sum(ex, axis=0, keepdims=True)
            lse[0, pl.ds(2 * p + h, 1), :] = top + jnp.log(total)
            probs = (ex * (1.0 / total)).astype(BF)
            outs.append(nn(v_t[h * HEAD_DIM : (h + 1) * HEAD_DIM, :], probs))
        o_out[0, :, cs] = jnp.concatenate(outs, axis=0).T.astype(BF)
        return carry

    lax.fori_loop(0, HEADS // 2, pair, 0)
    need(1)
    x1 = e_out[0] + nn(o_out[0], w[1])
    x1_out[0] = x1
    a2 = (layer_stats(x1)[0] * gain[1:2, :]).astype(BF)
    acc = x1
    for j in range(cuts):
        need(6 + j)
        hid = nn(a2, w[6 + j])
        act = (hid * (0.5 * (1.0 + jnp.tanh(GELU_A * (hid + GELU_B * hid * hid * hid))))).astype(BF)
        need(6 + cuts + j)
        acc = acc + nn(act, w[6 + cuts + j])
    x2_out[0] = acc

    @pl.when(role == 0)
    def _():
        t = layer_stats(x2_out[0])[0].astype(BF)
        tgt[0] = t
        t = t.astype(F32)
        for m in range(IMGS):
            inside = seg_col == m
            size = jnp.sum(jnp.where(inside, 1.0, 0.0), axis=0, keepdims=True)
            pooled = jnp.sum(jnp.where(inside, t, 0.0), axis=0, keepdims=True) / size
            unit = pooled * lax.rsqrt(jnp.sum(pooled * pooled, axis=-1, keepdims=True) + 1e-06)
            bank[0, m : m + 1, :] = unit.astype(BF)


def forward(patch, seg, pos, gains, teacher_gains, w):
    batches, slots, width = patch.shape
    pieces = w.shape[0]
    tok = lambda dt: jax.ShapeDtypeStruct((batches, slots, width), dt)
    row = pl.BlockSpec((1, slots, width), lambda i: (i, 0, 0))
    return pl.pallas_call(
        fwd_kernel,
        name="forward",
        grid=(batches,),
        out_shape=(
            tok(F32),
            jax.ShapeDtypeStruct((3, batches * slots, width), BF),
            jax.ShapeDtypeStruct((batches, HEADS, slots), F32),
            tok(BF),
            tok(F32),
            tok(F32),
            tok(BF),
            jax.ShapeDtypeStruct((batches, IMGS, width), BF),
        ),
        in_specs=[
            row,
            pl.BlockSpec((1, 1, slots), lambda i: (i, 0, 0)),
            pl.BlockSpec((1, 1, pos.shape[2]), lambda i: (i, 0, 0)),
            pl.BlockSpec((4, width), lambda i: (0, 0)),
            pl.BlockSpec((4, width), lambda i: (0, 0)),
            any_spec(),
        ],
        out_specs=(
            row,
            pl.BlockSpec((3, slots, width), lambda i: (0, i, 0)),
            pl.BlockSpec((1, HEADS, slots), lambda i: (i, 0, 0)),
            row,
            row,
            row,
            row,
            pl.BlockSpec((1, IMGS, width), lambda i: (i, 0, 0)),
        ),
        scratch_shapes=[
            pltpu.VMEM((pieces, width, width), BF),
            pltpu.VMEM((slots, slots), F32),
            pltpu.VMEM((4, width), F32),
            pltpu.SemaphoreType.DMA((pieces,)),
        ],
        compiler_params=pltpu.CompilerParams(vmem_limit_bytes=VMEM_LIMIT),
        cost_estimate=pl.CostEstimate(
            flops=2 * batches * slots * width * width * pieces, bytes_accessed=2 * w.size, transcendentals=0
        ),
    )(patch, seg, pos, gains, teacher_gains, w)


def norm_back(grad_out, normed, scaled, gain_vec):
    grad_hat = grad_out * gain_vec
    inner = jnp.mean(grad_hat * normed, axis=-1, keepdims=True)
    grad_in = scaled * (grad_hat - jnp.mean(grad_hat, axis=-1, keepdims=True) - normed * inner)
    return grad_in, jnp.sum(grad_out * normed, axis=0, keepdims=True)


def bwd_kernel(
    seg, pos, gain, lse, banks, e_hbm, qkv_hbm, x1_hbm, x2_hbm, tgt_hbm, w_own, w_far,
    head_out, attn_out, ffn_out, act_out, de_out, mid_out, pred_out, dqkv_out, du_out, down_out, small,
    w, bias, top_scr, pool_scr, bank_scr, e_in, qkv, x1_in, x2_in, tgt,
    head_v, attn_v, ffn_v, act_v, de_v, mid_v, pred_v, dqkv, du_v, down_v, sem, in_sem, out_sem,
):
    role, chip = lax.axis_index("group"), lax.axis_index("dp")
    slots, width = e_in.shape
    chips = banks.shape[0]
    pieces = w_own.shape[0]
    cuts = (pieces - 6) // 2
    tokens = pl.ds(pl.multiple_of(role * slots, slots), slots)

    def bring(k, source, target):
        copy = pltpu.make_async_copy(source, target, in_sem.at[k])
        copy.start()
        return copy

    def bring_piece(u):
        @pl.when(role == 0)
        def _():
            pltpu.make_async_copy(w_far.at[u], w.at[u - 1], sem.at[u]).start()

        @pl.when(role != 0)
        def _():
            pltpu.make_async_copy(w_own.at[u], w.at[u - 1], sem.at[u]).start()

    def need(u):
        pltpu.make_async_copy(w_own.at[u], w.at[u - 1], sem.at[u]).wait()

    taken = []

    def keep(source, target):
        copy = pltpu.make_async_copy(source, target, out_sem.at[len(taken)])
        copy.start()
        taken.append(copy)

    x2_copy = bring(0, x2_hbm.at[role], x2_in)
    bring_piece(2)
    tgt_copy = bring(1, tgt_hbm.at[role], tgt)
    x1_copy = bring(2, x1_hbm.at[role], x1_in)
    for j in range(cuts):
        bring_piece(6 + cuts + j)
        bring_piece(6 + j)
    bring_piece(1)
    qkv_copy = bring(3, qkv_hbm.at[:, tokens, :], qkv)
    for j in range(3):
        bring_piece(3 + j)
    e_copy = bring(4, e_hbm.at[role], e_in)
    small[...] = jnp.zeros_like(small)

    seg_row = seg[role]
    seg_col = column_of(seg_row)
    fill_bias(bias, seg_col, seg_row)
    flags = flag_column(pos[role], slots)
    x2_copy.wait()
    n3, r3 = layer_stats(x2_in[...])
    head_in = (n3 * gain[2:3, :]).astype(BF)
    head_v[...] = head_in
    keep(head_v, head_out.at[0])
    need(2)
    pred = nn(head_in, w[1])
    valid = jnp.where(seg_col < IMGS, flags, 0).astype(F32)
    tgt_copy.wait()
    diff = pred - tgt[...].astype(F32)
    size = jnp.abs(diff)
    huber = jnp.where(size < 1.0, 0.5 * diff * diff, size - 0.5)
    regress = jnp.sum(jnp.sum(valid * huber, axis=1, keepdims=True), axis=0, keepdims=True)
    count = float(MASKED * chips * MICRO_BATCHES * width)
    grad_pred = valid * (jnp.clip(diff, -1.0, 1.0) / count)
    pool_scr[...] = jnp.zeros_like(pool_scr)
    for m in range(IMGS):
        inside = seg_col == m
        tally = jnp.sum(jnp.where(inside, 1.0, 0.0), axis=0, keepdims=True)
        pool_scr[m : m + 1, :] = jnp.sum(jnp.where(inside, pred, 0.0), axis=0, keepdims=True) / tally
    pooled = pool_scr[...]
    length = lax.rsqrt(jnp.sum(pooled * pooled, axis=-1, keepdims=True) + 1e-06)
    unit = pooled * length
    for k in range(chips):
        bank_scr[k * IMGS : (k + 1) * IMGS, :] = banks[k].astype(F32)
    memory = bank_scr[...].astype(BF)
    choices = memory.shape[0]
    logits = nt(unit.astype(BF), memory) / SOFTMAX_TEMPER
    row_id = lax.broadcasted_iota(jnp.int32, logits.shape, 0)
    real = row_id < IMGS
    picked = jnp.where(
        real & (lax.broadcasted_iota(jnp.int32, logits.shape, 1) == chip * IMGS + row_id), 1.0, 0.0
    )
    peak = jnp.max(logits, axis=-1, keepdims=True)
    ex = jnp.exp(logits - peak)
    total = jnp.sum(ex, axis=-1, keepdims=True)
    each = peak + jnp.log(total) - jnp.sum(logits * picked, axis=-1, keepdims=True)
    contrast = jnp.sum(jnp.where(real[:, 0:1], each, 0.0), axis=0, keepdims=True)
    scale = choices * MICRO_BATCHES
    grad_logits = (jnp.where(real, ex / total - picked, 0.0) / scale / SOFTMAX_TEMPER).astype(BF)
    grad_unit = nn(grad_logits, memory)
    grad_pool = length * (grad_unit - unit * jnp.sum(grad_unit * unit, axis=1, keepdims=True))
    pool_scr[...] = grad_pool
    for m in range(IMGS):
        inside = seg_col == m
        tally = jnp.sum(jnp.where(inside, 1.0, 0.0), axis=0, keepdims=True)
        grad_pred = grad_pred + jnp.where(inside, pool_scr[m : m + 1, :] / tally, 0.0)
    low = grad_pred.astype(BF)
    pred_v[...] = low
    keep(pred_v, pred_out.at[0])
    loss = regress / count + contrast / scale
    small[4:5, :] += jnp.broadcast_to(loss, (1, width))
    grad_top, gain_three = norm_back(nt(low, w[1]), n3, r3, gain[2:3, :])
    small[2:3, :] += gain_three
    top_scr[...] = grad_top
    down = grad_top.astype(BF)
    down_v[...] = down
    keep(down_v, down_out.at[0])
    x1_copy.wait()
    n2, r2 = layer_stats(x1_in[...])
    ffn_in = (n2 * gain[1:2, :]).astype(BF)
    ffn_v[...] = ffn_in
    keep(ffn_v, ffn_out.at[0])
    acc = None
    for j in range(cuts):
        need(6 + cuts + j)
        grad_act = nt(down, w[5 + cuts + j])
        need(6 + j)
        hid = nn(ffn_in, w[5 + j])
        th = jnp.tanh(GELU_A * (hid + GELU_B * hid * hid * hid))
        cdf = 0.5 * (1.0 + th)
        act_v[j] = (hid * cdf).astype(BF)
        keep(act_v.at[j], act_out.at[j])
        slope = cdf + hid * (0.5 * (1.0 - th * th)) * (GELU_A * (1.0 + 3.0 * GELU_B * hid * hid))
        du = (grad_act * slope).astype(BF)
        du_v[j] = du
        keep(du_v.at[j], du_out.at[j])
        part = nt(du, w[5 + j])
        acc = part if acc is None else acc + part
    grad_ffn, gain_two = norm_back(acc, n2, r2, gain[1:2, :])
    small[1:2, :] += gain_two
    mid = top_scr[...] + grad_ffn
    top_scr[...] = mid
    mid_low = mid.astype(BF)
    mid_v[...] = mid_low
    keep(mid_v, mid_out.at[0])
    need(1)
    de_v[...] = nt(mid_low, w[0]).astype(BF)
    qkv_copy.wait()

    def pair(p, carry):
        cs = pl.ds(pl.multiple_of(p * LANES, LANES), LANES)
        q2, k2, v2, g2 = qkv[0, :, cs], qkv[1, :, cs], qkv[2, :, cs], de_v[:, cs]
        k_scaled = k2 * jnp.asarray(HEAD_DIM**-0.5, BF)
        k_t = k2.T
        dq, dk, dv = [], 0.0, 0.0
        for h in range(2):
            s = nt(half(k_scaled, h), q2) + bias[...]
            probs = jnp.exp(s - lse[role, pl.ds(2 * p + h, 1), :])
            dp = nt(half(v2, h), g2)
            centre = jnp.sum(probs * dp, axis=0, keepdims=True)
            ds = (probs * (dp - centre)).astype(BF)
            dv = dv + nn(probs.astype(BF), half(g2, h))
            dk = dk + nn(ds, half(q2, h))
            dq.append(nn(k_t[h * HEAD_DIM : (h + 1) * HEAD_DIM, :], ds))
        dqkv[0, :, cs] = (jnp.concatenate(dq, axis=0) * HEAD_DIM**-0.5).T.astype(BF)
        dqkv[1, :, cs] = (dk * HEAD_DIM**-0.5).astype(BF)
        dqkv[2, :, cs] = dv.astype(BF)
        return carry

    lax.fori_loop(0, HEADS // 2, pair, 0)
    keep(dqkv, dqkv_out)
    acc = None
    for j in range(3):
        need(3 + j)
        part = nt(dqkv[j], w[2 + j])
        acc = part if acc is None else acc + part
    e_copy.wait()
    n1, r1 = layer_stats(e_in[...])
    attn_v[...] = (n1 * gain[0:1, :]).astype(BF)
    keep(attn_v, attn_out.at[0])
    grad_attn, gain_one = norm_back(acc, n1, r1, gain[0:1, :])
    small[0:1, :] += gain_one
    start = top_scr[...] + grad_attn
    hidden_slot = flags > 0
    small[3:4, :] += jnp.sum(jnp.where(hidden_slot, start, 0.0), axis=0, keepdims=True)
    de_v[...] = jnp.where(hidden_slot, 0.0, start).astype(BF)
    keep(de_v, de_out.at[0])
    for copy in taken:
        copy.wait()


def backward(seg, pos, gain, lse, banks, e, qkv, x1, x2, tgt, w_own, w_far):
    _, slots, width = e.shape
    pieces = w_own.shape[0]
    cuts = (pieces - 6) // 2
    counts = (1, 1, 1, cuts, 1, 1, 1, 3, cuts, 1)
    vmem = pl.BlockSpec(memory_space=pltpu.VMEM)
    tok = lambda n, dt: pltpu.VMEM((n, slots, width) if n > 1 else (slots, width), dt)
    return pl.pallas_call(
        bwd_kernel,
        name="backward",
        out_shape=tuple(jax.ShapeDtypeStruct((n, slots, width), BF) for n in counts)
        + (jax.ShapeDtypeStruct((SUBLANES, width), F32),),
        in_specs=[vmem] * 5 + [any_spec()] * 7,
        out_specs=(any_spec(),) * len(counts) + (vmem,),
        scratch_shapes=[
            pltpu.VMEM((pieces - 1, width, width), BF),
            pltpu.VMEM((slots, slots), F32),
            pltpu.VMEM((slots, width), F32),
            pltpu.VMEM((SUBLANES, width), F32),
            pltpu.VMEM((banks.shape[0] * IMGS, width), F32),
            tok(1, F32),
            tok(3, BF),
            tok(1, F32),
            tok(1, F32),
            tok(1, BF),
        ]
        + [tok(n, BF) for n in counts]
        + [
            pltpu.SemaphoreType.DMA((pieces,)),
            pltpu.SemaphoreType.DMA((5,)),
            pltpu.SemaphoreType.DMA((sum(counts),)),
        ],
        compiler_params=pltpu.CompilerParams(vmem_limit_bytes=VMEM_LIMIT),
    )(seg, pos, gain, lse, banks, e, qkv, x1, x2, tgt, w_own, w_far)


def grads_kernel(
    plan, places, patch, mixed, head, attn, ffn, act, de, mid, pred, dqkv, du, down, out,
    rows_scr, x_buf, x_t, g_buf, stage, outbuf, x_sem, g_sem, out_sem,
):
    blocks, rows, width = out.shape
    cols = width // LANES
    deep, wide_out = x_buf.shape[0], outbuf.shape[0]
    group = max([g for g in range(SUBLANES, 49, SUBLANES) if rows % g == 0], default=rows)
    lefts = {"patch": patch, "mixed": mixed, "head": head, "attn": attn, "ffn": ffn, "act": act}
    rights = {"de": de, "mid": mid, "pred": pred, "dqkv": dqkv, "du": du, "down": down}

    def left_of(key):
        name, index = key
        return lefts[name].at[lax.axis_index("group") if name in ("patch", "mixed") else index]

    lcopies, rcopies = [], []
    lkeys, rkeys = [], []
    steps = []
    for u, (left, right) in enumerate(plan):
        if not lkeys or lkeys[-1] != left:
            slot = len(lkeys) % deep
            lcopies.append(pltpu.make_async_copy(left_of(left), x_buf.at[slot], x_sem.at[slot]))
            lkeys.append(left)
            fresh_l = True
        else:
            fresh_l = False
        if not rkeys or rkeys[-1] != right:
            slot = len(rkeys) % deep
            rcopies.append(pltpu.make_async_copy(rights[right[0]].at[right[1]], g_buf.at[slot], g_sem.at[slot]))
            rkeys.append(right)
            fresh_r = True
        else:
            fresh_r = False
        steps.append((u, len(lkeys) - 1, fresh_l, len(rkeys) - 1, fresh_r))
    for copy in lcopies[: deep - 1] + rcopies[: deep - 1]:
        copy.start()
    for u, li, fresh_l, ri, fresh_r in steps:
        if fresh_l:
            lcopies[li].wait()
            if li + deep - 1 < len(lcopies):
                lcopies[li + deep - 1].start()
            x_t[...] = x_buf[li % deep].T
        if fresh_r:
            rcopies[ri].wait()
            if ri + deep - 1 < len(rcopies):
                rcopies[ri + deep - 1].start()
        wide = 2 * LANES

        def tile(n, carry):
            part = nn(x_t[...], g_buf[ri % deep, :, pl.ds(pl.multiple_of(n * wide, wide), wide)])
            for c in range(2):
                rows_scr[pl.ds(u * width * SUBLANES + 2 * n + c, width, stride=SUBLANES), :] = part[
                    :, c * LANES : (c + 1) * LANES
                ]
            return carry

        lax.fori_loop(0, width // wide, tile, 0)

    def block(b, carry):
        slot = lax.rem(b, wide_out)

        def move(q, carry):
            came = [pl.multiple_of(places[b * rows + q * group + j] * SUBLANES, SUBLANES) for j in range(group)]
            held = [rows_scr[pl.ds(first, SUBLANES), :] for first in came]
            for j in range(group):
                to = q * (group // SUBLANES) * TILE + j // SUBLANES * TILE + j % SUBLANES
                stage[pl.ds(to, SUBLANES, stride=SUBLANES), :] = held[j]
            return carry

        lax.fori_loop(0, rows // group, move, 0)

        @pl.when(b >= wide_out)
        def _():
            pltpu.make_async_copy(outbuf.at[slot], out.at[b - wide_out], out_sem.at[slot]).wait()

        for first in range(0, rows, 16):
            tall = min(16, rows - first)
            for c in range(cols):
                at = first * SUBLANES + c * SUBLANES
                both = jnp.concatenate([stage[at : at + SUBLANES, :], stage[at + TILE : at + TILE + SUBLANES, :]], 0)
                outbuf[slot, first : first + tall, c * LANES : (c + 1) * LANES] = both[:tall].astype(BF)
        pltpu.make_async_copy(outbuf.at[slot], out.at[b], out_sem.at[slot]).start()
        return carry

    lax.fori_loop(0, blocks, block, 0)
    for b in range(blocks - wide_out, blocks):
        pltpu.make_async_copy(outbuf.at[b % wide_out], out.at[b], out_sem.at[b % wide_out]).wait()


def weight_grads(places, lefts, rights, blocks):
    tokens, width = lefts[0].shape[1:]
    cuts = lefts[-1].shape[0]
    total = places.shape[0]
    rows = total // blocks
    plan = (
        [(("patch", 0), ("de", 0)), (("mixed", 0), ("mid", 0)), (("head", 0), ("pred", 0))]
        + [(("attn", 0), ("dqkv", j)) for j in range(3)]
        + [(("ffn", 0), ("du", j)) for j in range(cuts)]
        + [(("act", j), ("down", 0)) for j in range(cuts)]
    )
    return pl.pallas_call(
        functools.partial(grads_kernel, plan),
        name="weight_grads",
        out_shape=jax.ShapeDtypeStruct((blocks, rows, width), BF),
        in_specs=[smem_spec()] + [any_spec()] * 12,
        out_specs=any_spec(),
        scratch_shapes=[
            pltpu.VMEM((total * SUBLANES, LANES), F32),
            pltpu.VMEM((4, tokens, width), BF),
            pltpu.VMEM((width, tokens), BF),
            pltpu.VMEM((4, tokens, width), BF),
            pltpu.VMEM((pl.cdiv(rows, 16) * 2 * TILE, LANES), F32),
            pltpu.VMEM((4, rows, width), BF),
            pltpu.SemaphoreType.DMA((4,)),
            pltpu.SemaphoreType.DMA((4,)),
            pltpu.SemaphoreType.DMA((4,)),
        ],
        compiler_params=pltpu.CompilerParams(vmem_limit_bytes=VMEM_LIMIT),
    )(places, *lefts, *rights)


def power_of(base, exponent):
    return lax.fori_loop(0, exponent, lambda _, product: product * base, jnp.float32(1.0))


def update_kernel(
    step, total, gains, gone, gtwo, grad, master, one, two, teacher,
    loss_out, norm_out, one_out, two_out, master_out, teacher_out, gone_out, gtwo_out,
):
    gain_grad = total[0:4, :]
    square = jnp.sum(total[5:6, :], axis=1, keepdims=True)
    square = square + jnp.sum(jnp.sum(gain_grad * gain_grad, axis=1, keepdims=True), axis=0, keepdims=True)
    norm = jnp.sqrt(square)
    factor = jnp.minimum(1.0, CLIP / norm)
    fix_one = 1.0 - power_of(BETA_ONE, step[0])
    fix_two = 1.0 - power_of(BETA_TWO, step[0])

    def moments(first, second, gradient):
        first = BETA_ONE * first + (1.0 - BETA_ONE) * gradient
        second = BETA_TWO * second + (1.0 - BETA_TWO) * gradient * gradient
        return first, second

    @pl.when(pl.program_id(0) == 0)
    def _():
        loss_out[0] = jnp.sum(total[4:5, 0:1])
        norm_out[0] = jnp.sum(norm)
        gone_out[...], gtwo_out[...] = moments(gone[...], gtwo[...], gain_grad * factor)

    first, second = moments(one[...], two[...], grad[...] * factor)
    change = first / fix_one / (jnp.sqrt(second / fix_two) + ADAM_EPS)
    weight = master[...]
    weight = weight - RATE * (change + DECAY * weight)
    one_out[...] = first
    two_out[...] = second
    master_out[...] = weight
    teacher_out[...] = EMA_KEEP * teacher[...] + (1.0 - EMA_KEEP) * weight


def update(step, total, gains, gone, gtwo, grad, master, one, two, teacher):
    rows, width = grad.shape
    tall = max([t for t in range(SUBLANES, 113, SUBLANES) if rows % t == 0], default=rows)
    part = pl.BlockSpec((tall, width), lambda i: (i, 0))
    whole = lambda a: pl.BlockSpec(a.shape, lambda i: (0, 0))
    scalar = jax.ShapeDtypeStruct((1,), F32)
    same = lambda a: jax.ShapeDtypeStruct(a.shape, F32)
    return pl.pallas_call(
        update_kernel,
        name="update",
        grid=(rows // tall,),
        out_shape=(scalar, scalar, same(one), same(two), same(master), same(teacher), same(gone), same(gtwo)),
        in_specs=[smem_spec(), whole(total), whole(gains), whole(gone), whole(gtwo)] + [part] * 5,
        out_specs=(smem_spec(), smem_spec(), part, part, part, part, whole(gone), whole(gtwo)),
    )(step, total, gains, gone, gtwo, grad, master, one, two, teacher)


def body(
    patches,
    segments,
    positions,
    owners,
    master,
    moment_one,
    moment_two,
    teacher,
    gains,
    gain_one,
    gain_two,
    teacher_gains,
    step_count,
):
    core = lax.axis_index("group")
    width = patches.shape[3]
    slots = patches.shape[2]
    row_total = owners.shape[0]
    inner = (row_total - 6 * width) // 2
    places = piece_rows(owners, width, inner)
    spots = places // SUBLANES * TILE + places % SUBLANES
    chips = lax.axis_size("dp")
    devices = lax.axis_size("group") * chips
    own_rows = row_total // devices

    if chips <= KERNEL_CHIPS:
        model = gather_weights(master, teacher, chips)
    else:
        parts = lax.all_gather(jnp.stack([teacher, master]).astype(BF), ("dp", "group"), axis=1)
        model = jnp.where(core == 1, parts[1], parts[0]).reshape(chips, 2, own_rows, width)
    w = place_weights(spots, model)
    w_far = lax.ppermute(w, "group", [(1, 0)])
    patch = patches[:, 0]
    seg = segments
    pos = positions
    e, qkv, lse, mixed, x1, x2, tgt, bank = forward(patch, seg, pos, gains, teacher_gains, w)
    (e, qkv, lse, mixed, x1, x2, tgt), banks = exchange_states((e, qkv, lse, mixed, x1, x2, tgt), bank, chips)
    head, attn, ffn, act, de, mid, pred, dqkv, du, down, small = backward(
        seg, pos, gains, lse, banks, e, qkv, x1, x2, tgt, w, w_far
    )
    blocked = weight_grads(
        places, (patch, mixed, head, attn, ffn, act), (de, mid, pred, dqkv, du, down), devices
    )
    if chips <= KERNEL_CHIPS:
        owned_grad, total = reduce_grads(blocked.reshape(2, chips, own_rows, width), small, chips)
    else:
        owned_grad = lax.psum_scatter(blocked, ("group", "dp"), scatter_dimension=0, tiled=True)
        owned_grad = owned_grad.reshape(own_rows, width).astype(F32)
        squares = jnp.sum(owned_grad * owned_grad, axis=0, keepdims=True)
        row_id = lax.broadcasted_iota(jnp.int32, small.shape, 0)
        total = lax.psum(jnp.where(row_id == 5, squares, small), ("group", "dp"))
    return update(
        step_count, total, gains, gain_one, gain_two, owned_grad, master, moment_one, moment_two, teacher
    )


def solution(mesh):
    rows = P(("group", "dp"), None)
    in_specs = (
        P(None, "dp", None, None),
        P(None, "dp", None),
        P(None, "dp", None),
        P(),
        rows,
        rows,
        rows,
        rows,
        P(),
        P(),
        P(),
        P(),
        P(),
    )
    out_specs = (P(), P(), rows, rows, rows, rows, P(), P())
    return jax.shard_map(body, mesh=mesh, in_specs=in_specs, out_specs=out_specs, check_vma=False)
```

```python
import functools

import jax
import jax.numpy as jnp
from jax import lax
from jax.experimental import pallas as pl
from jax.experimental.pallas import tpu as pltpu
from jax.sharding import PartitionSpec as P

HEADS = 12
HEAD_DIM = 64
IMGS = 4
MASKED = 320
MICRO_BATCHES = 2
LANES = 128
SUBLANES = 8
TILE = SUBLANES * SUBLANES

SOFTMAX_TEMPER = 0.05
CLIP = 0.004
RATE = 0.05
BETA_ONE = 0.9
BETA_TWO = 0.999
ADAM_EPS = 1e-08
DECAY = 0.05
EMA_KEEP = 0.9
MASK_FILL = -1000000000.0

BF = jnp.bfloat16
F32 = jnp.float32
VMEM_LIMIT = 67_000_000
GELU_A = 0.7978845608028654
GELU_B = 0.044715


def nn(a, b):
    return jnp.dot(a, b, preferred_element_type=F32)


def nt(a, b):
    return lax.dot_general(a, b, (((1,), (1,)), ((), ())), preferred_element_type=F32)


def piece_rows(flat, width, inner):
    cuts = inner // width
    qkv, up = flat - 3 * width, flat - 6 * width
    inside = jnp.where(flat < 6 * width, (3 + qkv % 3) * width + qkv // 3, (6 + up % cuts) * width + up // cuts)
    return jnp.where((flat >= 3 * width) & (flat < 6 * width + inner), inside, flat)


def any_spec():
    return pl.BlockSpec(memory_space=pl.ANY)


def smem_spec():
    return pl.BlockSpec(memory_space=pltpu.SMEM)


MESH = pl.DeviceIdType.MESH
KERNEL_CHIPS = 16


def chip_grid(chips):
    sizes, turn, left, prime = [1, 1, 1], 0, chips, 2
    while left > 1:
        while left % prime:
            prime += 1
        sizes[turn % 3] *= prime
        turn += 1
        left //= prime
    return tuple(sizes)


def strides_of(grid):
    return (grid[1] * grid[2], grid[2], 1)


def coords_of(index, grid):
    return (index // (grid[1] * grid[2]), lax.rem(index // grid[2], grid[1]), lax.rem(index, grid[2]))


def guarded(conditions, action):
    conditions = [c for c in conditions if c is not None]
    if not conditions:
        return action()
    both = conditions[0]
    for c in conditions[1:]:
        both = jnp.logical_and(both, c)
    pl.when(both)(action)


def lanes_of(width):
    unit = width // 6
    orders = [((1, 0, 2), 2), ((2, 0, 1), 2), ((0, 2, 1), 1), ((0, 1, 2), 1)]
    routes, first = [], 0
    for order, share in orders:
        routes.append((order, first, share * unit))
        first += share * unit
    return routes


def offsets(length):
    if length <= 2:
        return list(range(length))
    return [0] + [sign * far for far in range(1, length) for sign in (1, -1)]


def route_events(grid, routes):
    events = []
    for c, (order, _, _) in enumerate(routes):
        stack = [()]
        for d in order:
            stack = [r + (o,) for r in stack for o in offsets(grid[d])]
        events += [(sum(abs(o) * 2**i for i, o in enumerate(r)), c, r) for r in stack]
    return [(c, r) for _, c, r in sorted(events, key=lambda e: e[0])]


def onward(grid, order, r):
    last = max([i for i in range(3) if r[i]], default=-1)
    outs = []
    if last >= 0 and grid[order[last]] > 2:
        outs.append((order[last], 1 if r[last] > 0 else -1))
    for d in order[last + 1 :]:
        if grid[d] == 2:
            outs.append((d, 1))
        elif grid[d] > 2:
            outs += [(d, 1), (d, -1)]
    return outs


def neighbour(me, coords, grid, d, sign):
    step = strides_of(grid)[d]
    if grid[d] == 2:
        return me + (1 - 2 * coords[d]) * step, None
    place = coords[d] + sign
    return me + sign * step, jnp.logical_and(place >= 0, place < grid[d])


def origin(me, coords, grid, order, r):
    index, conditions = me, []
    for d, o in zip(order, r):
        if o == 0:
            continue
        step = strides_of(grid)[d]
        if grid[d] == 2:
            index = index + (1 - 2 * coords[d]) * step
        else:
            place = coords[d] - o
            index = index - o * step
            conditions.append(jnp.logical_and(place >= 0, place < grid[d]))
    return index, conditions


def slot_of(grid, d, sign):
    first = sum([1 if n <= 2 else 2 for n in grid[:d]])
    return first if grid[d] <= 2 or sign > 0 else first + 1


def slots_of(grid):
    return sum([1 if n <= 2 else 2 for n in grid])


def greet(me, coords, grid, group):
    barrier = pltpu.get_barrier_semaphore()
    near = [neighbour(me, coords, grid, d, s) for d in range(3) for s in ((1,) if grid[d] == 2 else (1, -1)) if grid[d] > 1]
    for index, there in near:
        guarded([there], lambda: pl.semaphore_signal(barrier, 1, device_id={"dp": index}, device_id_type=MESH))
    pl.semaphore_signal(barrier, 1, device_id={"group": 1 - group}, device_id_type=MESH)
    pl.semaphore_wait(barrier, 1 + sum([1 if there is None else there.astype(jnp.int32) for _, there in near]))


def gather_kernel(grid, learn, teach, out, both, swap_sem, half_sem, send_sem, recv_sem):
    group, me = lax.axis_index("group"), lax.axis_index("dp")
    coords = coords_of(me, grid)
    routes = lanes_of(both.shape[2])
    events = route_events(grid, routes)
    both[0] = teach[...].astype(BF)
    both[1] = learn[...].astype(BF)
    greet(me, coords, grid, group)
    keep = pltpu.make_async_copy(both.at[group], out.at[me, group], swap_sem.at[2])
    keep.start()
    swap = pltpu.make_async_remote_copy(
        both.at[1 - group], out.at[me, group], swap_sem.at[0], swap_sem.at[1], {"group": 1 - group}, MESH
    )
    swap.start()

    def first_sends(half, source):
        copies = []
        for c, (order, first, wide) in enumerate(routes):
            for d, sign in onward(grid, order, (0, 0, 0)):
                index, there = neighbour(me, coords, grid, d, sign)
                copy = pltpu.make_async_remote_copy(
                    source.at[:, first : first + wide],
                    out.at[me, half, :, first : first + wide],
                    half_sem.at[half, c, slot_of(grid, d, sign)],
                    recv_sem.at[c, me],
                    {"dp": index},
                    MESH,
                )
                copies.append((there, copy))
        for there, copy in copies:
            guarded([there], copy.start)
        return copies

    firsts = first_sends(group, both.at[group])
    swap.wait()
    firsts += first_sends(1 - group, out.at[me, 1 - group])

    def visit(c, r, act):
        order, first, wide = routes[c]
        block, real = origin(me, coords, grid, order, r)
        part = out.at[block, :, :, first : first + wide]

        def run():
            copies = []
            for d, sign in onward(grid, order, r):
                index, there = neighbour(me, coords, grid, d, sign)
                copies.append(
                    (
                        there,
                        pltpu.make_async_remote_copy(
                            part,
                            part,
                            send_sem.at[c, slot_of(grid, d, sign), block],
                            recv_sem.at[c, block],
                            {"dp": index},
                            MESH,
                        ),
                    )
                )
            act(part, recv_sem.at[c, block], copies)

        guarded(real, run)

    def forward_on(part, arrival_sem, copies):
        pltpu.make_async_remote_copy(part, part, swap_sem.at[0], arrival_sem, {"dp": me}, MESH).wait_recv()
        for there, copy in copies:
            guarded([there], copy.start)

    def finish(part, arrival_sem, copies):
        for there, copy in copies:
            guarded([there], copy.wait_send)

    for c, r in events:
        if any(r):
            visit(c, r, forward_on)
    for c, r in events:
        if any(r):
            visit(c, r, finish)
    keep.wait()
    for there, copy in firsts:
        guarded([there], copy.wait_send)


def gather_weights(learn, teach, chips):
    grid = chip_grid(chips)
    rows, width = learn.shape
    return pl.pallas_call(
        functools.partial(gather_kernel, grid),
        name="gather_weights",
        out_shape=jax.ShapeDtypeStruct((chips, 2, rows, width), BF),
        in_specs=[pl.BlockSpec(memory_space=pltpu.VMEM)] * 2,
        out_specs=any_spec(),
        scratch_shapes=[
            pltpu.VMEM((2, rows, width), BF),
            pltpu.SemaphoreType.DMA((3,)),
            pltpu.SemaphoreType.DMA((2, 4, slots_of(grid))),
            pltpu.SemaphoreType.DMA((4, slots_of(grid), chips)),
            pltpu.SemaphoreType.DMA((4, chips)),
        ],
        compiler_params=pltpu.CompilerParams(
            collective_id=1, has_side_effects=True, vmem_limit_bytes=VMEM_LIMIT
        ),
    )(learn, teach)


def sum_peers(group, me, grid):
    plane = grid[1] * grid[2]
    at, level = lax.rem(me, plane), me // plane
    place = (group * plane + at, level)
    sizes = (2 * plane, grid[0])
    peers = []
    for k in range(1, sizes[0]):
        other = lax.rem(place[0] + k, sizes[0])
        peers.append((0, k, (other // plane, level * plane + lax.rem(other, plane))))
    for k in range(1, sizes[1]):
        peers.append((1, k, (group, lax.rem(level + k, sizes[1]) * plane + at)))
    return place, sizes, peers


def sum_stages(place, sizes, peers, total, notes, note_send, note_recv):
    for s, size in enumerate(sizes):
        notes[s, place[s]] = total[...]
        copies = [
            pltpu.make_async_remote_copy(
                notes.at[s, place[s]], notes.at[s, place[s]], note_send.at[s, k], note_recv.at[s, place[s]], device, MESH
            )
            for t, k, device in peers
            if t == s
        ]
        for copy in copies:
            copy.start()
        for k in range(1, size):
            other = lax.rem(place[s] + k, size)
            part = notes.at[s, other]
            pltpu.make_async_remote_copy(
                part, part, note_send.at[s, k], note_recv.at[s, other], peers[0][2], MESH
            ).wait_recv()
        result = notes[s, 0]
        for k in range(1, size):
            result = result + notes[s, k]
        total[...] = result
        for copy in copies:
            copy.wait_send()


def reduce_kernel(
    grid, blocked, small, out, total, acc, heard, notes, load_sem, half_sem, send_sem, recv_sem, note_send, note_recv
):
    group, me = lax.axis_index("group"), lax.axis_index("dp")
    coords = coords_of(me, grid)
    rows, width = out.shape
    routes = lanes_of(width)
    events = route_events(grid, routes)[::-1]
    across = slots_of(grid)
    tall = max([t for t in range(16, 49, 16) if rows % t == 0], default=rows)

    def spot(c, r):
        return tuple(r[routes[c][0].index(d)] for d in range(3))

    firsts = list(dict.fromkeys([spot(c, r) for c, r in events]))
    place, sizes, peers = sum_peers(group, me, grid)
    barrier = pltpu.get_barrier_semaphore()
    for _, _, device in peers:
        pl.semaphore_signal(barrier, 1, device_id=device, device_id_type=MESH)
    pl.semaphore_wait(barrier, len(peers))

    def load(where, act):
        block, real = origin(me, coords, grid, (0, 1, 2), where)
        local = pltpu.make_async_copy(blocked.at[group, block], acc.at[block], load_sem.at[block])
        half = pltpu.make_async_remote_copy(
            blocked.at[1 - group, block],
            heard.at[across, block],
            half_sem.at[0, block],
            half_sem.at[1, block],
            {"group": 1 - group},
            MESH,
        )
        guarded(real, lambda: act(local, half))

    def load_start(local, half):
        half.start()
        local.start()

    def load_wait(local, half):
        local.wait()
        half.wait_recv()

    def load_end(local, half):
        half.wait_send()

    for where in firsts:
        load(where, load_start)

    def parent(c, r, block):
        order, first, wide = routes[c]
        i = max([i for i in range(3) if r[i]])
        sign = 1 if r[i] > 0 else -1
        index, _ = neighbour(me, coords, grid, order[i], -sign)
        slot = slot_of(grid, order[i], sign)
        return pltpu.make_async_remote_copy(
            acc.at[block, :, first : first + wide],
            heard.at[slot, block, :, first : first + wide],
            send_sem.at[c, block],
            recv_sem.at[c, slot, block],
            {"dp": index},
            MESH,
        )

    def visit(c, r):
        order, first, wide = routes[c]
        block, real = origin(me, coords, grid, order, r)

        def run():
            children = [(slot_of(grid, d, s), neighbour(me, coords, grid, d, s)[1]) for d, s in onward(grid, order, r)]
            for slot, there in children:
                part = heard.at[slot, block, :, first : first + wide]
                arrival = pltpu.make_async_remote_copy(
                    part, part, send_sem.at[c, block], recv_sem.at[c, slot, block], {"dp": me}, MESH
                )
                guarded([there], arrival.wait_recv)
            children = [(across, None)] + children

            if any(r):
                for slot, there in children:

                    def total(slot=slot):
                        def piece(k, carry):
                            at = (pl.ds(pl.multiple_of(k * tall, tall), tall), slice(first, first + wide))
                            acc[(block,) + at] = (
                                acc[(block,) + at].astype(F32) + heard[(slot, block) + at].astype(F32)
                            ).astype(BF)
                            return carry

                        lax.fori_loop(0, rows // tall, piece, 0)

                    guarded([there], total)
                parent(c, r, block).start()
            else:

                def first_piece(k, carry):
                    at = (pl.ds(pl.multiple_of(k * tall, tall), tall), slice(first, first + wide))
                    out[at] = acc[(block,) + at].astype(F32)
                    return carry

                lax.fori_loop(0, rows // tall, first_piece, 0)
                for slot, there in children:

                    def total(slot=slot):
                        def piece(k, carry):
                            at = (pl.ds(pl.multiple_of(k * tall, tall), tall), slice(first, first + wide))
                            out[at] = out[at] + heard[(slot, block) + at].astype(F32)
                            return carry

                        lax.fori_loop(0, rows // tall, piece, 0)

                    guarded([there], total)

        guarded(real, run)

    ready = set()
    for c, r in events:
        if spot(c, r) not in ready:
            ready.add(spot(c, r))
            load(spot(c, r), load_wait)
        visit(c, r)
    def squares(k, carry):
        part = out[pl.ds(pl.multiple_of(k * tall, tall), tall), :]
        return carry + jnp.sum(part * part, axis=0, keepdims=True)

    square = lax.fori_loop(0, rows // tall, squares, jnp.zeros((1, width), F32))
    row_id = lax.broadcasted_iota(jnp.int32, total.shape, 0)
    total[...] = jnp.where(row_id == 5, square, small[...])
    sum_stages(place, sizes, peers, total, notes, note_send, note_recv)
    for c, r in events:
        if any(r):
            block, real = origin(me, coords, grid, routes[c][0], r)
            guarded(real, parent(c, r, block).wait_send)
    for where in firsts:
        load(where, load_end)


def reduce_grads(blocked, small, chips):
    grid = chip_grid(chips)
    _, _, rows, width = blocked.shape
    most = max(grid[0], 2 * grid[1] * grid[2])
    return pl.pallas_call(
        functools.partial(reduce_kernel, grid),
        name="reduce_grads",
        out_shape=(jax.ShapeDtypeStruct((rows, width), F32), jax.ShapeDtypeStruct(small.shape, F32)),
        in_specs=[any_spec(), pl.BlockSpec(memory_space=pltpu.VMEM)],
        out_specs=(pl.BlockSpec(memory_space=pltpu.VMEM),) * 2,
        scratch_shapes=[
            pltpu.VMEM((chips, rows, width), BF),
            pltpu.VMEM((slots_of(grid) + 1, chips, rows, width), BF),
            pltpu.VMEM((2, most) + small.shape, F32),
            pltpu.SemaphoreType.DMA((chips,)),
            pltpu.SemaphoreType.DMA((2, chips)),
            pltpu.SemaphoreType.DMA((4, chips)),
            pltpu.SemaphoreType.DMA((4, slots_of(grid), chips)),
            pltpu.SemaphoreType.DMA((2, most)),
            pltpu.SemaphoreType.DMA((2, most)),
        ],
        compiler_params=pltpu.CompilerParams(
            collective_id=2, has_side_effects=True, vmem_limit_bytes=VMEM_LIMIT
        ),
    )(blocked, small)


def exchange_kernel(*refs):
    count = (len(refs) - 7) // 2
    bank, states, banks = refs[count], refs[count + 1 : 2 * count + 1], refs[2 * count + 1]
    state_send, state_recv, send_sem, recv_sem, own_sem = refs[2 * count + 2 :]
    group, me = lax.axis_index("group"), lax.axis_index("dp")
    chips = banks.shape[0]
    barrier = pltpu.get_barrier_semaphore()

    def hail(target):
        def one(k, carry):
            pl.semaphore_signal(barrier, 1, device_id=(target, lax.rem(me + k, chips)), device_id_type=MESH)
            return carry

        return one

    @pl.when(group == 0)
    def _():
        lax.fori_loop(1, chips, hail(0), 0)
        lax.fori_loop(0, chips, hail(1), 0)

    @pl.when(group == 1)
    def _():
        lax.fori_loop(0, chips, hail(0), 0)

    pl.semaphore_wait(barrier, chips + (1 - group) * (chips - 1))

    def crossing(k):
        ref = states[k]
        if k == count - 1:
            part = ref.at[1]
        elif len(ref.shape) == 3 and ref.shape[0] == 3:
            part = ref.at[:, : ref.shape[1] // MICRO_BATCHES, :]
        else:
            part = ref.at[0]
        return pltpu.make_async_remote_copy(
            part, part, state_send.at[k], state_recv.at[k], {"group": 1 - group}, MESH
        )

    def note(core, k):
        return pltpu.make_async_remote_copy(
            bank.at[core],
            banks.at[me],
            send_sem.at[core, k],
            recv_sem.at[me],
            (core, lax.rem(me + k, chips)),
            MESH,
        )

    def each(core, act):
        def one(k, carry):
            act(note(core, k))
            return carry

        return one

    def take(k, carry):
        pltpu.make_async_remote_copy(
            bank.at[0], banks.at[k], send_sem.at[0, 0], recv_sem.at[k], (1 - group, me), MESH
        ).wait_recv()
        return carry

    @pl.when(group == 0)
    def _():
        own = pltpu.make_async_copy(bank.at[0], banks.at[me], own_sem)
        own.start()
        lax.fori_loop(1, chips, each(0, lambda copy: copy.start()), 0)
        lax.fori_loop(0, chips, each(1, lambda copy: copy.start()), 0)
        targets = crossing(count - 1)
        targets.start()
        own.wait()
        lax.fori_loop(1, chips, lambda k, carry: take(lax.rem(me + k, chips), carry), 0)
        for k in range(count - 1):
            crossing(k).wait_recv()
        lax.fori_loop(1, chips, each(0, lambda copy: copy.wait_send()), 0)
        lax.fori_loop(0, chips, each(1, lambda copy: copy.wait_send()), 0)
        targets.wait_send()

    @pl.when(group == 1)
    def _():
        copies = [crossing(k) for k in range(count - 1)]
        for copy in copies:
            copy.start()
        lax.fori_loop(0, chips, take, 0)
        crossing(count - 1).wait_recv()
        for copy in copies:
            copy.wait_send()


def exchange_states(states, bank, chips):
    count = len(states)
    outs = pl.pallas_call(
        exchange_kernel,
        name="exchange_states",
        out_shape=tuple(jax.ShapeDtypeStruct(a.shape, a.dtype) for a in states)
        + (jax.ShapeDtypeStruct((chips,) + bank.shape[1:], BF),),
        in_specs=[any_spec()] * (count + 1),
        out_specs=(any_spec(),) * (count + 1),
        scratch_shapes=[
            pltpu.SemaphoreType.DMA((count,)),
            pltpu.SemaphoreType.DMA((count,)),
            pltpu.SemaphoreType.DMA((2, chips)),
            pltpu.SemaphoreType.DMA((chips,)),
            pltpu.SemaphoreType.DMA,
        ],
        input_output_aliases={k: k for k in range(count)},
        compiler_params=pltpu.CompilerParams(collective_id=3, has_side_effects=True),
    )(*states, bank)
    return outs[:-1], outs[-1]


def place_kernel(spots, model, out, rows_scr, inbuf, stage, outbuf, in_sem, out_sem):
    chips, cores, rows, width = model.shape
    blocks = cores * chips
    cols = width // LANES
    deep, wide = inbuf.shape[0], outbuf.shape[0]
    group = max([g for g in range(1, 17) if rows % g == 0])

    def fetch(b, slot):
        return pltpu.make_async_copy(model.at[lax.rem(b, chips), b // chips], inbuf.at[slot], in_sem.at[slot])

    for b in range(deep - 1):
        fetch(b, b).start()

    def block(b, carry):
        slot = lax.rem(b, deep)
        fetch(b, slot).wait()

        @pl.when(b + deep - 1 < blocks)
        def _():
            fetch(b + deep - 1, lax.rem(b + deep - 1, deep)).start()

        for c in range(cols):
            stage[pl.ds(c, rows, stride=SUBLANES), :] = inbuf[slot, :, c * LANES : (c + 1) * LANES].astype(F32)

        def move(q, carry):
            first = q * group
            to = [spots[b * rows + first + j] for j in range(group)]
            held = [stage[pl.ds(pl.multiple_of((first + j) * SUBLANES, SUBLANES), SUBLANES), :] for j in range(group)]
            for j in range(group):
                rows_scr[pl.ds(to[j], SUBLANES, stride=SUBLANES), :] = held[j]
            return carry

        return lax.fori_loop(0, rows // group, move, carry)

    lax.fori_loop(0, blocks, block, 0)
    pieces = out.shape[0]
    for u in range(pieces):
        slot = u % wide
        if u >= wide:
            pltpu.make_async_copy(outbuf.at[slot], out.at[u - wide], out_sem.at[slot]).wait()

        def pack(k, carry):
            to = pl.ds(pl.multiple_of(k * 16, 16), 16)
            for c in range(cols):
                first = (u * width // SUBLANES + 2 * k) * TILE + c * SUBLANES
                halves = [rows_scr[pl.ds(pl.multiple_of(first + TILE * h, SUBLANES), SUBLANES), :] for h in range(2)]
                outbuf[slot, to, c * LANES : (c + 1) * LANES] = jnp.concatenate(halves, axis=0).astype(BF)
            return carry

        lax.fori_loop(0, width // 16, pack, 0)
        pltpu.make_async_copy(outbuf.at[slot], out.at[u], out_sem.at[slot]).start()
    for u in range(pieces - wide, pieces):
        pltpu.make_async_copy(outbuf.at[u % wide], out.at[u], out_sem.at[u % wide]).wait()


def place_weights(spots, model):
    _, _, rows, width = model.shape
    total = spots.shape[0]
    return pl.pallas_call(
        place_kernel,
        name="place_weights",
        out_shape=jax.ShapeDtypeStruct((total // width, width, width), BF),
        in_specs=[smem_spec(), any_spec()],
        out_specs=any_spec(),
        scratch_shapes=[
            pltpu.VMEM((total * SUBLANES, LANES), F32),
            pltpu.VMEM((8, rows, width), BF),
            pltpu.VMEM((rows * SUBLANES, LANES), F32),
            pltpu.VMEM((4, width, width), BF),
            pltpu.SemaphoreType.DMA((8,)),
            pltpu.SemaphoreType.DMA((4,)),
        ],
        compiler_params=pltpu.CompilerParams(vmem_limit_bytes=VMEM_LIMIT),
    )(spots, model)


def layer_stats(tensor):
    centre = tensor - jnp.mean(tensor, axis=-1, keepdims=True)
    scaled = lax.rsqrt(jnp.mean(centre * centre, axis=-1, keepdims=True) + 1e-06)
    return centre * scaled, scaled


def column_of(row):
    n = row.shape[1]
    eye = lax.broadcasted_iota(jnp.int32, (n, n), 0) == lax.broadcasted_iota(jnp.int32, (n, n), 1)
    return jnp.sum(jnp.where(eye, row, 0), axis=1, keepdims=True)


def flag_column(pos, slots):
    hit = lax.broadcasted_iota(jnp.int32, (slots, pos.shape[1]), 0) == pos
    return jnp.max(jnp.where(hit, 1, 0), axis=1, keepdims=True)


def fill_bias(bias, seg_col, seg_row):
    bias[...] = jnp.where(seg_col == seg_row, 0.0, MASK_FILL)


def half(x, h):
    low = lax.broadcasted_iota(jnp.int32, (1, LANES), 1) < HEAD_DIM
    keep = low if h == 0 else jnp.logical_not(low)
    return jnp.where(keep, x, jnp.zeros_like(x))


def fwd_kernel(
    patch, seg, pos, gains, teacher_gains, w_hbm,
    e_out, qkv_out, lse_out, o_out, x1_out, x2_out, tgt_out, bank_out,
    w, bias, gain, a2, e_v, qkv, lse, o_v, x1_v, x2_v, tgt, bank, sem, out_sem,
):
    i = pl.program_id(0)
    role = lax.axis_index("group")
    gain[...] = jnp.where(role == 0, teacher_gains[...], gains[...])
    batches, slots, width = e_out.shape
    pieces = w_hbm.shape[0]
    cuts = (pieces - 6) // 2
    order = [0, 3, 4, 5, 1]
    for j in range(cuts):
        order += [6 + j, 6 + cuts + j]

    @pl.when(i == 0)
    def _():
        for u in order:
            pltpu.make_async_copy(w_hbm.at[u], w.at[u], sem.at[u]).start()

    def need(u):
        @pl.when(i == 0)
        def _():
            pltpu.make_async_copy(w_hbm.at[u], w.at[u], sem.at[u]).wait()

    def leave(k, b):
        tokens = pl.ds(pl.multiple_of(b * slots, slots), slots)
        source, target = [
            (e_v.at[b], e_out.at[b]),
            (qkv.at[b], qkv_out.at[:, tokens, :]),
            (lse.at[b], lse_out.at[b]),
            (o_v.at[b], o_out.at[b]),
            (x1_v.at[b], x1_out.at[b]),
            (x2_v.at[b], x2_out.at[b]),
            (tgt.at[b], tgt_out.at[b]),
            (bank.at[b], bank_out.at[b]),
        ][k]
        return pltpu.make_async_copy(source, target, out_sem.at[b, k])

    seg_row = seg[0]
    seg_col = column_of(seg_row)
    fill_bias(bias, seg_col, seg_row)
    flags = flag_column(pos[0], slots) * role
    need(0)
    e = nn(patch[0], w[0])
    e = jnp.where(flags > 0, gain[3:4, :], e)
    e_v[i] = e
    leave(0, i).start()
    a2[...] = (layer_stats(e)[0] * gain[0:1, :]).astype(BF)

    def project(j, carry):
        need(3 + j)
        qkv[i, j] = nn(a2[...], w[3 + j]).astype(BF)
        return carry

    lax.fori_loop(0, 3, project, 0)
    leave(1, i).start()

    def pair(p, carry):
        cs = pl.ds(pl.multiple_of(p * LANES, LANES), LANES)
        q2, k2, v2 = qkv[i, 0, :, cs], qkv[i, 1, :, cs], qkv[i, 2, :, cs]
        k2 = k2 * jnp.asarray(HEAD_DIM**-0.5, BF)
        v_t = v2.T
        outs = []
        for h in range(2):
            s = nt(half(k2, h), q2) + bias[...]
            top = jnp.max(s, axis=0, keepdims=True)
            ex = jnp.exp(s - top)
            total = jnp.sum(ex, axis=0, keepdims=True)
            lse[i, pl.ds(2 * p + h, 1), :] = top + jnp.log(total)
            probs = (ex * (1.0 / total)).astype(BF)
            outs.append(nn(v_t[h * HEAD_DIM : (h + 1) * HEAD_DIM, :], probs))
        o_v[i, :, cs] = jnp.concatenate(outs, axis=0).T.astype(BF)
        return carry

    lax.fori_loop(0, HEADS // 2, pair, 0)
    leave(2, i).start()
    leave(3, i).start()
    need(1)
    x1 = e_v[i] + nn(o_v[i], w[1])
    x1_v[i] = x1
    leave(4, i).start()
    a2[...] = (layer_stats(x1)[0] * gain[1:2, :]).astype(BF)
    x2_v[i] = x1

    def ffn(j, carry):
        need(6 + j)
        hid = nn(a2[...], w[6 + j])
        act = (hid * (0.5 * (1.0 + jnp.tanh(GELU_A * (hid + GELU_B * hid * hid * hid))))).astype(BF)
        need(6 + cuts + j)
        x2_v[i] += nn(act, w[6 + cuts + j])
        return carry

    lax.fori_loop(0, cuts, ffn, 0)
    leave(5, i).start()

    @pl.when(role == 0)
    def _():
        t = layer_stats(x2_v[i])[0].astype(BF)
        tgt[i] = t
        leave(6, i).start()
        t = t.astype(F32)
        for m in range(IMGS):
            inside = seg_col == m
            size = jnp.sum(jnp.where(inside, 1.0, 0.0), axis=0, keepdims=True)
            pooled = jnp.sum(jnp.where(inside, t, 0.0), axis=0, keepdims=True) / size
            unit = pooled * lax.rsqrt(jnp.sum(pooled * pooled, axis=-1, keepdims=True) + 1e-06)
            bank[i, m : m + 1, :] = unit.astype(BF)
        leave(7, i).start()

    @pl.when(i == batches - 1)
    def _():
        for b in range(batches):
            for k in range(6):
                leave(k, b).wait()

        @pl.when(role == 0)
        def _():
            for b in range(batches):
                leave(6, b).wait()
                leave(7, b).wait()


def forward(patch, seg, pos, gains, teacher_gains, w):
    batches, slots, width = patch.shape
    pieces = w.shape[0]
    tok = lambda n, dt: ((batches,) + ((3,) if n == 3 else ()) + (slots, width), dt)
    kinds = [
        tok(1, F32),
        tok(3, BF),
        ((batches, HEADS, slots), F32),
        tok(1, BF),
        tok(1, F32),
        tok(1, F32),
        tok(1, BF),
        ((batches, IMGS, width), BF),
    ]
    outs = [jax.ShapeDtypeStruct(shape, dt) for shape, dt in kinds]
    outs[1] = jax.ShapeDtypeStruct((3, batches * slots, width), BF)
    return pl.pallas_call(
        fwd_kernel,
        name="forward",
        grid=(batches,),
        out_shape=tuple(outs),
        in_specs=[
            pl.BlockSpec((1, slots, width), lambda i: (i, 0, 0)),
            pl.BlockSpec((1, 1, slots), lambda i: (i, 0, 0)),
            pl.BlockSpec((1, 1, pos.shape[2]), lambda i: (i, 0, 0)),
            pl.BlockSpec((4, width), lambda i: (0, 0)),
            pl.BlockSpec((4, width), lambda i: (0, 0)),
            any_spec(),
        ],
        out_specs=(any_spec(),) * len(outs),
        scratch_shapes=[
            pltpu.VMEM((pieces, width, width), BF),
            pltpu.VMEM((slots, slots), F32),
            pltpu.VMEM((4, width), F32),
            pltpu.VMEM((slots, width), BF),
        ]
        + [pltpu.VMEM(shape, dt) for shape, dt in kinds]
        + [
            pltpu.SemaphoreType.DMA((pieces,)),
            pltpu.SemaphoreType.DMA((batches, len(kinds))),
        ],
        compiler_params=pltpu.CompilerParams(vmem_limit_bytes=VMEM_LIMIT),
        cost_estimate=pl.CostEstimate(
            flops=2 * batches * slots * width * width * pieces, bytes_accessed=2 * w.size, transcendentals=0
        ),
    )(patch, seg, pos, gains, teacher_gains, w)


def norm_back(grad_out, normed, scaled, gain_vec):
    grad_hat = grad_out * gain_vec
    inner = jnp.mean(grad_hat * normed, axis=-1, keepdims=True)
    grad_in = scaled * (grad_hat - jnp.mean(grad_hat, axis=-1, keepdims=True) - normed * inner)
    return grad_in, jnp.sum(grad_out * normed, axis=0, keepdims=True)


def bwd_kernel(
    seg, pos, gain, lse, banks, e_hbm, qkv_hbm, x1_hbm, x2_hbm, tgt_hbm, w_own, w_far,
    head_out, attn_out, ffn_out, act_out, de_out, mid_out, pred_out, dqkv_out, du_out, down_out, small,
    w, bias, top_scr, acc_scr, pool_scr, bank_scr, e_in, qkv, x1_in, x2_in, tgt,
    head_v, attn_v, ffn_v, act_v, de_v, mid_v, pred_v, dqkv, du_v, down_v, sem, in_sem, out_sem,
):
    role, chip = lax.axis_index("group"), lax.axis_index("dp")
    slots, width = e_in.shape
    chips = banks.shape[0]
    pieces = w_own.shape[0]
    cuts = (pieces - 6) // 2
    tokens = pl.ds(pl.multiple_of(role * slots, slots), slots)

    def bring(k, source, target):
        copy = pltpu.make_async_copy(source, target, in_sem.at[k])
        copy.start()
        return copy

    def bring_piece(u):
        @pl.when(role == 0)
        def _():
            pltpu.make_async_copy(w_far.at[u], w.at[u - 1], sem.at[u]).start()

        @pl.when(role != 0)
        def _():
            pltpu.make_async_copy(w_own.at[u], w.at[u - 1], sem.at[u]).start()

    def need(u):
        pltpu.make_async_copy(w_own.at[u], w.at[u - 1], sem.at[u]).wait()

    taken = []

    def keep(source, target):
        copy = pltpu.make_async_copy(source, target, out_sem.at[len(taken)])
        copy.start()
        taken.append(copy)

    x2_copy = bring(0, x2_hbm.at[role], x2_in)
    bring_piece(2)
    tgt_copy = bring(1, tgt_hbm.at[role], tgt)
    x1_copy = bring(2, x1_hbm.at[role], x1_in)
    for j in range(cuts):
        bring_piece(6 + cuts + j)
        bring_piece(6 + j)
    bring_piece(1)
    qkv_copy = bring(3, qkv_hbm.at[:, tokens, :], qkv)
    for j in range(3):
        bring_piece(3 + j)
    e_copy = bring(4, e_hbm.at[role], e_in)
    small[...] = jnp.zeros_like(small)

    seg_row = seg[role]
    seg_col = column_of(seg_row)
    fill_bias(bias, seg_col, seg_row)
    flags = flag_column(pos[role], slots)
    x2_copy.wait()
    n3, r3 = layer_stats(x2_in[...])
    head_in = (n3 * gain[2:3, :]).astype(BF)
    head_v[...] = head_in
    keep(head_v, head_out.at[0])
    need(2)
    pred = nn(head_in, w[1])
    valid = jnp.where(seg_col < IMGS, flags, 0).astype(F32)
    tgt_copy.wait()
    diff = pred - tgt[...].astype(F32)
    size = jnp.abs(diff)
    huber = jnp.where(size < 1.0, 0.5 * diff * diff, size - 0.5)
    regress = jnp.sum(jnp.sum(valid * huber, axis=1, keepdims=True), axis=0, keepdims=True)
    count = float(MASKED * chips * MICRO_BATCHES * width)
    grad_pred = valid * (jnp.clip(diff, -1.0, 1.0) / count)
    pool_scr[...] = jnp.zeros_like(pool_scr)
    for m in range(IMGS):
        inside = seg_col == m
        tally = jnp.sum(jnp.where(inside, 1.0, 0.0), axis=0, keepdims=True)
        pool_scr[m : m + 1, :] = jnp.sum(jnp.where(inside, pred, 0.0), axis=0, keepdims=True) / tally
    pooled = pool_scr[...]
    length = lax.rsqrt(jnp.sum(pooled * pooled, axis=-1, keepdims=True) + 1e-06)
    unit = pooled * length
    for k in range(chips):
        bank_scr[k * IMGS : (k + 1) * IMGS, :] = banks[k].astype(F32)
    memory = bank_scr[...].astype(BF)
    choices = memory.shape[0]
    logits = nt(unit.astype(BF), memory) / SOFTMAX_TEMPER
    row_id = lax.broadcasted_iota(jnp.int32, logits.shape, 0)
    real = row_id < IMGS
    picked = jnp.where(
        real & (lax.broadcasted_iota(jnp.int32, logits.shape, 1) == chip * IMGS + row_id), 1.0, 0.0
    )
    peak = jnp.max(logits, axis=-1, keepdims=True)
    ex = jnp.exp(logits - peak)
    total = jnp.sum(ex, axis=-1, keepdims=True)
    each = peak + jnp.log(total) - jnp.sum(logits * picked, axis=-1, keepdims=True)
    contrast = jnp.sum(jnp.where(real[:, 0:1], each, 0.0), axis=0, keepdims=True)
    scale = choices * MICRO_BATCHES
    grad_logits = (jnp.where(real, ex / total - picked, 0.0) / scale / SOFTMAX_TEMPER).astype(BF)
    grad_unit = nn(grad_logits, memory)
    grad_pool = length * (grad_unit - unit * jnp.sum(grad_unit * unit, axis=1, keepdims=True))
    pool_scr[...] = grad_pool
    for m in range(IMGS):
        inside = seg_col == m
        tally = jnp.sum(jnp.where(inside, 1.0, 0.0), axis=0, keepdims=True)
        grad_pred = grad_pred + jnp.where(inside, pool_scr[m : m + 1, :] / tally, 0.0)
    low = grad_pred.astype(BF)
    pred_v[...] = low
    keep(pred_v, pred_out.at[0])
    loss = regress / count + contrast / scale
    small[4:5, :] += jnp.broadcast_to(loss, (1, width))
    grad_top, gain_three = norm_back(nt(low, w[1]), n3, r3, gain[2:3, :])
    small[2:3, :] += gain_three
    top_scr[...] = grad_top
    down = grad_top.astype(BF)
    down_v[...] = down
    keep(down_v, down_out.at[0])
    x1_copy.wait()
    n2, r2 = layer_stats(x1_in[...])
    ffn_in = (n2 * gain[1:2, :]).astype(BF)
    ffn_v[...] = ffn_in
    keep(ffn_v, ffn_out.at[0])
    acc_scr[...] = jnp.zeros_like(acc_scr)
    loop_sem = len(taken)

    def leave(j):
        return (
            pltpu.make_async_copy(act_v.at[j], act_out.at[j], out_sem.at[loop_sem + 2 * j]),
            pltpu.make_async_copy(du_v.at[j], du_out.at[j], out_sem.at[loop_sem + 2 * j + 1]),
        )

    def ffn(j, carry):
        need(6 + cuts + j)
        grad_act = nt(down_v[...], w[5 + cuts + j])
        need(6 + j)
        hid = nn(ffn_v[...], w[5 + j])
        th = jnp.tanh(GELU_A * (hid + GELU_B * hid * hid * hid))
        cdf = 0.5 * (1.0 + th)
        act_v[j] = (hid * cdf).astype(BF)
        slope = cdf + hid * (0.5 * (1.0 - th * th)) * (GELU_A * (1.0 + 3.0 * GELU_B * hid * hid))
        du = (grad_act * slope).astype(BF)
        du_v[j] = du
        for copy in leave(j):
            copy.start()
        acc_scr[...] += nt(du, w[5 + j])
        return carry

    lax.fori_loop(0, cuts, ffn, 0)
    for j in range(cuts):
        taken.extend(leave(j))
    grad_ffn, gain_two = norm_back(acc_scr[...], n2, r2, gain[1:2, :])
    small[1:2, :] += gain_two
    mid = top_scr[...] + grad_ffn
    top_scr[...] = mid
    mid_low = mid.astype(BF)
    mid_v[...] = mid_low
    keep(mid_v, mid_out.at[0])
    need(1)
    de_v[...] = nt(mid_low, w[0]).astype(BF)
    qkv_copy.wait()

    def pair(p, carry):
        cs = pl.ds(pl.multiple_of(p * LANES, LANES), LANES)
        q2, k2, v2, g2 = qkv[0, :, cs], qkv[1, :, cs], qkv[2, :, cs], de_v[:, cs]
        k_scaled = k2 * jnp.asarray(HEAD_DIM**-0.5, BF)
        k_t = k2.T
        dq, dk, dv = [], 0.0, 0.0
        for h in range(2):
            s = nt(half(k_scaled, h), q2) + bias[...]
            probs = jnp.exp(s - lse[role, pl.ds(2 * p + h, 1), :])
            dp = nt(half(v2, h), g2)
            centre = jnp.sum(probs * dp, axis=0, keepdims=True)
            ds = (probs * (dp - centre)).astype(BF)
            dv = dv + nn(probs.astype(BF), half(g2, h))
            dk = dk + nn(ds, half(q2, h))
            dq.append(nn(k_t[h * HEAD_DIM : (h + 1) * HEAD_DIM, :], ds))
        dqkv[0, :, cs] = (jnp.concatenate(dq, axis=0) * HEAD_DIM**-0.5).T.astype(BF)
        dqkv[1, :, cs] = (dk * HEAD_DIM**-0.5).astype(BF)
        dqkv[2, :, cs] = dv.astype(BF)
        return carry

    lax.fori_loop(0, HEADS // 2, pair, 0)
    keep(dqkv, dqkv_out)
    acc_scr[...] = jnp.zeros_like(acc_scr)

    def project(j, carry):
        need(3 + j)
        acc_scr[...] += nt(dqkv[j], w[2 + j])
        return carry

    lax.fori_loop(0, 3, project, 0)
    e_copy.wait()
    n1, r1 = layer_stats(e_in[...])
    attn_v[...] = (n1 * gain[0:1, :]).astype(BF)
    keep(attn_v, attn_out.at[0])
    grad_attn, gain_one = norm_back(acc_scr[...], n1, r1, gain[0:1, :])
    small[0:1, :] += gain_one
    start = top_scr[...] + grad_attn
    hidden_slot = flags > 0
    small[3:4, :] += jnp.sum(jnp.where(hidden_slot, start, 0.0), axis=0, keepdims=True)
    de_v[...] = jnp.where(hidden_slot, 0.0, start).astype(BF)
    keep(de_v, de_out.at[0])
    for copy in taken:
        copy.wait()


def backward(seg, pos, gain, lse, banks, e, qkv, x1, x2, tgt, w_own, w_far):
    _, slots, width = e.shape
    pieces = w_own.shape[0]
    cuts = (pieces - 6) // 2
    counts = (1, 1, 1, cuts, 1, 1, 1, 3, cuts, 1)
    vmem = pl.BlockSpec(memory_space=pltpu.VMEM)
    tok = lambda n, dt: pltpu.VMEM((n, slots, width) if n > 1 else (slots, width), dt)
    return pl.pallas_call(
        bwd_kernel,
        name="backward",
        out_shape=tuple(jax.ShapeDtypeStruct((n, slots, width), BF) for n in counts)
        + (jax.ShapeDtypeStruct((SUBLANES, width), F32),),
        in_specs=[vmem] * 5 + [any_spec()] * 7,
        out_specs=(any_spec(),) * len(counts) + (vmem,),
        scratch_shapes=[
            pltpu.VMEM((pieces - 1, width, width), BF),
            pltpu.VMEM((slots, slots), F32),
            pltpu.VMEM((slots, width), F32),
            pltpu.VMEM((slots, width), F32),
            pltpu.VMEM((SUBLANES, width), F32),
            pltpu.VMEM((banks.shape[0] * IMGS, width), F32),
            tok(1, F32),
            tok(3, BF),
            tok(1, F32),
            tok(1, F32),
            tok(1, BF),
        ]
        + [tok(n, BF) for n in counts]
        + [
            pltpu.SemaphoreType.DMA((pieces,)),
            pltpu.SemaphoreType.DMA((5,)),
            pltpu.SemaphoreType.DMA((sum(counts),)),
        ],
        compiler_params=pltpu.CompilerParams(vmem_limit_bytes=VMEM_LIMIT),
    )(seg, pos, gain, lse, banks, e, qkv, x1, x2, tgt, w_own, w_far)


def grads_kernel(
    plan, places, patch, mixed, head, attn, ffn, act, de, mid, pred, dqkv, du, down, out,
    rows_scr, x_buf, x_t, g_buf, stage, outbuf, x_sem, g_sem, out_sem,
):
    blocks, rows, width = out.shape
    cols = width // LANES
    deep, wide_out = x_buf.shape[0], outbuf.shape[0]
    group = max([g for g in range(SUBLANES, 49, SUBLANES) if rows % g == 0], default=rows)
    lefts = {"patch": patch, "mixed": mixed, "head": head, "attn": attn, "ffn": ffn, "act": act}
    rights = {"de": de, "mid": mid, "pred": pred, "dqkv": dqkv, "du": du, "down": down}

    def left_of(key):
        name, index = key
        return lefts[name].at[lax.axis_index("group") if name in ("patch", "mixed") else index]

    lcopies, rcopies = [], []
    lkeys, rkeys = [], []
    steps = []
    for u, (left, right) in enumerate(plan):
        if not lkeys or lkeys[-1] != left:
            slot = len(lkeys) % deep
            lcopies.append(pltpu.make_async_copy(left_of(left), x_buf.at[slot], x_sem.at[slot]))
            lkeys.append(left)
            fresh_l = True
        else:
            fresh_l = False
        if not rkeys or rkeys[-1] != right:
            slot = len(rkeys) % deep
            rcopies.append(pltpu.make_async_copy(rights[right[0]].at[right[1]], g_buf.at[slot], g_sem.at[slot]))
            rkeys.append(right)
            fresh_r = True
        else:
            fresh_r = False
        steps.append((u, len(lkeys) - 1, fresh_l, len(rkeys) - 1, fresh_r))
    for copy in lcopies[: deep - 1] + rcopies[: deep - 1]:
        copy.start()
    for u, li, fresh_l, ri, fresh_r in steps:
        if fresh_l:
            lcopies[li].wait()
            if li + deep - 1 < len(lcopies):
                lcopies[li + deep - 1].start()
            x_t[...] = x_buf[li % deep].T
        if fresh_r:
            rcopies[ri].wait()
            if ri + deep - 1 < len(rcopies):
                rcopies[ri + deep - 1].start()
        wide = 2 * LANES

        def tile(n, carry):
            part = nn(x_t[...], g_buf[ri % deep, :, pl.ds(pl.multiple_of(n * wide, wide), wide)])
            for c in range(2):
                rows_scr[pl.ds(u * width * SUBLANES + 2 * n + c, width, stride=SUBLANES), :] = part[
                    :, c * LANES : (c + 1) * LANES
                ]
            return carry

        lax.fori_loop(0, width // wide, tile, 0)

    def block(b, carry):
        slot = lax.rem(b, wide_out)

        def move(q, carry):
            came = [pl.multiple_of(places[b * rows + q * group + j] * SUBLANES, SUBLANES) for j in range(group)]
            held = [rows_scr[pl.ds(first, SUBLANES), :] for first in came]
            for j in range(group):
                to = q * (group // SUBLANES) * TILE + j // SUBLANES * TILE + j % SUBLANES
                stage[pl.ds(to, SUBLANES, stride=SUBLANES), :] = held[j]
            return carry

        lax.fori_loop(0, rows // group, move, 0)

        @pl.when(b >= wide_out)
        def _():
            pltpu.make_async_copy(outbuf.at[slot], out.at[b - wide_out], out_sem.at[slot]).wait()

        for first in range(0, rows, 16):
            tall = min(16, rows - first)
            for c in range(cols):
                at = first * SUBLANES + c * SUBLANES
                both = jnp.concatenate([stage[at : at + SUBLANES, :], stage[at + TILE : at + TILE + SUBLANES, :]], 0)
                outbuf[slot, first : first + tall, c * LANES : (c + 1) * LANES] = both[:tall].astype(BF)
        pltpu.make_async_copy(outbuf.at[slot], out.at[b], out_sem.at[slot]).start()
        return carry

    lax.fori_loop(0, blocks, block, 0)
    for b in range(blocks - wide_out, blocks):
        pltpu.make_async_copy(outbuf.at[b % wide_out], out.at[b], out_sem.at[b % wide_out]).wait()


def weight_grads(places, lefts, rights, blocks):
    tokens, width = lefts[0].shape[1:]
    cuts = lefts[-1].shape[0]
    total = places.shape[0]
    rows = total // blocks
    plan = (
        [(("patch", 0), ("de", 0)), (("mixed", 0), ("mid", 0)), (("head", 0), ("pred", 0))]
        + [(("attn", 0), ("dqkv", j)) for j in range(3)]
        + [(("ffn", 0), ("du", j)) for j in range(cuts)]
        + [(("act", j), ("down", 0)) for j in range(cuts)]
    )
    return pl.pallas_call(
        functools.partial(grads_kernel, plan),
        name="weight_grads",
        out_shape=jax.ShapeDtypeStruct((blocks, rows, width), BF),
        in_specs=[smem_spec()] + [any_spec()] * 12,
        out_specs=any_spec(),
        scratch_shapes=[
            pltpu.VMEM((total * SUBLANES, LANES), F32),
            pltpu.VMEM((4, tokens, width), BF),
            pltpu.VMEM((width, tokens), BF),
            pltpu.VMEM((4, tokens, width), BF),
            pltpu.VMEM((pl.cdiv(rows, 16) * 2 * TILE, LANES), F32),
            pltpu.VMEM((4, rows, width), BF),
            pltpu.SemaphoreType.DMA((4,)),
            pltpu.SemaphoreType.DMA((4,)),
            pltpu.SemaphoreType.DMA((4,)),
        ],
        compiler_params=pltpu.CompilerParams(vmem_limit_bytes=VMEM_LIMIT),
    )(places, *lefts, *rights)


def power_of(base, exponent):
    return lax.fori_loop(0, exponent, lambda _, product: product * base, jnp.float32(1.0))


def update_kernel(
    step, total, gains, gone, gtwo, grad, master, one, two, teacher,
    loss_out, norm_out, one_out, two_out, master_out, teacher_out, gone_out, gtwo_out,
):
    gain_grad = total[0:4, :]
    square = jnp.sum(total[5:6, :], axis=1, keepdims=True)
    square = square + jnp.sum(jnp.sum(gain_grad * gain_grad, axis=1, keepdims=True), axis=0, keepdims=True)
    norm = jnp.sqrt(square)
    factor = jnp.minimum(1.0, CLIP / norm)
    fix_one = 1.0 - power_of(BETA_ONE, step[0])
    fix_two = 1.0 - power_of(BETA_TWO, step[0])

    def moments(first, second, gradient):
        first = BETA_ONE * first + (1.0 - BETA_ONE) * gradient
        second = BETA_TWO * second + (1.0 - BETA_TWO) * gradient * gradient
        return first, second

    @pl.when(pl.program_id(0) == 0)
    def _():
        loss_out[0] = jnp.sum(total[4:5, 0:1])
        norm_out[0] = jnp.sum(norm)
        gone_out[...], gtwo_out[...] = moments(gone[...], gtwo[...], gain_grad * factor)

    first, second = moments(one[...], two[...], grad[...] * factor)
    change = first / fix_one / (jnp.sqrt(second / fix_two) + ADAM_EPS)
    weight = master[...]
    weight = weight - RATE * (change + DECAY * weight)
    one_out[...] = first
    two_out[...] = second
    master_out[...] = weight
    teacher_out[...] = EMA_KEEP * teacher[...] + (1.0 - EMA_KEEP) * weight


def update(step, total, gains, gone, gtwo, grad, master, one, two, teacher):
    rows, width = grad.shape
    tall = max([t for t in range(SUBLANES, 113, SUBLANES) if rows % t == 0], default=rows)
    part = pl.BlockSpec((tall, width), lambda i: (i, 0))
    whole = lambda a: pl.BlockSpec(a.shape, lambda i: (0, 0))
    scalar = jax.ShapeDtypeStruct((1,), F32)
    same = lambda a: jax.ShapeDtypeStruct(a.shape, F32)
    return pl.pallas_call(
        update_kernel,
        name="update",
        grid=(rows // tall,),
        out_shape=(scalar, scalar, same(one), same(two), same(master), same(teacher), same(gone), same(gtwo)),
        in_specs=[smem_spec(), whole(total), whole(gains), whole(gone), whole(gtwo)] + [part] * 5,
        out_specs=(smem_spec(), smem_spec(), part, part, part, part, whole(gone), whole(gtwo)),
    )(step, total, gains, gone, gtwo, grad, master, one, two, teacher)


def body(
    patches,
    segments,
    positions,
    owners,
    master,
    moment_one,
    moment_two,
    teacher,
    gains,
    gain_one,
    gain_two,
    teacher_gains,
    step_count,
):
    core = lax.axis_index("group")
    width = patches.shape[3]
    slots = patches.shape[2]
    row_total = owners.shape[0]
    inner = (row_total - 6 * width) // 2
    places = piece_rows(owners, width, inner)
    spots = places // SUBLANES * TILE + places % SUBLANES
    chips = lax.axis_size("dp")
    devices = lax.axis_size("group") * chips
    own_rows = row_total // devices

    if chips <= KERNEL_CHIPS:
        model = gather_weights(master, teacher, chips)
    else:
        parts = lax.all_gather(jnp.stack([teacher, master]).astype(BF), ("dp", "group"), axis=1)
        model = jnp.where(core == 1, parts[1], parts[0]).reshape(chips, 2, own_rows, width)
    w = place_weights(spots, model)
    w_far = lax.ppermute(w, "group", [(1, 0)])
    patch = patches[:, 0]
    seg = segments
    pos = positions
    e, qkv, lse, mixed, x1, x2, tgt, bank = forward(patch, seg, pos, gains, teacher_gains, w)
    (e, qkv, lse, mixed, x1, x2, tgt), banks = exchange_states((e, qkv, lse, mixed, x1, x2, tgt), bank, chips)
    head, attn, ffn, act, de, mid, pred, dqkv, du, down, small = backward(
        seg, pos, gains, lse, banks, e, qkv, x1, x2, tgt, w, w_far
    )
    blocked = weight_grads(
        places, (patch, mixed, head, attn, ffn, act), (de, mid, pred, dqkv, du, down), devices
    )
    if chips <= KERNEL_CHIPS:
        owned_grad, total = reduce_grads(blocked.reshape(2, chips, own_rows, width), small, chips)
    else:
        owned_grad = lax.psum_scatter(blocked, ("group", "dp"), scatter_dimension=0, tiled=True)
        owned_grad = owned_grad.reshape(own_rows, width).astype(F32)
        squares = jnp.sum(owned_grad * owned_grad, axis=0, keepdims=True)
        row_id = lax.broadcasted_iota(jnp.int32, small.shape, 0)
        total = lax.psum(jnp.where(row_id == 5, squares, small), ("group", "dp"))
    return update(
        step_count, total, gains, gain_one, gain_two, owned_grad, master, moment_one, moment_two, teacher
    )


def solution(mesh):
    rows = P(("group", "dp"), None)
    in_specs = (
        P(None, "dp", None, None),
        P(None, "dp", None),
        P(None, "dp", None),
        P(),
        rows,
        rows,
        rows,
        rows,
        P(),
        P(),
        P(),
        P(),
        P(),
    )
    out_specs = (P(), P(), rows, rows, rows, rows, P(), P())
    return jax.shard_map(body, mesh=mesh, in_specs=in_specs, out_specs=out_specs, check_vma=False)
```

```python
import functools

import jax
import jax.numpy as jnp
from jax import lax
from jax.experimental import pallas as pl
from jax.experimental.pallas import tpu as pltpu
from jax.sharding import PartitionSpec as P

HEADS = 12
HEAD_DIM = 64
IMGS = 4
MASKED = 320
MICRO_BATCHES = 2
LANES = 128
SUBLANES = 8
TILE = SUBLANES * SUBLANES

SOFTMAX_TEMPER = 0.05
CLIP = 0.004
RATE = 0.05
BETA_ONE = 0.9
BETA_TWO = 0.999
ADAM_EPS = 1e-08
DECAY = 0.05
EMA_KEEP = 0.9
MASK_FILL = -1000000000.0

BF = jnp.bfloat16
F32 = jnp.float32
VMEM_LIMIT = 67_000_000
GELU_A = 0.7978845608028654
GELU_B = 0.044715


def nn(a, b):
    return jnp.dot(a, b, preferred_element_type=F32)


def nt(a, b):
    return lax.dot_general(a, b, (((1,), (1,)), ((), ())), preferred_element_type=F32)


def piece_rows(flat, width, inner):
    cuts = inner // width
    qkv, up = flat - 3 * width, flat - 6 * width
    inside = jnp.where(flat < 6 * width, (3 + qkv % 3) * width + qkv // 3, (6 + up % cuts) * width + up // cuts)
    return jnp.where((flat >= 3 * width) & (flat < 6 * width + inner), inside, flat)


def any_spec():
    return pl.BlockSpec(memory_space=pl.ANY)


def smem_spec():
    return pl.BlockSpec(memory_space=pltpu.SMEM)


MESH = pl.DeviceIdType.MESH
KERNEL_CHIPS = 16
AHEAD = 8


def chip_grid(chips):
    sizes, turn, left, prime = [1, 1, 1], 0, chips, 2
    while left > 1:
        while left % prime:
            prime += 1
        sizes[turn % 3] *= prime
        turn += 1
        left //= prime
    return tuple(sizes)


def strides_of(grid):
    return (grid[1] * grid[2], grid[2], 1)


def coords_of(index, grid):
    return (index // (grid[1] * grid[2]), lax.rem(index // grid[2], grid[1]), lax.rem(index, grid[2]))


def guarded(conditions, action):
    conditions = [c for c in conditions if c is not None]
    if not conditions:
        return action()
    both = conditions[0]
    for c in conditions[1:]:
        both = jnp.logical_and(both, c)
    pl.when(both)(action)


def lanes_of(width):
    unit = width // 6
    orders = [((1, 0, 2), 2), ((2, 0, 1), 2), ((0, 2, 1), 1), ((0, 1, 2), 1)]
    routes, first = [], 0
    for order, share in orders:
        routes.append((order, first, share * unit))
        first += share * unit
    return routes


def offsets(length):
    if length <= 2:
        return list(range(length))
    return [0] + [sign * far for far in range(1, length) for sign in (1, -1)]


def route_events(grid, routes):
    events = []
    for c, (order, _, _) in enumerate(routes):
        stack = [()]
        for d in order:
            stack = [r + (o,) for r in stack for o in offsets(grid[d])]
        events += [(sum(abs(o) * 2**i for i, o in enumerate(r)), c, r) for r in stack]
    return [(c, r) for _, c, r in sorted(events, key=lambda e: e[0])]


def onward(grid, order, r):
    last = max([i for i in range(3) if r[i]], default=-1)
    outs = []
    if last >= 0 and grid[order[last]] > 2:
        outs.append((order[last], 1 if r[last] > 0 else -1))
    for d in order[last + 1 :]:
        if grid[d] == 2:
            outs.append((d, 1))
        elif grid[d] > 2:
            outs += [(d, 1), (d, -1)]
    return outs


def neighbour(me, coords, grid, d, sign):
    step = strides_of(grid)[d]
    if grid[d] == 2:
        return me + (1 - 2 * coords[d]) * step, None
    place = coords[d] + sign
    return me + sign * step, jnp.logical_and(place >= 0, place < grid[d])


def origin(me, coords, grid, order, r):
    index, conditions = me, []
    for d, o in zip(order, r):
        if o == 0:
            continue
        step = strides_of(grid)[d]
        if grid[d] == 2:
            index = index + (1 - 2 * coords[d]) * step
        else:
            place = coords[d] - o
            index = index - o * step
            conditions.append(jnp.logical_and(place >= 0, place < grid[d]))
    return index, conditions


def slot_of(grid, d, sign):
    first = sum([1 if n <= 2 else 2 for n in grid[:d]])
    return first if grid[d] <= 2 or sign > 0 else first + 1


def slots_of(grid):
    return sum([1 if n <= 2 else 2 for n in grid])


def greet(me, coords, grid, group):
    barrier = pltpu.get_barrier_semaphore()
    near = [neighbour(me, coords, grid, d, s) for d in range(3) for s in ((1,) if grid[d] == 2 else (1, -1)) if grid[d] > 1]
    for index, there in near:
        guarded([there], lambda: pl.semaphore_signal(barrier, 1, device_id={"dp": index}, device_id_type=MESH))
    pl.semaphore_signal(barrier, 1, device_id={"group": 1 - group}, device_id_type=MESH)
    pl.semaphore_wait(barrier, 1 + sum([1 if there is None else there.astype(jnp.int32) for _, there in near]))


def gather_kernel(grid, learn, teach, out, both, swap_sem, half_sem, send_sem, recv_sem):
    group, me = lax.axis_index("group"), lax.axis_index("dp")
    coords = coords_of(me, grid)
    routes = lanes_of(both.shape[2])
    events = route_events(grid, routes)
    both[0] = teach[...].astype(BF)
    both[1] = learn[...].astype(BF)
    greet(me, coords, grid, group)
    keep = pltpu.make_async_copy(both.at[group], out.at[me, group], swap_sem.at[2])
    keep.start()
    swap = pltpu.make_async_remote_copy(
        both.at[1 - group], out.at[me, group], swap_sem.at[0], swap_sem.at[1], {"group": 1 - group}, MESH
    )
    swap.start()

    def first_sends(half, source):
        copies = []
        for c, (order, first, wide) in enumerate(routes):
            for d, sign in onward(grid, order, (0, 0, 0)):
                index, there = neighbour(me, coords, grid, d, sign)
                copy = pltpu.make_async_remote_copy(
                    source.at[:, first : first + wide],
                    out.at[me, half, :, first : first + wide],
                    half_sem.at[half, c, slot_of(grid, d, sign)],
                    recv_sem.at[c, me],
                    {"dp": index},
                    MESH,
                )
                copies.append((there, copy))
        for there, copy in copies:
            guarded([there], copy.start)
        return copies

    firsts = first_sends(group, both.at[group])
    swap.wait()
    firsts += first_sends(1 - group, out.at[me, 1 - group])

    def visit(c, r, act):
        order, first, wide = routes[c]
        block, real = origin(me, coords, grid, order, r)
        part = out.at[block, :, :, first : first + wide]

        def run():
            copies = []
            for d, sign in onward(grid, order, r):
                index, there = neighbour(me, coords, grid, d, sign)
                copies.append(
                    (
                        there,
                        pltpu.make_async_remote_copy(
                            part,
                            part,
                            send_sem.at[c, slot_of(grid, d, sign), block],
                            recv_sem.at[c, block],
                            {"dp": index},
                            MESH,
                        ),
                    )
                )
            act(part, recv_sem.at[c, block], copies)

        guarded(real, run)

    def forward_on(part, arrival_sem, copies):
        pltpu.make_async_remote_copy(part, part, swap_sem.at[0], arrival_sem, {"dp": me}, MESH).wait_recv()
        for there, copy in copies:
            guarded([there], copy.start)

    def finish(part, arrival_sem, copies):
        for there, copy in copies:
            guarded([there], copy.wait_send)

    for c, r in events:
        if any(r):
            visit(c, r, forward_on)
    for c, r in events:
        if any(r):
            visit(c, r, finish)
    keep.wait()
    for there, copy in firsts:
        guarded([there], copy.wait_send)


def gather_weights(learn, teach, chips):
    grid = chip_grid(chips)
    rows, width = learn.shape
    return pl.pallas_call(
        functools.partial(gather_kernel, grid),
        name="gather_weights",
        out_shape=jax.ShapeDtypeStruct((chips, 2, rows, width), BF),
        in_specs=[pl.BlockSpec(memory_space=pltpu.VMEM)] * 2,
        out_specs=any_spec(),
        scratch_shapes=[
            pltpu.VMEM((2, rows, width), BF),
            pltpu.SemaphoreType.DMA((3,)),
            pltpu.SemaphoreType.DMA((2, 4, slots_of(grid))),
            pltpu.SemaphoreType.DMA((4, slots_of(grid), chips)),
            pltpu.SemaphoreType.DMA((4, chips)),
        ],
        compiler_params=pltpu.CompilerParams(
            collective_id=1, has_side_effects=True, vmem_limit_bytes=VMEM_LIMIT
        ),
    )(learn, teach)


def sum_peers(group, me, grid):
    plane = grid[1] * grid[2]
    at, level = lax.rem(me, plane), me // plane
    place = (group * plane + at, level)
    sizes = (2 * plane, grid[0])
    peers = []
    for k in range(1, sizes[0]):
        other = lax.rem(place[0] + k, sizes[0])
        peers.append((0, k, (other // plane, level * plane + lax.rem(other, plane))))
    for k in range(1, sizes[1]):
        peers.append((1, k, (group, lax.rem(level + k, sizes[1]) * plane + at)))
    return place, sizes, peers


def sum_stages(place, sizes, peers, total, notes, note_send, note_recv):
    for s, size in enumerate(sizes):
        notes[s, place[s]] = total[...]
        copies = [
            pltpu.make_async_remote_copy(
                notes.at[s, place[s]], notes.at[s, place[s]], note_send.at[s, k], note_recv.at[s, place[s]], device, MESH
            )
            for t, k, device in peers
            if t == s
        ]
        for copy in copies:
            copy.start()
        for k in range(1, size):
            other = lax.rem(place[s] + k, size)
            part = notes.at[s, other]
            pltpu.make_async_remote_copy(
                part, part, note_send.at[s, k], note_recv.at[s, other], peers[0][2], MESH
            ).wait_recv()
        result = notes[s, 0]
        for k in range(1, size):
            result = result + notes[s, k]
        total[...] = result
        for copy in copies:
            copy.wait_send()


def reduce_kernel(
    grid, blocked, small, out, total, acc, heard, notes, load_sem, half_sem, send_sem, recv_sem, note_send, note_recv
):
    group, me = lax.axis_index("group"), lax.axis_index("dp")
    coords = coords_of(me, grid)
    rows, width = out.shape
    routes = lanes_of(width)
    events = route_events(grid, routes)[::-1]
    across = slots_of(grid)
    tall = max([t for t in range(16, 49, 16) if rows % t == 0], default=rows)

    def spot(c, r):
        return tuple(r[routes[c][0].index(d)] for d in range(3))

    firsts = list(dict.fromkeys([spot(c, r) for c, r in events]))
    place, sizes, peers = sum_peers(group, me, grid)
    barrier = pltpu.get_barrier_semaphore()
    for _, _, device in peers:
        pl.semaphore_signal(barrier, 1, device_id=device, device_id_type=MESH)
    pl.semaphore_wait(barrier, len(peers))

    def load(where, act):
        block, real = origin(me, coords, grid, (0, 1, 2), where)
        local = pltpu.make_async_copy(blocked.at[group, block], acc.at[block], load_sem.at[block])
        half = pltpu.make_async_remote_copy(
            blocked.at[1 - group, block],
            heard.at[across, block],
            half_sem.at[0, block],
            half_sem.at[1, block],
            {"group": 1 - group},
            MESH,
        )
        guarded(real, lambda: act(local, half))

    def load_start(local, half):
        half.start()
        local.start()

    def load_wait(local, half):
        local.wait()
        half.wait_recv()

    def load_end(local, half):
        half.wait_send()

    for where in firsts[:AHEAD]:
        load(where, load_start)

    def parent(c, r, block):
        order, first, wide = routes[c]
        i = max([i for i in range(3) if r[i]])
        sign = 1 if r[i] > 0 else -1
        index, _ = neighbour(me, coords, grid, order[i], -sign)
        slot = slot_of(grid, order[i], sign)
        return pltpu.make_async_remote_copy(
            acc.at[block, :, first : first + wide],
            heard.at[slot, block, :, first : first + wide],
            send_sem.at[c, block],
            recv_sem.at[c, slot, block],
            {"dp": index},
            MESH,
        )

    def visit(c, r):
        order, first, wide = routes[c]
        block, real = origin(me, coords, grid, order, r)

        def run():
            children = [(slot_of(grid, d, s), neighbour(me, coords, grid, d, s)[1]) for d, s in onward(grid, order, r)]
            for slot, there in children:
                part = heard.at[slot, block, :, first : first + wide]
                arrival = pltpu.make_async_remote_copy(
                    part, part, send_sem.at[c, block], recv_sem.at[c, slot, block], {"dp": me}, MESH
                )
                guarded([there], arrival.wait_recv)
            sure = [across] + [slot for slot, there in children if there is None]

            def add(slots, source, target):
                def piece(k, carry):
                    at = (pl.ds(pl.multiple_of(k * tall, tall), tall), slice(first, first + wide))
                    total = source[at].astype(F32)
                    for slot in slots:
                        total = total + heard[(slot, block) + at].astype(F32)
                    target[at] = total.astype(target.dtype)
                    return carry

                lax.fori_loop(0, rows // tall, piece, 0)

            target = acc.at[block] if any(r) else out
            add(sure, acc.at[block], target)
            for slot, there in children:
                if there is not None:
                    pl.when(there)(functools.partial(add, [slot], target, target))
            if any(r):
                parent(c, r, block).start()

        guarded(real, run)

    ready = set()
    for c, r in events:
        if spot(c, r) not in ready:
            ready.add(spot(c, r))
            load(spot(c, r), load_wait)
            for where in firsts[len(ready) + AHEAD - 1 : len(ready) + AHEAD]:
                load(where, load_start)
        visit(c, r)
    def squares(k, carry):
        part = out[pl.ds(pl.multiple_of(k * tall, tall), tall), :]
        return carry + jnp.sum(part * part, axis=0, keepdims=True)

    square = lax.fori_loop(0, rows // tall, squares, jnp.zeros((1, width), F32))
    row_id = lax.broadcasted_iota(jnp.int32, total.shape, 0)
    total[...] = jnp.where(row_id == 5, square, small[...])
    sum_stages(place, sizes, peers, total, notes, note_send, note_recv)
    for c, r in events:
        if any(r):
            block, real = origin(me, coords, grid, routes[c][0], r)
            guarded(real, parent(c, r, block).wait_send)
    for where in firsts:
        load(where, load_end)


def reduce_grads(blocked, small, chips):
    grid = chip_grid(chips)
    _, _, rows, width = blocked.shape
    most = max(grid[0], 2 * grid[1] * grid[2])
    return pl.pallas_call(
        functools.partial(reduce_kernel, grid),
        name="reduce_grads",
        out_shape=(jax.ShapeDtypeStruct((rows, width), F32), jax.ShapeDtypeStruct(small.shape, F32)),
        in_specs=[any_spec(), pl.BlockSpec(memory_space=pltpu.VMEM)],
        out_specs=(pl.BlockSpec(memory_space=pltpu.VMEM),) * 2,
        scratch_shapes=[
            pltpu.VMEM((chips, rows, width), BF),
            pltpu.VMEM((slots_of(grid) + 1, chips, rows, width), BF),
            pltpu.VMEM((2, most) + small.shape, F32),
            pltpu.SemaphoreType.DMA((chips,)),
            pltpu.SemaphoreType.DMA((2, chips)),
            pltpu.SemaphoreType.DMA((4, chips)),
            pltpu.SemaphoreType.DMA((4, slots_of(grid), chips)),
            pltpu.SemaphoreType.DMA((2, most)),
            pltpu.SemaphoreType.DMA((2, most)),
        ],
        compiler_params=pltpu.CompilerParams(
            collective_id=2, has_side_effects=True, vmem_limit_bytes=VMEM_LIMIT
        ),
    )(blocked, small)


def exchange_kernel(*refs):
    count = (len(refs) - 7) // 2
    bank, states, banks = refs[count], refs[count + 1 : 2 * count + 1], refs[2 * count + 1]
    state_send, state_recv, send_sem, recv_sem, own_sem = refs[2 * count + 2 :]
    group, me = lax.axis_index("group"), lax.axis_index("dp")
    chips = banks.shape[0]
    barrier = pltpu.get_barrier_semaphore()

    def hail(target):
        def one(k, carry):
            pl.semaphore_signal(barrier, 1, device_id=(target, lax.rem(me + k, chips)), device_id_type=MESH)
            return carry

        return one

    @pl.when(group == 0)
    def _():
        lax.fori_loop(1, chips, hail(0), 0)
        lax.fori_loop(0, chips, hail(1), 0)

    @pl.when(group == 1)
    def _():
        lax.fori_loop(0, chips, hail(0), 0)

    pl.semaphore_wait(barrier, chips + (1 - group) * (chips - 1))

    def crossing(k):
        ref = states[k]
        if k == count - 1:
            part = ref.at[1]
        elif len(ref.shape) == 3 and ref.shape[0] == 3:
            part = ref.at[:, : ref.shape[1] // MICRO_BATCHES, :]
        else:
            part = ref.at[0]
        return pltpu.make_async_remote_copy(
            part, part, state_send.at[k], state_recv.at[k], {"group": 1 - group}, MESH
        )

    def note(core, k):
        return pltpu.make_async_remote_copy(
            bank.at[core],
            banks.at[me],
            send_sem.at[core, k],
            recv_sem.at[me],
            (core, lax.rem(me + k, chips)),
            MESH,
        )

    def each(core, act):
        def one(k, carry):
            act(note(core, k))
            return carry

        return one

    def take(k, carry):
        pltpu.make_async_remote_copy(
            bank.at[0], banks.at[k], send_sem.at[0, 0], recv_sem.at[k], (1 - group, me), MESH
        ).wait_recv()
        return carry

    @pl.when(group == 0)
    def _():
        own = pltpu.make_async_copy(bank.at[0], banks.at[me], own_sem)
        own.start()
        lax.fori_loop(1, chips, each(0, lambda copy: copy.start()), 0)
        lax.fori_loop(0, chips, each(1, lambda copy: copy.start()), 0)
        targets = crossing(count - 1)
        targets.start()
        own.wait()
        lax.fori_loop(1, chips, lambda k, carry: take(lax.rem(me + k, chips), carry), 0)
        for k in range(count - 1):
            crossing(k).wait_recv()
        lax.fori_loop(1, chips, each(0, lambda copy: copy.wait_send()), 0)
        lax.fori_loop(0, chips, each(1, lambda copy: copy.wait_send()), 0)
        targets.wait_send()

    @pl.when(group == 1)
    def _():
        copies = [crossing(k) for k in range(count - 1)]
        for copy in copies:
            copy.start()
        lax.fori_loop(0, chips, take, 0)
        crossing(count - 1).wait_recv()
        for copy in copies:
            copy.wait_send()


def exchange_states(states, bank, chips):
    count = len(states)
    outs = pl.pallas_call(
        exchange_kernel,
        name="exchange_states",
        out_shape=tuple(jax.ShapeDtypeStruct(a.shape, a.dtype) for a in states)
        + (jax.ShapeDtypeStruct((chips,) + bank.shape[1:], BF),),
        in_specs=[any_spec()] * (count + 1),
        out_specs=(any_spec(),) * (count + 1),
        scratch_shapes=[
            pltpu.SemaphoreType.DMA((count,)),
            pltpu.SemaphoreType.DMA((count,)),
            pltpu.SemaphoreType.DMA((2, chips)),
            pltpu.SemaphoreType.DMA((chips,)),
            pltpu.SemaphoreType.DMA,
        ],
        input_output_aliases={k: k for k in range(count)},
        compiler_params=pltpu.CompilerParams(collective_id=3, has_side_effects=True),
    )(*states, bank)
    return outs[:-1], outs[-1]


def place_kernel(spots, model, out, rows_scr, inbuf, stage, outbuf, in_sem, out_sem):
    chips, cores, rows, width = model.shape
    blocks = cores * chips
    cols = width // LANES
    deep, wide = inbuf.shape[0], outbuf.shape[0]
    group = max([g for g in range(1, 17) if rows % g == 0])

    def fetch(b, slot):
        return pltpu.make_async_copy(model.at[lax.rem(b, chips), b // chips], inbuf.at[slot], in_sem.at[slot])

    for b in range(deep - 1):
        fetch(b, b).start()

    def block(b, carry):
        slot = lax.rem(b, deep)
        fetch(b, slot).wait()

        @pl.when(b + deep - 1 < blocks)
        def _():
            fetch(b + deep - 1, lax.rem(b + deep - 1, deep)).start()

        for c in range(cols):
            stage[pl.ds(c, rows, stride=SUBLANES), :] = inbuf[slot, :, c * LANES : (c + 1) * LANES].astype(F32)

        def move(q, carry):
            first = q * group
            to = [spots[b * rows + first + j] for j in range(group)]
            held = [stage[pl.ds(pl.multiple_of((first + j) * SUBLANES, SUBLANES), SUBLANES), :] for j in range(group)]
            for j in range(group):
                rows_scr[pl.ds(to[j], SUBLANES, stride=SUBLANES), :] = held[j]
            return carry

        return lax.fori_loop(0, rows // group, move, carry)

    lax.fori_loop(0, blocks, block, 0)
    pieces = out.shape[0]
    for u in range(pieces):
        slot = u % wide
        if u >= wide:
            pltpu.make_async_copy(outbuf.at[slot], out.at[u - wide], out_sem.at[slot]).wait()

        def pack(k, carry):
            to = pl.ds(pl.multiple_of(k * 16, 16), 16)
            for c in range(cols):
                first = (u * width // SUBLANES + 2 * k) * TILE + c * SUBLANES
                halves = [rows_scr[pl.ds(pl.multiple_of(first + TILE * h, SUBLANES), SUBLANES), :] for h in range(2)]
                outbuf[slot, to, c * LANES : (c + 1) * LANES] = jnp.concatenate(halves, axis=0).astype(BF)
            return carry

        lax.fori_loop(0, width // 16, pack, 0)
        pltpu.make_async_copy(outbuf.at[slot], out.at[u], out_sem.at[slot]).start()
    for u in range(pieces - wide, pieces):
        pltpu.make_async_copy(outbuf.at[u % wide], out.at[u], out_sem.at[u % wide]).wait()


def place_weights(spots, model):
    _, _, rows, width = model.shape
    total = spots.shape[0]
    return pl.pallas_call(
        place_kernel,
        name="place_weights",
        out_shape=jax.ShapeDtypeStruct((total // width, width, width), BF),
        in_specs=[smem_spec(), any_spec()],
        out_specs=any_spec(),
        scratch_shapes=[
            pltpu.VMEM((total * SUBLANES, LANES), F32),
            pltpu.VMEM((8, rows, width), BF),
            pltpu.VMEM((rows * SUBLANES, LANES), F32),
            pltpu.VMEM((4, width, width), BF),
            pltpu.SemaphoreType.DMA((8,)),
            pltpu.SemaphoreType.DMA((4,)),
        ],
        compiler_params=pltpu.CompilerParams(vmem_limit_bytes=VMEM_LIMIT),
    )(spots, model)


def layer_stats(tensor):
    centre = tensor - jnp.mean(tensor, axis=-1, keepdims=True)
    scaled = lax.rsqrt(jnp.mean(centre * centre, axis=-1, keepdims=True) + 1e-06)
    return centre * scaled, scaled


def column_of(row):
    n = row.shape[1]
    eye = lax.broadcasted_iota(jnp.int32, (n, n), 0) == lax.broadcasted_iota(jnp.int32, (n, n), 1)
    return jnp.sum(jnp.where(eye, row, 0), axis=1, keepdims=True)


def flag_column(pos, slots):
    hit = lax.broadcasted_iota(jnp.int32, (slots, pos.shape[1]), 0) == pos
    return jnp.max(jnp.where(hit, 1, 0), axis=1, keepdims=True)


def fill_bias(bias, seg_col, seg_row):
    bias[...] = jnp.where(seg_col == seg_row, 0.0, MASK_FILL)


def half(x, h):
    low = lax.broadcasted_iota(jnp.int32, (1, LANES), 1) < HEAD_DIM
    keep = low if h == 0 else jnp.logical_not(low)
    return jnp.where(keep, x, jnp.zeros_like(x))


def fwd_kernel(
    patch, seg, pos, gains, teacher_gains, w_hbm,
    e_out, qkv_out, lse_out, o_out, x1_out, x2_out, tgt_out, bank_out,
    w, bias, gain, a2, e_v, qkv, lse, o_v, x1_v, x2_v, tgt, bank, sem, out_sem,
):
    i = pl.program_id(0)
    role = lax.axis_index("group")
    gain[...] = jnp.where(role == 0, teacher_gains[...], gains[...])
    batches, slots, width = e_out.shape
    pieces = w_hbm.shape[0]
    cuts = (pieces - 6) // 2
    order = [0, 3, 4, 5, 1]
    for j in range(cuts):
        order += [6 + j, 6 + cuts + j]

    def bring(which):
        @pl.when(i == 0)
        def _():
            for u in which:
                pltpu.make_async_copy(w_hbm.at[u], w.at[u], sem.at[u]).start()

    def need(u):
        @pl.when(i == 0)
        def _():
            pltpu.make_async_copy(w_hbm.at[u], w.at[u], sem.at[u]).wait()

    bring(order[:2])

    def leave(k, b):
        tokens = pl.ds(pl.multiple_of(b * slots, slots), slots)
        source, target = [
            (e_v.at[b], e_out.at[b]),
            (qkv.at[b], qkv_out.at[:, tokens, :]),
            (lse.at[b], lse_out.at[b]),
            (o_v.at[b], o_out.at[b]),
            (x1_v.at[b], x1_out.at[b]),
            (x2_v.at[b], x2_out.at[b]),
            (tgt.at[b], tgt_out.at[b]),
            (bank.at[b], bank_out.at[b]),
        ][k]
        return pltpu.make_async_copy(source, target, out_sem.at[b, k])

    seg_row = seg[0]
    seg_col = column_of(seg_row)
    fill_bias(bias, seg_col, seg_row)
    flags = flag_column(pos[0], slots) * role
    need(0)
    bring(order[2:])
    e = nn(patch[0], w[0])
    e = jnp.where(flags > 0, gain[3:4, :], e)
    e_v[i] = e
    leave(0, i).start()
    a2[...] = (layer_stats(e)[0] * gain[0:1, :]).astype(BF)

    def project(j, carry):
        need(3 + j)
        qkv[i, j] = nn(a2[...], w[3 + j]).astype(BF)
        return carry

    lax.fori_loop(0, 3, project, 0)
    leave(1, i).start()

    def pair(p, carry):
        cs = pl.ds(pl.multiple_of(p * LANES, LANES), LANES)
        q2, k2, v2 = qkv[i, 0, :, cs], qkv[i, 1, :, cs], qkv[i, 2, :, cs]
        k2 = k2 * jnp.asarray(HEAD_DIM**-0.5, BF)
        v_t = v2.T
        outs = []
        for h in range(2):
            s = nt(half(k2, h), q2) + bias[...]
            top = jnp.max(s, axis=0, keepdims=True)
            ex = jnp.exp(s - top)
            total = jnp.sum(ex, axis=0, keepdims=True)
            lse[i, pl.ds(2 * p + h, 1), :] = top + jnp.log(total)
            probs = (ex * (1.0 / total)).astype(BF)
            outs.append(nn(v_t[h * HEAD_DIM : (h + 1) * HEAD_DIM, :], probs))
        o_v[i, :, cs] = jnp.concatenate(outs, axis=0).T.astype(BF)
        return carry

    lax.fori_loop(0, HEADS // 2, pair, 0)
    leave(2, i).start()
    leave(3, i).start()
    need(1)
    x1 = e_v[i] + nn(o_v[i], w[1])
    x1_v[i] = x1
    leave(4, i).start()
    a2[...] = (layer_stats(x1)[0] * gain[1:2, :]).astype(BF)
    x2_v[i] = x1

    def ffn(j, carry):
        need(6 + j)
        hid = nn(a2[...], w[6 + j])
        act = (hid * (0.5 * (1.0 + jnp.tanh(GELU_A * (hid + GELU_B * hid * hid * hid))))).astype(BF)
        need(6 + cuts + j)
        x2_v[i] += nn(act, w[6 + cuts + j])
        return carry

    lax.fori_loop(0, cuts, ffn, 0)
    leave(5, i).start()

    @pl.when(role == 0)
    def _():
        t = layer_stats(x2_v[i])[0].astype(BF)
        tgt[i] = t
        leave(6, i).start()
        t = t.astype(F32)
        for m in range(IMGS):
            inside = seg_col == m
            size = jnp.sum(jnp.where(inside, 1.0, 0.0), axis=0, keepdims=True)
            pooled = jnp.sum(jnp.where(inside, t, 0.0), axis=0, keepdims=True) / size
            unit = pooled * lax.rsqrt(jnp.sum(pooled * pooled, axis=-1, keepdims=True) + 1e-06)
            bank[i, m : m + 1, :] = unit.astype(BF)
        leave(7, i).start()

    @pl.when(i == batches - 1)
    def _():
        for b in range(batches):
            for k in range(6):
                leave(k, b).wait()

        @pl.when(role == 0)
        def _():
            for b in range(batches):
                leave(6, b).wait()
                leave(7, b).wait()


def forward(patch, seg, pos, gains, teacher_gains, w):
    batches, slots, width = patch.shape
    pieces = w.shape[0]
    tok = lambda n, dt: ((batches,) + ((3,) if n == 3 else ()) + (slots, width), dt)
    kinds = [
        tok(1, F32),
        tok(3, BF),
        ((batches, HEADS, slots), F32),
        tok(1, BF),
        tok(1, F32),
        tok(1, F32),
        tok(1, BF),
        ((batches, IMGS, width), BF),
    ]
    outs = [jax.ShapeDtypeStruct(shape, dt) for shape, dt in kinds]
    outs[1] = jax.ShapeDtypeStruct((3, batches * slots, width), BF)
    return pl.pallas_call(
        fwd_kernel,
        name="forward",
        grid=(batches,),
        out_shape=tuple(outs),
        in_specs=[
            pl.BlockSpec((1, slots, width), lambda i: (i, 0, 0)),
            pl.BlockSpec((1, 1, slots), lambda i: (i, 0, 0)),
            pl.BlockSpec((1, 1, pos.shape[2]), lambda i: (i, 0, 0)),
            pl.BlockSpec((4, width), lambda i: (0, 0)),
            pl.BlockSpec((4, width), lambda i: (0, 0)),
            any_spec(),
        ],
        out_specs=(any_spec(),) * len(outs),
        scratch_shapes=[
            pltpu.VMEM((pieces, width, width), BF),
            pltpu.VMEM((slots, slots), F32),
            pltpu.VMEM((4, width), F32),
            pltpu.VMEM((slots, width), BF),
        ]
        + [pltpu.VMEM(shape, dt) for shape, dt in kinds]
        + [
            pltpu.SemaphoreType.DMA((pieces,)),
            pltpu.SemaphoreType.DMA((batches, len(kinds))),
        ],
        compiler_params=pltpu.CompilerParams(vmem_limit_bytes=VMEM_LIMIT),
        cost_estimate=pl.CostEstimate(
            flops=2 * batches * slots * width * width * pieces, bytes_accessed=2 * w.size, transcendentals=0
        ),
    )(patch, seg, pos, gains, teacher_gains, w)


def norm_back(grad_out, normed, scaled, gain_vec):
    grad_hat = grad_out * gain_vec
    inner = jnp.mean(grad_hat * normed, axis=-1, keepdims=True)
    grad_in = scaled * (grad_hat - jnp.mean(grad_hat, axis=-1, keepdims=True) - normed * inner)
    return grad_in, jnp.sum(grad_out * normed, axis=0, keepdims=True)


def bwd_kernel(
    seg, pos, gain, lse, banks, e_hbm, qkv_hbm, x1_hbm, x2_hbm, tgt_hbm, w_own, w_far,
    head_out, attn_out, ffn_out, act_out, de_out, mid_out, pred_out, dqkv_out, du_out, down_out, small,
    w, bias, top_scr, acc_scr, pool_scr, bank_scr, e_in, qkv, x1_in, x2_in, tgt,
    head_v, attn_v, ffn_v, act_v, de_v, mid_v, pred_v, dqkv, du_v, down_v, sem, in_sem, out_sem,
):
    role, chip = lax.axis_index("group"), lax.axis_index("dp")
    slots, width = e_in.shape
    chips = banks.shape[0]
    pieces = w_own.shape[0]
    cuts = (pieces - 6) // 2
    tokens = pl.ds(pl.multiple_of(role * slots, slots), slots)

    def bring(k, source, target):
        copy = pltpu.make_async_copy(source, target, in_sem.at[k])
        copy.start()
        return copy

    def bring_piece(u):
        @pl.when(role == 0)
        def _():
            pltpu.make_async_copy(w_far.at[u], w.at[u - 1], sem.at[u]).start()

        @pl.when(role != 0)
        def _():
            pltpu.make_async_copy(w_own.at[u], w.at[u - 1], sem.at[u]).start()

    def need(u):
        pltpu.make_async_copy(w_own.at[u], w.at[u - 1], sem.at[u]).wait()

    taken = []

    def keep(source, target):
        copy = pltpu.make_async_copy(source, target, out_sem.at[len(taken)])
        copy.start()
        taken.append(copy)

    x2_copy = bring(0, x2_hbm.at[role], x2_in)
    bring_piece(2)
    tgt_copy = bring(1, tgt_hbm.at[role], tgt)
    small[...] = jnp.zeros_like(small)

    seg_row = seg[role]
    seg_col = column_of(seg_row)
    fill_bias(bias, seg_col, seg_row)
    flags = flag_column(pos[role], slots)
    x2_copy.wait()
    x1_copy = bring(2, x1_hbm.at[role], x1_in)
    for j in range(cuts):
        bring_piece(6 + cuts + j)
        bring_piece(6 + j)
    bring_piece(1)
    qkv_copy = bring(3, qkv_hbm.at[:, tokens, :], qkv)
    for j in range(3):
        bring_piece(3 + j)
    e_copy = bring(4, e_hbm.at[role], e_in)
    n3, r3 = layer_stats(x2_in[...])
    head_in = (n3 * gain[2:3, :]).astype(BF)
    head_v[...] = head_in
    keep(head_v, head_out.at[0])
    need(2)
    pred = nn(head_in, w[1])
    valid = jnp.where(seg_col < IMGS, flags, 0).astype(F32)
    tgt_copy.wait()
    diff = pred - tgt[...].astype(F32)
    size = jnp.abs(diff)
    huber = jnp.where(size < 1.0, 0.5 * diff * diff, size - 0.5)
    regress = jnp.sum(jnp.sum(valid * huber, axis=1, keepdims=True), axis=0, keepdims=True)
    count = float(MASKED * chips * MICRO_BATCHES * width)
    grad_pred = valid * (jnp.clip(diff, -1.0, 1.0) / count)
    pool_scr[...] = jnp.zeros_like(pool_scr)
    for m in range(IMGS):
        inside = seg_col == m
        tally = jnp.sum(jnp.where(inside, 1.0, 0.0), axis=0, keepdims=True)
        pool_scr[m : m + 1, :] = jnp.sum(jnp.where(inside, pred, 0.0), axis=0, keepdims=True) / tally
    pooled = pool_scr[...]
    length = lax.rsqrt(jnp.sum(pooled * pooled, axis=-1, keepdims=True) + 1e-06)
    unit = pooled * length
    for k in range(chips):
        bank_scr[k * IMGS : (k + 1) * IMGS, :] = banks[k].astype(F32)
    memory = bank_scr[...].astype(BF)
    choices = memory.shape[0]
    logits = nt(unit.astype(BF), memory) / SOFTMAX_TEMPER
    row_id = lax.broadcasted_iota(jnp.int32, logits.shape, 0)
    real = row_id < IMGS
    picked = jnp.where(
        real & (lax.broadcasted_iota(jnp.int32, logits.shape, 1) == chip * IMGS + row_id), 1.0, 0.0
    )
    peak = jnp.max(logits, axis=-1, keepdims=True)
    ex = jnp.exp(logits - peak)
    total = jnp.sum(ex, axis=-1, keepdims=True)
    each = peak + jnp.log(total) - jnp.sum(logits * picked, axis=-1, keepdims=True)
    contrast = jnp.sum(jnp.where(real[:, 0:1], each, 0.0), axis=0, keepdims=True)
    scale = choices * MICRO_BATCHES
    grad_logits = (jnp.where(real, ex / total - picked, 0.0) / scale / SOFTMAX_TEMPER).astype(BF)
    grad_unit = nn(grad_logits, memory)
    grad_pool = length * (grad_unit - unit * jnp.sum(grad_unit * unit, axis=1, keepdims=True))
    pool_scr[...] = grad_pool
    for m in range(IMGS):
        inside = seg_col == m
        tally = jnp.sum(jnp.where(inside, 1.0, 0.0), axis=0, keepdims=True)
        grad_pred = grad_pred + jnp.where(inside, pool_scr[m : m + 1, :] / tally, 0.0)
    low = grad_pred.astype(BF)
    pred_v[...] = low
    keep(pred_v, pred_out.at[0])
    loss = regress / count + contrast / scale
    small[4:5, :] += jnp.broadcast_to(loss, (1, width))
    grad_top, gain_three = norm_back(nt(low, w[1]), n3, r3, gain[2:3, :])
    small[2:3, :] += gain_three
    top_scr[...] = grad_top
    down = grad_top.astype(BF)
    down_v[...] = down
    keep(down_v, down_out.at[0])
    x1_copy.wait()
    n2, r2 = layer_stats(x1_in[...])
    ffn_in = (n2 * gain[1:2, :]).astype(BF)
    ffn_v[...] = ffn_in
    keep(ffn_v, ffn_out.at[0])
    acc_scr[...] = jnp.zeros_like(acc_scr)
    loop_sem = len(taken)

    def leave(j):
        return (
            pltpu.make_async_copy(act_v.at[j], act_out.at[j], out_sem.at[loop_sem + 2 * j]),
            pltpu.make_async_copy(du_v.at[j], du_out.at[j], out_sem.at[loop_sem + 2 * j + 1]),
        )

    def ffn(j, carry):
        need(6 + cuts + j)
        grad_act = nt(down_v[...], w[5 + cuts + j])
        need(6 + j)
        hid = nn(ffn_v[...], w[5 + j])
        th = jnp.tanh(GELU_A * (hid + GELU_B * hid * hid * hid))
        cdf = 0.5 * (1.0 + th)
        act_v[j] = (hid * cdf).astype(BF)
        slope = cdf + hid * (0.5 * (1.0 - th * th)) * (GELU_A * (1.0 + 3.0 * GELU_B * hid * hid))
        du = (grad_act * slope).astype(BF)
        du_v[j] = du
        for copy in leave(j):
            copy.start()
        acc_scr[...] += nt(du, w[5 + j])
        return carry

    lax.fori_loop(0, cuts, ffn, 0)
    for j in range(cuts):
        taken.extend(leave(j))
    grad_ffn, gain_two = norm_back(acc_scr[...], n2, r2, gain[1:2, :])
    small[1:2, :] += gain_two
    mid = top_scr[...] + grad_ffn
    top_scr[...] = mid
    mid_low = mid.astype(BF)
    mid_v[...] = mid_low
    keep(mid_v, mid_out.at[0])
    need(1)
    de_v[...] = nt(mid_low, w[0]).astype(BF)
    qkv_copy.wait()

    def pair(p, carry):
        cs = pl.ds(pl.multiple_of(p * LANES, LANES), LANES)
        q2, k2, v2, g2 = qkv[0, :, cs], qkv[1, :, cs], qkv[2, :, cs], de_v[:, cs]
        k_scaled = k2 * jnp.asarray(HEAD_DIM**-0.5, BF)
        k_t = k2.T
        dq, dk, dv = [], 0.0, 0.0
        for h in range(2):
            s = nt(half(k_scaled, h), q2) + bias[...]
            probs = jnp.exp(s - lse[role, pl.ds(2 * p + h, 1), :])
            dp = nt(half(v2, h), g2)
            centre = jnp.sum(probs * dp, axis=0, keepdims=True)
            ds = (probs * (dp - centre)).astype(BF)
            dv = dv + nn(probs.astype(BF), half(g2, h))
            dk = dk + nn(ds, half(q2, h))
            dq.append(nn(k_t[h * HEAD_DIM : (h + 1) * HEAD_DIM, :], ds))
        dqkv[0, :, cs] = (jnp.concatenate(dq, axis=0) * HEAD_DIM**-0.5).T.astype(BF)
        dqkv[1, :, cs] = (dk * HEAD_DIM**-0.5).astype(BF)
        dqkv[2, :, cs] = dv.astype(BF)
        return carry

    lax.fori_loop(0, HEADS // 2, pair, 0)
    keep(dqkv, dqkv_out)
    acc_scr[...] = jnp.zeros_like(acc_scr)

    def project(j, carry):
        need(3 + j)
        acc_scr[...] += nt(dqkv[j], w[2 + j])
        return carry

    lax.fori_loop(0, 3, project, 0)
    e_copy.wait()
    n1, r1 = layer_stats(e_in[...])
    attn_v[...] = (n1 * gain[0:1, :]).astype(BF)
    keep(attn_v, attn_out.at[0])
    grad_attn, gain_one = norm_back(acc_scr[...], n1, r1, gain[0:1, :])
    small[0:1, :] += gain_one
    start = top_scr[...] + grad_attn
    hidden_slot = flags > 0
    small[3:4, :] += jnp.sum(jnp.where(hidden_slot, start, 0.0), axis=0, keepdims=True)
    de_v[...] = jnp.where(hidden_slot, 0.0, start).astype(BF)
    keep(de_v, de_out.at[0])
    for copy in taken:
        copy.wait()


def backward(seg, pos, gain, lse, banks, e, qkv, x1, x2, tgt, w_own, w_far):
    _, slots, width = e.shape
    pieces = w_own.shape[0]
    cuts = (pieces - 6) // 2
    counts = (1, 1, 1, cuts, 1, 1, 1, 3, cuts, 1)
    vmem = pl.BlockSpec(memory_space=pltpu.VMEM)
    tok = lambda n, dt: pltpu.VMEM((n, slots, width) if n > 1 else (slots, width), dt)
    return pl.pallas_call(
        bwd_kernel,
        name="backward",
        out_shape=tuple(jax.ShapeDtypeStruct((n, slots, width), BF) for n in counts)
        + (jax.ShapeDtypeStruct((SUBLANES, width), F32),),
        in_specs=[vmem] * 5 + [any_spec()] * 7,
        out_specs=(any_spec(),) * len(counts) + (vmem,),
        scratch_shapes=[
            pltpu.VMEM((pieces - 1, width, width), BF),
            pltpu.VMEM((slots, slots), F32),
            pltpu.VMEM((slots, width), F32),
            pltpu.VMEM((slots, width), F32),
            pltpu.VMEM((SUBLANES, width), F32),
            pltpu.VMEM((banks.shape[0] * IMGS, width), F32),
            tok(1, F32),
            tok(3, BF),
            tok(1, F32),
            tok(1, F32),
            tok(1, BF),
        ]
        + [tok(n, BF) for n in counts]
        + [
            pltpu.SemaphoreType.DMA((pieces,)),
            pltpu.SemaphoreType.DMA((5,)),
            pltpu.SemaphoreType.DMA((sum(counts),)),
        ],
        compiler_params=pltpu.CompilerParams(vmem_limit_bytes=VMEM_LIMIT),
    )(seg, pos, gain, lse, banks, e, qkv, x1, x2, tgt, w_own, w_far)


def grads_kernel(
    plan, places, patch, mixed, head, attn, ffn, act, de, mid, pred, dqkv, du, down, out,
    rows_scr, x_buf, x_t, g_buf, stage, outbuf, x_sem, g_sem, out_sem,
):
    blocks, rows, width = out.shape
    cols = width // LANES
    deep, wide_out = x_buf.shape[0], outbuf.shape[0]
    group = max([g for g in range(SUBLANES, 49, SUBLANES) if rows % g == 0], default=rows)
    lefts = {"patch": patch, "mixed": mixed, "head": head, "attn": attn, "ffn": ffn, "act": act}
    rights = {"de": de, "mid": mid, "pred": pred, "dqkv": dqkv, "du": du, "down": down}

    def left_of(key):
        name, index = key
        return lefts[name].at[lax.axis_index("group") if name in ("patch", "mixed") else index]

    lcopies, rcopies = [], []
    lkeys, rkeys = [], []
    steps = []
    for u, (left, right) in enumerate(plan):
        if not lkeys or lkeys[-1] != left:
            slot = len(lkeys) % deep
            lcopies.append(pltpu.make_async_copy(left_of(left), x_buf.at[slot], x_sem.at[slot]))
            lkeys.append(left)
            fresh_l = True
        else:
            fresh_l = False
        if not rkeys or rkeys[-1] != right:
            slot = len(rkeys) % deep
            rcopies.append(pltpu.make_async_copy(rights[right[0]].at[right[1]], g_buf.at[slot], g_sem.at[slot]))
            rkeys.append(right)
            fresh_r = True
        else:
            fresh_r = False
        steps.append((u, len(lkeys) - 1, fresh_l, len(rkeys) - 1, fresh_r))
    for copy in lcopies[: deep - 1] + rcopies[: deep - 1]:
        copy.start()
    for u, li, fresh_l, ri, fresh_r in steps:
        if fresh_l:
            lcopies[li].wait()
            if li + deep - 1 < len(lcopies):
                lcopies[li + deep - 1].start()
            x_t[...] = x_buf[li % deep].T
        if fresh_r:
            rcopies[ri].wait()
            if ri + deep - 1 < len(rcopies):
                rcopies[ri + deep - 1].start()
        wide = 2 * LANES

        def tile(n, carry):
            part = nn(x_t[...], g_buf[ri % deep, :, pl.ds(pl.multiple_of(n * wide, wide), wide)])
            for c in range(2):
                rows_scr[pl.ds(u * width * SUBLANES + 2 * n + c, width, stride=SUBLANES), :] = part[
                    :, c * LANES : (c + 1) * LANES
                ]
            return carry

        lax.fori_loop(0, width // wide, tile, 0)

    def block(b, carry):
        slot = lax.rem(b, wide_out)

        def move(q, carry):
            came = [pl.multiple_of(places[b * rows + q * group + j] * SUBLANES, SUBLANES) for j in range(group)]
            held = [rows_scr[pl.ds(first, SUBLANES), :] for first in came]
            for j in range(group):
                to = q * (group // SUBLANES) * TILE + j // SUBLANES * TILE + j % SUBLANES
                stage[pl.ds(to, SUBLANES, stride=SUBLANES), :] = held[j]
            return carry

        lax.fori_loop(0, rows // group, move, 0)

        @pl.when(b >= wide_out)
        def _():
            pltpu.make_async_copy(outbuf.at[slot], out.at[b - wide_out], out_sem.at[slot]).wait()

        for first in range(0, rows, 16):
            tall = min(16, rows - first)
            for c in range(cols):
                at = first * SUBLANES + c * SUBLANES
                both = jnp.concatenate([stage[at : at + SUBLANES, :], stage[at + TILE : at + TILE + SUBLANES, :]], 0)
                outbuf[slot, first : first + tall, c * LANES : (c + 1) * LANES] = both[:tall].astype(BF)
        pltpu.make_async_copy(outbuf.at[slot], out.at[b], out_sem.at[slot]).start()
        return carry

    lax.fori_loop(0, blocks, block, 0)
    for b in range(blocks - wide_out, blocks):
        pltpu.make_async_copy(outbuf.at[b % wide_out], out.at[b], out_sem.at[b % wide_out]).wait()


def weight_grads(places, lefts, rights, blocks):
    tokens, width = lefts[0].shape[1:]
    cuts = lefts[-1].shape[0]
    total = places.shape[0]
    rows = total // blocks
    plan = (
        [(("patch", 0), ("de", 0)), (("mixed", 0), ("mid", 0)), (("head", 0), ("pred", 0))]
        + [(("attn", 0), ("dqkv", j)) for j in range(3)]
        + [(("ffn", 0), ("du", j)) for j in range(cuts)]
        + [(("act", j), ("down", 0)) for j in range(cuts)]
    )
    return pl.pallas_call(
        functools.partial(grads_kernel, plan),
        name="weight_grads",
        out_shape=jax.ShapeDtypeStruct((blocks, rows, width), BF),
        in_specs=[smem_spec()] + [any_spec()] * 12,
        out_specs=any_spec(),
        scratch_shapes=[
            pltpu.VMEM((total * SUBLANES, LANES), F32),
            pltpu.VMEM((4, tokens, width), BF),
            pltpu.VMEM((width, tokens), BF),
            pltpu.VMEM((4, tokens, width), BF),
            pltpu.VMEM((pl.cdiv(rows, 16) * 2 * TILE, LANES), F32),
            pltpu.VMEM((4, rows, width), BF),
            pltpu.SemaphoreType.DMA((4,)),
            pltpu.SemaphoreType.DMA((4,)),
            pltpu.SemaphoreType.DMA((4,)),
        ],
        compiler_params=pltpu.CompilerParams(vmem_limit_bytes=VMEM_LIMIT),
    )(places, *lefts, *rights)


def power_of(base, exponent):
    return lax.fori_loop(0, exponent, lambda _, product: product * base, jnp.float32(1.0))


def update_kernel(
    step, total, gains, gone, gtwo, grad, master, one, two, teacher,
    loss_out, norm_out, one_out, two_out, master_out, teacher_out, gone_out, gtwo_out,
):
    gain_grad = total[0:4, :]
    square = jnp.sum(total[5:6, :], axis=1, keepdims=True)
    square = square + jnp.sum(jnp.sum(gain_grad * gain_grad, axis=1, keepdims=True), axis=0, keepdims=True)
    norm = jnp.sqrt(square)
    factor = jnp.minimum(1.0, CLIP / norm)
    fix_one = 1.0 - power_of(BETA_ONE, step[0])
    fix_two = 1.0 - power_of(BETA_TWO, step[0])

    def moments(first, second, gradient):
        first = BETA_ONE * first + (1.0 - BETA_ONE) * gradient
        second = BETA_TWO * second + (1.0 - BETA_TWO) * gradient * gradient
        return first, second

    @pl.when(pl.program_id(0) == 0)
    def _():
        loss_out[0] = jnp.sum(total[4:5, 0:1])
        norm_out[0] = jnp.sum(norm)
        gone_out[...], gtwo_out[...] = moments(gone[...], gtwo[...], gain_grad * factor)

    first, second = moments(one[...], two[...], grad[...] * factor)
    change = first / fix_one / (jnp.sqrt(second / fix_two) + ADAM_EPS)
    weight = master[...]
    weight = weight - RATE * (change + DECAY * weight)
    one_out[...] = first
    two_out[...] = second
    master_out[...] = weight
    teacher_out[...] = EMA_KEEP * teacher[...] + (1.0 - EMA_KEEP) * weight


def update(step, total, gains, gone, gtwo, grad, master, one, two, teacher):
    rows, width = grad.shape
    tall = max([t for t in range(SUBLANES, 113, SUBLANES) if rows % t == 0], default=rows)
    part = pl.BlockSpec((tall, width), lambda i: (i, 0))
    whole = lambda a: pl.BlockSpec(a.shape, lambda i: (0, 0))
    scalar = jax.ShapeDtypeStruct((1,), F32)
    same = lambda a: jax.ShapeDtypeStruct(a.shape, F32)
    return pl.pallas_call(
        update_kernel,
        name="update",
        grid=(rows // tall,),
        out_shape=(scalar, scalar, same(one), same(two), same(master), same(teacher), same(gone), same(gtwo)),
        in_specs=[smem_spec(), whole(total), whole(gains), whole(gone), whole(gtwo)] + [part] * 5,
        out_specs=(smem_spec(), smem_spec(), part, part, part, part, whole(gone), whole(gtwo)),
    )(step, total, gains, gone, gtwo, grad, master, one, two, teacher)


def body(
    patches,
    segments,
    positions,
    owners,
    master,
    moment_one,
    moment_two,
    teacher,
    gains,
    gain_one,
    gain_two,
    teacher_gains,
    step_count,
):
    core = lax.axis_index("group")
    width = patches.shape[3]
    slots = patches.shape[2]
    row_total = owners.shape[0]
    inner = (row_total - 6 * width) // 2
    places = piece_rows(owners, width, inner)
    spots = places // SUBLANES * TILE + places % SUBLANES
    chips = lax.axis_size("dp")
    devices = lax.axis_size("group") * chips
    own_rows = row_total // devices

    if chips <= KERNEL_CHIPS:
        model = gather_weights(master, teacher, chips)
    else:
        parts = lax.all_gather(jnp.stack([teacher, master]).astype(BF), ("dp", "group"), axis=1)
        model = jnp.where(core == 1, parts[1], parts[0]).reshape(chips, 2, own_rows, width)
    w = place_weights(spots, model)
    w_far = lax.ppermute(w, "group", [(1, 0)])
    patch = patches[:, 0]
    seg = segments
    pos = positions
    e, qkv, lse, mixed, x1, x2, tgt, bank = forward(patch, seg, pos, gains, teacher_gains, w)
    (e, qkv, lse, mixed, x1, x2, tgt), banks = exchange_states((e, qkv, lse, mixed, x1, x2, tgt), bank, chips)
    head, attn, ffn, act, de, mid, pred, dqkv, du, down, small = backward(
        seg, pos, gains, lse, banks, e, qkv, x1, x2, tgt, w, w_far
    )
    blocked = weight_grads(
        places, (patch, mixed, head, attn, ffn, act), (de, mid, pred, dqkv, du, down), devices
    )
    if chips <= KERNEL_CHIPS:
        owned_grad, total = reduce_grads(blocked.reshape(2, chips, own_rows, width), small, chips)
    else:
        owned_grad = lax.psum_scatter(blocked, ("group", "dp"), scatter_dimension=0, tiled=True)
        owned_grad = owned_grad.reshape(own_rows, width).astype(F32)
        squares = jnp.sum(owned_grad * owned_grad, axis=0, keepdims=True)
        row_id = lax.broadcasted_iota(jnp.int32, small.shape, 0)
        total = lax.psum(jnp.where(row_id == 5, squares, small), ("group", "dp"))
    return update(
        step_count, total, gains, gain_one, gain_two, owned_grad, master, moment_one, moment_two, teacher
    )


def solution(mesh):
    rows = P(("group", "dp"), None)
    in_specs = (
        P(None, "dp", None, None),
        P(None, "dp", None),
        P(None, "dp", None),
        P(),
        rows,
        rows,
        rows,
        rows,
        P(),
        P(),
        P(),
        P(),
        P(),
    )
    out_specs = (P(), P(), rows, rows, rows, rows, P(), P())
    return jax.shard_map(body, mesh=mesh, in_specs=in_specs, out_specs=out_specs, check_vma=False)
```

```python
import functools

import jax
import jax.numpy as jnp
from jax import lax
from jax.experimental import pallas as pl
from jax.experimental.pallas import tpu as pltpu
from jax.sharding import PartitionSpec as P

HEADS = 12
HEAD_DIM = 64
IMGS = 4
MASKED = 320
MICRO_BATCHES = 2
LANES = 128
SUBLANES = 8
TILE = SUBLANES * SUBLANES

SOFTMAX_TEMPER = 0.05
CLIP = 0.004
RATE = 0.05
BETA_ONE = 0.9
BETA_TWO = 0.999
ADAM_EPS = 1e-08
DECAY = 0.05
EMA_KEEP = 0.9
MASK_FILL = -1000000000.0

BF = jnp.bfloat16
F32 = jnp.float32
VMEM_LIMIT = 67_000_000
GELU_A = 0.7978845608028654
GELU_B = 0.044715


def nn(a, b):
    return jnp.dot(a, b, preferred_element_type=F32)


def nt(a, b):
    return lax.dot_general(a, b, (((1,), (1,)), ((), ())), preferred_element_type=F32)


def piece_rows(flat, width, inner):
    cuts = inner // width
    qkv, up = flat - 3 * width, flat - 6 * width
    inside = jnp.where(flat < 6 * width, (3 + qkv % 3) * width + qkv // 3, (6 + up % cuts) * width + up // cuts)
    return jnp.where((flat >= 3 * width) & (flat < 6 * width + inner), inside, flat)


def any_spec():
    return pl.BlockSpec(memory_space=pl.ANY)


def smem_spec():
    return pl.BlockSpec(memory_space=pltpu.SMEM)


MESH = pl.DeviceIdType.MESH
KERNEL_CHIPS = 16
AHEAD = 8


def chip_grid(chips):
    sizes, turn, left, prime = [1, 1, 1], 0, chips, 2
    while left > 1:
        while left % prime:
            prime += 1
        sizes[turn % 3] *= prime
        turn += 1
        left //= prime
    return tuple(sizes)


def strides_of(grid):
    return (grid[1] * grid[2], grid[2], 1)


def coords_of(index, grid):
    return (index // (grid[1] * grid[2]), lax.rem(index // grid[2], grid[1]), lax.rem(index, grid[2]))


def guarded(conditions, action):
    conditions = [c for c in conditions if c is not None]
    if not conditions:
        return action()
    both = conditions[0]
    for c in conditions[1:]:
        both = jnp.logical_and(both, c)
    pl.when(both)(action)


def lanes_of(width):
    unit = width // 6
    orders = [((1, 0, 2), 2), ((2, 0, 1), 2), ((0, 2, 1), 1), ((0, 1, 2), 1)]
    routes, first = [], 0
    for order, share in orders:
        routes.append((order, first, share * unit))
        first += share * unit
    return routes


def offsets(length):
    if length <= 2:
        return list(range(length))
    return [0] + [sign * far for far in range(1, length) for sign in (1, -1)]


def route_events(grid, routes):
    events = []
    for c, (order, _, _) in enumerate(routes):
        stack = [()]
        for d in order:
            stack = [r + (o,) for r in stack for o in offsets(grid[d])]
        events += [(sum(abs(o) * 2**i for i, o in enumerate(r)), c, r) for r in stack]
    return [(c, r) for _, c, r in sorted(events, key=lambda e: e[0])]


def onward(grid, order, r):
    last = max([i for i in range(3) if r[i]], default=-1)
    outs = []
    if last >= 0 and grid[order[last]] > 2:
        outs.append((order[last], 1 if r[last] > 0 else -1))
    for d in order[last + 1 :]:
        if grid[d] == 2:
            outs.append((d, 1))
        elif grid[d] > 2:
            outs += [(d, 1), (d, -1)]
    return outs


def neighbour(me, coords, grid, d, sign):
    step = strides_of(grid)[d]
    if grid[d] == 2:
        return me + (1 - 2 * coords[d]) * step, None
    place = coords[d] + sign
    return me + sign * step, jnp.logical_and(place >= 0, place < grid[d])


def origin(me, coords, grid, order, r):
    index, conditions = me, []
    for d, o in zip(order, r):
        if o == 0:
            continue
        step = strides_of(grid)[d]
        if grid[d] == 2:
            index = index + (1 - 2 * coords[d]) * step
        else:
            place = coords[d] - o
            index = index - o * step
            conditions.append(jnp.logical_and(place >= 0, place < grid[d]))
    return index, conditions


def slot_of(grid, d, sign):
    first = sum([1 if n <= 2 else 2 for n in grid[:d]])
    return first if grid[d] <= 2 or sign > 0 else first + 1


def slots_of(grid):
    return sum([1 if n <= 2 else 2 for n in grid])


def greet(me, coords, grid, group):
    barrier = pltpu.get_barrier_semaphore()
    near = [neighbour(me, coords, grid, d, s) for d in range(3) for s in ((1,) if grid[d] == 2 else (1, -1)) if grid[d] > 1]
    for index, there in near:
        guarded([there], lambda: pl.semaphore_signal(barrier, 1, device_id={"dp": index}, device_id_type=MESH))
    pl.semaphore_signal(barrier, 1, device_id={"group": 1 - group}, device_id_type=MESH)
    pl.semaphore_wait(barrier, 1 + sum([1 if there is None else there.astype(jnp.int32) for _, there in near]))


def gather_kernel(grid, learn, teach, out, both, swap_sem, half_sem, send_sem, recv_sem):
    group, me = lax.axis_index("group"), lax.axis_index("dp")
    coords = coords_of(me, grid)
    routes = lanes_of(both.shape[2])
    events = route_events(grid, routes)
    both[0] = teach[...].astype(BF)
    both[1] = learn[...].astype(BF)
    greet(me, coords, grid, group)
    keep = pltpu.make_async_copy(both.at[group], out.at[me, group], swap_sem.at[2])
    keep.start()
    swap = pltpu.make_async_remote_copy(
        both.at[1 - group], out.at[me, group], swap_sem.at[0], swap_sem.at[1], {"group": 1 - group}, MESH
    )
    swap.start()

    def first_sends(half, source):
        copies = []
        for c, (order, first, wide) in enumerate(routes):
            for d, sign in onward(grid, order, (0, 0, 0)):
                index, there = neighbour(me, coords, grid, d, sign)
                copy = pltpu.make_async_remote_copy(
                    source.at[:, first : first + wide],
                    out.at[me, half, :, first : first + wide],
                    half_sem.at[half, c, slot_of(grid, d, sign)],
                    recv_sem.at[c, me],
                    {"dp": index},
                    MESH,
                )
                copies.append((there, copy))
        for there, copy in copies:
            guarded([there], copy.start)
        return copies

    firsts = first_sends(group, both.at[group])
    swap.wait()
    firsts += first_sends(1 - group, out.at[me, 1 - group])

    def visit(c, r, act):
        order, first, wide = routes[c]
        block, real = origin(me, coords, grid, order, r)
        part = out.at[block, :, :, first : first + wide]

        def run():
            copies = []
            for d, sign in onward(grid, order, r):
                index, there = neighbour(me, coords, grid, d, sign)
                copies.append(
                    (
                        there,
                        pltpu.make_async_remote_copy(
                            part,
                            part,
                            send_sem.at[c, slot_of(grid, d, sign), block],
                            recv_sem.at[c, block],
                            {"dp": index},
                            MESH,
                        ),
                    )
                )
            act(part, recv_sem.at[c, block], copies)

        guarded(real, run)

    def forward_on(part, arrival_sem, copies):
        pltpu.make_async_remote_copy(part, part, swap_sem.at[0], arrival_sem, {"dp": me}, MESH).wait_recv()
        for there, copy in copies:
            guarded([there], copy.start)

    def finish(part, arrival_sem, copies):
        for there, copy in copies:
            guarded([there], copy.wait_send)

    for c, r in events:
        if any(r):
            visit(c, r, forward_on)
    for c, r in events:
        if any(r):
            visit(c, r, finish)
    keep.wait()
    for there, copy in firsts:
        guarded([there], copy.wait_send)


def gather_weights(learn, teach, chips):
    grid = chip_grid(chips)
    rows, width = learn.shape
    return pl.pallas_call(
        functools.partial(gather_kernel, grid),
        name="gather_weights",
        out_shape=jax.ShapeDtypeStruct((chips, 2, rows, width), BF),
        in_specs=[pl.BlockSpec(memory_space=pltpu.VMEM)] * 2,
        out_specs=any_spec(),
        scratch_shapes=[
            pltpu.VMEM((2, rows, width), BF),
            pltpu.SemaphoreType.DMA((3,)),
            pltpu.SemaphoreType.DMA((2, 4, slots_of(grid))),
            pltpu.SemaphoreType.DMA((4, slots_of(grid), chips)),
            pltpu.SemaphoreType.DMA((4, chips)),
        ],
        compiler_params=pltpu.CompilerParams(
            collective_id=1, has_side_effects=True, vmem_limit_bytes=VMEM_LIMIT
        ),
    )(learn, teach)


def sum_peers(group, me, grid):
    plane = grid[1] * grid[2]
    at, level = lax.rem(me, plane), me // plane
    place = (group * plane + at, level)
    sizes = (2 * plane, grid[0])
    peers = []
    for k in range(1, sizes[0]):
        other = lax.rem(place[0] + k, sizes[0])
        peers.append((0, k, (other // plane, level * plane + lax.rem(other, plane))))
    for k in range(1, sizes[1]):
        peers.append((1, k, (group, lax.rem(level + k, sizes[1]) * plane + at)))
    return place, sizes, peers


def sum_stages(place, sizes, peers, total, notes, note_send, note_recv):
    for s, size in enumerate(sizes):
        notes[s, place[s]] = total[...]
        copies = [
            pltpu.make_async_remote_copy(
                notes.at[s, place[s]], notes.at[s, place[s]], note_send.at[s, k], note_recv.at[s, place[s]], device, MESH
            )
            for t, k, device in peers
            if t == s
        ]
        for copy in copies:
            copy.start()
        for k in range(1, size):
            other = lax.rem(place[s] + k, size)
            part = notes.at[s, other]
            pltpu.make_async_remote_copy(
                part, part, note_send.at[s, k], note_recv.at[s, other], peers[0][2], MESH
            ).wait_recv()
        result = notes[s, 0]
        for k in range(1, size):
            result = result + notes[s, k]
        total[...] = result
        for copy in copies:
            copy.wait_send()


def reduce_kernel(
    grid, blocked, small, out, total, acc, heard, notes, load_sem, half_sem, send_sem, recv_sem, note_send, note_recv
):
    group, me = lax.axis_index("group"), lax.axis_index("dp")
    coords = coords_of(me, grid)
    rows, width = out.shape
    routes = lanes_of(width)
    events = route_events(grid, routes)[::-1]
    across = slots_of(grid)
    tall = max([t for t in range(16, 49, 16) if rows % t == 0], default=rows)

    def spot(c, r):
        return tuple(r[routes[c][0].index(d)] for d in range(3))

    firsts = list(dict.fromkeys([spot(c, r) for c, r in events]))
    place, sizes, peers = sum_peers(group, me, grid)
    barrier = pltpu.get_barrier_semaphore()
    for _, _, device in peers:
        pl.semaphore_signal(barrier, 1, device_id=device, device_id_type=MESH)
    pl.semaphore_wait(barrier, len(peers))

    def load(where, act):
        block, real = origin(me, coords, grid, (0, 1, 2), where)
        local = pltpu.make_async_copy(blocked.at[group, block], acc.at[block], load_sem.at[block])
        half = pltpu.make_async_remote_copy(
            blocked.at[1 - group, block],
            heard.at[across, block],
            half_sem.at[0, block],
            half_sem.at[1, block],
            {"group": 1 - group},
            MESH,
        )
        guarded(real, lambda: act(local, half))

    def load_start(local, half):
        half.start()
        local.start()

    def load_wait(local, half):
        local.wait()
        half.wait_recv()

    def load_end(local, half):
        half.wait_send()

    for where in firsts[:AHEAD]:
        load(where, load_start)

    def parent(c, r, block):
        order, first, wide = routes[c]
        i = max([i for i in range(3) if r[i]])
        sign = 1 if r[i] > 0 else -1
        index, _ = neighbour(me, coords, grid, order[i], -sign)
        slot = slot_of(grid, order[i], sign)
        return pltpu.make_async_remote_copy(
            acc.at[block, :, first : first + wide],
            heard.at[slot, block, :, first : first + wide],
            send_sem.at[c, block],
            recv_sem.at[c, slot, block],
            {"dp": index},
            MESH,
        )

    def visit(c, r):
        order, first, wide = routes[c]
        block, real = origin(me, coords, grid, order, r)

        def run():
            children = [(slot_of(grid, d, s), neighbour(me, coords, grid, d, s)[1]) for d, s in onward(grid, order, r)]
            for slot, there in children:
                part = heard.at[slot, block, :, first : first + wide]
                arrival = pltpu.make_async_remote_copy(
                    part, part, send_sem.at[c, block], recv_sem.at[c, slot, block], {"dp": me}, MESH
                )
                guarded([there], arrival.wait_recv)
            sure = [across] + [slot for slot, there in children if there is None]

            def add(slots, source, target):
                def piece(k, carry):
                    at = (pl.ds(pl.multiple_of(k * tall, tall), tall), slice(first, first + wide))
                    total = source[at].astype(F32)
                    for slot in slots:
                        total = total + heard[(slot, block) + at].astype(F32)
                    target[at] = total.astype(target.dtype)
                    return carry

                lax.fori_loop(0, rows // tall, piece, 0)

            target = acc.at[block] if any(r) else out
            add(sure, acc.at[block], target)
            for slot, there in children:
                if there is not None:
                    pl.when(there)(functools.partial(add, [slot], target, target))
            if any(r):
                parent(c, r, block).start()

        guarded(real, run)

    ready = set()
    for c, r in events:
        if spot(c, r) not in ready:
            ready.add(spot(c, r))
            load(spot(c, r), load_wait)
            for where in firsts[len(ready) + AHEAD - 1 : len(ready) + AHEAD]:
                load(where, load_start)
        visit(c, r)
    def squares(k, carry):
        part = out[pl.ds(pl.multiple_of(k * tall, tall), tall), :]
        return carry + jnp.sum(part * part, axis=0, keepdims=True)

    square = lax.fori_loop(0, rows // tall, squares, jnp.zeros((1, width), F32))
    row_id = lax.broadcasted_iota(jnp.int32, total.shape, 0)
    total[...] = jnp.where(row_id == 5, square, small[...])
    sum_stages(place, sizes, peers, total, notes, note_send, note_recv)
    for c, r in events:
        if any(r):
            block, real = origin(me, coords, grid, routes[c][0], r)
            guarded(real, parent(c, r, block).wait_send)
    for where in firsts:
        load(where, load_end)


def reduce_grads(blocked, small, chips):
    grid = chip_grid(chips)
    _, _, rows, width = blocked.shape
    most = max(grid[0], 2 * grid[1] * grid[2])
    return pl.pallas_call(
        functools.partial(reduce_kernel, grid),
        name="reduce_grads",
        out_shape=(jax.ShapeDtypeStruct((rows, width), F32), jax.ShapeDtypeStruct(small.shape, F32)),
        in_specs=[any_spec(), pl.BlockSpec(memory_space=pltpu.VMEM)],
        out_specs=(pl.BlockSpec(memory_space=pltpu.VMEM),) * 2,
        scratch_shapes=[
            pltpu.VMEM((chips, rows, width), BF),
            pltpu.VMEM((slots_of(grid) + 1, chips, rows, width), BF),
            pltpu.VMEM((2, most) + small.shape, F32),
            pltpu.SemaphoreType.DMA((chips,)),
            pltpu.SemaphoreType.DMA((2, chips)),
            pltpu.SemaphoreType.DMA((4, chips)),
            pltpu.SemaphoreType.DMA((4, slots_of(grid), chips)),
            pltpu.SemaphoreType.DMA((2, most)),
            pltpu.SemaphoreType.DMA((2, most)),
        ],
        compiler_params=pltpu.CompilerParams(
            collective_id=2, has_side_effects=True, vmem_limit_bytes=VMEM_LIMIT
        ),
    )(blocked, small)


def exchange_kernel(*refs):
    count = (len(refs) - 7) // 2
    bank, states, banks = refs[count], refs[count + 1 : 2 * count + 1], refs[2 * count + 1]
    state_send, state_recv, send_sem, recv_sem, own_sem = refs[2 * count + 2 :]
    group, me = lax.axis_index("group"), lax.axis_index("dp")
    chips = banks.shape[0]
    barrier = pltpu.get_barrier_semaphore()

    def hail(target):
        def one(k, carry):
            pl.semaphore_signal(barrier, 1, device_id=(target, lax.rem(me + k, chips)), device_id_type=MESH)
            return carry

        return one

    @pl.when(group == 0)
    def _():
        lax.fori_loop(1, chips, hail(0), 0)
        lax.fori_loop(0, chips, hail(1), 0)

    @pl.when(group == 1)
    def _():
        lax.fori_loop(0, chips, hail(0), 0)

    pl.semaphore_wait(barrier, chips + (1 - group) * (chips - 1))

    def crossing(k):
        ref = states[k]
        if k == count - 1:
            part = ref.at[1]
        elif len(ref.shape) == 3 and ref.shape[0] == 3:
            part = ref.at[:, : ref.shape[1] // MICRO_BATCHES, :]
        else:
            part = ref.at[0]
        return pltpu.make_async_remote_copy(
            part, part, state_send.at[k], state_recv.at[k], {"group": 1 - group}, MESH
        )

    def note(core, k):
        return pltpu.make_async_remote_copy(
            bank.at[core],
            banks.at[me],
            send_sem.at[core, k],
            recv_sem.at[me],
            (core, lax.rem(me + k, chips)),
            MESH,
        )

    def each(core, act):
        def one(k, carry):
            act(note(core, k))
            return carry

        return one

    def take(k, carry):
        pltpu.make_async_remote_copy(
            bank.at[0], banks.at[k], send_sem.at[0, 0], recv_sem.at[k], (1 - group, me), MESH
        ).wait_recv()
        return carry

    @pl.when(group == 0)
    def _():
        own = pltpu.make_async_copy(bank.at[0], banks.at[me], own_sem)
        own.start()
        lax.fori_loop(1, chips, each(0, lambda copy: copy.start()), 0)
        lax.fori_loop(0, chips, each(1, lambda copy: copy.start()), 0)
        targets = crossing(count - 1)
        targets.start()
        own.wait()
        lax.fori_loop(1, chips, lambda k, carry: take(lax.rem(me + k, chips), carry), 0)
        for k in range(count - 1):
            crossing(k).wait_recv()
        lax.fori_loop(1, chips, each(0, lambda copy: copy.wait_send()), 0)
        lax.fori_loop(0, chips, each(1, lambda copy: copy.wait_send()), 0)
        targets.wait_send()

    @pl.when(group == 1)
    def _():
        copies = [crossing(k) for k in range(count - 1)]
        for copy in copies:
            copy.start()
        lax.fori_loop(0, chips, take, 0)
        crossing(count - 1).wait_recv()
        for copy in copies:
            copy.wait_send()


def exchange_states(states, bank, chips):
    count = len(states)
    outs = pl.pallas_call(
        exchange_kernel,
        name="exchange_states",
        out_shape=tuple(jax.ShapeDtypeStruct(a.shape, a.dtype) for a in states)
        + (jax.ShapeDtypeStruct((chips,) + bank.shape[1:], BF),),
        in_specs=[any_spec()] * (count + 1),
        out_specs=(any_spec(),) * (count + 1),
        scratch_shapes=[
            pltpu.SemaphoreType.DMA((count,)),
            pltpu.SemaphoreType.DMA((count,)),
            pltpu.SemaphoreType.DMA((2, chips)),
            pltpu.SemaphoreType.DMA((chips,)),
            pltpu.SemaphoreType.DMA,
        ],
        input_output_aliases={k: k for k in range(count)},
        compiler_params=pltpu.CompilerParams(collective_id=3, has_side_effects=True),
    )(*states, bank)
    return outs[:-1], outs[-1]


def place_kernel(spots, model, out, rows_scr, inbuf, stage, outbuf, in_sem, out_sem):
    chips, cores, rows, width = model.shape
    blocks = cores * chips
    cols = width // LANES
    deep, wide = inbuf.shape[0], outbuf.shape[0]
    group = max([g for g in range(1, 49) if rows % g == 0])

    def fetch(b, slot):
        return pltpu.make_async_copy(model.at[lax.rem(b, chips), b // chips], inbuf.at[slot], in_sem.at[slot])

    for b in range(deep - 1):
        fetch(b, b).start()

    def block(b, carry):
        slot = lax.rem(b, deep)
        fetch(b, slot).wait()

        @pl.when(b + deep - 1 < blocks)
        def _():
            fetch(b + deep - 1, lax.rem(b + deep - 1, deep)).start()

        for c in range(cols):
            stage[pl.ds(c, rows, stride=SUBLANES), :] = inbuf[slot, :, c * LANES : (c + 1) * LANES].astype(F32)

        def move(q, carry):
            first = q * group
            to = [spots[b * rows + first + j] for j in range(group)]
            held = [stage[pl.ds(pl.multiple_of((first + j) * SUBLANES, SUBLANES), SUBLANES), :] for j in range(group)]
            for j in range(group):
                rows_scr[pl.ds(to[j], SUBLANES, stride=SUBLANES), :] = held[j]
            return carry

        return lax.fori_loop(0, rows // group, move, carry)

    lax.fori_loop(0, blocks, block, 0)
    pieces = out.shape[0]
    for u in range(pieces):
        slot = u % wide
        if u >= wide:
            pltpu.make_async_copy(outbuf.at[slot], out.at[u - wide], out_sem.at[slot]).wait()

        def pack(k, carry):
            to = pl.ds(pl.multiple_of(k * 16, 16), 16)
            for c in range(cols):
                first = (u * width // SUBLANES + 2 * k) * TILE + c * SUBLANES
                halves = [rows_scr[pl.ds(pl.multiple_of(first + TILE * h, SUBLANES), SUBLANES), :] for h in range(2)]
                outbuf[slot, to, c * LANES : (c + 1) * LANES] = jnp.concatenate(halves, axis=0).astype(BF)
            return carry

        lax.fori_loop(0, width // 16, pack, 0)
        pltpu.make_async_copy(outbuf.at[slot], out.at[u], out_sem.at[slot]).start()
    for u in range(pieces - wide, pieces):
        pltpu.make_async_copy(outbuf.at[u % wide], out.at[u], out_sem.at[u % wide]).wait()


def place_weights(spots, model):
    _, _, rows, width = model.shape
    total = spots.shape[0]
    return pl.pallas_call(
        place_kernel,
        name="place_weights",
        out_shape=jax.ShapeDtypeStruct((total // width, width, width), BF),
        in_specs=[smem_spec(), any_spec()],
        out_specs=any_spec(),
        scratch_shapes=[
            pltpu.VMEM((total * SUBLANES, LANES), F32),
            pltpu.VMEM((8, rows, width), BF),
            pltpu.VMEM((rows * SUBLANES, LANES), F32),
            pltpu.VMEM((4, width, width), BF),
            pltpu.SemaphoreType.DMA((8,)),
            pltpu.SemaphoreType.DMA((4,)),
        ],
        compiler_params=pltpu.CompilerParams(vmem_limit_bytes=VMEM_LIMIT),
    )(spots, model)


def layer_stats(tensor):
    centre = tensor - jnp.mean(tensor, axis=-1, keepdims=True)
    scaled = lax.rsqrt(jnp.mean(centre * centre, axis=-1, keepdims=True) + 1e-06)
    return centre * scaled, scaled


def column_of(row):
    n = row.shape[1]
    eye = lax.broadcasted_iota(jnp.int32, (n, n), 0) == lax.broadcasted_iota(jnp.int32, (n, n), 1)
    return jnp.sum(jnp.where(eye, row, 0), axis=1, keepdims=True)


def flag_column(pos, slots):
    hit = lax.broadcasted_iota(jnp.int32, (slots, pos.shape[1]), 0) == pos
    return jnp.max(jnp.where(hit, 1, 0), axis=1, keepdims=True)


def fill_masks(k_mask, q_mask, seg_col):
    lane = lax.broadcasted_iota(jnp.int32, (1, LANES), 1)
    for h in range(2):
        at = lane - (HEAD_DIM if h == 0 else 0)
        same = at == seg_col
        other = jnp.logical_and(jnp.logical_and(at >= 0, at <= IMGS), jnp.logical_not(same))
        k_mask[h] = jnp.where(same, 1.0, 0.0).astype(BF)
        q_mask[h] = jnp.where(other, MASK_FILL, 0.0).astype(BF)


def masked(x, mask, h):
    low = lax.broadcasted_iota(jnp.int32, (1, LANES), 1) < HEAD_DIM
    return jnp.where(low if h == 0 else jnp.logical_not(low), x, mask[h])


def half(x, h):
    low = lax.broadcasted_iota(jnp.int32, (1, LANES), 1) < HEAD_DIM
    keep = low if h == 0 else jnp.logical_not(low)
    return jnp.where(keep, x, jnp.zeros_like(x))


def fwd_kernel(
    patch, seg, pos, gains, teacher_gains, w_hbm,
    e_out, qkv_out, lse_out, o_out, x1_out, x2_out, tgt_out, bank_out,
    w, k_mask, q_mask, gain, a2, e_v, qkv, lse, o_v, x1_v, x2_v, tgt, bank, sem, out_sem,
):
    i = pl.program_id(0)
    role = lax.axis_index("group")
    gain[...] = jnp.where(role == 0, teacher_gains[...], gains[...])
    batches, slots, width = e_out.shape
    pieces = w_hbm.shape[0]
    cuts = (pieces - 6) // 2
    order = [0, 3, 4, 5, 1]
    for j in range(cuts):
        order += [6 + j, 6 + cuts + j]

    def bring(which):
        @pl.when(i == 0)
        def _():
            for u in which:
                pltpu.make_async_copy(w_hbm.at[u], w.at[u], sem.at[u]).start()

    def need(u):
        @pl.when(i == 0)
        def _():
            pltpu.make_async_copy(w_hbm.at[u], w.at[u], sem.at[u]).wait()

    bring(order[:2])

    def leave(k, b):
        tokens = pl.ds(pl.multiple_of(b * slots, slots), slots)
        source, target = [
            (e_v.at[b], e_out.at[b]),
            (qkv.at[b], qkv_out.at[:, tokens, :]),
            (lse.at[b], lse_out.at[b]),
            (o_v.at[b], o_out.at[b]),
            (x1_v.at[b], x1_out.at[b]),
            (x2_v.at[b], x2_out.at[b]),
            (tgt.at[b], tgt_out.at[b]),
            (bank.at[b], bank_out.at[b]),
        ][k]
        return pltpu.make_async_copy(source, target, out_sem.at[b, k])

    seg_row = seg[0]
    seg_col = column_of(seg_row)
    fill_masks(k_mask, q_mask, seg_col)
    flags = flag_column(pos[0], slots) * role
    need(0)
    bring(order[2:])
    e = nn(patch[0], w[0])
    e = jnp.where(flags > 0, gain[3:4, :], e)
    e_v[i] = e
    leave(0, i).start()
    a2[...] = (layer_stats(e)[0] * gain[0:1, :]).astype(BF)

    def project(j, carry):
        need(3 + j)
        qkv[i, j] = nn(a2[...], w[3 + j]).astype(BF)
        return carry

    lax.fori_loop(0, 3, project, 0)
    leave(1, i).start()

    def pair(p, carry):
        cs = pl.ds(pl.multiple_of(p * LANES, LANES), LANES)
        q2, k2, v2 = qkv[i, 0, :, cs], qkv[i, 1, :, cs], qkv[i, 2, :, cs]
        k2 = k2 * jnp.asarray(HEAD_DIM**-0.5, BF)
        v_t = v2.T
        outs = []
        for h in range(2):
            s = nt(masked(k2, k_mask, h), masked(q2, q_mask, h))
            top = jnp.max(s, axis=0, keepdims=True)
            ex = jnp.exp(s - top)
            total = jnp.sum(ex, axis=0, keepdims=True)
            lse[i, pl.ds(2 * p + h, 1), :] = top + jnp.log(total)
            probs = (ex * (1.0 / total)).astype(BF)
            outs.append(nn(v_t[h * HEAD_DIM : (h + 1) * HEAD_DIM, :], probs))
        o_v[i, :, cs] = jnp.concatenate(outs, axis=0).T.astype(BF)
        return carry

    lax.fori_loop(0, HEADS // 2, pair, 0)
    leave(2, i).start()
    leave(3, i).start()
    need(1)
    x1 = e_v[i] + nn(o_v[i], w[1])
    x1_v[i] = x1
    leave(4, i).start()
    a2[...] = (layer_stats(x1)[0] * gain[1:2, :]).astype(BF)
    x2_v[i] = x1

    def ffn(j, carry):
        need(6 + j)
        hid = nn(a2[...], w[6 + j])
        act = (hid * (0.5 * (1.0 + jnp.tanh(GELU_A * (hid + GELU_B * hid * hid * hid))))).astype(BF)
        need(6 + cuts + j)
        x2_v[i] += nn(act, w[6 + cuts + j])
        return carry

    lax.fori_loop(0, cuts, ffn, 0)
    leave(5, i).start()

    @pl.when(role == 0)
    def _():
        t = layer_stats(x2_v[i])[0].astype(BF)
        tgt[i] = t
        leave(6, i).start()
        t = t.astype(F32)
        for m in range(IMGS):
            inside = seg_col == m
            size = jnp.sum(jnp.where(inside, 1.0, 0.0), axis=0, keepdims=True)
            pooled = jnp.sum(jnp.where(inside, t, 0.0), axis=0, keepdims=True) / size
            unit = pooled * lax.rsqrt(jnp.sum(pooled * pooled, axis=-1, keepdims=True) + 1e-06)
            bank[i, m : m + 1, :] = unit.astype(BF)
        leave(7, i).start()

    @pl.when(i == batches - 1)
    def _():
        for b in range(batches):
            for k in range(6):
                leave(k, b).wait()

        @pl.when(role == 0)
        def _():
            for b in range(batches):
                leave(6, b).wait()
                leave(7, b).wait()


def forward(patch, seg, pos, gains, teacher_gains, w):
    batches, slots, width = patch.shape
    pieces = w.shape[0]
    tok = lambda n, dt: ((batches,) + ((3,) if n == 3 else ()) + (slots, width), dt)
    kinds = [
        tok(1, F32),
        tok(3, BF),
        ((batches, HEADS, slots), F32),
        tok(1, BF),
        tok(1, F32),
        tok(1, F32),
        tok(1, BF),
        ((batches, IMGS, width), BF),
    ]
    outs = [jax.ShapeDtypeStruct(shape, dt) for shape, dt in kinds]
    outs[1] = jax.ShapeDtypeStruct((3, batches * slots, width), BF)
    return pl.pallas_call(
        fwd_kernel,
        name="forward",
        grid=(batches,),
        out_shape=tuple(outs),
        in_specs=[
            pl.BlockSpec((1, slots, width), lambda i: (i, 0, 0)),
            pl.BlockSpec((1, 1, slots), lambda i: (i, 0, 0)),
            pl.BlockSpec((1, 1, pos.shape[2]), lambda i: (i, 0, 0)),
            pl.BlockSpec((4, width), lambda i: (0, 0)),
            pl.BlockSpec((4, width), lambda i: (0, 0)),
            any_spec(),
        ],
        out_specs=(any_spec(),) * len(outs),
        scratch_shapes=[
            pltpu.VMEM((pieces, width, width), BF),
            pltpu.VMEM((2, slots, LANES), BF),
            pltpu.VMEM((2, slots, LANES), BF),
            pltpu.VMEM((4, width), F32),
            pltpu.VMEM((slots, width), BF),
        ]
        + [pltpu.VMEM(shape, dt) for shape, dt in kinds]
        + [
            pltpu.SemaphoreType.DMA((pieces,)),
            pltpu.SemaphoreType.DMA((batches, len(kinds))),
        ],
        compiler_params=pltpu.CompilerParams(vmem_limit_bytes=VMEM_LIMIT),
        cost_estimate=pl.CostEstimate(
            flops=2 * batches * slots * width * width * pieces, bytes_accessed=2 * w.size, transcendentals=0
        ),
    )(patch, seg, pos, gains, teacher_gains, w)


def norm_back(grad_out, normed, scaled, gain_vec):
    grad_hat = grad_out * gain_vec
    inner = jnp.mean(grad_hat * normed, axis=-1, keepdims=True)
    grad_in = scaled * (grad_hat - jnp.mean(grad_hat, axis=-1, keepdims=True) - normed * inner)
    return grad_in, jnp.sum(grad_out * normed, axis=0, keepdims=True)


def bwd_kernel(
    seg, pos, gain, lse, banks, e_hbm, qkv_hbm, x1_hbm, x2_hbm, tgt_hbm, w_own, w_far,
    head_out, attn_out, ffn_out, act_out, de_out, mid_out, pred_out, dqkv_out, du_out, down_out, small,
    w, k_mask, q_mask, top_scr, acc_scr, pool_scr, bank_scr, e_in, qkv, x1_in, x2_in, tgt,
    head_v, attn_v, ffn_v, act_v, de_v, mid_v, pred_v, dqkv, du_v, down_v, sem, in_sem, out_sem,
):
    role, chip = lax.axis_index("group"), lax.axis_index("dp")
    slots, width = e_in.shape
    chips = banks.shape[0]
    pieces = w_own.shape[0]
    cuts = (pieces - 6) // 2
    tokens = pl.ds(pl.multiple_of(role * slots, slots), slots)

    def bring(k, source, target):
        copy = pltpu.make_async_copy(source, target, in_sem.at[k])
        copy.start()
        return copy

    def bring_piece(u):
        @pl.when(role == 0)
        def _():
            pltpu.make_async_copy(w_far.at[u], w.at[u - 1], sem.at[u]).start()

        @pl.when(role != 0)
        def _():
            pltpu.make_async_copy(w_own.at[u], w.at[u - 1], sem.at[u]).start()

    def need(u):
        pltpu.make_async_copy(w_own.at[u], w.at[u - 1], sem.at[u]).wait()

    taken = []

    def keep(source, target):
        copy = pltpu.make_async_copy(source, target, out_sem.at[len(taken)])
        copy.start()
        taken.append(copy)

    x2_copy = bring(0, x2_hbm.at[role], x2_in)
    bring_piece(2)
    tgt_copy = bring(1, tgt_hbm.at[role], tgt)
    small[...] = jnp.zeros_like(small)

    seg_row = seg[role]
    seg_col = column_of(seg_row)
    fill_masks(k_mask, q_mask, seg_col)
    flags = flag_column(pos[role], slots)
    x2_copy.wait()
    x1_copy = bring(2, x1_hbm.at[role], x1_in)
    for j in range(cuts):
        bring_piece(6 + cuts + j)
        bring_piece(6 + j)
    bring_piece(1)
    qkv_copy = bring(3, qkv_hbm.at[:, tokens, :], qkv)
    for j in range(3):
        bring_piece(3 + j)
    e_copy = bring(4, e_hbm.at[role], e_in)
    n3, r3 = layer_stats(x2_in[...])
    head_in = (n3 * gain[2:3, :]).astype(BF)
    head_v[...] = head_in
    keep(head_v, head_out.at[0])
    need(2)
    pred = nn(head_in, w[1])
    valid = jnp.where(seg_col < IMGS, flags, 0).astype(F32)
    tgt_copy.wait()
    diff = pred - tgt[...].astype(F32)
    size = jnp.abs(diff)
    huber = jnp.where(size < 1.0, 0.5 * diff * diff, size - 0.5)
    regress = jnp.sum(jnp.sum(valid * huber, axis=1, keepdims=True), axis=0, keepdims=True)
    count = float(MASKED * chips * MICRO_BATCHES * width)
    grad_pred = valid * (jnp.clip(diff, -1.0, 1.0) / count)
    pool_scr[...] = jnp.zeros_like(pool_scr)
    for m in range(IMGS):
        inside = seg_col == m
        tally = jnp.sum(jnp.where(inside, 1.0, 0.0), axis=0, keepdims=True)
        pool_scr[m : m + 1, :] = jnp.sum(jnp.where(inside, pred, 0.0), axis=0, keepdims=True) / tally
    pooled = pool_scr[...]
    length = lax.rsqrt(jnp.sum(pooled * pooled, axis=-1, keepdims=True) + 1e-06)
    unit = pooled * length
    for k in range(chips):
        bank_scr[k * IMGS : (k + 1) * IMGS, :] = banks[k].astype(F32)
    memory = bank_scr[...].astype(BF)
    choices = memory.shape[0]
    logits = nt(unit.astype(BF), memory) / SOFTMAX_TEMPER
    row_id = lax.broadcasted_iota(jnp.int32, logits.shape, 0)
    real = row_id < IMGS
    picked = jnp.where(
        real & (lax.broadcasted_iota(jnp.int32, logits.shape, 1) == chip * IMGS + row_id), 1.0, 0.0
    )
    peak = jnp.max(logits, axis=-1, keepdims=True)
    ex = jnp.exp(logits - peak)
    total = jnp.sum(ex, axis=-1, keepdims=True)
    each = peak + jnp.log(total) - jnp.sum(logits * picked, axis=-1, keepdims=True)
    contrast = jnp.sum(jnp.where(real[:, 0:1], each, 0.0), axis=0, keepdims=True)
    scale = choices * MICRO_BATCHES
    grad_logits = (jnp.where(real, ex / total - picked, 0.0) / scale / SOFTMAX_TEMPER).astype(BF)
    grad_unit = nn(grad_logits, memory)
    grad_pool = length * (grad_unit - unit * jnp.sum(grad_unit * unit, axis=1, keepdims=True))
    pool_scr[...] = grad_pool
    for m in range(IMGS):
        inside = seg_col == m
        tally = jnp.sum(jnp.where(inside, 1.0, 0.0), axis=0, keepdims=True)
        grad_pred = grad_pred + jnp.where(inside, pool_scr[m : m + 1, :] / tally, 0.0)
    low = grad_pred.astype(BF)
    pred_v[...] = low
    keep(pred_v, pred_out.at[0])
    loss = regress / count + contrast / scale
    small[4:5, :] += jnp.broadcast_to(loss, (1, width))
    grad_top, gain_three = norm_back(nt(low, w[1]), n3, r3, gain[2:3, :])
    small[2:3, :] += gain_three
    top_scr[...] = grad_top
    down = grad_top.astype(BF)
    down_v[...] = down
    keep(down_v, down_out.at[0])
    x1_copy.wait()
    n2, r2 = layer_stats(x1_in[...])
    ffn_in = (n2 * gain[1:2, :]).astype(BF)
    ffn_v[...] = ffn_in
    keep(ffn_v, ffn_out.at[0])
    acc_scr[...] = jnp.zeros_like(acc_scr)
    loop_sem = len(taken)

    def leave(j):
        return (
            pltpu.make_async_copy(act_v.at[j], act_out.at[j], out_sem.at[loop_sem + 2 * j]),
            pltpu.make_async_copy(du_v.at[j], du_out.at[j], out_sem.at[loop_sem + 2 * j + 1]),
        )

    def ffn(j, carry):
        need(6 + cuts + j)
        grad_act = nt(down_v[...], w[5 + cuts + j])
        need(6 + j)
        hid = nn(ffn_v[...], w[5 + j])
        th = jnp.tanh(GELU_A * (hid + GELU_B * hid * hid * hid))
        cdf = 0.5 * (1.0 + th)
        act_v[j] = (hid * cdf).astype(BF)
        slope = cdf + hid * (0.5 * (1.0 - th * th)) * (GELU_A * (1.0 + 3.0 * GELU_B * hid * hid))
        du = (grad_act * slope).astype(BF)
        du_v[j] = du
        for copy in leave(j):
            copy.start()
        acc_scr[...] += nt(du, w[5 + j])
        return carry

    lax.fori_loop(0, cuts, ffn, 0)
    for j in range(cuts):
        taken.extend(leave(j))
    grad_ffn, gain_two = norm_back(acc_scr[...], n2, r2, gain[1:2, :])
    small[1:2, :] += gain_two
    mid = top_scr[...] + grad_ffn
    top_scr[...] = mid
    mid_low = mid.astype(BF)
    mid_v[...] = mid_low
    keep(mid_v, mid_out.at[0])
    need(1)
    de_v[...] = nt(mid_low, w[0]).astype(BF)
    qkv_copy.wait()

    def pair(p, carry):
        cs = pl.ds(pl.multiple_of(p * LANES, LANES), LANES)
        q2, k2, v2, g2 = qkv[0, :, cs], qkv[1, :, cs], qkv[2, :, cs], de_v[:, cs]
        k_scaled = k2 * jnp.asarray(HEAD_DIM**-0.5, BF)
        k_t = k2.T
        dq, dk, dv = [], 0.0, 0.0
        for h in range(2):
            s = nt(masked(k_scaled, k_mask, h), masked(q2, q_mask, h))
            probs = jnp.exp(s - lse[role, pl.ds(2 * p + h, 1), :])
            dp = nt(half(v2, h), g2)
            centre = jnp.sum(probs * dp, axis=0, keepdims=True)
            ds = (probs * (dp - centre)).astype(BF)
            dv = dv + nn(probs.astype(BF), half(g2, h))
            dk = dk + nn(ds, half(q2, h))
            dq.append(nn(k_t[h * HEAD_DIM : (h + 1) * HEAD_DIM, :], ds))
        dqkv[0, :, cs] = (jnp.concatenate(dq, axis=0) * HEAD_DIM**-0.5).T.astype(BF)
        dqkv[1, :, cs] = (dk * HEAD_DIM**-0.5).astype(BF)
        dqkv[2, :, cs] = dv.astype(BF)
        return carry

    lax.fori_loop(0, HEADS // 2, pair, 0)
    keep(dqkv, dqkv_out)
    acc_scr[...] = jnp.zeros_like(acc_scr)

    def project(j, carry):
        need(3 + j)
        acc_scr[...] += nt(dqkv[j], w[2 + j])
        return carry

    lax.fori_loop(0, 3, project, 0)
    e_copy.wait()
    n1, r1 = layer_stats(e_in[...])
    attn_v[...] = (n1 * gain[0:1, :]).astype(BF)
    keep(attn_v, attn_out.at[0])
    grad_attn, gain_one = norm_back(acc_scr[...], n1, r1, gain[0:1, :])
    small[0:1, :] += gain_one
    start = top_scr[...] + grad_attn
    hidden_slot = flags > 0
    small[3:4, :] += jnp.sum(jnp.where(hidden_slot, start, 0.0), axis=0, keepdims=True)
    de_v[...] = jnp.where(hidden_slot, 0.0, start).astype(BF)
    keep(de_v, de_out.at[0])
    for copy in taken:
        copy.wait()


def backward(seg, pos, gain, lse, banks, e, qkv, x1, x2, tgt, w_own, w_far):
    _, slots, width = e.shape
    pieces = w_own.shape[0]
    cuts = (pieces - 6) // 2
    counts = (1, 1, 1, cuts, 1, 1, 1, 3, cuts, 1)
    vmem = pl.BlockSpec(memory_space=pltpu.VMEM)
    tok = lambda n, dt: pltpu.VMEM((n, slots, width) if n > 1 else (slots, width), dt)
    return pl.pallas_call(
        bwd_kernel,
        name="backward",
        out_shape=tuple(jax.ShapeDtypeStruct((n, slots, width), BF) for n in counts)
        + (jax.ShapeDtypeStruct((SUBLANES, width), F32),),
        in_specs=[vmem] * 5 + [any_spec()] * 7,
        out_specs=(any_spec(),) * len(counts) + (vmem,),
        scratch_shapes=[
            pltpu.VMEM((pieces - 1, width, width), BF),
            pltpu.VMEM((2, slots, LANES), BF),
            pltpu.VMEM((2, slots, LANES), BF),
            pltpu.VMEM((slots, width), F32),
            pltpu.VMEM((slots, width), F32),
            pltpu.VMEM((SUBLANES, width), F32),
            pltpu.VMEM((banks.shape[0] * IMGS, width), F32),
            tok(1, F32),
            tok(3, BF),
            tok(1, F32),
            tok(1, F32),
            tok(1, BF),
        ]
        + [tok(n, BF) for n in counts]
        + [
            pltpu.SemaphoreType.DMA((pieces,)),
            pltpu.SemaphoreType.DMA((5,)),
            pltpu.SemaphoreType.DMA((sum(counts),)),
        ],
        compiler_params=pltpu.CompilerParams(vmem_limit_bytes=VMEM_LIMIT),
    )(seg, pos, gain, lse, banks, e, qkv, x1, x2, tgt, w_own, w_far)


def grads_kernel(
    plan, places, patch, mixed, head, attn, ffn, act, de, mid, pred, dqkv, du, down, out,
    rows_scr, x_buf, x_t, g_buf, stage, outbuf, x_sem, g_sem, out_sem,
):
    blocks, rows, width = out.shape
    cols = width // LANES
    deep, wide_out = x_buf.shape[0], outbuf.shape[0]
    group = max([g for g in range(SUBLANES, 49, SUBLANES) if rows % g == 0], default=rows)
    lefts = {"patch": patch, "mixed": mixed, "head": head, "attn": attn, "ffn": ffn, "act": act}
    rights = {"de": de, "mid": mid, "pred": pred, "dqkv": dqkv, "du": du, "down": down}

    def left_of(key):
        name, index = key
        return lefts[name].at[lax.axis_index("group") if name in ("patch", "mixed") else index]

    lcopies, rcopies = [], []
    lkeys, rkeys = [], []
    steps = []
    for u, (left, right) in enumerate(plan):
        if not lkeys or lkeys[-1] != left:
            slot = len(lkeys) % deep
            lcopies.append(pltpu.make_async_copy(left_of(left), x_buf.at[slot], x_sem.at[slot]))
            lkeys.append(left)
            fresh_l = True
        else:
            fresh_l = False
        if not rkeys or rkeys[-1] != right:
            slot = len(rkeys) % deep
            rcopies.append(pltpu.make_async_copy(rights[right[0]].at[right[1]], g_buf.at[slot], g_sem.at[slot]))
            rkeys.append(right)
            fresh_r = True
        else:
            fresh_r = False
        steps.append((u, len(lkeys) - 1, fresh_l, len(rkeys) - 1, fresh_r))
    lcopies[0].start()
    rcopies[0].start()
    for u, li, fresh_l, ri, fresh_r in steps:
        if fresh_l:
            lcopies[li].wait()
            for copy in lcopies[1:deep] if li == 0 else lcopies[li + deep - 1 : li + deep]:
                copy.start()
            x_t[...] = x_buf[li % deep].T
        if fresh_r:
            rcopies[ri].wait()
            for copy in rcopies[1:deep] if ri == 0 else rcopies[ri + deep - 1 : ri + deep]:
                copy.start()
        wide = 2 * LANES

        def tile(n, carry):
            part = nn(x_t[...], g_buf[ri % deep, :, pl.ds(pl.multiple_of(n * wide, wide), wide)])
            for c in range(2):
                rows_scr[pl.ds(u * width * SUBLANES + 2 * n + c, width, stride=SUBLANES), :] = part[
                    :, c * LANES : (c + 1) * LANES
                ]
            return carry

        lax.fori_loop(0, width // wide, tile, 0)

    def block(b, carry):
        slot = lax.rem(b, wide_out)

        def move(q, carry):
            came = [pl.multiple_of(places[b * rows + q * group + j] * SUBLANES, SUBLANES) for j in range(group)]
            held = [rows_scr[pl.ds(first, SUBLANES), :] for first in came]
            for j in range(group):
                to = q * (group // SUBLANES) * TILE + j // SUBLANES * TILE + j % SUBLANES
                stage[pl.ds(to, SUBLANES, stride=SUBLANES), :] = held[j]
            return carry

        lax.fori_loop(0, rows // group, move, 0)

        @pl.when(b >= wide_out)
        def _():
            pltpu.make_async_copy(outbuf.at[slot], out.at[b - wide_out], out_sem.at[slot]).wait()

        for first in range(0, rows, 16):
            tall = min(16, rows - first)
            for c in range(cols):
                at = first * SUBLANES + c * SUBLANES
                both = jnp.concatenate([stage[at : at + SUBLANES, :], stage[at + TILE : at + TILE + SUBLANES, :]], 0)
                outbuf[slot, first : first + tall, c * LANES : (c + 1) * LANES] = both[:tall].astype(BF)
        pltpu.make_async_copy(outbuf.at[slot], out.at[b], out_sem.at[slot]).start()
        return carry

    lax.fori_loop(0, blocks, block, 0)
    for b in range(blocks - wide_out, blocks):
        pltpu.make_async_copy(outbuf.at[b % wide_out], out.at[b], out_sem.at[b % wide_out]).wait()


def weight_grads(places, lefts, rights, blocks):
    tokens, width = lefts[0].shape[1:]
    cuts = lefts[-1].shape[0]
    total = places.shape[0]
    rows = total // blocks
    plan = (
        [(("patch", 0), ("de", 0)), (("mixed", 0), ("mid", 0)), (("head", 0), ("pred", 0))]
        + [(("attn", 0), ("dqkv", j)) for j in range(3)]
        + [(("ffn", 0), ("du", j)) for j in range(cuts)]
        + [(("act", j), ("down", 0)) for j in range(cuts)]
    )
    return pl.pallas_call(
        functools.partial(grads_kernel, plan),
        name="weight_grads",
        out_shape=jax.ShapeDtypeStruct((blocks, rows, width), BF),
        in_specs=[smem_spec()] + [any_spec()] * 12,
        out_specs=any_spec(),
        scratch_shapes=[
            pltpu.VMEM((total * SUBLANES, LANES), F32),
            pltpu.VMEM((4, tokens, width), BF),
            pltpu.VMEM((width, tokens), BF),
            pltpu.VMEM((4, tokens, width), BF),
            pltpu.VMEM((pl.cdiv(rows, 16) * 2 * TILE, LANES), F32),
            pltpu.VMEM((4, rows, width), BF),
            pltpu.SemaphoreType.DMA((4,)),
            pltpu.SemaphoreType.DMA((4,)),
            pltpu.SemaphoreType.DMA((4,)),
        ],
        compiler_params=pltpu.CompilerParams(vmem_limit_bytes=VMEM_LIMIT),
    )(places, *lefts, *rights)


def power_of(base, exponent):
    return lax.fori_loop(0, exponent, lambda _, product: product * base, jnp.float32(1.0))


def update_kernel(
    step, total, gains, gone, gtwo, grad, master, one, two, teacher,
    loss_out, norm_out, one_out, two_out, master_out, teacher_out, gone_out, gtwo_out,
):
    gain_grad = total[0:4, :]
    square = jnp.sum(total[5:6, :], axis=1, keepdims=True)
    square = square + jnp.sum(jnp.sum(gain_grad * gain_grad, axis=1, keepdims=True), axis=0, keepdims=True)
    norm = jnp.sqrt(square)
    factor = jnp.minimum(1.0, CLIP / norm)
    fix_one = 1.0 - power_of(BETA_ONE, step[0])
    fix_two = 1.0 - power_of(BETA_TWO, step[0])

    def moments(first, second, gradient):
        first = BETA_ONE * first + (1.0 - BETA_ONE) * gradient
        second = BETA_TWO * second + (1.0 - BETA_TWO) * gradient * gradient
        return first, second

    @pl.when(pl.program_id(0) == 0)
    def _():
        loss_out[0] = jnp.sum(total[4:5, 0:1])
        norm_out[0] = jnp.sum(norm)
        gone_out[...], gtwo_out[...] = moments(gone[...], gtwo[...], gain_grad * factor)

    first, second = moments(one[...], two[...], grad[...] * factor)
    change = first / fix_one / (jnp.sqrt(second / fix_two) + ADAM_EPS)
    weight = master[...]
    weight = weight - RATE * (change + DECAY * weight)
    one_out[...] = first
    two_out[...] = second
    master_out[...] = weight
    teacher_out[...] = EMA_KEEP * teacher[...] + (1.0 - EMA_KEEP) * weight


def update(step, total, gains, gone, gtwo, grad, master, one, two, teacher):
    rows, width = grad.shape
    tall = max([t for t in range(SUBLANES, 113, SUBLANES) if rows % t == 0], default=rows)
    part = pl.BlockSpec((tall, width), lambda i: (i, 0))
    whole = lambda a: pl.BlockSpec(a.shape, lambda i: (0, 0))
    scalar = jax.ShapeDtypeStruct((1,), F32)
    same = lambda a: jax.ShapeDtypeStruct(a.shape, F32)
    return pl.pallas_call(
        update_kernel,
        name="update",
        grid=(rows // tall,),
        out_shape=(scalar, scalar, same(one), same(two), same(master), same(teacher), same(gone), same(gtwo)),
        in_specs=[smem_spec(), whole(total), whole(gains), whole(gone), whole(gtwo)] + [part] * 5,
        out_specs=(smem_spec(), smem_spec(), part, part, part, part, whole(gone), whole(gtwo)),
    )(step, total, gains, gone, gtwo, grad, master, one, two, teacher)


def body(
    patches,
    segments,
    positions,
    owners,
    master,
    moment_one,
    moment_two,
    teacher,
    gains,
    gain_one,
    gain_two,
    teacher_gains,
    step_count,
):
    core = lax.axis_index("group")
    width = patches.shape[3]
    slots = patches.shape[2]
    row_total = owners.shape[0]
    inner = (row_total - 6 * width) // 2
    places = piece_rows(owners, width, inner)
    spots = places // SUBLANES * TILE + places % SUBLANES
    chips = lax.axis_size("dp")
    devices = lax.axis_size("group") * chips
    own_rows = row_total // devices

    if chips <= KERNEL_CHIPS:
        model = gather_weights(master, teacher, chips)
    else:
        parts = lax.all_gather(jnp.stack([teacher, master]).astype(BF), ("dp", "group"), axis=1)
        model = jnp.where(core == 1, parts[1], parts[0]).reshape(chips, 2, own_rows, width)
    w = place_weights(spots, model)
    w_far = lax.ppermute(w, "group", [(1, 0)])
    patch = patches[:, 0]
    seg = segments
    pos = positions
    e, qkv, lse, mixed, x1, x2, tgt, bank = forward(patch, seg, pos, gains, teacher_gains, w)
    (e, qkv, lse, mixed, x1, x2, tgt), banks = exchange_states((e, qkv, lse, mixed, x1, x2, tgt), bank, chips)
    head, attn, ffn, act, de, mid, pred, dqkv, du, down, small = backward(
        seg, pos, gains, lse, banks, e, qkv, x1, x2, tgt, w, w_far
    )
    blocked = weight_grads(
        places, (patch, mixed, head, attn, ffn, act), (de, mid, pred, dqkv, du, down), devices
    )
    if chips <= KERNEL_CHIPS:
        owned_grad, total = reduce_grads(blocked.reshape(2, chips, own_rows, width), small, chips)
    else:
        owned_grad = lax.psum_scatter(blocked, ("group", "dp"), scatter_dimension=0, tiled=True)
        owned_grad = owned_grad.reshape(own_rows, width).astype(F32)
        squares = jnp.sum(owned_grad * owned_grad, axis=0, keepdims=True)
        row_id = lax.broadcasted_iota(jnp.int32, small.shape, 0)
        total = lax.psum(jnp.where(row_id == 5, squares, small), ("group", "dp"))
    return update(
        step_count, total, gains, gain_one, gain_two, owned_grad, master, moment_one, moment_two, teacher
    )


def solution(mesh):
    rows = P(("group", "dp"), None)
    in_specs = (
        P(None, "dp", None, None),
        P(None, "dp", None),
        P(None, "dp", None),
        P(),
        rows,
        rows,
        rows,
        rows,
        P(),
        P(),
        P(),
        P(),
        P(),
    )
    out_specs = (P(), P(), rows, rows, rows, rows, P(), P())
    return jax.shard_map(body, mesh=mesh, in_specs=in_specs, out_specs=out_specs, check_vma=False)
```
